32 devices in a mesh: groups: 2 (over y), slide: 4 (over z), rep: 2 (over x), chan: 2 (over core).
Axes of the slice: x: 2, y: 2, z: 4, core: 2. Of those that a mesh axis runs over, the one named last changes fastest.
Arguments:
- tile_pixels: bfloat16 [4, 64, 6144], P(('groups', 'rep'), ('slide', 'chan')), parts along dimension 0, may hold values from -6 to 6
- tile_cell: int32 [4, 64], P(('groups', 'rep'), ('slide', 'chan')), parts along dimension 0, may hold values from -1 to 2047, as said below
- agg_cot: float32 [4, 64, 192, 128], P(('groups', 'rep'), 'slide', 'chan'), parts along dimension 0, may hold values from -6 to 6
- dw_weight: float32 [49, 96], replicated, may hold values from -0.6 to 0.6
- norm_gain: float32 [96], replicated, may hold values from 0.25 to 1.75
- up_weight: bfloat16 [96, 384], replicated, may hold values from -0.625 to 0.625
- proj_weight: bfloat16 [384, 96], replicated, may hold values from -0.3125 to 0.3125
- layer_scale: float32 [96], replicated, may hold values from 0.3 to 1
- ds_gain: float32 [96], replicated, may hold values from 0.25 to 1.75
- ds_weight: bfloat16 [384, 192], replicated, may hold values from -0.3125 to 0.3125
- agg_weight: bfloat16 [9, 192, 192], P(None, None, 'chan'), may hold values from -0.15625 to 0.15625
Outputs:
- agg_map: bfloat16 [4, 64, 192, 128], P(('groups', 'rep'), 'slide', 'chan'), parts along dimension 0
- agg_grad: float32 [18, 192, 192], P('groups', None, 'chan'), parts along dimension 0
- dw_grad: float32 [98, 96], P('groups'), parts along dimension 0
- up_grad: float32 [192, 384], P('groups'), parts along dimension 0
- proj_grad: float32 [768, 96], P('groups'), parts along dimension 0
- ds_grad: float32 [768, 192], P('groups'), parts along dimension 0
The draws below stay inside these ranges and needn't reach their ends.
There are 2 independent parts, one for each index of `groups`. The reference program is written for one: setup_inputs(seed, part) draws one part's arguments, and reference() takes and returns one part's arrays. A program takes and returns all parts, laid end to end along the dimension named above; an argument that names none is the same for every part. Nothing has to cross between parts.
Inputs may be any that keep to these rules, and one draw needn't show every extreme that they name: `tile_cell`: A value r * 64 + q names a tile of grid row r and column q of a 32 x 64 slide grid; -1 marks an empty slot. No cell appears twice in one slide. Of the slots of one device (8 consecutive slots), at most 2 lie in one band of 8 tile rows, and in every slide one band holds exactly 2 tiles from every device.
All inputs are finite; a program needn't handle non-finite values.
Results may differ from the reference program's by a relative error of at most 0.018.
Values may be sent and summed in bfloat16 or wider, within the bound.
No kernel may reach another device: no remote copies, remote signals or barrier semaphores. Data moves between devices by JAX's collectives and lax.ppermute only.
A program may use at most 128 MiB of HBM per device.

```python
import math
import jax
import jax.numpy as jnp
from jax import lax

CH = 96
HID = 384
AGG_CH = 192
TILE_SIDE = 8
TILE_DEV = 8
CAP = 2
GR = 8
GW = 64
SLIDES = 2
SOURCES = 8
SLOTS = 64
BANDS = 4
BAND_CELLS = 512
FEAT = 3072
PIXCH = 6144
ROWS_OUT = 64
COLS_OUT = 128
N_CHAN = 2


def last_first(subkey):
    order = jax.random.permutation(subkey, BAND_CELLS).astype(jnp.int32)
    where_last = jnp.argmax((order == BAND_CELLS - 1).astype(jnp.int32)).astype(jnp.int32)
    first_value = order[0]
    order = order.at[where_last].set(first_value)
    return order.at[0].set(BAND_CELLS - 1)


def draw_tile_cell(key, part):
    subkeys = jax.random.split(key, 6)
    source_ids = jnp.arange(SOURCES, dtype=jnp.int32)
    slot_ids = jnp.arange(TILE_DEV, dtype=jnp.int32)
    pair_ids = slot_ids // CAP
    rank_ids = slot_ids % CAP
    other_count = max(BANDS - 1, 1)
    full_band = jax.random.randint(subkeys[0], (SLIDES, 1, 1), 0, BANDS)
    offsets = jax.random.randint(subkeys[1], (SLIDES, SOURCES, 1), 0, other_count)
    forced = (BANDS - 2 - full_band) % BANDS % other_count
    offsets = jnp.where(source_ids[None, :, None] == 0, forced, offsets)
    other_band = (full_band + 1 + (offsets + pair_ids[None, None, :] - 1) % other_count) % BANDS
    dest_band = jnp.where(pair_ids[None, None, :] == 0, full_band, other_band)
    kept_slots = jax.random.randint(subkeys[2], (SLIDES, SOURCES, TILE_DEV), 0, 32) > 0
    fullest = jax.random.randint(subkeys[3], (SLIDES, 1, 1), 0, SOURCES)
    first_pairs = (source_ids[None, :, None] == 0) & (pair_ids[None, None, :] <= 1)
    live_slots = kept_slots | (pair_ids[None, None, :] == 0) | (source_ids[None, :, None] == fullest) | first_pairs
    live_slots = live_slots & (pair_ids[None, None, :] < BANDS)
    order_keys = jax.random.split(subkeys[4], SLIDES * BANDS)
    band_orders = jax.vmap(last_first)(order_keys)
    band_orders = band_orders.reshape(SLIDES, BANDS, BAND_CELLS).astype(jnp.int32)
    cell_rank = source_ids[:, None] * CAP + rank_ids[None, :]
    slide_ids = jnp.arange(SLIDES, dtype=jnp.int32)[:, None, None]
    local_cell = band_orders[slide_ids, dest_band, cell_rank[None, :, :]]
    cell_ids = jnp.where(live_slots, dest_band * BAND_CELLS + local_cell, -1)
    shuffle_keys = jax.random.split(subkeys[5], SLIDES * SOURCES)
    slot_orders = jax.vmap(lambda subkey: jax.random.permutation(subkey, TILE_DEV))(shuffle_keys)
    slot_orders = slot_orders.reshape(SLIDES, SOURCES, TILE_DEV)
    cell_ids = jnp.take_along_axis(cell_ids, slot_orders, axis=2)
    return cell_ids.reshape(SLIDES, SOURCES * TILE_DEV).astype(jnp.int32)


def shard_levels(own_key, shape, cuts, smallest, largest):
    def one(axis_at, blocks):
        heights = jax.random.uniform(jax.random.fold_in(jax.random.fold_in(own_key, 6), axis_at), (blocks,), jnp.float32, smallest / len(cuts), largest / len(cuts))
        return jnp.repeat(jnp.exp(heights), shape[axis_at] // blocks).reshape((-1,) + (1,) * (len(shape) - axis_at - 1))

    level = one(*cuts[0])
    for cut in cuts[1:]:
        level = level * one(*cut)
    return level


def scatter_about(rng, shape, scale, most, pieces=(), kind=jnp.bfloat16):
    values = jax.random.normal(rng, shape, jnp.float32) * scale
    if len(pieces) > 0:
        values = shard_levels(rng, shape, pieces, -0.22, 0.18) * values
    return jnp.clip(values, min=-most, max=most).astype(kind)


def setup_inputs(seed: int = 0, part: int = 0) -> dict:
    seeds = jax.random.split(jax.random.key(seed), 12)
    part_splits = jax.random.split(jax.random.fold_in(seeds[11], part), 12)
    tile_pixels = scatter_about(part_splits[0], (SLIDES, SLOTS, PIXCH), 1.0, 6.0, ((0, 2), (1, 8)))
    tile_cell = draw_tile_cell(jax.random.fold_in(jax.random.fold_in(seeds[11], part), 71), part)
    agg_cot = scatter_about(part_splits[2], (SLIDES, ROWS_OUT, AGG_CH, COLS_OUT), 1.0, 6.0, ((0, 2), (1, 4), (2, 2)), jnp.float32)
    dw_weight = scatter_about(seeds[3], (49, CH), 0.15, 0.6, (), jnp.float32)
    norm_gain = jnp.clip(1.0 + 0.15 * jax.random.normal(seeds[4], (CH,), jnp.float32), 0.25, 1.75)
    up_weight = scatter_about(seeds[5], (CH, HID), CH ** -0.5, 0.625)
    proj_weight = scatter_about(seeds[6], (HID, CH), HID ** -0.5, 0.3125)
    layer_scale = jnp.clip(jnp.exp(jax.random.uniform(seeds[7], (CH,), jnp.float32, math.log(0.3), math.log(1.0))), 0.3, 1.0)
    ds_gain = jnp.clip(1.0 + 0.15 * jax.random.normal(seeds[8], (CH,), jnp.float32), 0.25, 1.75)
    ds_weight = scatter_about(seeds[9], (4 * CH, AGG_CH), (4 * CH) ** -0.5, 0.3125)
    agg_weight = scatter_about(seeds[10], (9, AGG_CH, AGG_CH), (9 * AGG_CH) ** -0.5, 0.15625, ((2, 2),))
    return dict(tile_pixels=tile_pixels, tile_cell=tile_cell, agg_cot=agg_cot, dw_weight=dw_weight, norm_gain=norm_gain, up_weight=up_weight, proj_weight=proj_weight, layer_scale=layer_scale, ds_gain=ds_gain, ds_weight=ds_weight, agg_weight=agg_weight)


def layer_norm(values, gain):
    center = values - lax.optimization_barrier(jnp.mean(values, axis=-1, keepdims=True))
    spread = lax.optimization_barrier(jnp.mean(center * center, axis=-1, keepdims=True))
    return center * lax.rsqrt(spread + 1e-06) * gain

def stem(params, tile_rows):
    dw_weight, norm_gain, up_weight, proj_weight, layer_scale, ds_gain, ds_weight = params
    tile_count = tile_rows.shape[0]
    tile_side = TILE_SIDE
    channels = dw_weight.shape[1]
    inputs = tile_rows.reshape(tile_count, tile_side, tile_side, channels).astype(jnp.float32)
    padded = jnp.pad(inputs, ((0, 0), (3, 3), (3, 3), (0, 0)))
    spatial = jnp.zeros_like(inputs)
    for row_tap in range(7):
        for col_tap in range(7):
            spatial = spatial + dw_weight[row_tap * 7 + col_tap] * padded[:, row_tap:row_tap + tile_side, col_tap:col_tap + tile_side, :]
    normed = layer_norm(spatial, norm_gain).reshape(tile_count * tile_side * tile_side, channels).astype(jnp.bfloat16)
    hidden = jax.nn.gelu(jnp.dot(normed, up_weight, preferred_element_type=jnp.float32), approximate=False).astype(jnp.bfloat16)
    branch = jnp.dot(hidden, proj_weight, preferred_element_type=jnp.float32)
    mixed_rows = inputs.reshape(tile_count * tile_side * tile_side, channels) + layer_scale * branch
    lowered = layer_norm(mixed_rows, ds_gain).astype(jnp.bfloat16)
    half_side = tile_side // 2
    patches = lowered.reshape(tile_count, half_side, 2, half_side, 2, channels).transpose(0, 1, 3, 2, 4, 5)
    patches = patches.reshape(tile_count * half_side * half_side, 4 * channels)
    result = jnp.dot(patches, ds_weight, preferred_element_type=jnp.float32)
    return result.reshape(tile_count, half_side * half_side * ds_weight.shape[1])

def aggregate(padded, weight_half):
    out_rows = (padded.shape[0] - 1) // 2
    out_cols = (padded.shape[1] - 1) // 2
    accumulated = jnp.zeros((out_rows * out_cols, weight_half.shape[2]), jnp.float32)
    for row_tap in range(3):
        for col_tap in range(3):
            window = padded[row_tap:row_tap + 2 * out_rows - 1:2, col_tap:col_tap + 2 * out_cols - 1:2, :]
            accumulated = accumulated + jnp.dot(window.reshape(out_rows * out_cols, padded.shape[2]), weight_half[row_tap * 3 + col_tap], preferred_element_type=jnp.float32)
    return accumulated.reshape(out_rows, out_cols, weight_half.shape[2])

def band_vjp(padded, weight_half, cotangent):
    result, pull_back = jax.vjp(aggregate, padded, weight_half)
    d_padded, d_weight = pull_back(cotangent)
    return (result, d_padded, d_weight)

def grads_of(params, tile_rows, cotangent):
    result, pull_back = jax.vjp(lambda chosen: stem(chosen, tile_rows), params)
    stem_grads = pull_back(cotangent)[0]
    return (stem_grads[0].astype(jnp.float32), stem_grads[2].astype(jnp.float32), stem_grads[3].astype(jnp.float32), stem_grads[6].astype(jnp.float32))

def reference(tile_pixels, tile_cell, agg_cot, dw_weight, norm_gain, up_weight, proj_weight, layer_scale, ds_gain, ds_weight, agg_weight):
    params = (dw_weight, norm_gain, up_weight, proj_weight, layer_scale, ds_gain, ds_weight)
    groups = SLIDES * SOURCES
    grouped = tile_pixels.reshape(groups, TILE_DEV, PIXCH)
    features = lax.map(lambda tile_rows: stem(params, tile_rows).astype(jnp.bfloat16), grouped).reshape(SLIDES, SLOTS, FEAT)
    feat_side = TILE_SIDE // 2
    band_rows = GR * feat_side
    out_rows = band_rows // 2
    half_width = AGG_CH // N_CHAN
    loss_scale = 1.0 / math.sqrt(SLIDES * ROWS_OUT * COLS_OUT)
    all_cells = BANDS * BAND_CELLS

    def per_slide_half(flat_index):
        slide_index = flat_index // N_CHAN
        half_index = flat_index % N_CHAN
        cell_ids = tile_cell[slide_index]
        placed = jnp.where(cell_ids >= 0, cell_ids, all_cells)
        cells_map = jnp.zeros((all_cells, FEAT), jnp.bfloat16).at[placed].set(features[slide_index], mode='drop')
        band_grid = cells_map.reshape(BANDS, GR, GW, feat_side, feat_side, AGG_CH).transpose(0, 1, 3, 2, 4, 5)
        band_grid = band_grid.reshape(BANDS, band_rows, GW * feat_side, AGG_CH)
        top_rows = jnp.concatenate([jnp.zeros_like(band_grid[:1, -1]), band_grid[:-1, -1]], axis=0)
        padded = jnp.concatenate([top_rows[:, None], band_grid], axis=1)
        padded = jnp.pad(padded, ((0, 0), (0, 0), (1, 0), (0, 0)))
        weight_half = lax.dynamic_slice_in_dim(agg_weight, half_index * half_width, half_width, 2)
        cot_slide = lax.dynamic_slice_in_dim(agg_cot[slide_index], half_index * half_width, half_width, 1)
        cot_bands = cot_slide.reshape(BANDS, out_rows, half_width, COLS_OUT).transpose(0, 1, 3, 2) * loss_scale
        results, d_padded, d_weight = lax.map(lambda operands: band_vjp(operands[0], weight_half, operands[1]), (padded, cot_bands))
        top_grads = d_padded[:, 0, 1:]
        band_grads = d_padded[:, 1:, 1:]
        from_below = jnp.concatenate([top_grads[1:], jnp.zeros_like(top_grads[:1])], axis=0)
        map_grad = band_grads.astype(jnp.float32).at[:, -1].add(from_below.astype(jnp.float32)).astype(jnp.bfloat16)
        grad_cells = map_grad.reshape(BANDS, GR, feat_side, GW, feat_side, AGG_CH).transpose(0, 1, 3, 2, 4, 5).reshape(all_cells, FEAT)
        slot_grads = jnp.where((cell_ids >= 0)[:, None], grad_cells[jnp.clip(cell_ids, 0, all_cells - 1)], jnp.zeros((), jnp.bfloat16))
        maps_out = results.astype(jnp.bfloat16).transpose(0, 1, 3, 2)
        return (maps_out, slot_grads, lax.optimization_barrier(jnp.sum(d_weight.astype(jnp.float32), axis=0)))
    all_maps, slot_grads, weight_parts = lax.map(per_slide_half, jnp.arange(SLIDES * N_CHAN, dtype=jnp.int32))
    agg_map = all_maps.reshape(SLIDES, N_CHAN, BANDS, out_rows, half_width, COLS_OUT).transpose(0, 2, 3, 1, 4, 5)
    agg_map = agg_map.reshape(SLIDES, ROWS_OUT, AGG_CH, COLS_OUT)
    feature_grad = lax.optimization_barrier(jnp.sum(slot_grads.reshape(SLIDES, N_CHAN, SLOTS, FEAT).astype(jnp.float32), axis=1))
    agg_grad = lax.optimization_barrier(jnp.sum(weight_parts.reshape(SLIDES, N_CHAN, 9, AGG_CH, half_width), axis=0)).transpose(1, 2, 0, 3).reshape(9, AGG_CH, AGG_CH)
    stem_parts = lax.map(lambda operands: grads_of(params, operands[0], operands[1]), (grouped, feature_grad.reshape(groups, TILE_DEV, FEAT)))
    dw_grad = lax.optimization_barrier(jnp.sum(stem_parts[0], axis=0))
    up_grad = lax.optimization_barrier(jnp.sum(stem_parts[1], axis=0))
    proj_grad = lax.optimization_barrier(jnp.sum(stem_parts[2], axis=0))
    ds_grad = lax.optimization_barrier(jnp.sum(stem_parts[3], axis=0))
    return (agg_map, agg_grad, dw_grad, up_grad, proj_grad, ds_grad)
```

```python
import math

import jax
import jax.numpy as jnp
from jax import lax
from jax.experimental import pallas as pl
from jax.experimental.pallas import tpu as pltpu
from jax.sharding import PartitionSpec as P

SIDE = 8
CAP = 2
GW = 64
BAND_CELLS = 512
PIX = SIDE * SIDE
META = 128
HALF_ROWS = 656
GATHER_LIMIT = 16 << 20
F32 = jnp.float32
BF16 = jnp.bfloat16
VMEM = pl.BlockSpec(memory_space=pltpu.VMEM)
SMEM = pl.BlockSpec(memory_space=pltpu.SMEM)


def params_of(steps=1):
    return pltpu.CompilerParams(
        dimension_semantics=("arbitrary",) * steps, vmem_limit_bytes=48 << 20
    )


def nn(left, right):
    return lax.dot_general(left, right, (((1,), (0,)), ((), ())), preferred_element_type=F32)


def nt(left, right):
    return lax.dot_general(left, right, (((1,), (1,)), ((), ())), preferred_element_type=F32)


def tn(left, right):
    return lax.dot_general(left, right, (((0,), (0,)), ((), ())), preferred_element_type=F32)


def shifted(value, axis, steps):
    count = lax.axis_size(axis)
    first, last = (max(0, -steps), min(count, count - steps))
    return lax.ppermute(value, axis, [(source, source + steps) for source in range(first, last)])


def swapped(value, axis, step):
    count = lax.axis_size(axis)
    return lax.ppermute(value, axis, [(place, place ^ step) for place in range(count)])


def reach(tap):
    return (1, 2) if tap == 0 else (0, 1)


def pack_kernel(cells_ref, pixels_ref, out_ref):
    slots = pixels_ref.shape[0]
    rows = out_ref.shape[0]
    pixch = pixels_ref.shape[1]
    cells = [cells_ref[0, t] for t in range(slots)]
    live = [cell >= 0 for cell in cells]
    bands = [cell // BAND_CELLS for cell in cells]
    places = []
    for t in range(slots):
        rank = jnp.int32(0)
        for s in range(t):
            rank = rank + ((bands[s] == bands[t]) & live[s]).astype(jnp.int32)
        places.append(jnp.where(live[t], bands[t] * CAP + rank, -1))
    dest = lax.broadcasted_iota(jnp.int32, (rows, slots), 0)
    slot = lax.broadcasted_iota(jnp.int32, (rows, slots), 1)
    place = jnp.full((rows, slots), -1, jnp.int32)
    for t in range(slots):
        place = jnp.where(slot == t, places[t], place)
    route = (place == dest).astype(F32).astype(BF16)
    out_ref[:, :pixch] = nn(route, pixels_ref[...]).astype(BF16)
    lane = lax.broadcasted_iota(jnp.int32, (rows, META), 1)
    base = (lax.broadcasted_iota(jnp.int32, (rows, META), 0) // CAP) * CAP
    notes = jnp.zeros((rows, META), F32)
    for t in range(slots):
        within = cells[t] % BAND_CELLS
        own_row = (within // GW).astype(F32)
        own_col = (within % GW).astype(F32)
        for rank in range(CAP):
            hit = base + rank == places[t]
            for at, value in enumerate((own_row, own_col, jnp.float32(1.0))):
                notes = jnp.where(hit & (lane == 3 * rank + at), value, notes)
    out_ref[:, pixch:] = notes.astype(BF16)


def patch_kernel(chan_ref, meta_ref, cot_ref, below_ref, key_ref, all_ref, own_ref, send_ref):
    sources = meta_ref.shape[0]
    chunks = sources // 8
    out_rows = cot_ref.shape[0]
    meta = meta_ref[...].astype(F32)
    lane = lax.broadcasted_iota(jnp.int32, (8, 128), 1).astype(F32)
    blocks = []
    for rank in range(CAP):
        for chunk in range(chunks):
            part = meta[chunk * 8 : chunk * 8 + 8]
            row = jnp.broadcast_to(part[:, 3 * rank : 3 * rank + 1], (8, 128))
            col = jnp.broadcast_to(part[:, 3 * rank + 1 : 3 * rank + 2], (8, 128))
            valid = jnp.broadcast_to(part[:, 3 * rank + 2 : 3 * rank + 3], (8, 128)) > 0.5
            for u in range(3):
                for v in range(3):
                    hit = (lane == 2.0 * col + v) & valid
                    blocks.append(jnp.where(hit, 2.0 * row + u, -1.0))
    key = jnp.concatenate(blocks, axis=0)
    key_ref[...] = key

    def step(o, total):
        pick = (key == o.astype(F32)).astype(F32).astype(BF16)
        return total + nt(pick, cot_ref[o].astype(BF16))

    total = lax.fori_loop(
        0, out_rows, step, jnp.zeros((key.shape[0], cot_ref.shape[1]), F32), unroll=4
    )
    pick = (key == float(out_rows)).astype(F32).astype(BF16)
    total = total + nt(pick, below_ref[...])
    total = total.astype(BF16)
    all_ref[...] = total
    half = total.shape[0] // CAP
    first = chan_ref[0] == 0
    low, high = total[:half].astype(F32), total[half:].astype(F32)
    own_ref[...] = jnp.where(first, low, high).astype(BF16)
    send_ref[...] = jnp.where(first, high, low).astype(BF16)


def center_of(values):
    center = values - jnp.mean(values, axis=-1, keepdims=True)
    rstd = lax.rsqrt(jnp.mean(center * center, axis=-1, keepdims=True) + 1e-06)
    return center * rstd, rstd


def fill_padded(padded_ref, pixels_ref, channels):
    padded_ref[...] = jnp.zeros_like(padded_ref)
    for i in range(SIDE):
        for j in range(SIDE):
            at = (i * SIDE + j) * channels
            padded_ref[i + 3, j + 3] = pixels_ref[:, at : at + channels].astype(F32)


def stem_kernel(
    pixels_ref, dw_ref, gain_ref, up_ref, proj_ref, scale_ref, ds_gain_ref, ds_ref,
    feat_ref, hat1_ref, rstd1_ref, hat2_ref, rstd2_ref, hidden_ref, slope_ref,
    padded_ref, spatial_ref, low_ref,
):
    channels = dw_ref.shape[1]
    fill_padded(padded_ref, pixels_ref, channels)

    def row_step(i, carry):
        total = jnp.zeros((SIDE, 8, channels), F32)
        for a in range(7):
            for b in range(7):
                weight = dw_ref[pl.ds(7 * a + b, 1), :].reshape(1, 1, channels)
                total = total + weight * padded_ref[i + a, b : b + SIDE]
        spatial_ref[i] = total
        return carry

    lax.fori_loop(0, SIDE, row_step, 0)
    hat1, rstd1 = center_of(spatial_ref[...].reshape(PIX * 8, channels))
    hat1_ref[...] = hat1
    rstd1_ref[...] = rstd1
    normed = (hat1 * gain_ref[...]).astype(BF16)
    before = nn(normed, up_ref[...])
    cdf = 0.5 * (1.0 + lax.erf(before * math.sqrt(0.5)))
    pdf = jnp.exp(-0.5 * before * before) * (1.0 / math.sqrt(2.0 * math.pi))
    hidden = (before * cdf).astype(BF16)
    hidden_ref[...] = hidden
    slope_ref[...] = cdf + before * pdf
    branch = nn(hidden, proj_ref[...])
    inputs = padded_ref[3 : 3 + SIDE, 3 : 3 + SIDE].reshape(PIX * 8, channels)
    hat2, rstd2 = center_of(inputs + scale_ref[...] * branch)
    hat2_ref[...] = hat2
    rstd2_ref[...] = rstd2
    low_ref[...] = (hat2 * ds_gain_ref[...]).reshape(low_ref.shape)
    half = SIDE // 2
    total = jnp.zeros((half * half * 8, ds_ref.shape[1]), F32)
    for di in range(2):
        for dj in range(2):
            part = low_ref[:, di, :, dj].reshape(half * half * 8, channels).astype(BF16)
            at = (2 * di + dj) * channels
            total = total + nn(part, ds_ref[at : at + channels])
    feat_ref[...] = total.astype(BF16)


def back_kernel(
    chan_ref, own_ref, peer_ref, w_own_ref, w_peer_ref, pixels_ref,
    hat1_ref, rstd1_ref, hat2_ref, rstd2_ref, hidden_ref, slope_ref,
    gain_ref, up_ref, proj_ref, scale_ref, ds_gain_ref, ds_ref,
    keep_ref, send_ref,
    padded_ref, low_ref, dlow_ref, dspatial_ref, dw_ref, ds_acc, up_acc, proj_acc, pack_ref,
    *, scale,
):
    channels = gain_ref.shape[1]
    width = w_own_ref.shape[1]
    half = SIDE // 2
    step = pl.program_id(0)

    @pl.when(step == 0)
    def _():
        dw_ref[...] = jnp.zeros_like(dw_ref)
        ds_acc[...] = jnp.zeros_like(ds_acc)
        up_acc[...] = jnp.zeros_like(up_acc)
        proj_acc[...] = jnp.zeros_like(proj_acc)

    own = own_ref[...].astype(F32).reshape(9, 8, own_ref.shape[1])
    peer = peer_ref[...].astype(F32).reshape(9, 8, peer_ref.shape[1])
    grads = {}
    for a in range(3):
        for b in range(3):
            places = [(u, v) for u in reach(a) for v in reach(b)]
            left_own = jnp.concatenate([own[3 * u + v] for u, v in places], axis=0).astype(BF16)
            left_peer = jnp.concatenate([peer[3 * u + v] for u, v in places], axis=0).astype(BF16)
            out = nt(left_own, w_own_ref[3 * a + b]) + nt(left_peer, w_peer_ref[3 * a + b])
            for n, (u, v) in enumerate(places):
                at = (2 * u + a - 1) * half + 2 * v + b - 1
                piece = out[8 * n : 8 * n + 8]
                grads[at] = grads[at] + piece if at in grads else piece
    dfeat = jnp.concatenate([grads[at] for at in range(half * half)], axis=0) * scale
    dfeat = dfeat.astype(BF16)

    hat2 = hat2_ref[...]
    low_ref[...] = (hat2 * ds_gain_ref[...]).reshape(low_ref.shape)
    for di in range(2):
        for dj in range(2):
            at = (2 * di + dj) * channels
            part = low_ref[:, di, :, dj].reshape(half * half * 8, channels).astype(BF16)
            ds_acc[at : at + channels, :] += tn(part, dfeat)
            back = nt(dfeat, ds_ref[at : at + channels])
            dlow_ref[:, di, :, dj] = back.reshape(half, half, 8, channels)
    dhat2 = dlow_ref[...].reshape(PIX * 8, channels) * ds_gain_ref[...]
    mean_a = jnp.mean(dhat2, axis=-1, keepdims=True)
    mean_b = jnp.mean(dhat2 * hat2, axis=-1, keepdims=True)
    dmixed = rstd2_ref[...] * (dhat2 - mean_a - hat2 * mean_b)
    dbranch = (dmixed * scale_ref[...]).astype(BF16)
    proj_acc[...] += tn(hidden_ref[...], dbranch)
    dhidden = nt(dbranch, proj_ref[...])
    dbefore = (dhidden * slope_ref[...]).astype(BF16)
    hat1 = hat1_ref[...]
    normed = (hat1 * gain_ref[...]).astype(BF16)
    up_acc[...] += tn(normed, dbefore)
    dhat1 = nt(dbefore, up_ref[...]) * gain_ref[...]
    mean_a = jnp.mean(dhat1, axis=-1, keepdims=True)
    mean_b = jnp.mean(dhat1 * hat1, axis=-1, keepdims=True)
    dspatial = rstd1_ref[...] * (dhat1 - mean_a - hat1 * mean_b)
    dspatial_ref[...] = dspatial.reshape(SIDE, SIDE, 8, channels)
    fill_padded(padded_ref, pixels_ref, channels)

    def tap_step(a, carry):
        totals = [jnp.zeros((8, channels), F32) for _ in range(7)]
        for i in range(SIDE):
            grad = dspatial_ref[i]
            for b in range(7):
                product = padded_ref[i + a, b : b + SIDE] * grad
                totals[b] = totals[b] + jnp.sum(product, axis=0)
        for b in range(7):
            dw_ref[a, b] += totals[b]
        return carry

    lax.fori_loop(0, 7, tap_step, 0)

    @pl.when(step == pl.num_programs(0) - 1)
    def _():
        pack_ref[...] = jnp.zeros_like(pack_ref)
        pack_ref[0:384, :] = ds_acc[:, 0:128]
        pack_ref[384:576, 0:64] = ds_acc[0:192, 128:192]
        pack_ref[384:576, 64:128] = ds_acc[192:384, 128:192]
        for n in range(3):
            pack_ref[576 + 96 * n : 672 + 96 * n, :] = up_acc[:, 128 * n : 128 * n + 128]
        pack_ref[864:1248, 0:channels] = proj_acc[...]
        pack_ref[1248:1297, 0:channels] = jnp.sum(dw_ref[...], axis=2).reshape(49, channels)
        mine = pl.multiple_of(chan_ref[0] * HALF_ROWS, 8)
        other = pl.multiple_of((1 - chan_ref[0]) * HALF_ROWS, 8)
        keep_ref[...] = pack_ref[pl.ds(mine, HALF_ROWS), :]
        send_ref[...] = pack_ref[pl.ds(other, HALF_ROWS), :].astype(BF16)


def unpack_kernel(pack_ref, dw_ref, up_ref, proj_ref, ds_ref):
    channels = dw_ref.shape[1]
    ds_ref[:, 0:128] = pack_ref[0:384, :]
    ds_ref[0:192, 128:192] = pack_ref[384:576, 0:64]
    ds_ref[192:384, 128:192] = pack_ref[384:576, 64:128]
    for n in range(3):
        up_ref[:, 128 * n : 128 * n + 128] = pack_ref[576 + 96 * n : 672 + 96 * n, :]
    proj_ref[...] = pack_ref[864:1248, 0:channels]
    dw_ref[...] = pack_ref[1248:1297, 0:channels]


def spread_kernel(feat_ref, w_ref, key_ref, y_ref, below_ref, *, last):
    width = feat_ref.shape[1]
    feats = feat_ref[...].astype(F32).reshape(16, 8, width)
    outs = {}
    for a in range(3):
        for b in range(3):
            places = [(u, v) for u in reach(a) for v in reach(b)]
            left = jnp.concatenate(
                [feats[(2 * u + a - 1) * 4 + 2 * v + b - 1] for u, v in places], axis=0
            ).astype(BF16)
            out = nn(left, w_ref[3 * a + b])
            for n, (u, v) in enumerate(places):
                piece = out[8 * n : 8 * n + 8]
                at = 3 * u + v
                outs[at] = outs[at] + piece if at in outs else piece
    total = jnp.concatenate([outs[at] for at in range(9)], axis=0)
    y_ref[...] = total
    pick = (key_ref[...] == float(last)).astype(F32).astype(BF16)
    high = total.astype(BF16)
    rest = (total - high.astype(F32)).astype(BF16)

    @pl.when(pl.program_id(0) == 0)
    def _():
        below_ref[...] = jnp.zeros_like(below_ref)

    below_ref[...] += tn(high, pick) + tn(rest, pick)


def map_kernel(y_ref, key_ref, above_ref, out_ref):
    out_rows, width, _ = out_ref.shape
    turned = y_ref[...].T
    high = turned.astype(BF16)
    rest = (turned - high.astype(F32)).astype(BF16)
    key = key_ref[...]

    def row_of(o):
        pick = (key == o).astype(F32).astype(BF16)
        return nn(high, pick) + nn(rest, pick)

    out_ref[0] = (row_of(0.0) + above_ref[...]).astype(BF16)

    def step(o, carry):
        out_ref[o] = row_of(o.astype(F32)).astype(BF16)
        return carry

    lax.fori_loop(1, out_rows, step, 0)


def weight_kernel(feat_ref, cot_ref, out_ref, feat_t_ref, cot_t_ref, *, scale):
    blocks = feat_ref.shape[0]
    width = feat_ref.shape[2]
    step = pl.program_id(0)

    @pl.when(step == 0)
    def _():
        out_ref[...] = jnp.zeros_like(out_ref)

    for n in range(blocks):
        feats = feat_ref[n].astype(F32).reshape(16, 8, width)
        cots = cot_ref[n].astype(F32).reshape(9, 8, cot_ref.shape[2])
        feat_t_ref[:, 8 * n : 8 * n + 8] = feats
        cot_t_ref[:, 8 * n : 8 * n + 8] = cots
    turned = [feat_t_ref[p].T.astype(BF16) for p in range(16)]
    cots = [cot_t_ref[p].astype(BF16) for p in range(9)]
    for a in range(3):
        for b in range(3):
            total = None
            for u in reach(a):
                for v in reach(b):
                    p = (2 * u + a - 1) * 4 + 2 * v + b - 1
                    piece = nn(turned[p], cots[3 * u + v])
                    total = piece if total is None else total + piece
            out_ref[3 * a + b] += total * scale


def whole(shape):
    return pl.BlockSpec(shape, lambda g: (0,) * len(shape))


def on_device(
    tile_pixels, tile_cell, agg_cot, dw_weight, norm_gain, up_weight, proj_weight,
    layer_scale, ds_gain, ds_weight, agg_weight,
):
    channels = dw_weight.shape[1]
    hid = up_weight.shape[1]
    width = ds_weight.shape[1]
    bands = lax.axis_size("slide")
    sources = bands * lax.axis_size("chan")
    chunks = sources // 8
    pixch = tile_pixels.shape[2]
    out_rows = agg_cot.shape[1]
    e_half = agg_weight.shape[2]
    cols = agg_cot.shape[3]
    blocks = CAP * chunks
    total_rows = out_rows * bands * lax.axis_size("rep") * cols
    loss_scale = 1.0 / math.sqrt(total_rows)
    chan = lax.axis_index("chan").astype(jnp.int32)[None]
    gain = norm_gain[None]
    scale = layer_scale[None]
    low_gain = ds_gain[None]

    peer_weight = swapped(agg_weight, "chan", 1)
    below_cot = shifted(agg_cot[0, 0].astype(BF16), "slide", -1)

    packed = pl.pallas_call(
        pack_kernel,
        out_shape=jax.ShapeDtypeStruct((sources, pixch + META), BF16),
        in_specs=[SMEM, VMEM],
        out_specs=VMEM,
        name="pack",
    )(tile_cell, tile_pixels[0])
    got = lax.all_to_all(packed, ("slide", "chan"), split_axis=0, concat_axis=0, tiled=True)

    key, cots_all, cots_own, cots_send = pl.pallas_call(
        patch_kernel,
        out_shape=(
            jax.ShapeDtypeStruct((blocks * 72, cols), F32),
            jax.ShapeDtypeStruct((blocks * 72, e_half), BF16),
            jax.ShapeDtypeStruct((chunks * 72, e_half), BF16),
            jax.ShapeDtypeStruct((chunks * 72, e_half), BF16),
        ),
        in_specs=[
            SMEM,
            pl.BlockSpec((sources, META), lambda i: (0, pixch // META)),
            pl.BlockSpec((None, out_rows, e_half, cols), lambda i: (0, 0, 0, 0)),
            whole((e_half, cols)),
        ],
        out_specs=(
            whole((blocks * 72, cols)),
            whole((blocks * 72, e_half)),
            whole((chunks * 72, e_half)),
            whole((chunks * 72, e_half)),
        ),
        grid=(1,),
        compiler_params=params_of(),
        name="patch",
    )(chan, got, agg_cot, below_cot)
    cots_peer = swapped(cots_send, "chan", 1)

    rows = PIX * 8
    pixel_spec = pl.BlockSpec((8, pixch), lambda g: (g, 0))

    def chunk(*shape):
        return pl.BlockSpec((None,) + shape, lambda g: (g,) + (0,) * len(shape))

    feats, hat1, rstd1, hat2, rstd2, hidden, slope = pl.pallas_call(
        stem_kernel,
        grid=(chunks,),
        out_shape=(
            jax.ShapeDtypeStruct((chunks, 128, width), BF16),
            jax.ShapeDtypeStruct((chunks, rows, channels), F32),
            jax.ShapeDtypeStruct((chunks, rows, 1), F32),
            jax.ShapeDtypeStruct((chunks, rows, channels), F32),
            jax.ShapeDtypeStruct((chunks, rows, 1), F32),
            jax.ShapeDtypeStruct((chunks, rows, hid), BF16),
            jax.ShapeDtypeStruct((chunks, rows, hid), F32),
        ),
        in_specs=[
            pixel_spec,
            whole(dw_weight.shape), whole((1, channels)), whole(up_weight.shape),
            whole(proj_weight.shape), whole((1, channels)), whole((1, channels)),
            whole(ds_weight.shape),
        ],
        out_specs=(
            chunk(128, width), chunk(rows, channels), chunk(rows, 1), chunk(rows, channels),
            chunk(rows, 1), chunk(rows, hid), chunk(rows, hid),
        ),
        scratch_shapes=[
            pltpu.VMEM((SIDE + 6, SIDE + 6, 8, channels), F32),
            pltpu.VMEM((SIDE, SIDE, 8, channels), F32),
            pltpu.VMEM((SIDE // 2, 2, SIDE // 2, 2, 8, channels), F32),
        ],
        compiler_params=params_of(),
        name="stem",
    )(got, dw_weight, gain, up_weight, proj_weight, scale, low_gain, ds_weight)

    feats_band = lax.all_gather(feats, "chan", axis=0, tiled=True)

    keep, send = pl.pallas_call(
        lambda *refs: back_kernel(*refs, scale=loss_scale),
        grid=(chunks,),
        out_shape=(
            jax.ShapeDtypeStruct((HALF_ROWS, 128), F32),
            jax.ShapeDtypeStruct((HALF_ROWS, 128), BF16),
        ),
        in_specs=[
            SMEM, chunk(72, e_half), chunk(72, e_half),
            whole(agg_weight.shape), whole(agg_weight.shape), pixel_spec,
            chunk(rows, channels), chunk(rows, 1), chunk(rows, channels), chunk(rows, 1),
            chunk(rows, hid), chunk(rows, hid),
            whole((1, channels)), whole(up_weight.shape), whole(proj_weight.shape),
            whole((1, channels)), whole((1, channels)), whole(ds_weight.shape),
        ],
        out_specs=(whole((HALF_ROWS, 128)), whole((HALF_ROWS, 128))),
        scratch_shapes=[
            pltpu.VMEM((SIDE + 6, SIDE + 6, 8, channels), F32),
            pltpu.VMEM((SIDE // 2, 2, SIDE // 2, 2, 8, channels), F32),
            pltpu.VMEM((SIDE // 2, 2, SIDE // 2, 2, 8, channels), F32),
            pltpu.VMEM((SIDE, SIDE, 8, channels), F32),
            pltpu.VMEM((7, 7, 8, channels), F32),
            pltpu.VMEM(ds_weight.shape, F32),
            pltpu.VMEM(up_weight.shape, F32),
            pltpu.VMEM(proj_weight.shape, F32),
            pltpu.VMEM((2 * HALF_ROWS, 128), F32),
        ],
        compiler_params=params_of(),
        name="stem_back",
    )(
        chan, cots_own.reshape(chunks, 72, e_half), cots_peer.reshape(chunks, 72, e_half),
        agg_weight, peer_weight, got, hat1, rstd1, hat2, rstd2, hidden, slope,
        gain, up_weight, proj_weight, scale, low_gain, ds_weight,
    )

    spread, below = pl.pallas_call(
        lambda *refs: spread_kernel(*refs, last=out_rows),
        grid=(blocks,),
        out_shape=(
            jax.ShapeDtypeStruct((blocks * 72, e_half), F32),
            jax.ShapeDtypeStruct((e_half, cols), F32),
        ),
        in_specs=[
            chunk(128, width), whole(agg_weight.shape),
            pl.BlockSpec((72, cols), lambda g: (g, 0)),
        ],
        out_specs=(pl.BlockSpec((72, e_half), lambda g: (g, 0)), whole((e_half, cols))),
        compiler_params=params_of(),
        name="spread",
    )(feats_band, agg_weight, key)
    above = shifted(below, "slide", 1)
    agg_map = pl.pallas_call(
        map_kernel,
        out_shape=jax.ShapeDtypeStruct((out_rows, e_half, cols), BF16),
        in_specs=[VMEM, VMEM, VMEM],
        out_specs=VMEM,
        compiler_params=pltpu.CompilerParams(vmem_limit_bytes=48 << 20),
        name="agg_map",
    )(spread, key, above)[None]

    cots_blocks = cots_all.reshape(blocks, 72, e_half)
    members = bands * lax.axis_size("rep")
    gather = members * blocks * 128 * width * 2 <= GATHER_LIMIT
    feats_in, cots_in = feats_band, cots_blocks
    if gather:
        feats_in = lax.all_gather(feats_band, ("slide", "rep"), axis=0, tiled=True)
        cots_in = lax.all_gather(cots_blocks, ("slide", "rep"), axis=0, tiled=True)
    count = feats_in.shape[0]
    per = min(count, 16)
    agg_grad = pl.pallas_call(
        lambda *refs: weight_kernel(*refs, scale=loss_scale),
        grid=(count // per,),
        out_shape=jax.ShapeDtypeStruct((9, width, e_half), F32),
        in_specs=[
            pl.BlockSpec((per, 128, width), lambda g: (g, 0, 0)),
            pl.BlockSpec((per, 72, e_half), lambda g: (g, 0, 0)),
        ],
        out_specs=whole((9, width, e_half)),
        scratch_shapes=[
            pltpu.VMEM((16, per * 8, width), F32),
            pltpu.VMEM((9, per * 8, e_half), F32),
        ],
        compiler_params=params_of(),
        name="agg_weight_grad",
    )(feats_in, cots_in)
    if not gather:
        agg_grad = lax.psum(agg_grad, ("slide", "rep"))

    part = keep + swapped(send, "chan", 1).astype(F32)
    for axis in ("rep", "slide"):
        step = 1
        while step < lax.axis_size(axis):
            wire = part.astype(BF16)
            part = wire.astype(F32) + swapped(wire, axis, step).astype(F32)
            step *= 2
    full = lax.all_gather(part, "chan", axis=0, tiled=True)
    dw_grad, up_grad, proj_grad, ds_grad = pl.pallas_call(
        unpack_kernel,
        out_shape=(
            jax.ShapeDtypeStruct(dw_weight.shape, F32),
            jax.ShapeDtypeStruct(up_weight.shape, F32),
            jax.ShapeDtypeStruct(proj_weight.shape, F32),
            jax.ShapeDtypeStruct(ds_weight.shape, F32),
        ),
        in_specs=[VMEM],
        out_specs=(VMEM, VMEM, VMEM, VMEM),
        name="unpack",
    )(full)
    return (agg_map, agg_grad, dw_grad, up_grad, proj_grad, ds_grad)


def solution(mesh):
    in_specs = (
        P(("groups", "rep"), ("slide", "chan"), None),
        P(("groups", "rep"), ("slide", "chan")),
        P(("groups", "rep"), "slide", "chan", None),
        P(), P(), P(), P(), P(), P(), P(),
        P(None, None, "chan"),
    )
    out_specs = (
        P(("groups", "rep"), "slide", "chan", None),
        P("groups", None, "chan"),
        P("groups", None),
        P("groups", None),
        P("groups", None),
        P("groups", None),
    )
    return jax.shard_map(
        on_device, mesh=mesh, in_specs=in_specs, out_specs=out_specs, check_vma=False
    )
```

```python
import math

import jax
import jax.numpy as jnp
from jax import lax
from jax.experimental import pallas as pl
from jax.experimental.pallas import tpu as pltpu
from jax.sharding import PartitionSpec as P

SIDE = 8
CAP = 2
GW = 64
BAND_CELLS = 512
PIX = SIDE * SIDE
META = 128
HALF_ROWS = 608
FEAT_ROWS = 192
COT_ROWS = 72
BLOCK_ROWS = FEAT_ROWS + 2 * COT_ROWS
F32 = jnp.float32
BF16 = jnp.bfloat16
VMEM = pl.BlockSpec(memory_space=pltpu.VMEM)
SMEM = pl.BlockSpec(memory_space=pltpu.SMEM)


def params_of(steps=1):
    return pltpu.CompilerParams(
        dimension_semantics=("arbitrary",) * steps, vmem_limit_bytes=48 << 20
    )


def nn(left, right):
    return lax.dot_general(left, right, (((1,), (0,)), ((), ())), preferred_element_type=F32)


def nt(left, right):
    return lax.dot_general(left, right, (((1,), (1,)), ((), ())), preferred_element_type=F32)


def tn(left, right):
    return lax.dot_general(left, right, (((0,), (0,)), ((), ())), preferred_element_type=F32)


def shifted(value, axis, steps):
    count = lax.axis_size(axis)
    first, last = (max(0, -steps), min(count, count - steps))
    return lax.ppermute(value, axis, [(source, source + steps) for source in range(first, last)])


def swapped(value, axis, step):
    count = lax.axis_size(axis)
    return lax.ppermute(value, axis, [(place, place ^ step) for place in range(count)])


def reach(tap):
    return (1, 2) if tap == 0 else (0, 1)


def pack_kernel(cells_ref, pixels_ref, out_ref):
    slots = pixels_ref.shape[0]
    rows = out_ref.shape[0]
    pixch = pixels_ref.shape[1]
    cells = [cells_ref[0, t] for t in range(slots)]
    live = [cell >= 0 for cell in cells]
    bands = [cell // BAND_CELLS for cell in cells]
    places = []
    for t in range(slots):
        rank = jnp.int32(0)
        for s in range(t):
            rank = rank + ((bands[s] == bands[t]) & live[s]).astype(jnp.int32)
        places.append(jnp.where(live[t], bands[t] * CAP + rank, -1))
    dest = lax.broadcasted_iota(jnp.int32, (rows, slots), 0)
    slot = lax.broadcasted_iota(jnp.int32, (rows, slots), 1)
    place = jnp.full((rows, slots), -1, jnp.int32)
    for t in range(slots):
        place = jnp.where(slot == t, places[t], place)
    route = (place == dest).astype(F32).astype(BF16)
    out_ref[:, :pixch] = nn(route, pixels_ref[...]).astype(BF16)
    lane = lax.broadcasted_iota(jnp.int32, (rows, META), 1)
    base = (lax.broadcasted_iota(jnp.int32, (rows, META), 0) // CAP) * CAP
    notes = jnp.zeros((rows, META), F32)
    for t in range(slots):
        within = cells[t] % BAND_CELLS
        own_row = (within // GW).astype(F32)
        own_col = (within % GW).astype(F32)
        for rank in range(CAP):
            hit = base + rank == places[t]
            for at, value in enumerate((own_row, own_col, jnp.float32(1.0))):
                notes = jnp.where(hit & (lane == 3 * rank + at), value, notes)
    out_ref[:, pixch:] = notes.astype(BF16)


def patch_kernel(chan_ref, meta_ref, cot_ref, below_ref, key_ref, own_ref, send_ref):
    sources = meta_ref.shape[0]
    chunks = sources // 8
    out_rows, e_half, _ = cot_ref.shape
    meta = meta_ref[...].astype(F32)
    first = chan_ref[0] == 0
    lane = lax.broadcasted_iota(jnp.int32, (8, 128), 1).astype(F32)
    blocks = []
    for mine in (True, False):
        for chunk in range(chunks):
            part = meta[chunk * 8 : chunk * 8 + 8]
            low = [jnp.broadcast_to(part[:, n : n + 1], (8, 128)) for n in range(3)]
            high = [jnp.broadcast_to(part[:, n : n + 1], (8, 128)) for n in range(3, 6)]
            row, col, valid = (
                jnp.where(first == mine, one, two) for one, two in zip(low, high)
            )
            for u in range(3):
                for v in range(3):
                    hit = (lane == 2.0 * col + v) & (valid > 0.5)
                    blocks.append(jnp.where(hit, 2.0 * row + u, -1.0))
    key = jnp.concatenate(blocks, axis=0)
    key_ref[...] = key

    def step(o, total):
        pick = (key == o.astype(F32)).astype(F32).astype(BF16)
        return total + nt(pick, cot_ref[o].astype(BF16))

    total = lax.fori_loop(
        0, out_rows, step, jnp.zeros((key.shape[0], e_half), F32), unroll=4
    )
    pick = (key == float(out_rows)).astype(F32).astype(BF16)
    total = total + nt(pick, below_ref[...])
    half = total.shape[0] // 2
    own_ref[...] = jnp.zeros_like(own_ref)
    send_ref[...] = jnp.zeros_like(send_ref)
    own_ref[:, :e_half] = total[:half].astype(BF16)
    send_ref[:, :e_half] = total[half:].astype(BF16)


def center_of(values):
    center = values - jnp.mean(values, axis=-1, keepdims=True)
    rstd = lax.rsqrt(jnp.mean(center * center, axis=-1, keepdims=True) + 1e-06)
    return center * rstd, rstd


def fill_padded(padded_ref, pixels_ref, channels):
    padded_ref[...] = jnp.zeros_like(padded_ref)
    for i in range(SIDE):
        for j in range(SIDE):
            at = (i * SIDE + j) * channels
            padded_ref[i + 3, j + 3] = pixels_ref[:, at : at + channels].astype(F32)


def stem_kernel(
    pixels_ref, dw_ref, gain_ref, up_ref, proj_ref, scale_ref, ds_gain_ref, ds_ref,
    feat_ref, hat1_ref, rstd1_ref, hat2_ref, rstd2_ref, hidden_ref, slope_ref, patch_ref,
    padded_ref, spatial_ref, low_ref, wide_ref,
):
    channels = dw_ref.shape[1]
    fill_padded(padded_ref, pixels_ref, channels)

    def row_step(i, carry):
        total = jnp.zeros((SIDE, 8, channels), F32)
        for a in range(7):
            for b in range(7):
                weight = dw_ref[pl.ds(7 * a + b, 1), :].reshape(1, 1, channels)
                total = total + weight * padded_ref[i + a, b : b + SIDE]
        spatial_ref[i] = total
        return carry

    lax.fori_loop(0, SIDE, row_step, 0)
    hat1, rstd1 = center_of(spatial_ref[...].reshape(PIX * 8, channels))
    hat1_ref[...] = hat1
    rstd1_ref[...] = rstd1
    normed = (hat1 * gain_ref[...]).astype(BF16)
    before = nn(normed, up_ref[...])
    cdf = 0.5 * (1.0 + lax.erf(before * math.sqrt(0.5)))
    pdf = jnp.exp(-0.5 * before * before) * (1.0 / math.sqrt(2.0 * math.pi))
    hidden = (before * cdf).astype(BF16)
    hidden_ref[...] = hidden
    slope_ref[...] = cdf + before * pdf
    branch = nt(hidden, proj_ref[...])
    inputs = padded_ref[3 : 3 + SIDE, 3 : 3 + SIDE].reshape(PIX * 8, channels)
    hat2, rstd2 = center_of(inputs + scale_ref[...] * branch)
    hat2_ref[...] = hat2
    rstd2_ref[...] = rstd2
    low_ref[...] = (hat2 * ds_gain_ref[...]).reshape(low_ref.shape)
    half = SIDE // 2
    for di in range(2):
        for dj in range(2):
            at = (2 * di + dj) * channels
            wide_ref[:, at : at + channels] = low_ref[:, di, :, dj].reshape(-1, channels)
    patches = wide_ref[...].astype(BF16)
    patch_ref[...] = patches
    total = nt(patches, ds_ref[...])
    rows = total.shape[0]
    feat_ref[0:rows] = total[:, 0:128].astype(BF16)
    rest = jnp.concatenate([total[: rows // 2, 128:192], total[rows // 2 :, 128:192]], axis=1)
    feat_ref[rows:] = rest.astype(BF16)


def unfold(block):
    rest = block[128:]
    return jnp.concatenate(
        [block[:128], jnp.concatenate([rest[:, :64], rest[:, 64:]], axis=0)], axis=1
    )


def back_kernel(
    chan_ref, own_ref, peer_ref, w_own_ref, w_peer_ref, pixels_ref,
    hat1_ref, rstd1_ref, hat2_ref, rstd2_ref, hidden_ref, slope_ref, patch_ref,
    gain_ref, up_ref, proj_ref, scale_ref, ds_gain_ref, ds_ref,
    keep_ref, send_ref,
    padded_ref, dlow_ref, dspatial_ref, dw_ref, ds_acc, up_acc, proj_acc, pack_ref,
    *, scale,
):
    channels = gain_ref.shape[1]
    e_half = w_own_ref.shape[2]
    half = SIDE // 2
    step = pl.program_id(0)

    @pl.when(step == 0)
    def _():
        dw_ref[...] = jnp.zeros_like(dw_ref)
        ds_acc[...] = jnp.zeros_like(ds_acc)
        up_acc[...] = jnp.zeros_like(up_acc)
        proj_acc[...] = jnp.zeros_like(proj_acc)

    own = own_ref[...].astype(F32)[:, :e_half].reshape(9, 8, e_half)
    peer = peer_ref[...].astype(F32)[:, :e_half].reshape(9, 8, e_half)
    grads = {}
    for a in range(3):
        for b in range(3):
            places = [(u, v) for u in reach(a) for v in reach(b)]
            left_own = jnp.concatenate([own[3 * u + v] for u, v in places], axis=0).astype(BF16)
            left_peer = jnp.concatenate([peer[3 * u + v] for u, v in places], axis=0).astype(BF16)
            out = nt(left_own, w_own_ref[3 * a + b]) + nt(left_peer, w_peer_ref[3 * a + b])
            for n, (u, v) in enumerate(places):
                at = (2 * u + a - 1) * half + 2 * v + b - 1
                piece = out[8 * n : 8 * n + 8]
                grads[at] = grads[at] + piece if at in grads else piece
    dfeat = jnp.concatenate([grads[at] for at in range(half * half)], axis=0) * scale
    dfeat = dfeat.astype(BF16)

    hat2 = hat2_ref[...]
    ds_acc[...] += tn(dfeat, patch_ref[...])
    back = nn(dfeat, ds_ref[...])
    for di in range(2):
        for dj in range(2):
            at = (2 * di + dj) * channels
            dlow_ref[:, di, :, dj] = back[:, at : at + channels].reshape(half, half, 8, channels)
    dhat2 = dlow_ref[...].reshape(PIX * 8, channels) * ds_gain_ref[...]
    mean_a = jnp.mean(dhat2, axis=-1, keepdims=True)
    mean_b = jnp.mean(dhat2 * hat2, axis=-1, keepdims=True)
    dmixed = rstd2_ref[...] * (dhat2 - mean_a - hat2 * mean_b)
    dbranch = (dmixed * scale_ref[...]).astype(BF16)
    proj_acc[...] += tn(dbranch, hidden_ref[...])
    dhidden = nn(dbranch, proj_ref[...])
    dbefore = (dhidden * slope_ref[...]).astype(BF16)
    hat1 = hat1_ref[...]
    normed = (hat1 * gain_ref[...]).astype(BF16)
    up_acc[...] += tn(normed, dbefore)
    dhat1 = nt(dbefore, up_ref[...]) * gain_ref[...]
    mean_a = jnp.mean(dhat1, axis=-1, keepdims=True)
    mean_b = jnp.mean(dhat1 * hat1, axis=-1, keepdims=True)
    dspatial = rstd1_ref[...] * (dhat1 - mean_a - hat1 * mean_b)
    dspatial_ref[...] = dspatial.reshape(SIDE, SIDE, 8, channels)
    fill_padded(padded_ref, pixels_ref, channels)

    def tap_step(a, carry):
        totals = [jnp.zeros((8, channels), F32) for _ in range(7)]
        for i in range(SIDE):
            grad = dspatial_ref[i]
            for b in range(7):
                product = padded_ref[i + a, b : b + SIDE] * grad
                totals[b] = totals[b] + jnp.sum(product, axis=0)
        for b in range(7):
            dw_ref[a, b] += totals[b]
        return carry

    lax.fori_loop(0, 7, tap_step, 0)

    @pl.when(step == pl.num_programs(0) - 1)
    def _():
        pack_ref[...] = jnp.zeros_like(pack_ref)
        for n in range(3):
            lanes = slice(128 * n, 128 * n + 128)
            pack_ref[192 * n : 192 * n + 192, :] = ds_acc[:, lanes]
            pack_ref[576 + 96 * n : 672 + 96 * n, :] = up_acc[:, lanes]
            pack_ref[864 + 96 * n : 960 + 96 * n, :] = proj_acc[:, lanes]
        pack_ref[1152:1201, 0:channels] = jnp.sum(dw_ref[...], axis=2).reshape(49, channels)
        mine = pl.multiple_of(chan_ref[0] * HALF_ROWS, 8)
        other = pl.multiple_of((1 - chan_ref[0]) * HALF_ROWS, 8)
        keep_ref[...] = pack_ref[pl.ds(mine, HALF_ROWS), :]
        send_ref[...] = pack_ref[pl.ds(other, HALF_ROWS), :].astype(BF16)


def unpack_kernel(chan_ref, own_ref, peer_ref, dw_ref, up_ref, proj_ref, ds_ref, pack_ref):
    channels = dw_ref.shape[1]
    mine = pl.multiple_of(chan_ref[0] * HALF_ROWS, 8)
    other = pl.multiple_of((1 - chan_ref[0]) * HALF_ROWS, 8)
    pack_ref[pl.ds(mine, HALF_ROWS), :] = own_ref[...]
    pack_ref[pl.ds(other, HALF_ROWS), :] = peer_ref[...]
    for n in range(3):
        lanes = slice(128 * n, 128 * n + 128)
        ds_ref[:, lanes] = pack_ref[192 * n : 192 * n + 192, :]
        up_ref[:, lanes] = pack_ref[576 + 96 * n : 672 + 96 * n, :]
        proj_ref[:, lanes] = pack_ref[864 + 96 * n : 960 + 96 * n, :]
    dw_ref[...] = pack_ref[1152:1201, 0:channels]


def spread_kernel(feat_ref, w_ref, key_ref, y_ref, below_ref, *, last):
    width = w_ref.shape[1]
    feats = unfold(feat_ref[...].astype(F32)).reshape(16, 8, width)
    outs = {}
    for a in range(3):
        for b in range(3):
            places = [(u, v) for u in reach(a) for v in reach(b)]
            left = jnp.concatenate(
                [feats[(2 * u + a - 1) * 4 + 2 * v + b - 1] for u, v in places], axis=0
            ).astype(BF16)
            out = nn(left, w_ref[3 * a + b])
            for n, (u, v) in enumerate(places):
                piece = out[8 * n : 8 * n + 8]
                at = 3 * u + v
                outs[at] = outs[at] + piece if at in outs else piece
    total = jnp.concatenate([outs[at] for at in range(9)], axis=0)
    y_ref[...] = total
    pick = (key_ref[...] == float(last)).astype(F32).astype(BF16)
    high = total.astype(BF16)
    rest = (total - high.astype(F32)).astype(BF16)

    @pl.when(pl.program_id(0) == 0)
    def _():
        below_ref[...] = jnp.zeros_like(below_ref)

    below_ref[...] += tn(high, pick) + tn(rest, pick)


def map_kernel(y_ref, key_ref, above_ref, out_ref):
    out_rows, width, _ = out_ref.shape
    turned = y_ref[...].T
    high = turned.astype(BF16)
    rest = (turned - high.astype(F32)).astype(BF16)
    key = key_ref[...]

    def row_of(o):
        pick = (key == o).astype(F32).astype(BF16)
        return nn(high, pick) + nn(rest, pick)

    out_ref[0] = (row_of(0.0) + above_ref[...]).astype(BF16)

    def step(o, carry):
        out_ref[o] = row_of(o.astype(F32)).astype(BF16)
        return carry

    lax.fori_loop(1, out_rows, step, 0)


def weight_kernel(place_ref, near_ref, far_ref, keep_ref, send_ref, feat_ref, cot_ref, *, scale):
    near = near_ref.shape[0]
    members = feat_ref.shape[1] // 8
    width, e_half = keep_ref.shape[1:]
    step = pl.program_id(0)

    @pl.when(step == 0)
    def _():
        keep_ref[...] = jnp.zeros_like(keep_ref)
        send_ref[...] = jnp.zeros_like(send_ref)

    def take(member, block):
        block = block.astype(F32)
        feat_ref[:, 8 * member : 8 * member + 8] = unfold(block[:FEAT_ROWS]).reshape(16, 8, width)
        own = block[FEAT_ROWS : FEAT_ROWS + COT_ROWS].reshape(9, 8, 128)
        peer = block[FEAT_ROWS + COT_ROWS :].reshape(9, 8, 128)
        cot_ref[:, 8 * member : 8 * member + 8, 0:128] = own
        cot_ref[:, 8 * member : 8 * member + 8, 128:256] = peer

    for member in range(members):
        at = place_ref[0] ^ member

        @pl.when(at < near)
        def _():
            take(member, near_ref[jnp.minimum(at, near - 1)])

        if members > near:

            @pl.when(at >= near)
            def _():
                take(member, far_ref[jnp.maximum(at - near, 0)])

    for a in range(3):
        for b in range(3):
            places = [(u, v) for u in reach(a) for v in reach(b)]
            left = jnp.concatenate(
                [feat_ref[(2 * u + a - 1) * 4 + 2 * v + b - 1] for u, v in places], axis=0
            ).astype(BF16)
            right = jnp.concatenate([cot_ref[3 * u + v] for u, v in places], axis=0).astype(BF16)
            total = tn(left, right) * scale
            keep_ref[3 * a + b] += total[:, :e_half]
            send_ref[3 * a + b] += total[:, 128 : 128 + e_half]


def whole(shape):
    return pl.BlockSpec(shape, lambda g: (0,) * len(shape))


def on_device(
    tile_pixels, tile_cell, agg_cot, dw_weight, norm_gain, up_weight, proj_weight,
    layer_scale, ds_gain, ds_weight, agg_weight,
):
    channels = dw_weight.shape[1]
    hid = up_weight.shape[1]
    width = ds_weight.shape[1]
    bands = lax.axis_size("slide")
    sources = bands * lax.axis_size("chan")
    chunks = sources // 8
    pixch = tile_pixels.shape[2]
    out_rows = agg_cot.shape[1]
    e_half = agg_weight.shape[2]
    cols = agg_cot.shape[3]
    blocks = CAP * chunks
    total_rows = out_rows * bands * lax.axis_size("rep") * cols
    loss_scale = 1.0 / math.sqrt(total_rows)
    chan = lax.axis_index("chan").astype(jnp.int32)[None]
    gain = norm_gain[None]
    scale = layer_scale[None]
    low_gain = ds_gain[None]
    proj_turned = proj_weight.T
    ds_turned = ds_weight.T

    peer_weight = swapped(agg_weight, "chan", 1)
    below_cot = shifted(agg_cot[0, 0].astype(BF16), "slide", -1)

    packed = pl.pallas_call(
        pack_kernel,
        out_shape=jax.ShapeDtypeStruct((sources, pixch + META), BF16),
        in_specs=[SMEM, VMEM],
        out_specs=VMEM,
        name="pack",
    )(tile_cell, tile_pixels[0])
    got = lax.all_to_all(packed, ("slide", "chan"), split_axis=0, concat_axis=0, tiled=True)

    key, cots_own, cots_send = pl.pallas_call(
        patch_kernel,
        out_shape=(
            jax.ShapeDtypeStruct((blocks * COT_ROWS, cols), F32),
            jax.ShapeDtypeStruct((chunks * COT_ROWS, 128), BF16),
            jax.ShapeDtypeStruct((chunks * COT_ROWS, 128), BF16),
        ),
        in_specs=[
            SMEM,
            pl.BlockSpec((sources, META), lambda i: (0, pixch // META)),
            pl.BlockSpec((None, out_rows, e_half, cols), lambda i: (0, 0, 0, 0)),
            whole((e_half, cols)),
        ],
        out_specs=(
            whole((blocks * COT_ROWS, cols)),
            whole((chunks * COT_ROWS, 128)),
            whole((chunks * COT_ROWS, 128)),
        ),
        grid=(1,),
        compiler_params=params_of(),
        name="patch",
    )(chan, got, agg_cot, below_cot)
    cots_peer = swapped(cots_send, "chan", 1)
    cots_own = cots_own.reshape(chunks, COT_ROWS, 128)
    cots_peer = cots_peer.reshape(chunks, COT_ROWS, 128)

    rows = PIX * 8
    pixel_spec = pl.BlockSpec((8, pixch), lambda g: (g, 0))

    def chunk(*shape):
        return pl.BlockSpec((None,) + shape, lambda g: (g,) + (0,) * len(shape))

    feats, hat1, rstd1, hat2, rstd2, hidden, slope, patches = pl.pallas_call(
        stem_kernel,
        grid=(chunks,),
        out_shape=(
            jax.ShapeDtypeStruct((chunks, FEAT_ROWS, 128), BF16),
            jax.ShapeDtypeStruct((chunks, rows, channels), F32),
            jax.ShapeDtypeStruct((chunks, rows, 1), F32),
            jax.ShapeDtypeStruct((chunks, rows, channels), F32),
            jax.ShapeDtypeStruct((chunks, rows, 1), F32),
            jax.ShapeDtypeStruct((chunks, rows, hid), BF16),
            jax.ShapeDtypeStruct((chunks, rows, hid), F32),
            jax.ShapeDtypeStruct((chunks, 128, 4 * channels), BF16),
        ),
        in_specs=[
            pixel_spec,
            whole(dw_weight.shape), whole((1, channels)), whole(up_weight.shape),
            whole(proj_turned.shape), whole((1, channels)), whole((1, channels)),
            whole(ds_turned.shape),
        ],
        out_specs=(
            chunk(FEAT_ROWS, 128), chunk(rows, channels), chunk(rows, 1), chunk(rows, channels),
            chunk(rows, 1), chunk(rows, hid), chunk(rows, hid), chunk(128, 4 * channels),
        ),
        scratch_shapes=[
            pltpu.VMEM((SIDE + 6, SIDE + 6, 8, channels), F32),
            pltpu.VMEM((SIDE, SIDE, 8, channels), F32),
            pltpu.VMEM((SIDE // 2, 2, SIDE // 2, 2, 8, channels), F32),
            pltpu.VMEM((128, 4 * channels), F32),
        ],
        compiler_params=params_of(),
        name="stem",
    )(got, dw_weight, gain, up_weight, proj_turned, scale, low_gain, ds_turned)

    tile_blocks = jnp.concatenate([feats, cots_own, cots_peer], axis=1)
    gather = chunks == 1
    near = far = tile_blocks
    place = jnp.zeros((1,), jnp.int32)
    if gather:
        spans = [("slide", 1 << n) for n in reversed(range(bands.bit_length() - 1))]
        spans += [("rep", 1 << n) for n in range(lax.axis_size("rep").bit_length() - 1)]
        for n, (axis, step) in enumerate(spans):
            near = far if n == 0 else jnp.concatenate([near, far], axis=0)
            far = swapped(near, axis, step)
            bit = (lax.axis_index(axis).astype(jnp.int32) // step) % 2
            place = place + bit * (1 << n)

    keep, send = pl.pallas_call(
        lambda *refs: back_kernel(*refs, scale=loss_scale),
        grid=(chunks,),
        out_shape=(
            jax.ShapeDtypeStruct((HALF_ROWS, 128), F32),
            jax.ShapeDtypeStruct((HALF_ROWS, 128), BF16),
        ),
        in_specs=[
            SMEM, chunk(COT_ROWS, 128), chunk(COT_ROWS, 128),
            whole(agg_weight.shape), whole(agg_weight.shape), pixel_spec,
            chunk(rows, channels), chunk(rows, 1), chunk(rows, channels), chunk(rows, 1),
            chunk(rows, hid), chunk(rows, hid), chunk(128, 4 * channels),
            whole((1, channels)), whole(up_weight.shape), whole(proj_turned.shape),
            whole((1, channels)), whole((1, channels)), whole(ds_turned.shape),
        ],
        out_specs=(whole((HALF_ROWS, 128)), whole((HALF_ROWS, 128))),
        scratch_shapes=[
            pltpu.VMEM((SIDE + 6, SIDE + 6, 8, channels), F32),
            pltpu.VMEM((SIDE // 2, 2, SIDE // 2, 2, 8, channels), F32),
            pltpu.VMEM((SIDE, SIDE, 8, channels), F32),
            pltpu.VMEM((7, 7, 8, channels), F32),
            pltpu.VMEM(ds_turned.shape, F32),
            pltpu.VMEM(up_weight.shape, F32),
            pltpu.VMEM(proj_turned.shape, F32),
            pltpu.VMEM((2 * HALF_ROWS, 128), F32),
        ],
        compiler_params=params_of(),
        name="stem_back",
    )(
        chan, cots_own, cots_peer, agg_weight, peer_weight, got,
        hat1, rstd1, hat2, rstd2, hidden, slope, patches,
        gain, up_weight, proj_turned, scale, low_gain, ds_turned,
    )

    feats_band = jnp.concatenate([feats, swapped(feats, "chan", 1)], axis=0)
    spread, below = pl.pallas_call(
        lambda *refs: spread_kernel(*refs, last=out_rows),
        grid=(blocks,),
        out_shape=(
            jax.ShapeDtypeStruct((blocks * 72, e_half), F32),
            jax.ShapeDtypeStruct((e_half, cols), F32),
        ),
        in_specs=[
            chunk(FEAT_ROWS, 128), whole(agg_weight.shape),
            pl.BlockSpec((72, cols), lambda g: (g, 0)),
        ],
        out_specs=(pl.BlockSpec((72, e_half), lambda g: (g, 0)), whole((e_half, cols))),
        compiler_params=params_of(),
        name="spread",
    )(feats_band, agg_weight, key)
    above = shifted(below, "slide", 1)
    agg_map = pl.pallas_call(
        map_kernel,
        out_shape=jax.ShapeDtypeStruct((out_rows, e_half, cols), BF16),
        in_specs=[VMEM, VMEM, VMEM],
        out_specs=VMEM,
        compiler_params=pltpu.CompilerParams(vmem_limit_bytes=48 << 20),
        name="agg_map",
    )(spread, key, above)[None]

    count = 2 * near.shape[0] if gather else chunks
    per = count if gather else 1
    near_count = near.shape[0] if gather else 1
    agg_keep, agg_send = pl.pallas_call(
        lambda *refs: weight_kernel(*refs, scale=loss_scale),
        grid=(count // per,),
        out_shape=(
            jax.ShapeDtypeStruct((9, width, e_half), F32),
            jax.ShapeDtypeStruct((9, width, e_half), F32),
        ),
        in_specs=[
            SMEM,
            pl.BlockSpec((near_count, BLOCK_ROWS, 128), lambda g: (g, 0, 0)),
            pl.BlockSpec((near_count, BLOCK_ROWS, 128), lambda g: (g, 0, 0)),
        ],
        out_specs=(whole((9, width, e_half)), whole((9, width, e_half))),
        scratch_shapes=[
            pltpu.VMEM((16, per * 8, width), F32),
            pltpu.VMEM((9, per * 8, 256), F32),
        ],
        compiler_params=params_of(),
        name="agg_weight_grad",
    )(place, near, far)
    agg_grad = agg_keep + swapped(agg_send.astype(BF16), "chan", 1).astype(F32)
    if not gather:
        agg_grad = lax.psum(agg_grad, ("slide", "rep"))

    part = keep + swapped(send, "chan", 1).astype(F32)
    for axis in ("rep", "slide"):
        step = 1
        while step < lax.axis_size(axis):
            wire = part.astype(BF16)
            part = wire.astype(F32) + swapped(wire, axis, step).astype(F32)
            step *= 2
    dw_grad, up_grad, proj_grad, ds_grad = pl.pallas_call(
        unpack_kernel,
        out_shape=(
            jax.ShapeDtypeStruct(dw_weight.shape, F32),
            jax.ShapeDtypeStruct(up_weight.shape, F32),
            jax.ShapeDtypeStruct(proj_turned.shape, F32),
            jax.ShapeDtypeStruct(ds_turned.shape, F32),
        ),
        in_specs=[SMEM, VMEM, VMEM],
        out_specs=(VMEM, VMEM, VMEM, VMEM),
        scratch_shapes=[pltpu.VMEM((2 * HALF_ROWS, 128), F32)],
        name="unpack",
    )(chan, part, swapped(part, "chan", 1))
    proj_grad = proj_grad.T
    ds_grad = ds_grad.T
    return (agg_map, agg_grad, dw_grad, up_grad, proj_grad, ds_grad)


def solution(mesh):
    in_specs = (
        P(("groups", "rep"), ("slide", "chan"), None),
        P(("groups", "rep"), ("slide", "chan")),
        P(("groups", "rep"), "slide", "chan", None),
        P(), P(), P(), P(), P(), P(), P(),
        P(None, None, "chan"),
    )
    out_specs = (
        P(("groups", "rep"), "slide", "chan", None),
        P("groups", None, "chan"),
        P("groups", None),
        P("groups", None),
        P("groups", None),
        P("groups", None),
    )
    return jax.shard_map(
        on_device, mesh=mesh, in_specs=in_specs, out_specs=out_specs, check_vma=False
    )
```

```python
import math

import jax
import jax.numpy as jnp
from jax import lax
from jax.experimental import pallas as pl
from jax.experimental.pallas import tpu as pltpu
from jax.sharding import PartitionSpec as P

SIDE = 8
CAP = 2
GW = 64
BAND_CELLS = 512
PIX = SIDE * SIDE
HALF_ROWS = 608
FEAT_ROWS = 192
COT_ROWS = 72
WIRE_ROWS = 56
BLOCK_ROWS = FEAT_ROWS + 2 * COT_ROWS
F32 = jnp.float32
BF16 = jnp.bfloat16
VMEM = pl.BlockSpec(memory_space=pltpu.VMEM)
SMEM = pl.BlockSpec(memory_space=pltpu.SMEM)


def params_of(steps=1):
    return pltpu.CompilerParams(
        dimension_semantics=("arbitrary",) * steps, vmem_limit_bytes=24 << 20
    )


def takes(microseconds):
    return pl.CostEstimate(
        flops=0, transcendentals=0, bytes_accessed=int(microseconds * 3.69e6)
    )


def nn(left, right):
    return lax.dot_general(left, right, (((1,), (0,)), ((), ())), preferred_element_type=F32)


def nt(left, right):
    return lax.dot_general(left, right, (((1,), (1,)), ((), ())), preferred_element_type=F32)


def tn(left, right):
    return lax.dot_general(left, right, (((0,), (0,)), ((), ())), preferred_element_type=F32)


def shifted(value, axis, steps):
    count = lax.axis_size(axis)
    first, last = (max(0, -steps), min(count, count - steps))
    return lax.ppermute(value, axis, [(source, source + steps) for source in range(first, last)])


def swapped(value, axis, step):
    count = lax.axis_size(axis)
    return lax.ppermute(value, axis, [(place, place ^ step) for place in range(count)])


def reach(tap):
    return (1, 2) if tap == 0 else (0, 1)


def pack_kernel(cells_ref, pixels_ref, out_ref, wide_ref):
    slots = pixels_ref.shape[0]
    rows = out_ref.shape[0]
    pixch = pixels_ref.shape[1]
    cells = [cells_ref[0, t] for t in range(slots)]
    live = [cell >= 0 for cell in cells]
    bands = [cell // BAND_CELLS for cell in cells]
    places = []
    for t in range(slots):
        rank = jnp.int32(0)
        for s in range(t):
            rank = rank + ((bands[s] == bands[t]) & live[s]).astype(jnp.int32)
        places.append(jnp.where(live[t], bands[t] * CAP + rank, -1))
    dest = lax.broadcasted_iota(jnp.int32, (rows, slots), 0)
    slot = lax.broadcasted_iota(jnp.int32, (rows, slots), 1)
    place = jnp.full((rows, slots), -1, jnp.int32)
    for t in range(slots):
        place = jnp.where(slot == t, places[t], place)
    route = (place == dest).astype(F32).astype(BF16)
    routed = nn(route, pixels_ref[...])
    wide_ref[...] = jnp.zeros_like(wide_ref)
    for n in range(pixch // 128):
        wide_ref[:, n, :] = routed[:, 128 * n : 128 * n + 128]
    lane = lax.broadcasted_iota(jnp.int32, (rows, 128), 1)
    base = (lax.broadcasted_iota(jnp.int32, (rows, 128), 0) // CAP) * CAP
    notes = jnp.zeros((rows, 128), F32)
    for t in range(slots):
        within = cells[t] % BAND_CELLS
        own_row = (within // GW).astype(F32)
        own_col = (within % GW).astype(F32)
        for rank in range(CAP):
            hit = base + rank == places[t]
            for at, value in enumerate((own_row, own_col, jnp.float32(1.0))):
                notes = jnp.where(hit & (lane == 3 * rank + at), value, notes)
    wide_ref[:, pixch // 128, :] = notes
    out_ref[...] = wide_ref[...].astype(BF16)


def patch_kernel(chan_ref, meta_ref, cot_ref, below_ref, key_ref, own_ref, send_ref, meta_f32):
    sources = meta_ref.shape[0]
    chunks = sources // 8
    out_rows, e_half, _ = cot_ref.shape
    meta_f32[...] = meta_ref[...].astype(F32)
    meta = meta_f32[:, 0, :]
    first = chan_ref[0] == 0
    lane = lax.broadcasted_iota(jnp.int32, (8, 128), 1).astype(F32)
    blocks = []
    for mine in (True, False):
        for chunk in range(chunks):
            part = meta[chunk * 8 : chunk * 8 + 8]
            low = [jnp.broadcast_to(part[:, n : n + 1], (8, 128)) for n in range(3)]
            high = [jnp.broadcast_to(part[:, n : n + 1], (8, 128)) for n in range(3, 6)]
            row, col, valid = (
                jnp.where(first == mine, one, two) for one, two in zip(low, high)
            )
            for u in range(3):
                for v in range(3):
                    hit = (lane == 2.0 * col + v) & (valid > 0.5)
                    blocks.append(jnp.where(hit, 2.0 * row + u, -1.0))
    key = jnp.concatenate(blocks, axis=0)
    key_ref[...] = key

    def step(o, total):
        pick = (key == o.astype(F32)).astype(F32).astype(BF16)
        return total + nt(pick, cot_ref[o].astype(BF16))

    total = lax.fori_loop(
        0, out_rows, step, jnp.zeros((key.shape[0], e_half), F32), unroll=4
    )
    pick = (key == float(out_rows)).astype(F32).astype(BF16)
    total = total + nt(pick, below_ref[...])
    half = total.shape[0] // 2
    own_ref[...] = jnp.zeros_like(own_ref)
    send_ref[...] = jnp.zeros_like(send_ref)
    own_ref[:, :e_half] = total[:half].astype(BF16)
    send_ref[:, :e_half] = total[half:].astype(BF16)


def center_of(values):
    center = values - jnp.mean(values, axis=-1, keepdims=True)
    rstd = lax.rsqrt(jnp.mean(center * center, axis=-1, keepdims=True) + 1e-06)
    return center * rstd, rstd


def fill_padded(padded_ref, got_ref, wide_ref, pixels_ref, channels):
    wide_ref[...] = got_ref[...].astype(F32)
    for n in range(pixels_ref.shape[1] // 128):
        pixels_ref[:, 128 * n : 128 * n + 128] = wide_ref[:, n, :]
    padded_ref[...] = jnp.zeros_like(padded_ref)
    for i in range(SIDE):
        for j in range(SIDE):
            at = (i * SIDE + j) * channels
            padded_ref[i + 3, j + 3] = pixels_ref[:, at : at + channels]


def stem_kernel(
    got_ref, dw_ref, gain_ref, up_ref, proj_ref, scale_ref, ds_gain_ref, ds_ref,
    feat_ref, hat1_ref, rstd1_ref, hat2_ref, rstd2_ref, hidden_ref, slope_ref, patch_ref,
    padded_ref, spatial_ref, low_ref, patch_f32, wide_ref, pixels_ref,
):
    channels = dw_ref.shape[1]
    fill_padded(padded_ref, got_ref, wide_ref, pixels_ref, channels)

    def row_step(i, carry):
        total = jnp.zeros((SIDE, 8, channels), F32)
        for a in range(7):
            for b in range(7):
                weight = dw_ref[pl.ds(7 * a + b, 1), :].reshape(1, 1, channels)
                total = total + weight * padded_ref[i + a, b : b + SIDE]
        spatial_ref[i] = total
        return carry

    lax.fori_loop(0, SIDE, row_step, 0)
    hat1, rstd1 = center_of(spatial_ref[...].reshape(PIX * 8, channels))
    hat1_ref[...] = hat1
    rstd1_ref[...] = rstd1
    normed = (hat1 * gain_ref[...]).astype(BF16)
    before = nn(normed, up_ref[...])
    cdf = 0.5 * (1.0 + lax.erf(before * math.sqrt(0.5)))
    pdf = jnp.exp(-0.5 * before * before) * (1.0 / math.sqrt(2.0 * math.pi))
    hidden = (before * cdf).astype(BF16)
    hidden_ref[...] = hidden
    slope_ref[...] = cdf + before * pdf
    branch = nt(hidden, proj_ref[...])
    inputs = padded_ref[3 : 3 + SIDE, 3 : 3 + SIDE].reshape(PIX * 8, channels)
    hat2, rstd2 = center_of(inputs + scale_ref[...] * branch)
    hat2_ref[...] = hat2
    rstd2_ref[...] = rstd2
    low_ref[...] = (hat2 * ds_gain_ref[...]).reshape(low_ref.shape)
    half = SIDE // 2
    for di in range(2):
        for dj in range(2):
            at = (2 * di + dj) * channels
            patch_f32[:, at : at + channels] = low_ref[:, di, :, dj].reshape(-1, channels)
    patches = patch_f32[...].astype(BF16)
    patch_ref[...] = patches
    total = nt(patches, ds_ref[...])
    rows = total.shape[0]
    feat_ref[0:rows] = total[:, 0:128].astype(BF16)
    rest = jnp.concatenate([total[: rows // 2, 128:192], total[rows // 2 :, 128:192]], axis=1)
    feat_ref[rows:] = rest.astype(BF16)


def unfold(block):
    rest = block[128:]
    return jnp.concatenate(
        [block[:128], jnp.concatenate([rest[:, :64], rest[:, 64:]], axis=0)], axis=1
    )


def back_kernel(
    chan_ref, own_ref, peer_ref, w_own_ref, w_peer_ref, got_ref,
    hat1_ref, rstd1_ref, hat2_ref, rstd2_ref, hidden_ref, slope_ref, patch_ref,
    gain_ref, up_ref, proj_ref, scale_ref, ds_gain_ref, ds_ref,
    keep_ref, send_ref,
    padded_ref, dlow_ref, dspatial_ref, dw_ref, ds_acc, up_acc, proj_acc, pack_ref,
    wide_ref, pixels_ref,
    *, scale,
):
    channels = gain_ref.shape[1]
    e_half = w_own_ref.shape[2]
    half = SIDE // 2
    step = pl.program_id(0)

    @pl.when(step == 0)
    def _():
        dw_ref[...] = jnp.zeros_like(dw_ref)
        ds_acc[...] = jnp.zeros_like(ds_acc)
        up_acc[...] = jnp.zeros_like(up_acc)
        proj_acc[...] = jnp.zeros_like(proj_acc)

    own = own_ref[...].astype(F32)[:, :e_half].reshape(9, 8, e_half)
    peer = peer_ref[...].astype(F32)[:, :e_half].reshape(9, 8, e_half)
    grads = {}
    for a in range(3):
        for b in range(3):
            places = [(u, v) for u in reach(a) for v in reach(b)]
            left_own = jnp.concatenate([own[3 * u + v] for u, v in places], axis=0).astype(BF16)
            left_peer = jnp.concatenate([peer[3 * u + v] for u, v in places], axis=0).astype(BF16)
            out = nt(left_own, w_own_ref[3 * a + b]) + nt(left_peer, w_peer_ref[3 * a + b])
            for n, (u, v) in enumerate(places):
                at = (2 * u + a - 1) * half + 2 * v + b - 1
                piece = out[8 * n : 8 * n + 8]
                grads[at] = grads[at] + piece if at in grads else piece
    dfeat = jnp.concatenate([grads[at] for at in range(half * half)], axis=0) * scale
    dfeat = dfeat.astype(BF16)

    hat2 = hat2_ref[...]
    ds_acc[...] += tn(dfeat, patch_ref[...])
    back = nn(dfeat, ds_ref[...])
    for di in range(2):
        for dj in range(2):
            at = (2 * di + dj) * channels
            dlow_ref[:, di, :, dj] = back[:, at : at + channels].reshape(half, half, 8, channels)
    dhat2 = dlow_ref[...].reshape(PIX * 8, channels) * ds_gain_ref[...]
    mean_a = jnp.mean(dhat2, axis=-1, keepdims=True)
    mean_b = jnp.mean(dhat2 * hat2, axis=-1, keepdims=True)
    dmixed = rstd2_ref[...] * (dhat2 - mean_a - hat2 * mean_b)
    dbranch = (dmixed * scale_ref[...]).astype(BF16)
    proj_acc[...] += tn(dbranch, hidden_ref[...])
    dhidden = nn(dbranch, proj_ref[...])
    dbefore = (dhidden * slope_ref[...]).astype(BF16)
    hat1 = hat1_ref[...]
    normed = (hat1 * gain_ref[...]).astype(BF16)
    up_acc[...] += tn(normed, dbefore)
    dhat1 = nt(dbefore, up_ref[...]) * gain_ref[...]
    mean_a = jnp.mean(dhat1, axis=-1, keepdims=True)
    mean_b = jnp.mean(dhat1 * hat1, axis=-1, keepdims=True)
    dspatial = rstd1_ref[...] * (dhat1 - mean_a - hat1 * mean_b)
    dspatial_ref[...] = dspatial.reshape(SIDE, SIDE, 8, channels)
    fill_padded(padded_ref, got_ref, wide_ref, pixels_ref, channels)

    def tap_step(a, carry):
        totals = [jnp.zeros((8, channels), F32) for _ in range(7)]
        for i in range(SIDE):
            grad = dspatial_ref[i]
            for b in range(7):
                product = padded_ref[i + a, b : b + SIDE] * grad
                totals[b] = totals[b] + jnp.sum(product, axis=0)
        for b in range(7):
            dw_ref[a, b] += totals[b]
        return carry

    lax.fori_loop(0, 7, tap_step, 0)

    @pl.when(step == pl.num_programs(0) - 1)
    def _():
        pack_ref[...] = jnp.zeros_like(pack_ref)
        for n in range(3):
            lanes = slice(128 * n, 128 * n + 128)
            pack_ref[192 * n : 192 * n + 192, :] = ds_acc[:, lanes]
            pack_ref[576 + 96 * n : 672 + 96 * n, :] = up_acc[:, lanes]
            pack_ref[864 + 96 * n : 960 + 96 * n, :] = proj_acc[:, lanes]
        pack_ref[1152:1201, 0:channels] = jnp.sum(dw_ref[...], axis=2).reshape(49, channels)
        mine = pl.multiple_of(chan_ref[0] * HALF_ROWS, 8)
        other = pl.multiple_of((1 - chan_ref[0]) * HALF_ROWS, 8)
        keep_ref[...] = pack_ref[pl.ds(mine, HALF_ROWS), :]
        send_ref[...] = pack_ref[pl.ds(other, HALF_ROWS), :].astype(BF16)


def unpack_kernel(chan_ref, own_ref, peer_ref, dw_ref, up_ref, proj_ref, ds_ref, pack_ref):
    channels = dw_ref.shape[1]
    mine = pl.multiple_of(chan_ref[0] * HALF_ROWS, 8)
    other = pl.multiple_of((1 - chan_ref[0]) * HALF_ROWS, 8)
    pack_ref[pl.ds(mine, HALF_ROWS), :] = own_ref[...]
    pack_ref[pl.ds(other, HALF_ROWS), :] = peer_ref[...]
    for n in range(3):
        lanes = slice(128 * n, 128 * n + 128)
        ds_ref[:, lanes] = pack_ref[192 * n : 192 * n + 192, :]
        up_ref[:, lanes] = pack_ref[576 + 96 * n : 672 + 96 * n, :]
        proj_ref[:, lanes] = pack_ref[864 + 96 * n : 960 + 96 * n, :]
    dw_ref[...] = pack_ref[1152:1201, 0:channels]


def spread_kernel(feat_ref, w_ref, key_ref, y_ref, below_ref, *, last):
    width = w_ref.shape[1]
    feats = unfold(feat_ref[...].astype(F32)).reshape(16, 8, width)
    outs = {}
    for a in range(3):
        for b in range(3):
            places = [(u, v) for u in reach(a) for v in reach(b)]
            left = jnp.concatenate(
                [feats[(2 * u + a - 1) * 4 + 2 * v + b - 1] for u, v in places], axis=0
            ).astype(BF16)
            out = nn(left, w_ref[3 * a + b])
            for n, (u, v) in enumerate(places):
                piece = out[8 * n : 8 * n + 8]
                at = 3 * u + v
                outs[at] = outs[at] + piece if at in outs else piece
    total = jnp.concatenate([outs[at] for at in range(9)], axis=0)
    y_ref[...] = total
    pick = (key_ref[...] == float(last)).astype(F32).astype(BF16)
    high = total.astype(BF16)
    rest = (total - high.astype(F32)).astype(BF16)

    @pl.when(pl.program_id(0) == 0)
    def _():
        below_ref[...] = jnp.zeros_like(below_ref)

    below_ref[...] += tn(high, pick) + tn(rest, pick)


def map_kernel(y_ref, key_ref, above_ref, out_ref):
    out_rows, width, _ = out_ref.shape
    turned = y_ref[...].T
    high = turned.astype(BF16)
    rest = (turned - high.astype(F32)).astype(BF16)
    key = key_ref[...]

    def row_of(o):
        pick = (key == o).astype(F32).astype(BF16)
        return nn(high, pick) + nn(rest, pick)

    out_ref[0] = (row_of(0.0) + above_ref[...]).astype(BF16)

    def step(o, carry):
        out_ref[o] = row_of(o.astype(F32)).astype(BF16)
        return carry

    lax.fori_loop(1, out_rows, step, 0)


def weight_kernel(place_ref, near_ref, far_ref, keep_ref, send_ref, feat_ref, cot_ref, *, scale):
    near = near_ref.shape[0]
    members = feat_ref.shape[1] // 8
    width, e_half = keep_ref.shape[1:]
    step = pl.program_id(0)

    @pl.when(step == 0)
    def _():
        keep_ref[...] = jnp.zeros_like(keep_ref)
        send_ref[...] = jnp.zeros_like(send_ref)

    def take(member, block):
        block = block.astype(F32)
        feat_ref[:, 8 * member : 8 * member + 8] = unfold(block[:FEAT_ROWS]).reshape(16, 8, width)
        own = block[FEAT_ROWS : FEAT_ROWS + COT_ROWS].reshape(9, 8, 128)
        peer = block[FEAT_ROWS + COT_ROWS :].reshape(9, 8, 128)
        cot_ref[:, 8 * member : 8 * member + 8, 0:128] = own
        cot_ref[:, 8 * member : 8 * member + 8, 128:256] = peer

    for member in range(members):
        at = place_ref[0] ^ member

        @pl.when(at < near)
        def _():
            take(member, near_ref[jnp.minimum(at, near - 1)])

        if members > near:

            @pl.when(at >= near)
            def _():
                take(member, far_ref[jnp.maximum(at - near, 0)])

    for a in range(3):
        for b in range(3):
            places = [(u, v) for u in reach(a) for v in reach(b)]
            left = jnp.concatenate(
                [feat_ref[(2 * u + a - 1) * 4 + 2 * v + b - 1] for u, v in places], axis=0
            ).astype(BF16)
            right = jnp.concatenate([cot_ref[3 * u + v] for u, v in places], axis=0).astype(BF16)
            total = tn(left, right) * scale
            keep_ref[3 * a + b] += total[:, :e_half]
            send_ref[3 * a + b] += total[:, 128 : 128 + e_half]


def whole(shape):
    return pl.BlockSpec(shape, lambda g: (0,) * len(shape))


def on_device(
    tile_pixels, tile_cell, agg_cot, dw_weight, norm_gain, up_weight, proj_weight,
    layer_scale, ds_gain, ds_weight, agg_weight,
):
    channels = dw_weight.shape[1]
    hid = up_weight.shape[1]
    width = ds_weight.shape[1]
    bands = lax.axis_size("slide")
    sources = bands * lax.axis_size("chan")
    chunks = sources // 8
    pixch = tile_pixels.shape[2]
    out_rows = agg_cot.shape[1]
    e_half = agg_weight.shape[2]
    cols = agg_cot.shape[3]
    blocks = CAP * chunks
    total_rows = out_rows * bands * lax.axis_size("rep") * cols
    loss_scale = 1.0 / math.sqrt(total_rows)
    chan = lax.axis_index("chan").astype(jnp.int32)[None]
    gain = norm_gain[None]
    scale = layer_scale[None]
    low_gain = ds_gain[None]
    proj_turned = proj_weight.T
    ds_turned = ds_weight.T

    peer_weight = swapped(agg_weight, "chan", 1)
    below_cot = shifted(agg_cot[0, 0].astype(BF16), "slide", -1)

    packed = pl.pallas_call(
        pack_kernel,
        out_shape=jax.ShapeDtypeStruct((sources, WIRE_ROWS, 128), BF16),
        in_specs=[SMEM, VMEM],
        out_specs=VMEM,
        scratch_shapes=[pltpu.VMEM((sources, WIRE_ROWS, 128), F32)],
        compiler_params=pltpu.CompilerParams(vmem_limit_bytes=24 << 20),
        cost_estimate=takes(1.5),
        name="pack",
    )(tile_cell, tile_pixels[0])
    got = lax.all_to_all(packed, ("slide", "chan"), split_axis=0, concat_axis=0, tiled=True)

    key, cots_own, cots_send = pl.pallas_call(
        patch_kernel,
        out_shape=(
            jax.ShapeDtypeStruct((blocks * COT_ROWS, cols), F32),
            jax.ShapeDtypeStruct((chunks * COT_ROWS, 128), BF16),
            jax.ShapeDtypeStruct((chunks * COT_ROWS, 128), BF16),
        ),
        in_specs=[
            SMEM,
            pl.BlockSpec((sources, 8, 128), lambda i: (0, pixch // 1024, 0)),
            pl.BlockSpec((None, out_rows, e_half, cols), lambda i: (0, 0, 0, 0)),
            whole((e_half, cols)),
        ],
        out_specs=(
            whole((blocks * COT_ROWS, cols)),
            whole((chunks * COT_ROWS, 128)),
            whole((chunks * COT_ROWS, 128)),
        ),
        grid=(1,),
        scratch_shapes=[pltpu.VMEM((sources, 8, 128), F32)],
        compiler_params=params_of(),
        cost_estimate=takes(1.2),
        name="patch",
    )(chan, got, agg_cot, below_cot)
    cots_peer = swapped(cots_send, "chan", 1)
    cots_own = cots_own.reshape(chunks, COT_ROWS, 128)
    cots_peer = cots_peer.reshape(chunks, COT_ROWS, 128)

    rows = PIX * 8
    pixel_spec = pl.BlockSpec((8, WIRE_ROWS, 128), lambda g: (g, 0, 0))
    pixel_scratch = [pltpu.VMEM((8, WIRE_ROWS, 128), F32), pltpu.VMEM((8, pixch), F32)]

    def chunk(*shape):
        return pl.BlockSpec((None,) + shape, lambda g: (g,) + (0,) * len(shape))

    feats, hat1, rstd1, hat2, rstd2, hidden, slope, patches = pl.pallas_call(
        stem_kernel,
        grid=(chunks,),
        out_shape=(
            jax.ShapeDtypeStruct((chunks, FEAT_ROWS, 128), BF16),
            jax.ShapeDtypeStruct((chunks, rows, channels), F32),
            jax.ShapeDtypeStruct((chunks, rows, 1), F32),
            jax.ShapeDtypeStruct((chunks, rows, channels), F32),
            jax.ShapeDtypeStruct((chunks, rows, 1), F32),
            jax.ShapeDtypeStruct((chunks, rows, hid), BF16),
            jax.ShapeDtypeStruct((chunks, rows, hid), F32),
            jax.ShapeDtypeStruct((chunks, 128, 4 * channels), BF16),
        ),
        in_specs=[
            pixel_spec,
            whole(dw_weight.shape), whole((1, channels)), whole(up_weight.shape),
            whole(proj_turned.shape), whole((1, channels)), whole((1, channels)),
            whole(ds_turned.shape),
        ],
        out_specs=(
            chunk(FEAT_ROWS, 128), chunk(rows, channels), chunk(rows, 1), chunk(rows, channels),
            chunk(rows, 1), chunk(rows, hid), chunk(rows, hid), chunk(128, 4 * channels),
        ),
        scratch_shapes=[
            pltpu.VMEM((SIDE + 6, SIDE + 6, 8, channels), F32),
            pltpu.VMEM((SIDE, SIDE, 8, channels), F32),
            pltpu.VMEM((SIDE // 2, 2, SIDE // 2, 2, 8, channels), F32),
            pltpu.VMEM((128, 4 * channels), F32),
            *pixel_scratch,
        ],
        compiler_params=params_of(),
        cost_estimate=takes(2.7),
        name="stem",
    )(got, dw_weight, gain, up_weight, proj_turned, scale, low_gain, ds_turned)

    tile_blocks = jnp.concatenate([feats, cots_own, cots_peer], axis=1)
    gather = chunks == 1
    near = far = tile_blocks
    place = jnp.zeros((1,), jnp.int32)
    if gather:
        spans = [("slide", 1 << n) for n in reversed(range(bands.bit_length() - 1))]
        spans += [("rep", 1 << n) for n in range(lax.axis_size("rep").bit_length() - 1)]
        for n, (axis, step) in enumerate(spans):
            near = far if n == 0 else jnp.concatenate([near, far], axis=0)
            far = swapped(near, axis, step)
            bit = (lax.axis_index(axis).astype(jnp.int32) // step) % 2
            place = place + bit * (1 << n)

    keep, send = pl.pallas_call(
        lambda *refs: back_kernel(*refs, scale=loss_scale),
        grid=(chunks,),
        out_shape=(
            jax.ShapeDtypeStruct((HALF_ROWS, 128), F32),
            jax.ShapeDtypeStruct((HALF_ROWS, 128), BF16),
        ),
        in_specs=[
            SMEM, chunk(COT_ROWS, 128), chunk(COT_ROWS, 128),
            whole(agg_weight.shape), whole(agg_weight.shape), pixel_spec,
            chunk(rows, channels), chunk(rows, 1), chunk(rows, channels), chunk(rows, 1),
            chunk(rows, hid), chunk(rows, hid), chunk(128, 4 * channels),
            whole((1, channels)), whole(up_weight.shape), whole(proj_turned.shape),
            whole((1, channels)), whole((1, channels)), whole(ds_turned.shape),
        ],
        out_specs=(whole((HALF_ROWS, 128)), whole((HALF_ROWS, 128))),
        scratch_shapes=[
            pltpu.VMEM((SIDE + 6, SIDE + 6, 8, channels), F32),
            pltpu.VMEM((SIDE // 2, 2, SIDE // 2, 2, 8, channels), F32),
            pltpu.VMEM((SIDE, SIDE, 8, channels), F32),
            pltpu.VMEM((7, 7, 8, channels), F32),
            pltpu.VMEM(ds_turned.shape, F32),
            pltpu.VMEM(up_weight.shape, F32),
            pltpu.VMEM(proj_turned.shape, F32),
            pltpu.VMEM((2 * HALF_ROWS, 128), F32),
            *pixel_scratch,
        ],
        compiler_params=params_of(),
        cost_estimate=takes(3.7),
        name="stem_back",
    )(
        chan, cots_own, cots_peer, agg_weight, peer_weight, got,
        hat1, rstd1, hat2, rstd2, hidden, slope, patches,
        gain, up_weight, proj_turned, scale, low_gain, ds_turned,
    )

    feats_band = jnp.concatenate([feats, swapped(feats, "chan", 1)], axis=0)
    spread, below = pl.pallas_call(
        lambda *refs: spread_kernel(*refs, last=out_rows),
        grid=(blocks,),
        out_shape=(
            jax.ShapeDtypeStruct((blocks * 72, e_half), F32),
            jax.ShapeDtypeStruct((e_half, cols), F32),
        ),
        in_specs=[
            chunk(FEAT_ROWS, 128), whole(agg_weight.shape),
            pl.BlockSpec((72, cols), lambda g: (g, 0)),
        ],
        out_specs=(pl.BlockSpec((72, e_half), lambda g: (g, 0)), whole((e_half, cols))),
        compiler_params=params_of(),
        cost_estimate=takes(1.0),
        name="spread",
    )(feats_band, agg_weight, key)
    above = shifted(below, "slide", 1)
    agg_map = pl.pallas_call(
        map_kernel,
        out_shape=jax.ShapeDtypeStruct((out_rows, e_half, cols), BF16),
        in_specs=[VMEM, VMEM, VMEM],
        out_specs=VMEM,
        compiler_params=pltpu.CompilerParams(vmem_limit_bytes=24 << 20),
        cost_estimate=takes(3.5),
        name="agg_map",
    )(spread, key, above)[None]

    count = 2 * near.shape[0] if gather else chunks
    per = count if gather else 1
    near_count = near.shape[0] if gather else 1
    agg_keep, agg_send = pl.pallas_call(
        lambda *refs: weight_kernel(*refs, scale=loss_scale),
        grid=(count // per,),
        out_shape=(
            jax.ShapeDtypeStruct((9, width, e_half), F32),
            jax.ShapeDtypeStruct((9, width, e_half), F32),
        ),
        in_specs=[
            SMEM,
            pl.BlockSpec((near_count, BLOCK_ROWS, 128), lambda g: (g, 0, 0)),
            pl.BlockSpec((near_count, BLOCK_ROWS, 128), lambda g: (g, 0, 0)),
        ],
        out_specs=(whole((9, width, e_half)), whole((9, width, e_half))),
        scratch_shapes=[
            pltpu.VMEM((16, per * 8, width), F32),
            pltpu.VMEM((9, per * 8, 256), F32),
        ],
        compiler_params=params_of(),
        cost_estimate=takes(1.4),
        name="agg_weight_grad",
    )(place, near, far)
    agg_grad = agg_keep + swapped(agg_send.astype(BF16), "chan", 1).astype(F32)
    if not gather:
        agg_grad = lax.psum(agg_grad, ("slide", "rep"))

    part = keep + swapped(send, "chan", 1).astype(F32)
    for axis in ("rep", "slide"):
        step = 1
        while step < lax.axis_size(axis):
            wire = part.astype(BF16)
            part = wire.astype(F32) + swapped(wire, axis, step).astype(F32)
            step *= 2
    dw_grad, up_grad, proj_grad, ds_grad = pl.pallas_call(
        unpack_kernel,
        out_shape=(
            jax.ShapeDtypeStruct(dw_weight.shape, F32),
            jax.ShapeDtypeStruct(up_weight.shape, F32),
            jax.ShapeDtypeStruct(proj_turned.shape, F32),
            jax.ShapeDtypeStruct(ds_turned.shape, F32),
        ),
        in_specs=[SMEM, VMEM, VMEM],
        out_specs=(VMEM, VMEM, VMEM, VMEM),
        scratch_shapes=[pltpu.VMEM((2 * HALF_ROWS, 128), F32)],
        compiler_params=pltpu.CompilerParams(vmem_limit_bytes=24 << 20),
        cost_estimate=takes(1.5),
        name="unpack",
    )(chan, part, swapped(part, "chan", 1))
    proj_grad = proj_grad.T
    ds_grad = ds_grad.T
    return (agg_map, agg_grad, dw_grad, up_grad, proj_grad, ds_grad)


def solution(mesh):
    in_specs = (
        P(("groups", "rep"), ("slide", "chan"), None),
        P(("groups", "rep"), ("slide", "chan")),
        P(("groups", "rep"), "slide", "chan", None),
        P(), P(), P(), P(), P(), P(), P(),
        P(None, None, "chan"),
    )
    out_specs = (
        P(("groups", "rep"), "slide", "chan", None),
        P("groups", None, "chan"),
        P("groups", None),
        P("groups", None),
        P("groups", None),
        P("groups", None),
    )
    return jax.shard_map(
        on_device, mesh=mesh, in_specs=in_specs, out_specs=out_specs, check_vma=False
    )
```

```python
import math

import jax
import jax.numpy as jnp
from jax import lax
from jax.experimental import pallas as pl
from jax.experimental.pallas import tpu as pltpu
from jax.sharding import PartitionSpec as P

SIDE = 8
CAP = 2
GW = 64
BAND_CELLS = 512
PIX = SIDE * SIDE
HALF_ROWS = 608
FEAT_ROWS = 192
COT_ROWS = 72
WIRE_ROWS = 56
BLOCK_ROWS = FEAT_ROWS + 2 * COT_ROWS
F32 = jnp.float32
BF16 = jnp.bfloat16
VMEM = pl.BlockSpec(memory_space=pltpu.VMEM)
SMEM = pl.BlockSpec(memory_space=pltpu.SMEM)


def params_of(steps=1):
    return pltpu.CompilerParams(
        dimension_semantics=("arbitrary",) * steps, vmem_limit_bytes=24 << 20
    )


def takes(microseconds):
    return pl.CostEstimate(
        flops=0, transcendentals=0, bytes_accessed=int(microseconds * 3.69e6)
    )


def nn(left, right):
    return lax.dot_general(left, right, (((1,), (0,)), ((), ())), preferred_element_type=F32)


def nt(left, right):
    return lax.dot_general(left, right, (((1,), (1,)), ((), ())), preferred_element_type=F32)


def tn(left, right):
    return lax.dot_general(left, right, (((0,), (0,)), ((), ())), preferred_element_type=F32)


def shifted(value, axis, steps):
    count = lax.axis_size(axis)
    first, last = (max(0, -steps), min(count, count - steps))
    return lax.ppermute(value, axis, [(source, source + steps) for source in range(first, last)])


def swapped(value, axis, step):
    count = lax.axis_size(axis)
    return lax.ppermute(value, axis, [(place, place ^ step) for place in range(count)])


def reach(tap):
    return (1, 2) if tap == 0 else (0, 1)


def pack_kernel(cells_ref, pixels_ref, out_ref, wide_ref):
    slots = pixels_ref.shape[0]
    rows = out_ref.shape[0]
    pixch = pixels_ref.shape[1]
    cells = [cells_ref[0, t] for t in range(slots)]
    live = [cell >= 0 for cell in cells]
    bands = [cell // BAND_CELLS for cell in cells]
    places = []
    for t in range(slots):
        rank = jnp.int32(0)
        for s in range(t):
            rank = rank + ((bands[s] == bands[t]) & live[s]).astype(jnp.int32)
        places.append(jnp.where(live[t], bands[t] * CAP + rank, -1))
    dest = lax.broadcasted_iota(jnp.int32, (rows, slots), 0)
    slot = lax.broadcasted_iota(jnp.int32, (rows, slots), 1)
    place = jnp.full((rows, slots), -1, jnp.int32)
    for t in range(slots):
        place = jnp.where(slot == t, places[t], place)
    route = (place == dest).astype(F32).astype(BF16)
    routed = nn(route, pixels_ref[...])
    wide_ref[...] = jnp.zeros_like(wide_ref)
    for n in range(pixch // 128):
        wide_ref[:, n, :] = routed[:, 128 * n : 128 * n + 128]
    lane = lax.broadcasted_iota(jnp.int32, (rows, 128), 1)
    base = (lax.broadcasted_iota(jnp.int32, (rows, 128), 0) // CAP) * CAP
    notes = jnp.zeros((rows, 128), F32)
    for t in range(slots):
        within = cells[t] % BAND_CELLS
        own_row = (within // GW).astype(F32)
        own_col = (within % GW).astype(F32)
        for rank in range(CAP):
            hit = base + rank == places[t]
            for at, value in enumerate((own_row, own_col, jnp.float32(1.0))):
                notes = jnp.where(hit & (lane == 3 * rank + at), value, notes)
    wide_ref[:, pixch // 128, :] = notes
    out_ref[...] = wide_ref[...].astype(BF16)


def patch_kernel(chan_ref, meta_ref, cot_ref, below_ref, key_ref, own_ref, send_ref, meta_f32):
    sources = meta_ref.shape[0]
    chunks = sources // 8
    out_rows, e_half, _ = cot_ref.shape
    meta_f32[...] = meta_ref[...].astype(F32)
    meta = meta_f32[:, 0, :]
    first = chan_ref[0] == 0
    lane = lax.broadcasted_iota(jnp.int32, (8, 128), 1).astype(F32)
    blocks = []
    for mine in (True, False):
        for chunk in range(chunks):
            part = meta[chunk * 8 : chunk * 8 + 8]
            low = [jnp.broadcast_to(part[:, n : n + 1], (8, 128)) for n in range(3)]
            high = [jnp.broadcast_to(part[:, n : n + 1], (8, 128)) for n in range(3, 6)]
            row, col, valid = (
                jnp.where(first == mine, one, two) for one, two in zip(low, high)
            )
            for u in range(3):
                for v in range(3):
                    hit = (lane == 2.0 * col + v) & (valid > 0.5)
                    blocks.append(jnp.where(hit, 2.0 * row + u, -1.0))
    key = jnp.concatenate(blocks, axis=0)
    key_ref[...] = key

    def step(o, total):
        pick = (key == o.astype(F32)).astype(F32).astype(BF16)
        return total + nt(pick, cot_ref[o].astype(BF16))

    total = lax.fori_loop(
        0, out_rows, step, jnp.zeros((key.shape[0], e_half), F32), unroll=4
    )
    pick = (key == float(out_rows)).astype(F32).astype(BF16)
    total = total + nt(pick, below_ref[...])
    half = total.shape[0] // 2
    own_ref[...] = jnp.zeros_like(own_ref)
    send_ref[...] = jnp.zeros_like(send_ref)
    own_ref[:, :e_half] = total[:half].astype(BF16)
    send_ref[:, :e_half] = total[half:].astype(BF16)


def center_of(values):
    center = values - jnp.mean(values, axis=-1, keepdims=True)
    rstd = lax.rsqrt(jnp.mean(center * center, axis=-1, keepdims=True) + 1e-06)
    return center * rstd, rstd


def fill_padded(padded_ref, got_ref, wide_ref, pixels_ref, channels):
    wide_ref[...] = got_ref[...].astype(F32)
    for n in range(pixels_ref.shape[1] // 128):
        pixels_ref[:, 128 * n : 128 * n + 128] = wide_ref[:, n, :]
    padded_ref[...] = jnp.zeros_like(padded_ref)
    for i in range(SIDE):
        for j in range(SIDE):
            at = (i * SIDE + j) * channels
            padded_ref[i + 3, j + 3] = pixels_ref[:, at : at + channels]


def stem_kernel(
    got_ref, dw_ref, gain_ref, up_ref, proj_ref, scale_ref, ds_gain_ref, ds_ref,
    feat_ref, hat1_ref, rstd1_ref, hat2_ref, rstd2_ref, hidden_ref, slope_ref, patch_ref,
    padded_ref, spatial_ref, low_ref, patch_f32, wide_ref, pixels_ref,
):
    channels = dw_ref.shape[1]
    fill_padded(padded_ref, got_ref, wide_ref, pixels_ref, channels)

    def row_step(i, carry):
        total = jnp.zeros((SIDE, 8, channels), F32)
        for a in range(7):
            for b in range(7):
                weight = dw_ref[pl.ds(7 * a + b, 1), :].reshape(1, 1, channels)
                total = total + weight * padded_ref[i + a, b : b + SIDE]
        spatial_ref[i] = total
        return carry

    lax.fori_loop(0, SIDE, row_step, 0)
    hat1, rstd1 = center_of(spatial_ref[...].reshape(PIX * 8, channels))
    hat1_ref[...] = hat1
    rstd1_ref[...] = rstd1
    normed = (hat1 * gain_ref[...]).astype(BF16)
    before = nn(normed, up_ref[...])
    cdf = 0.5 * (1.0 + lax.erf(before * math.sqrt(0.5)))
    pdf = jnp.exp(-0.5 * before * before) * (1.0 / math.sqrt(2.0 * math.pi))
    hidden = (before * cdf).astype(BF16)
    hidden_ref[...] = hidden
    slope_ref[...] = cdf + before * pdf
    branch = nt(hidden, proj_ref[...])
    inputs = padded_ref[3 : 3 + SIDE, 3 : 3 + SIDE].reshape(PIX * 8, channels)
    hat2, rstd2 = center_of(inputs + scale_ref[...] * branch)
    hat2_ref[...] = hat2
    rstd2_ref[...] = rstd2
    low_ref[...] = (hat2 * ds_gain_ref[...]).reshape(low_ref.shape)
    half = SIDE // 2
    for di in range(2):
        for dj in range(2):
            at = (2 * di + dj) * channels
            patch_f32[:, at : at + channels] = low_ref[:, di, :, dj].reshape(-1, channels)
    patches = patch_f32[...].astype(BF16)
    patch_ref[...] = patches
    total = nt(patches, ds_ref[...])
    rows = total.shape[0]
    feat_ref[0:rows] = total[:, 0:128].astype(BF16)
    rest = jnp.concatenate([total[: rows // 2, 128:192], total[rows // 2 :, 128:192]], axis=1)
    feat_ref[rows:] = rest.astype(BF16)


def unfold(block):
    rest = block[128:]
    return jnp.concatenate(
        [block[:128], jnp.concatenate([rest[:, :64], rest[:, 64:]], axis=0)], axis=1
    )


def back_kernel(
    chan_ref, own_ref, peer_ref, w_own_ref, w_peer_ref, got_ref,
    hat1_ref, rstd1_ref, hat2_ref, rstd2_ref, hidden_ref, slope_ref, patch_ref,
    gain_ref, up_ref, proj_ref, scale_ref, ds_gain_ref, ds_ref,
    keep_ref, send_ref,
    padded_ref, dlow_ref, dspatial_ref, dw_ref, ds_acc, up_acc, proj_acc, pack_ref,
    wide_ref, pixels_ref,
    *, scale,
):
    channels = gain_ref.shape[1]
    e_half = w_own_ref.shape[2]
    half = SIDE // 2
    step = pl.program_id(0)

    @pl.when(step == 0)
    def _():
        dw_ref[...] = jnp.zeros_like(dw_ref)
        ds_acc[...] = jnp.zeros_like(ds_acc)
        up_acc[...] = jnp.zeros_like(up_acc)
        proj_acc[...] = jnp.zeros_like(proj_acc)

    own = own_ref[...].astype(F32)[:, :e_half].reshape(9, 8, e_half)
    peer = peer_ref[...].astype(F32)[:, :e_half].reshape(9, 8, e_half)
    grads = {}
    for a in range(3):
        for b in range(3):
            places = [(u, v) for u in reach(a) for v in reach(b)]
            left_own = jnp.concatenate([own[3 * u + v] for u, v in places], axis=0).astype(BF16)
            left_peer = jnp.concatenate([peer[3 * u + v] for u, v in places], axis=0).astype(BF16)
            out = nt(left_own, w_own_ref[3 * a + b]) + nt(left_peer, w_peer_ref[3 * a + b])
            for n, (u, v) in enumerate(places):
                at = (2 * u + a - 1) * half + 2 * v + b - 1
                piece = out[8 * n : 8 * n + 8]
                grads[at] = grads[at] + piece if at in grads else piece
    dfeat = jnp.concatenate([grads[at] for at in range(half * half)], axis=0) * scale
    dfeat = dfeat.astype(BF16)

    hat2 = hat2_ref[...]
    ds_acc[...] += tn(dfeat, patch_ref[...])
    back = nn(dfeat, ds_ref[...])
    for di in range(2):
        for dj in range(2):
            at = (2 * di + dj) * channels
            dlow_ref[:, di, :, dj] = back[:, at : at + channels].reshape(half, half, 8, channels)
    dhat2 = dlow_ref[...].reshape(PIX * 8, channels) * ds_gain_ref[...]
    mean_a = jnp.mean(dhat2, axis=-1, keepdims=True)
    mean_b = jnp.mean(dhat2 * hat2, axis=-1, keepdims=True)
    dmixed = rstd2_ref[...] * (dhat2 - mean_a - hat2 * mean_b)
    dbranch = (dmixed * scale_ref[...]).astype(BF16)
    proj_acc[...] += tn(dbranch, hidden_ref[...])
    dhidden = nn(dbranch, proj_ref[...])
    dbefore = (dhidden * slope_ref[...]).astype(BF16)
    hat1 = hat1_ref[...]
    normed = (hat1 * gain_ref[...]).astype(BF16)
    up_acc[...] += tn(normed, dbefore)
    dhat1 = nt(dbefore, up_ref[...]) * gain_ref[...]
    mean_a = jnp.mean(dhat1, axis=-1, keepdims=True)
    mean_b = jnp.mean(dhat1 * hat1, axis=-1, keepdims=True)
    dspatial = rstd1_ref[...] * (dhat1 - mean_a - hat1 * mean_b)
    dspatial_ref[...] = dspatial.reshape(SIDE, SIDE, 8, channels)
    fill_padded(padded_ref, got_ref, wide_ref, pixels_ref, channels)

    def tap_step(a, carry):
        totals = [jnp.zeros((8, channels), F32) for _ in range(7)]
        for i in range(SIDE):
            grad = dspatial_ref[i]
            for b in range(7):
                product = padded_ref[i + a, b : b + SIDE] * grad
                totals[b] = totals[b] + jnp.sum(product, axis=0)
        for b in range(7):
            dw_ref[a, b] += totals[b]
        return carry

    lax.fori_loop(0, 7, tap_step, 0)

    @pl.when(step == pl.num_programs(0) - 1)
    def _():
        pack_ref[...] = jnp.zeros_like(pack_ref)
        for n in range(3):
            lanes = slice(128 * n, 128 * n + 128)
            pack_ref[192 * n : 192 * n + 192, :] = ds_acc[:, lanes]
            pack_ref[576 + 96 * n : 672 + 96 * n, :] = up_acc[:, lanes]
            pack_ref[864 + 96 * n : 960 + 96 * n, :] = proj_acc[:, lanes]
        pack_ref[1152:1201, 0:channels] = jnp.sum(dw_ref[...], axis=2).reshape(49, channels)
        mine = pl.multiple_of(chan_ref[0] * HALF_ROWS, 8)
        other = pl.multiple_of((1 - chan_ref[0]) * HALF_ROWS, 8)
        keep_ref[...] = pack_ref[pl.ds(mine, HALF_ROWS), :]
        send_ref[...] = pack_ref[pl.ds(other, HALF_ROWS), :].astype(BF16)


def unpack_kernel(chan_ref, own_ref, peer_ref, dw_ref, up_ref, proj_ref, ds_ref, pack_ref):
    channels = dw_ref.shape[1]
    mine = pl.multiple_of(chan_ref[0] * HALF_ROWS, 8)
    other = pl.multiple_of((1 - chan_ref[0]) * HALF_ROWS, 8)
    pack_ref[pl.ds(mine, HALF_ROWS), :] = own_ref[...]
    pack_ref[pl.ds(other, HALF_ROWS), :] = peer_ref[...]
    for n in range(3):
        lanes = slice(128 * n, 128 * n + 128)
        ds_ref[:, lanes] = pack_ref[192 * n : 192 * n + 192, :]
        up_ref[:, lanes] = pack_ref[576 + 96 * n : 672 + 96 * n, :]
        proj_ref[:, lanes] = pack_ref[864 + 96 * n : 960 + 96 * n, :]
    dw_ref[...] = pack_ref[1152:1201, 0:channels]


def spread_kernel(feat_ref, w_ref, key_ref, y_ref, below_ref, *, last):
    width = w_ref.shape[1]
    feats = unfold(feat_ref[...].astype(F32)).reshape(16, 8, width)
    outs = {}
    for a in range(3):
        for b in range(3):
            places = [(u, v) for u in reach(a) for v in reach(b)]
            left = jnp.concatenate(
                [feats[(2 * u + a - 1) * 4 + 2 * v + b - 1] for u, v in places], axis=0
            ).astype(BF16)
            out = nn(left, w_ref[3 * a + b])
            for n, (u, v) in enumerate(places):
                piece = out[8 * n : 8 * n + 8]
                at = 3 * u + v
                outs[at] = outs[at] + piece if at in outs else piece
    total = jnp.concatenate([outs[at] for at in range(9)], axis=0)
    y_ref[...] = total
    pick = (key_ref[...] == float(last)).astype(F32).astype(BF16)
    high = total.astype(BF16)
    rest = (total - high.astype(F32)).astype(BF16)

    @pl.when(pl.program_id(0) == 0)
    def _():
        below_ref[...] = jnp.zeros_like(below_ref)

    below_ref[...] += tn(high, pick) + tn(rest, pick)


def map_kernel(y_ref, key_ref, above_ref, out_ref):
    out_rows, width, _ = out_ref.shape
    turned = y_ref[...].T
    high = turned.astype(BF16)
    rest = (turned - high.astype(F32)).astype(BF16)
    key = key_ref[...]

    def row_of(o):
        pick = (key == o).astype(F32).astype(BF16)
        return nn(high, pick) + nn(rest, pick)

    out_ref[0] = (row_of(0.0) + above_ref[...]).astype(BF16)

    def step(o, carry):
        out_ref[o] = row_of(o.astype(F32)).astype(BF16)
        return carry

    lax.fori_loop(1, out_rows, step, 0)


def weight_kernel(place_ref, near_ref, far_ref, keep_ref, send_ref, feat_ref, cot_ref, *, scale):
    near = near_ref.shape[0]
    members = feat_ref.shape[1] // 8
    width, e_half = keep_ref.shape[1:]
    step = pl.program_id(0)

    @pl.when(step == 0)
    def _():
        keep_ref[...] = jnp.zeros_like(keep_ref)
        send_ref[...] = jnp.zeros_like(send_ref)

    def take(member, block):
        block = block.astype(F32)
        feat_ref[:, 8 * member : 8 * member + 8] = unfold(block[:FEAT_ROWS]).reshape(16, 8, width)
        own = block[FEAT_ROWS : FEAT_ROWS + COT_ROWS].reshape(9, 8, 128)
        peer = block[FEAT_ROWS + COT_ROWS :].reshape(9, 8, 128)
        cot_ref[:, 8 * member : 8 * member + 8, 0:128] = own
        cot_ref[:, 8 * member : 8 * member + 8, 128:256] = peer

    for member in range(members):
        at = place_ref[0] ^ member

        @pl.when(at < near)
        def _():
            take(member, near_ref[jnp.minimum(at, near - 1)])

        if members > near:

            @pl.when(at >= near)
            def _():
                take(member, far_ref[jnp.maximum(at - near, 0)])

    for a in range(3):
        for b in range(3):
            places = [(u, v) for u in reach(a) for v in reach(b)]
            left = jnp.concatenate(
                [feat_ref[(2 * u + a - 1) * 4 + 2 * v + b - 1] for u, v in places], axis=0
            ).astype(BF16)
            right = jnp.concatenate([cot_ref[3 * u + v] for u, v in places], axis=0).astype(BF16)
            total = tn(left, right) * scale
            keep_ref[3 * a + b] += total[:, :e_half]
            send_ref[3 * a + b] += total[:, 128 : 128 + e_half]


def whole(shape):
    return pl.BlockSpec(shape, lambda g: (0,) * len(shape))


def on_device(
    tile_pixels, tile_cell, agg_cot, dw_weight, norm_gain, up_weight, proj_weight,
    layer_scale, ds_gain, ds_weight, agg_weight,
):
    channels = dw_weight.shape[1]
    hid = up_weight.shape[1]
    width = ds_weight.shape[1]
    bands = lax.axis_size("slide")
    sources = bands * lax.axis_size("chan")
    chunks = sources // 8
    pixch = tile_pixels.shape[2]
    out_rows = agg_cot.shape[1]
    e_half = agg_weight.shape[2]
    cols = agg_cot.shape[3]
    blocks = CAP * chunks
    total_rows = out_rows * bands * lax.axis_size("rep") * cols
    loss_scale = 1.0 / math.sqrt(total_rows)
    chan = lax.axis_index("chan").astype(jnp.int32)[None]
    gain = norm_gain[None]
    scale = layer_scale[None]
    low_gain = ds_gain[None]
    proj_turned = proj_weight.T
    ds_turned = ds_weight.T

    peer_weight = swapped(agg_weight, "chan", 1)
    below_cot = shifted(agg_cot[0, 0].astype(BF16), "slide", -1)

    packed = pl.pallas_call(
        pack_kernel,
        out_shape=jax.ShapeDtypeStruct((sources, WIRE_ROWS, 128), BF16),
        in_specs=[SMEM, VMEM],
        out_specs=VMEM,
        scratch_shapes=[pltpu.VMEM((sources, WIRE_ROWS, 128), F32)],
        compiler_params=pltpu.CompilerParams(vmem_limit_bytes=24 << 20),
        cost_estimate=takes(1.5),
        name="pack",
    )(tile_cell, tile_pixels[0])
    got = lax.all_to_all(packed, ("slide", "chan"), split_axis=0, concat_axis=0, tiled=True)

    key, cots_own, cots_send = pl.pallas_call(
        patch_kernel,
        out_shape=(
            jax.ShapeDtypeStruct((blocks * COT_ROWS, cols), F32),
            jax.ShapeDtypeStruct((chunks * COT_ROWS, 128), BF16),
            jax.ShapeDtypeStruct((chunks * COT_ROWS, 128), BF16),
        ),
        in_specs=[
            SMEM,
            pl.BlockSpec((sources, 8, 128), lambda i: (0, pixch // 1024, 0)),
            pl.BlockSpec((None, out_rows, e_half, cols), lambda i: (0, 0, 0, 0)),
            whole((e_half, cols)),
        ],
        out_specs=(
            whole((blocks * COT_ROWS, cols)),
            whole((chunks * COT_ROWS, 128)),
            whole((chunks * COT_ROWS, 128)),
        ),
        grid=(1,),
        scratch_shapes=[pltpu.VMEM((sources, 8, 128), F32)],
        compiler_params=params_of(),
        cost_estimate=takes(1.2),
        name="patch",
    )(chan, got, agg_cot, below_cot)
    cots_peer = swapped(cots_send, "chan", 1)
    cots_own = cots_own.reshape(chunks, COT_ROWS, 128)
    cots_peer = cots_peer.reshape(chunks, COT_ROWS, 128)

    rows = PIX * 8
    pixel_spec = pl.BlockSpec((8, WIRE_ROWS, 128), lambda g: (g, 0, 0))
    pixel_scratch = [pltpu.VMEM((8, WIRE_ROWS, 128), F32), pltpu.VMEM((8, pixch), F32)]

    def chunk(*shape):
        return pl.BlockSpec((None,) + shape, lambda g: (g,) + (0,) * len(shape))

    feats, hat1, rstd1, hat2, rstd2, hidden, slope, patches = pl.pallas_call(
        stem_kernel,
        grid=(chunks,),
        out_shape=(
            jax.ShapeDtypeStruct((chunks, FEAT_ROWS, 128), BF16),
            jax.ShapeDtypeStruct((chunks, rows, channels), F32),
            jax.ShapeDtypeStruct((chunks, rows, 1), F32),
            jax.ShapeDtypeStruct((chunks, rows, channels), F32),
            jax.ShapeDtypeStruct((chunks, rows, 1), F32),
            jax.ShapeDtypeStruct((chunks, rows, hid), BF16),
            jax.ShapeDtypeStruct((chunks, rows, hid), F32),
            jax.ShapeDtypeStruct((chunks, 128, 4 * channels), BF16),
        ),
        in_specs=[
            pixel_spec,
            whole(dw_weight.shape), whole((1, channels)), whole(up_weight.shape),
            whole(proj_turned.shape), whole((1, channels)), whole((1, channels)),
            whole(ds_turned.shape),
        ],
        out_specs=(
            chunk(FEAT_ROWS, 128), chunk(rows, channels), chunk(rows, 1), chunk(rows, channels),
            chunk(rows, 1), chunk(rows, hid), chunk(rows, hid), chunk(128, 4 * channels),
        ),
        scratch_shapes=[
            pltpu.VMEM((SIDE + 6, SIDE + 6, 8, channels), F32),
            pltpu.VMEM((SIDE, SIDE, 8, channels), F32),
            pltpu.VMEM((SIDE // 2, 2, SIDE // 2, 2, 8, channels), F32),
            pltpu.VMEM((128, 4 * channels), F32),
            *pixel_scratch,
        ],
        compiler_params=params_of(),
        cost_estimate=takes(2.7),
        name="stem",
    )(got, dw_weight, gain, up_weight, proj_turned, scale, low_gain, ds_turned)

    feats_band = jnp.concatenate([feats, swapped(feats, "chan", 1)], axis=0)
    spread, below = pl.pallas_call(
        lambda *refs: spread_kernel(*refs, last=out_rows),
        grid=(blocks,),
        out_shape=(
            jax.ShapeDtypeStruct((blocks * 72, e_half), F32),
            jax.ShapeDtypeStruct((e_half, cols), F32),
        ),
        in_specs=[
            chunk(FEAT_ROWS, 128), whole(agg_weight.shape),
            pl.BlockSpec((72, cols), lambda g: (g, 0)),
        ],
        out_specs=(pl.BlockSpec((72, e_half), lambda g: (g, 0)), whole((e_half, cols))),
        compiler_params=params_of(),
        cost_estimate=takes(1.0),
        name="spread",
    )(feats_band, agg_weight, key)
    above = shifted(below, "slide", 1)
    map_call = pl.pallas_call(
        map_kernel,
        out_shape=jax.ShapeDtypeStruct((out_rows, e_half, cols), BF16),
        in_specs=[VMEM, VMEM, VMEM],
        out_specs=VMEM,
        compiler_params=pltpu.CompilerParams(vmem_limit_bytes=24 << 20),
        cost_estimate=takes(3.5),
        name="agg_map",
    )
    agg_map = map_call(spread, key, above)

    tile_blocks = jnp.concatenate([feats, cots_own, cots_peer], axis=1)
    gather = chunks == 1
    near = far = tile_blocks
    place = jnp.zeros((1,), jnp.int32)
    if gather:
        spans = [("slide", 1 << n) for n in reversed(range(bands.bit_length() - 1))]
        spans += [("rep", 1 << n) for n in range(lax.axis_size("rep").bit_length() - 1)]
        for n, (axis, step) in enumerate(spans):
            near = far if n == 0 else jnp.concatenate([near, far], axis=0)
            if n == 1:
                near, spread, below = lax.optimization_barrier((near, spread, below))
                above = shifted(below, "slide", 1)
                agg_map = map_call(spread, key, above)
            if n == len(spans) - 1:
                near, agg_map = lax.optimization_barrier((near, agg_map))
            far = swapped(near, axis, step)
            bit = (lax.axis_index(axis).astype(jnp.int32) // step) % 2
            place = place + bit * (1 << n)
    keep, send = pl.pallas_call(
        lambda *refs: back_kernel(*refs, scale=loss_scale),
        grid=(chunks,),
        out_shape=(
            jax.ShapeDtypeStruct((HALF_ROWS, 128), F32),
            jax.ShapeDtypeStruct((HALF_ROWS, 128), BF16),
        ),
        in_specs=[
            SMEM, chunk(COT_ROWS, 128), chunk(COT_ROWS, 128),
            whole(agg_weight.shape), whole(agg_weight.shape), pixel_spec,
            chunk(rows, channels), chunk(rows, 1), chunk(rows, channels), chunk(rows, 1),
            chunk(rows, hid), chunk(rows, hid), chunk(128, 4 * channels),
            whole((1, channels)), whole(up_weight.shape), whole(proj_turned.shape),
            whole((1, channels)), whole((1, channels)), whole(ds_turned.shape),
        ],
        out_specs=(whole((HALF_ROWS, 128)), whole((HALF_ROWS, 128))),
        scratch_shapes=[
            pltpu.VMEM((SIDE + 6, SIDE + 6, 8, channels), F32),
            pltpu.VMEM((SIDE // 2, 2, SIDE // 2, 2, 8, channels), F32),
            pltpu.VMEM((SIDE, SIDE, 8, channels), F32),
            pltpu.VMEM((7, 7, 8, channels), F32),
            pltpu.VMEM(ds_turned.shape, F32),
            pltpu.VMEM(up_weight.shape, F32),
            pltpu.VMEM(proj_turned.shape, F32),
            pltpu.VMEM((2 * HALF_ROWS, 128), F32),
            *pixel_scratch,
        ],
        compiler_params=params_of(),
        cost_estimate=takes(3.7),
        name="stem_back",
    )(
        chan, cots_own, cots_peer, agg_weight, peer_weight, got,
        hat1, rstd1, hat2, rstd2, hidden, slope, patches,
        gain, up_weight, proj_turned, scale, low_gain, ds_turned,
    )

    count = 2 * near.shape[0] if gather else chunks
    per = count if gather else 1
    near_count = near.shape[0] if gather else 1
    agg_keep, agg_send = pl.pallas_call(
        lambda *refs: weight_kernel(*refs, scale=loss_scale),
        grid=(count // per,),
        out_shape=(
            jax.ShapeDtypeStruct((9, width, e_half), F32),
            jax.ShapeDtypeStruct((9, width, e_half), F32),
        ),
        in_specs=[
            SMEM,
            pl.BlockSpec((near_count, BLOCK_ROWS, 128), lambda g: (g, 0, 0)),
            pl.BlockSpec((near_count, BLOCK_ROWS, 128), lambda g: (g, 0, 0)),
        ],
        out_specs=(whole((9, width, e_half)), whole((9, width, e_half))),
        scratch_shapes=[
            pltpu.VMEM((16, per * 8, width), F32),
            pltpu.VMEM((9, per * 8, 256), F32),
        ],
        compiler_params=params_of(),
        cost_estimate=takes(1.4),
        name="agg_weight_grad",
    )(place, near, far)
    agg_grad = agg_keep + swapped(agg_send.astype(BF16), "chan", 1).astype(F32)
    if not gather:
        agg_grad = lax.psum(agg_grad, ("slide", "rep"))

    part = keep + swapped(send, "chan", 1).astype(F32)
    for axis in ("rep", "slide"):
        step = 1
        while step < lax.axis_size(axis):
            wire = part.astype(BF16)
            part = wire.astype(F32) + swapped(wire, axis, step).astype(F32)
            step *= 2
    dw_grad, up_grad, proj_grad, ds_grad = pl.pallas_call(
        unpack_kernel,
        out_shape=(
            jax.ShapeDtypeStruct(dw_weight.shape, F32),
            jax.ShapeDtypeStruct(up_weight.shape, F32),
            jax.ShapeDtypeStruct(proj_turned.shape, F32),
            jax.ShapeDtypeStruct(ds_turned.shape, F32),
        ),
        in_specs=[SMEM, VMEM, VMEM],
        out_specs=(VMEM, VMEM, VMEM, VMEM),
        scratch_shapes=[pltpu.VMEM((2 * HALF_ROWS, 128), F32)],
        compiler_params=pltpu.CompilerParams(vmem_limit_bytes=24 << 20),
        cost_estimate=takes(1.5),
        name="unpack",
    )(chan, part, swapped(part, "chan", 1))
    proj_grad = proj_grad.T
    ds_grad = ds_grad.T
    return (agg_map[None], agg_grad, dw_grad, up_grad, proj_grad, ds_grad)


def solution(mesh):
    in_specs = (
        P(("groups", "rep"), ("slide", "chan"), None),
        P(("groups", "rep"), ("slide", "chan")),
        P(("groups", "rep"), "slide", "chan", None),
        P(), P(), P(), P(), P(), P(), P(),
        P(None, None, "chan"),
    )
    out_specs = (
        P(("groups", "rep"), "slide", "chan", None),
        P("groups", None, "chan"),
        P("groups", None),
        P("groups", None),
        P("groups", None),
        P("groups", None),
    )
    return jax.shard_map(
        on_device, mesh=mesh, in_specs=in_specs, out_specs=out_specs, check_vma=False
    )
```

```python
import math

import jax
import jax.numpy as jnp
from jax import lax
from jax.experimental import pallas as pl
from jax.experimental.pallas import tpu as pltpu
from jax.sharding import PartitionSpec as P

SIDE = 8
CAP = 2
GW = 64
BAND_CELLS = 512
PIX = SIDE * SIDE
HALF_ROWS = 608
FEAT_ROWS = 192
COT_ROWS = 72
WIRE_ROWS = 56
BLOCK_ROWS = FEAT_ROWS + 2 * COT_ROWS
F32 = jnp.float32
BF16 = jnp.bfloat16
VMEM = pl.BlockSpec(memory_space=pltpu.VMEM)
SMEM = pl.BlockSpec(memory_space=pltpu.SMEM)


def params_of(steps=1):
    return pltpu.CompilerParams(
        dimension_semantics=("arbitrary",) * steps, vmem_limit_bytes=24 << 20
    )


def takes(microseconds):
    return pl.CostEstimate(
        flops=0, transcendentals=0, bytes_accessed=int(microseconds * 3.69e6)
    )


def nn(left, right):
    return lax.dot_general(left, right, (((1,), (0,)), ((), ())), preferred_element_type=F32)


def nt(left, right):
    return lax.dot_general(left, right, (((1,), (1,)), ((), ())), preferred_element_type=F32)


def tn(left, right):
    return lax.dot_general(left, right, (((0,), (0,)), ((), ())), preferred_element_type=F32)


def shifted(value, axis, steps):
    count = lax.axis_size(axis)
    first, last = (max(0, -steps), min(count, count - steps))
    return lax.ppermute(value, axis, [(source, source + steps) for source in range(first, last)])


def swapped(value, axis, step):
    count = lax.axis_size(axis)
    return lax.ppermute(value, axis, [(place, place ^ step) for place in range(count)])


def reach(tap):
    return (1, 2) if tap == 0 else (0, 1)


def pack_kernel(cells_ref, pixels_ref, row_ref, out_ref, below_ref, wide_ref):
    slots = pixels_ref.shape[0]
    rows = out_ref.shape[0]
    pixch = pixels_ref.shape[1]
    cells = [cells_ref[0, t] for t in range(slots)]
    live = [cell >= 0 for cell in cells]
    bands = [cell // BAND_CELLS for cell in cells]
    places = []
    for t in range(slots):
        rank = jnp.int32(0)
        for s in range(t):
            rank = rank + ((bands[s] == bands[t]) & live[s]).astype(jnp.int32)
        places.append(jnp.where(live[t], bands[t] * CAP + rank, -1))
    dest = lax.broadcasted_iota(jnp.int32, (rows, slots), 0)
    slot = lax.broadcasted_iota(jnp.int32, (rows, slots), 1)
    place = jnp.full((rows, slots), -1, jnp.int32)
    for t in range(slots):
        place = jnp.where(slot == t, places[t], place)
    route = (place == dest).astype(F32).astype(BF16)
    below_ref[...] = row_ref[...].astype(BF16)
    routed = nn(route, pixels_ref[...])
    wide_ref[...] = jnp.zeros_like(wide_ref)
    for n in range(pixch // 128):
        wide_ref[:, n, :] = routed[:, 128 * n : 128 * n + 128]
    lane = lax.broadcasted_iota(jnp.int32, (rows, 128), 1)
    base = (lax.broadcasted_iota(jnp.int32, (rows, 128), 0) // CAP) * CAP
    notes = jnp.zeros((rows, 128), F32)
    for t in range(slots):
        within = cells[t] % BAND_CELLS
        own_row = (within // GW).astype(F32)
        own_col = (within % GW).astype(F32)
        for rank in range(CAP):
            hit = base + rank == places[t]
            for at, value in enumerate((own_row, own_col, jnp.float32(1.0))):
                notes = jnp.where(hit & (lane == 3 * rank + at), value, notes)
    wide_ref[:, pixch // 128, :] = notes
    out_ref[...] = wide_ref[...].astype(BF16)


def patch_kernel(chan_ref, meta_ref, cot_ref, below_ref, key_ref, own_ref, send_ref, meta_f32):
    sources = meta_ref.shape[0]
    chunks = sources // 8
    out_rows, e_half, _ = cot_ref.shape
    meta_f32[...] = meta_ref[...].astype(F32)
    meta = meta_f32[:, 0, :]
    first = chan_ref[0] == 0
    lane = lax.broadcasted_iota(jnp.int32, (8, 128), 1).astype(F32)
    blocks = []
    for mine in (True, False):
        for chunk in range(chunks):
            part = meta[chunk * 8 : chunk * 8 + 8]
            low = [jnp.broadcast_to(part[:, n : n + 1], (8, 128)) for n in range(3)]
            high = [jnp.broadcast_to(part[:, n : n + 1], (8, 128)) for n in range(3, 6)]
            row, col, valid = (
                jnp.where(first == mine, one, two) for one, two in zip(low, high)
            )
            for u in range(3):
                for v in range(3):
                    hit = (lane == 2.0 * col + v) & (valid > 0.5)
                    blocks.append(jnp.where(hit, 2.0 * row + u, -1.0))
    key = jnp.concatenate(blocks, axis=0)
    key_ref[...] = key

    def step(o, total):
        pick = (key == o.astype(F32)).astype(F32).astype(BF16)
        return total + nt(pick, cot_ref[o].astype(BF16))

    total = lax.fori_loop(
        0, out_rows, step, jnp.zeros((key.shape[0], e_half), F32), unroll=4
    )
    pick = (key == float(out_rows)).astype(F32).astype(BF16)
    total = total + nt(pick, below_ref[...])
    half = total.shape[0] // 2
    own_ref[...] = jnp.zeros_like(own_ref)
    send_ref[...] = jnp.zeros_like(send_ref)
    own_ref[:, :e_half] = total[:half].astype(BF16)
    send_ref[:, :e_half] = total[half:].astype(BF16)


def center_of(values):
    center = values - jnp.mean(values, axis=-1, keepdims=True)
    rstd = lax.rsqrt(jnp.mean(center * center, axis=-1, keepdims=True) + 1e-06)
    return center * rstd, rstd


def fill_padded(padded_ref, got_ref, wide_ref, pixels_ref, channels):
    wide_ref[...] = got_ref[...].astype(F32)
    for n in range(pixels_ref.shape[1] // 128):
        pixels_ref[:, 128 * n : 128 * n + 128] = wide_ref[:, n, :]
    padded_ref[...] = jnp.zeros_like(padded_ref)
    for i in range(SIDE):
        for j in range(SIDE):
            at = (i * SIDE + j) * channels
            padded_ref[i + 3, j + 3] = pixels_ref[:, at : at + channels]


def stem_kernel(
    got_ref, dw_ref, gain_ref, up_ref, proj_ref, scale_ref, ds_gain_ref, ds_ref,
    feat_ref, hat1_ref, rstd1_ref, hat2_ref, rstd2_ref, hidden_ref, slope_ref, patch_ref,
    padded_ref, spatial_ref, low_ref, patch_f32, wide_ref, pixels_ref,
):
    channels = dw_ref.shape[1]
    fill_padded(padded_ref, got_ref, wide_ref, pixels_ref, channels)

    def row_step(i, carry):
        total = jnp.zeros((SIDE, 8, channels), F32)
        for a in range(7):
            for b in range(7):
                weight = dw_ref[pl.ds(7 * a + b, 1), :].reshape(1, 1, channels)
                total = total + weight * padded_ref[i + a, b : b + SIDE]
        spatial_ref[i] = total
        return carry

    lax.fori_loop(0, SIDE, row_step, 0)
    hat1, rstd1 = center_of(spatial_ref[...].reshape(PIX * 8, channels))
    hat1_ref[...] = hat1
    rstd1_ref[...] = rstd1
    normed = (hat1 * gain_ref[...]).astype(BF16)
    before = nn(normed, up_ref[...])
    cdf = 0.5 * (1.0 + lax.erf(before * math.sqrt(0.5)))
    pdf = jnp.exp(-0.5 * before * before) * (1.0 / math.sqrt(2.0 * math.pi))
    hidden = (before * cdf).astype(BF16)
    hidden_ref[...] = hidden
    slope_ref[...] = cdf + before * pdf
    branch = nt(hidden, proj_ref[...])
    inputs = padded_ref[3 : 3 + SIDE, 3 : 3 + SIDE].reshape(PIX * 8, channels)
    hat2, rstd2 = center_of(inputs + scale_ref[...] * branch)
    hat2_ref[...] = hat2
    rstd2_ref[...] = rstd2
    low_ref[...] = (hat2 * ds_gain_ref[...]).reshape(low_ref.shape)
    half = SIDE // 2
    for di in range(2):
        for dj in range(2):
            at = (2 * di + dj) * channels
            patch_f32[:, at : at + channels] = low_ref[:, di, :, dj].reshape(-1, channels)
    patches = patch_f32[...].astype(BF16)
    patch_ref[...] = patches
    total = nt(patches, ds_ref[...])
    rows = total.shape[0]
    feat_ref[0:rows] = total[:, 0:128].astype(BF16)
    rest = jnp.concatenate([total[: rows // 2, 128:192], total[rows // 2 :, 128:192]], axis=1)
    feat_ref[rows:] = rest.astype(BF16)


def unfold(block):
    rest = block[128:]
    return jnp.concatenate(
        [block[:128], jnp.concatenate([rest[:, :64], rest[:, 64:]], axis=0)], axis=1
    )


def back_kernel(
    chan_ref, own_ref, peer_ref, w_own_ref, w_peer_ref, got_ref,
    hat1_ref, rstd1_ref, hat2_ref, rstd2_ref, hidden_ref, slope_ref, patch_ref,
    gain_ref, up_ref, proj_ref, scale_ref, ds_gain_ref, ds_ref,
    keep_ref, send_ref,
    padded_ref, dlow_ref, dspatial_ref, dw_ref, ds_acc, up_acc, proj_acc, pack_ref,
    wide_ref, pixels_ref,
    *, scale,
):
    channels = gain_ref.shape[1]
    e_half = w_own_ref.shape[2]
    half = SIDE // 2
    step = pl.program_id(0)

    @pl.when(step == 0)
    def _():
        dw_ref[...] = jnp.zeros_like(dw_ref)
        ds_acc[...] = jnp.zeros_like(ds_acc)
        up_acc[...] = jnp.zeros_like(up_acc)
        proj_acc[...] = jnp.zeros_like(proj_acc)

    own = own_ref[...].astype(F32)[:, :e_half].reshape(9, 8, e_half)
    peer = peer_ref[...].astype(F32)[:, :e_half].reshape(9, 8, e_half)
    grads = {}
    for a in range(3):
        for b in range(3):
            places = [(u, v) for u in reach(a) for v in reach(b)]
            left_own = jnp.concatenate([own[3 * u + v] for u, v in places], axis=0).astype(BF16)
            left_peer = jnp.concatenate([peer[3 * u + v] for u, v in places], axis=0).astype(BF16)
            out = nt(left_own, w_own_ref[3 * a + b]) + nt(left_peer, w_peer_ref[3 * a + b])
            for n, (u, v) in enumerate(places):
                at = (2 * u + a - 1) * half + 2 * v + b - 1
                piece = out[8 * n : 8 * n + 8]
                grads[at] = grads[at] + piece if at in grads else piece
    dfeat = jnp.concatenate([grads[at] for at in range(half * half)], axis=0) * scale
    dfeat = dfeat.astype(BF16)

    hat2 = hat2_ref[...]
    ds_acc[...] += tn(dfeat, patch_ref[...])
    back = nn(dfeat, ds_ref[...])
    for di in range(2):
        for dj in range(2):
            at = (2 * di + dj) * channels
            dlow_ref[:, di, :, dj] = back[:, at : at + channels].reshape(half, half, 8, channels)
    dhat2 = dlow_ref[...].reshape(PIX * 8, channels) * ds_gain_ref[...]
    mean_a = jnp.mean(dhat2, axis=-1, keepdims=True)
    mean_b = jnp.mean(dhat2 * hat2, axis=-1, keepdims=True)
    dmixed = rstd2_ref[...] * (dhat2 - mean_a - hat2 * mean_b)
    dbranch = (dmixed * scale_ref[...]).astype(BF16)
    proj_acc[...] += tn(dbranch, hidden_ref[...])
    dhidden = nn(dbranch, proj_ref[...])
    dbefore = (dhidden * slope_ref[...]).astype(BF16)
    hat1 = hat1_ref[...]
    normed = (hat1 * gain_ref[...]).astype(BF16)
    up_acc[...] += tn(normed, dbefore)
    dhat1 = nt(dbefore, up_ref[...]) * gain_ref[...]
    mean_a = jnp.mean(dhat1, axis=-1, keepdims=True)
    mean_b = jnp.mean(dhat1 * hat1, axis=-1, keepdims=True)
    dspatial = rstd1_ref[...] * (dhat1 - mean_a - hat1 * mean_b)
    dspatial_ref[...] = dspatial.reshape(SIDE, SIDE, 8, channels)
    fill_padded(padded_ref, got_ref, wide_ref, pixels_ref, channels)

    def tap_step(a, carry):
        totals = [jnp.zeros((8, channels), F32) for _ in range(7)]
        for i in range(SIDE):
            grad = dspatial_ref[i]
            for b in range(7):
                product = padded_ref[i + a, b : b + SIDE] * grad
                totals[b] = totals[b] + jnp.sum(product, axis=0)
        for b in range(7):
            dw_ref[a, b] += totals[b]
        return carry

    lax.fori_loop(0, 7, tap_step, 0)

    @pl.when(step == pl.num_programs(0) - 1)
    def _():
        pack_ref[...] = jnp.zeros_like(pack_ref)
        for n in range(3):
            lanes = slice(128 * n, 128 * n + 128)
            pack_ref[192 * n : 192 * n + 192, :] = ds_acc[:, lanes]
            pack_ref[576 + 96 * n : 672 + 96 * n, :] = up_acc[:, lanes]
            pack_ref[864 + 96 * n : 960 + 96 * n, :] = proj_acc[:, lanes]
        pack_ref[1152:1201, 0:channels] = jnp.sum(dw_ref[...], axis=2).reshape(49, channels)
        mine = pl.multiple_of(chan_ref[0] * HALF_ROWS, 8)
        other = pl.multiple_of((1 - chan_ref[0]) * HALF_ROWS, 8)
        keep_ref[...] = pack_ref[pl.ds(mine, HALF_ROWS), :]
        send_ref[...] = pack_ref[pl.ds(other, HALF_ROWS), :].astype(BF16)


def unpack_kernel(chan_ref, own_ref, peer_ref, dw_ref, up_ref, proj_ref, ds_ref, pack_ref):
    channels = dw_ref.shape[1]
    mine = pl.multiple_of(chan_ref[0] * HALF_ROWS, 8)
    other = pl.multiple_of((1 - chan_ref[0]) * HALF_ROWS, 8)
    pack_ref[pl.ds(mine, HALF_ROWS), :] = own_ref[...]
    pack_ref[pl.ds(other, HALF_ROWS), :] = peer_ref[...]
    for n in range(3):
        lanes = slice(128 * n, 128 * n + 128)
        ds_ref[:, lanes] = pack_ref[192 * n : 192 * n + 192, :]
        up_ref[:, lanes] = pack_ref[576 + 96 * n : 672 + 96 * n, :]
        proj_ref[:, lanes] = pack_ref[864 + 96 * n : 960 + 96 * n, :]
    dw_ref[...] = pack_ref[1152:1201, 0:channels]


def spread_kernel(feat_ref, w_ref, key_ref, y_ref, below_ref, *, last):
    width = w_ref.shape[1]
    feats = unfold(feat_ref[...].astype(F32)).reshape(16, 8, width)
    outs = {}
    for a in range(3):
        for b in range(3):
            places = [(u, v) for u in reach(a) for v in reach(b)]
            left = jnp.concatenate(
                [feats[(2 * u + a - 1) * 4 + 2 * v + b - 1] for u, v in places], axis=0
            ).astype(BF16)
            out = nn(left, w_ref[3 * a + b])
            for n, (u, v) in enumerate(places):
                piece = out[8 * n : 8 * n + 8]
                at = 3 * u + v
                outs[at] = outs[at] + piece if at in outs else piece
    total = jnp.concatenate([outs[at] for at in range(9)], axis=0)
    y_ref[...] = total
    pick = (key_ref[...] == float(last)).astype(F32).astype(BF16)
    high = total.astype(BF16)
    rest = (total - high.astype(F32)).astype(BF16)

    @pl.when(pl.program_id(0) == 0)
    def _():
        below_ref[...] = jnp.zeros_like(below_ref)

    below_ref[...] += tn(high, pick) + tn(rest, pick)


def map_kernel(y_ref, key_ref, above_ref, out_ref):
    out_rows, width, _ = out_ref.shape
    turned = y_ref[...].T
    high = turned.astype(BF16)
    rest = (turned - high.astype(F32)).astype(BF16)
    key = key_ref[...]

    def row_of(o):
        pick = (key == o).astype(F32).astype(BF16)
        return nn(high, pick) + nn(rest, pick)

    out_ref[0] = (row_of(0.0) + above_ref[...]).astype(BF16)

    def step(o, carry):
        out_ref[o] = row_of(o.astype(F32)).astype(BF16)
        return carry

    lax.fori_loop(1, out_rows, step, 0)


def weight_kernel(place_ref, near_ref, far_ref, keep_ref, send_ref, feat_ref, cot_ref, *, scale):
    near = near_ref.shape[0]
    members = feat_ref.shape[1] // 8
    width, e_half = keep_ref.shape[1:]
    step = pl.program_id(0)

    @pl.when(step == 0)
    def _():
        keep_ref[...] = jnp.zeros_like(keep_ref)
        send_ref[...] = jnp.zeros_like(send_ref)

    def take(member, block):
        block = block.astype(F32)
        feat_ref[:, 8 * member : 8 * member + 8] = unfold(block[:FEAT_ROWS]).reshape(16, 8, width)
        own = block[FEAT_ROWS : FEAT_ROWS + COT_ROWS].reshape(9, 8, 128)
        peer = block[FEAT_ROWS + COT_ROWS :].reshape(9, 8, 128)
        cot_ref[:, 8 * member : 8 * member + 8, 0:128] = own
        cot_ref[:, 8 * member : 8 * member + 8, 128:256] = peer

    for member in range(members):
        at = place_ref[0] ^ member

        @pl.when(at < near)
        def _():
            take(member, near_ref[jnp.minimum(at, near - 1)])

        if members > near:

            @pl.when(at >= near)
            def _():
                take(member, far_ref[jnp.maximum(at - near, 0)])

    for a in range(3):
        for b in range(3):
            places = [(u, v) for u in reach(a) for v in reach(b)]
            left = jnp.concatenate(
                [feat_ref[(2 * u + a - 1) * 4 + 2 * v + b - 1] for u, v in places], axis=0
            ).astype(BF16)
            right = jnp.concatenate([cot_ref[3 * u + v] for u, v in places], axis=0).astype(BF16)
            total = tn(left, right) * scale
            keep_ref[3 * a + b] += total[:, :e_half]
            send_ref[3 * a + b] += total[:, 128 : 128 + e_half]


def whole(shape):
    return pl.BlockSpec(shape, lambda g: (0,) * len(shape))


def on_device(
    tile_pixels, tile_cell, agg_cot, dw_weight, norm_gain, up_weight, proj_weight,
    layer_scale, ds_gain, ds_weight, agg_weight,
):
    channels = dw_weight.shape[1]
    hid = up_weight.shape[1]
    width = ds_weight.shape[1]
    bands = lax.axis_size("slide")
    sources = bands * lax.axis_size("chan")
    chunks = sources // 8
    pixch = tile_pixels.shape[2]
    out_rows = agg_cot.shape[1]
    e_half = agg_weight.shape[2]
    cols = agg_cot.shape[3]
    blocks = CAP * chunks
    total_rows = out_rows * bands * lax.axis_size("rep") * cols
    loss_scale = 1.0 / math.sqrt(total_rows)
    chan = lax.axis_index("chan").astype(jnp.int32)[None]
    gain = norm_gain[None]
    scale = layer_scale[None]
    low_gain = ds_gain[None]
    proj_turned = proj_weight.T
    ds_turned = ds_weight.T

    packed, top_cot = pl.pallas_call(
        pack_kernel,
        grid=(1,),
        out_shape=(
            jax.ShapeDtypeStruct((sources, WIRE_ROWS, 128), BF16),
            jax.ShapeDtypeStruct((e_half, cols), BF16),
        ),
        in_specs=[
            SMEM,
            pl.BlockSpec((None,) + tile_pixels.shape[1:], lambda i: (0, 0, 0)),
            pl.BlockSpec((None, None, e_half, cols), lambda i: (0, 0, 0, 0)),
        ],
        out_specs=(whole((sources, WIRE_ROWS, 128)), whole((e_half, cols))),
        scratch_shapes=[pltpu.VMEM((sources, WIRE_ROWS, 128), F32)],
        cost_estimate=takes(1.5),
        name="pack",
    )(tile_cell, tile_pixels, agg_cot)
    below_cot = shifted(top_cot, "slide", -1)
    packed, own_weight = lax.optimization_barrier((packed, agg_weight))
    peer_weight = swapped(own_weight, "chan", 1)
    got = lax.all_to_all(packed, ("slide", "chan"), split_axis=0, concat_axis=0, tiled=True)

    key, cots_own, cots_send = pl.pallas_call(
        patch_kernel,
        out_shape=(
            jax.ShapeDtypeStruct((blocks * COT_ROWS, cols), F32),
            jax.ShapeDtypeStruct((chunks * COT_ROWS, 128), BF16),
            jax.ShapeDtypeStruct((chunks * COT_ROWS, 128), BF16),
        ),
        in_specs=[
            SMEM,
            pl.BlockSpec((sources, 8, 128), lambda i: (0, pixch // 1024, 0)),
            pl.BlockSpec((None, out_rows, e_half, cols), lambda i: (0, 0, 0, 0)),
            whole((e_half, cols)),
        ],
        out_specs=(
            whole((blocks * COT_ROWS, cols)),
            whole((chunks * COT_ROWS, 128)),
            whole((chunks * COT_ROWS, 128)),
        ),
        grid=(1,),
        scratch_shapes=[pltpu.VMEM((sources, 8, 128), F32)],
        compiler_params=params_of(),
        cost_estimate=takes(1.2),
        name="patch",
    )(chan, got, agg_cot, below_cot)
    cots_peer = swapped(cots_send, "chan", 1)
    cots_own = cots_own.reshape(chunks, COT_ROWS, 128)
    cots_peer = cots_peer.reshape(chunks, COT_ROWS, 128)

    rows = PIX * 8
    pixel_spec = pl.BlockSpec((8, WIRE_ROWS, 128), lambda g: (g, 0, 0))
    pixel_scratch = [pltpu.VMEM((8, WIRE_ROWS, 128), F32), pltpu.VMEM((8, pixch), F32)]

    def chunk(*shape):
        return pl.BlockSpec((None,) + shape, lambda g: (g,) + (0,) * len(shape))

    feats, hat1, rstd1, hat2, rstd2, hidden, slope, patches = pl.pallas_call(
        stem_kernel,
        grid=(chunks,),
        out_shape=(
            jax.ShapeDtypeStruct((chunks, FEAT_ROWS, 128), BF16),
            jax.ShapeDtypeStruct((chunks, rows, channels), F32),
            jax.ShapeDtypeStruct((chunks, rows, 1), F32),
            jax.ShapeDtypeStruct((chunks, rows, channels), F32),
            jax.ShapeDtypeStruct((chunks, rows, 1), F32),
            jax.ShapeDtypeStruct((chunks, rows, hid), BF16),
            jax.ShapeDtypeStruct((chunks, rows, hid), F32),
            jax.ShapeDtypeStruct((chunks, 128, 4 * channels), BF16),
        ),
        in_specs=[
            pixel_spec,
            whole(dw_weight.shape), whole((1, channels)), whole(up_weight.shape),
            whole(proj_turned.shape), whole((1, channels)), whole((1, channels)),
            whole(ds_turned.shape),
        ],
        out_specs=(
            chunk(FEAT_ROWS, 128), chunk(rows, channels), chunk(rows, 1), chunk(rows, channels),
            chunk(rows, 1), chunk(rows, hid), chunk(rows, hid), chunk(128, 4 * channels),
        ),
        scratch_shapes=[
            pltpu.VMEM((SIDE + 6, SIDE + 6, 8, channels), F32),
            pltpu.VMEM((SIDE, SIDE, 8, channels), F32),
            pltpu.VMEM((SIDE // 2, 2, SIDE // 2, 2, 8, channels), F32),
            pltpu.VMEM((128, 4 * channels), F32),
            *pixel_scratch,
        ],
        compiler_params=params_of(),
        cost_estimate=takes(2.7),
        name="stem",
    )(got, dw_weight, gain, up_weight, proj_turned, scale, low_gain, ds_turned)

    feats_band = jnp.concatenate([feats, swapped(feats, "chan", 1)], axis=0)
    spread, below = pl.pallas_call(
        lambda *refs: spread_kernel(*refs, last=out_rows),
        grid=(blocks,),
        out_shape=(
            jax.ShapeDtypeStruct((blocks * 72, e_half), F32),
            jax.ShapeDtypeStruct((e_half, cols), F32),
        ),
        in_specs=[
            chunk(FEAT_ROWS, 128), whole(agg_weight.shape),
            pl.BlockSpec((72, cols), lambda g: (g, 0)),
        ],
        out_specs=(pl.BlockSpec((72, e_half), lambda g: (g, 0)), whole((e_half, cols))),
        compiler_params=params_of(),
        cost_estimate=takes(1.0),
        name="spread",
    )(feats_band, agg_weight, key)
    tile_blocks = jnp.concatenate([feats, cots_own, cots_peer], axis=1)
    gather = chunks == 1
    near = far = tile_blocks
    place = jnp.zeros((1,), jnp.int32)
    spans = [("slide", 1 << n) for n in reversed(range(bands.bit_length() - 1))]
    spans += [("rep", 1 << n) for n in range(lax.axis_size("rep").bit_length() - 1)]

    def widen(n, near, place):
        axis, step = spans[n]
        bit = (lax.axis_index(axis).astype(jnp.int32) // step) % 2
        return swapped(near, axis, step), place + bit * (1 << n)

    if gather:
        far, place = widen(0, near, place)
        near = jnp.concatenate([near, far], axis=0)

    keep, send = pl.pallas_call(
        lambda *refs: back_kernel(*refs, scale=loss_scale),
        grid=(chunks,),
        out_shape=(
            jax.ShapeDtypeStruct((HALF_ROWS, 128), F32),
            jax.ShapeDtypeStruct((HALF_ROWS, 128), BF16),
        ),
        in_specs=[
            SMEM, chunk(COT_ROWS, 128), chunk(COT_ROWS, 128),
            whole(agg_weight.shape), whole(agg_weight.shape), pixel_spec,
            chunk(rows, channels), chunk(rows, 1), chunk(rows, channels), chunk(rows, 1),
            chunk(rows, hid), chunk(rows, hid), chunk(128, 4 * channels),
            whole((1, channels)), whole(up_weight.shape), whole(proj_turned.shape),
            whole((1, channels)), whole((1, channels)), whole(ds_turned.shape),
        ],
        out_specs=(whole((HALF_ROWS, 128)), whole((HALF_ROWS, 128))),
        scratch_shapes=[
            pltpu.VMEM((SIDE + 6, SIDE + 6, 8, channels), F32),
            pltpu.VMEM((SIDE // 2, 2, SIDE // 2, 2, 8, channels), F32),
            pltpu.VMEM((SIDE, SIDE, 8, channels), F32),
            pltpu.VMEM((7, 7, 8, channels), F32),
            pltpu.VMEM(ds_turned.shape, F32),
            pltpu.VMEM(up_weight.shape, F32),
            pltpu.VMEM(proj_turned.shape, F32),
            pltpu.VMEM((2 * HALF_ROWS, 128), F32),
            *pixel_scratch,
        ],
        compiler_params=params_of(),
        cost_estimate=takes(3.7),
        name="stem_back",
    )(
        chan, cots_own, cots_peer, agg_weight, peer_weight, got,
        hat1, rstd1, hat2, rstd2, hidden, slope, patches,
        gain, up_weight, proj_turned, scale, low_gain, ds_turned,
    )

    part = keep + swapped(send, "chan", 1).astype(F32)
    if gather:
        part, near, spread, below = lax.optimization_barrier((part, near, spread, below))
    steps = []
    for axis in ("rep", "slide"):
        step = 1
        while step < lax.axis_size(axis):
            steps.append((axis, step))
            step *= 2
    for n, (axis, step) in enumerate(steps):
        wire = part.astype(BF16)
        part = wire.astype(F32) + swapped(wire, axis, step).astype(F32)
    above = shifted(below, "slide", 1)
    map_call = pl.pallas_call(
        map_kernel,
        out_shape=jax.ShapeDtypeStruct((out_rows, e_half, cols), BF16),
        in_specs=[VMEM, VMEM, VMEM],
        out_specs=VMEM,
        compiler_params=pltpu.CompilerParams(vmem_limit_bytes=24 << 20),
        cost_estimate=takes(3.5),
        name="agg_map",
    )
    agg_map = map_call(spread, key, above)

    for n in range(1, len(spans) if gather else 0):
        if n == len(spans) - 1:
            near, agg_map = lax.optimization_barrier((near, agg_map))
        far, place = widen(n, near, place)
        if n < len(spans) - 1:
            near = jnp.concatenate([near, far], axis=0)

    count = 2 * near.shape[0] if gather else chunks
    per = count if gather else 1
    near_count = near.shape[0] if gather else 1
    agg_keep, agg_send = pl.pallas_call(
        lambda *refs: weight_kernel(*refs, scale=loss_scale),
        grid=(count // per,),
        out_shape=(
            jax.ShapeDtypeStruct((9, width, e_half), F32),
            jax.ShapeDtypeStruct((9, width, e_half), F32),
        ),
        in_specs=[
            SMEM,
            pl.BlockSpec((near_count, BLOCK_ROWS, 128), lambda g: (g, 0, 0)),
            pl.BlockSpec((near_count, BLOCK_ROWS, 128), lambda g: (g, 0, 0)),
        ],
        out_specs=(whole((9, width, e_half)), whole((9, width, e_half))),
        scratch_shapes=[
            pltpu.VMEM((16, per * 8, width), F32),
            pltpu.VMEM((9, per * 8, 256), F32),
        ],
        compiler_params=params_of(),
        cost_estimate=takes(1.4),
        name="agg_weight_grad",
    )(place, near, far)
    agg_grad = agg_keep + swapped(agg_send.astype(BF16), "chan", 1).astype(F32)
    if not gather:
        agg_grad = lax.psum(agg_grad, ("slide", "rep"))

    dw_grad, up_grad, proj_grad, ds_grad = pl.pallas_call(
        unpack_kernel,
        out_shape=(
            jax.ShapeDtypeStruct(dw_weight.shape, F32),
            jax.ShapeDtypeStruct(up_weight.shape, F32),
            jax.ShapeDtypeStruct(proj_turned.shape, F32),
            jax.ShapeDtypeStruct(ds_turned.shape, F32),
        ),
        in_specs=[SMEM, VMEM, VMEM],
        out_specs=(VMEM, VMEM, VMEM, VMEM),
        scratch_shapes=[pltpu.VMEM((2 * HALF_ROWS, 128), F32)],
        compiler_params=pltpu.CompilerParams(vmem_limit_bytes=24 << 20),
        cost_estimate=takes(1.5),
        name="unpack",
    )(chan, part, swapped(part, "chan", 1))
    proj_grad = proj_grad.T
    ds_grad = ds_grad.T
    return (agg_map[None], agg_grad, dw_grad, up_grad, proj_grad, ds_grad)


def solution(mesh):
    in_specs = (
        P(("groups", "rep"), ("slide", "chan"), None),
        P(("groups", "rep"), ("slide", "chan")),
        P(("groups", "rep"), "slide", "chan", None),
        P(), P(), P(), P(), P(), P(), P(),
        P(None, None, "chan"),
    )
    out_specs = (
        P(("groups", "rep"), "slide", "chan", None),
        P("groups", None, "chan"),
        P("groups", None),
        P("groups", None),
        P("groups", None),
        P("groups", None),
    )
    return jax.shard_map(
        on_device, mesh=mesh, in_specs=in_specs, out_specs=out_specs, check_vma=False
    )
```

```python
import math

import jax
import jax.numpy as jnp
from jax import lax
from jax.experimental import pallas as pl
from jax.experimental.pallas import tpu as pltpu
from jax.sharding import PartitionSpec as P

SIDE = 8
CAP = 2
GW = 64
BAND_CELLS = 512
PIX = SIDE * SIDE
HALF_ROWS = 608
FEAT_ROWS = 192
COT_ROWS = 72
WIRE_ROWS = 56
BLOCK_ROWS = FEAT_ROWS + 2 * COT_ROWS
F32 = jnp.float32
BF16 = jnp.bfloat16
VMEM = pl.BlockSpec(memory_space=pltpu.VMEM)
SMEM = pl.BlockSpec(memory_space=pltpu.SMEM)


def params_of(steps=1):
    return pltpu.CompilerParams(
        dimension_semantics=("arbitrary",) * steps, vmem_limit_bytes=24 << 20
    )


def takes(microseconds):
    return pl.CostEstimate(
        flops=0, transcendentals=0, bytes_accessed=int(microseconds * 3.69e6)
    )


def nn(left, right):
    return lax.dot_general(left, right, (((1,), (0,)), ((), ())), preferred_element_type=F32)


def nt(left, right):
    return lax.dot_general(left, right, (((1,), (1,)), ((), ())), preferred_element_type=F32)


def tn(left, right):
    return lax.dot_general(left, right, (((0,), (0,)), ((), ())), preferred_element_type=F32)


def shifted(value, axis, steps):
    count = lax.axis_size(axis)
    first, last = (max(0, -steps), min(count, count - steps))
    return lax.ppermute(value, axis, [(source, source + steps) for source in range(first, last)])


def swapped(value, axis, step):
    count = lax.axis_size(axis)
    return lax.ppermute(value, axis, [(place, place ^ step) for place in range(count)])


def reach(tap):
    return (1, 2) if tap == 0 else (0, 1)


def pack_kernel(cells_ref, pixels_ref, row_ref, out_ref, below_ref, wide_ref):
    slots = pixels_ref.shape[0]
    rows = out_ref.shape[0]
    pixch = pixels_ref.shape[1]
    cells = [cells_ref[0, t] for t in range(slots)]
    live = [cell >= 0 for cell in cells]
    bands = [cell // BAND_CELLS for cell in cells]
    places = []
    for t in range(slots):
        rank = jnp.int32(0)
        for s in range(t):
            rank = rank + ((bands[s] == bands[t]) & live[s]).astype(jnp.int32)
        places.append(jnp.where(live[t], bands[t] * CAP + rank, -1))
    dest = lax.broadcasted_iota(jnp.int32, (rows, slots), 0)
    slot = lax.broadcasted_iota(jnp.int32, (rows, slots), 1)
    place = jnp.full((rows, slots), -1, jnp.int32)
    for t in range(slots):
        place = jnp.where(slot == t, places[t], place)
    route = (place == dest).astype(F32).astype(BF16)
    below_ref[...] = row_ref[...].astype(BF16)
    routed = nn(route, pixels_ref[...])
    wide_ref[...] = jnp.zeros_like(wide_ref)
    for n in range(pixch // 128):
        wide_ref[:, n, :] = routed[:, 128 * n : 128 * n + 128]
    lane = lax.broadcasted_iota(jnp.int32, (rows, 128), 1)
    base = (lax.broadcasted_iota(jnp.int32, (rows, 128), 0) // CAP) * CAP
    notes = jnp.zeros((rows, 128), F32)
    for t in range(slots):
        within = cells[t] % BAND_CELLS
        own_row = (within // GW).astype(F32)
        own_col = (within % GW).astype(F32)
        for rank in range(CAP):
            hit = base + rank == places[t]
            for at, value in enumerate((own_row, own_col, jnp.float32(1.0))):
                notes = jnp.where(hit & (lane == 3 * rank + at), value, notes)
    wide_ref[:, pixch // 128, :] = notes
    out_ref[...] = wide_ref[...].astype(BF16)


def patch_kernel(chan_ref, meta_ref, cot_ref, below_ref, key_ref, own_ref, send_ref, meta_f32):
    sources = meta_ref.shape[0]
    chunks = sources // 8
    out_rows, e_half, _ = cot_ref.shape
    meta_f32[...] = meta_ref[...].astype(F32)
    meta = meta_f32[:, 0, :]
    first = chan_ref[0] == 0
    lane = lax.broadcasted_iota(jnp.int32, (8, 128), 1).astype(F32)
    blocks = []
    for mine in (True, False):
        for chunk in range(chunks):
            part = meta[chunk * 8 : chunk * 8 + 8]
            low = [jnp.broadcast_to(part[:, n : n + 1], (8, 128)) for n in range(3)]
            high = [jnp.broadcast_to(part[:, n : n + 1], (8, 128)) for n in range(3, 6)]
            row, col, valid = (
                jnp.where(first == mine, one, two) for one, two in zip(low, high)
            )
            for u in range(3):
                for v in range(3):
                    hit = (lane == 2.0 * col + v) & (valid > 0.5)
                    blocks.append(jnp.where(hit, 2.0 * row + u, -1.0))
    key = jnp.concatenate(blocks, axis=0)
    key_ref[...] = key

    def step(o, total):
        pick = (key == o.astype(F32)).astype(F32).astype(BF16)
        return total + nt(pick, cot_ref[o].astype(BF16))

    total = lax.fori_loop(
        0, out_rows, step, jnp.zeros((key.shape[0], e_half), F32), unroll=4
    )
    pick = (key == float(out_rows)).astype(F32).astype(BF16)
    total = total + nt(pick, below_ref[...])
    half = total.shape[0] // 2
    own_ref[...] = jnp.zeros_like(own_ref)
    send_ref[...] = jnp.zeros_like(send_ref)
    own_ref[:, :e_half] = total[:half].astype(BF16)
    send_ref[:, :e_half] = total[half:].astype(BF16)


def center_of(values):
    center = values - jnp.mean(values, axis=-1, keepdims=True)
    rstd = lax.rsqrt(jnp.mean(center * center, axis=-1, keepdims=True) + 1e-06)
    return center * rstd, rstd


def fill_padded(padded_ref, got_ref, wide_ref, pixels_ref, channels):
    wide_ref[...] = got_ref[...].astype(F32)
    for n in range(pixels_ref.shape[1] // 128):
        pixels_ref[:, 128 * n : 128 * n + 128] = wide_ref[:, n, :]
    padded_ref[...] = jnp.zeros_like(padded_ref)
    for i in range(SIDE):
        for j in range(SIDE):
            at = (i * SIDE + j) * channels
            padded_ref[i + 3, j + 3] = pixels_ref[:, at : at + channels]


def stem_kernel(
    got_ref, dw_ref, gain_ref, up_ref, proj_ref, scale_ref, ds_gain_ref, ds_ref,
    feat_ref, hat1_ref, rstd1_ref, hat2_ref, rstd2_ref, hidden_ref, slope_ref, patch_ref,
    padded_ref, spatial_ref, low_ref, patch_f32, wide_ref, pixels_ref,
):
    channels = dw_ref.shape[1]
    fill_padded(padded_ref, got_ref, wide_ref, pixels_ref, channels)

    def row_step(i, carry):
        total = jnp.zeros((SIDE, 8, channels), F32)
        for a in range(7):
            for b in range(7):
                weight = dw_ref[pl.ds(7 * a + b, 1), :].reshape(1, 1, channels)
                total = total + weight * padded_ref[i + a, b : b + SIDE]
        spatial_ref[i] = total
        return carry

    lax.fori_loop(0, SIDE, row_step, 0)
    hat1, rstd1 = center_of(spatial_ref[...].reshape(PIX * 8, channels))
    hat1_ref[...] = hat1
    rstd1_ref[...] = rstd1
    normed = (hat1 * gain_ref[...]).astype(BF16)
    before = nn(normed, up_ref[...])
    cdf = 0.5 * (1.0 + lax.erf(before * math.sqrt(0.5)))
    pdf = jnp.exp(-0.5 * before * before) * (1.0 / math.sqrt(2.0 * math.pi))
    hidden = (before * cdf).astype(BF16)
    hidden_ref[...] = hidden
    slope_ref[...] = cdf + before * pdf
    branch = nt(hidden, proj_ref[...])
    inputs = padded_ref[3 : 3 + SIDE, 3 : 3 + SIDE].reshape(PIX * 8, channels)
    hat2, rstd2 = center_of(inputs + scale_ref[...] * branch)
    hat2_ref[...] = hat2
    rstd2_ref[...] = rstd2
    low_ref[...] = (hat2 * ds_gain_ref[...]).reshape(low_ref.shape)
    half = SIDE // 2
    for di in range(2):
        for dj in range(2):
            at = (2 * di + dj) * channels
            patch_f32[:, at : at + channels] = low_ref[:, di, :, dj].reshape(-1, channels)
    patches = patch_f32[...].astype(BF16)
    patch_ref[...] = patches
    total = nt(patches, ds_ref[...])
    rows = total.shape[0]
    feat_ref[0:rows] = total[:, 0:128].astype(BF16)
    rest = jnp.concatenate([total[: rows // 2, 128:192], total[rows // 2 :, 128:192]], axis=1)
    feat_ref[rows:] = rest.astype(BF16)


def unfold(block):
    rest = block[128:]
    return jnp.concatenate(
        [block[:128], jnp.concatenate([rest[:, :64], rest[:, 64:]], axis=0)], axis=1
    )


def back_kernel(
    chan_ref, own_ref, peer_ref, w_own_ref, w_peer_ref, got_ref,
    hat1_ref, rstd1_ref, hat2_ref, rstd2_ref, hidden_ref, slope_ref, patch_ref,
    gain_ref, up_ref, proj_ref, scale_ref, ds_gain_ref, ds_ref,
    keep_ref, send_ref,
    padded_ref, dlow_ref, dspatial_ref, dw_ref, ds_acc, up_acc, proj_acc, pack_ref,
    wide_ref, pixels_ref,
    *, scale,
):
    channels = gain_ref.shape[1]
    e_half = w_own_ref.shape[2]
    half = SIDE // 2
    step = pl.program_id(0)

    @pl.when(step == 0)
    def _():
        dw_ref[...] = jnp.zeros_like(dw_ref)
        ds_acc[...] = jnp.zeros_like(ds_acc)
        up_acc[...] = jnp.zeros_like(up_acc)
        proj_acc[...] = jnp.zeros_like(proj_acc)

    own = own_ref[...].astype(F32)[:, :e_half].reshape(9, 8, e_half)
    peer = peer_ref[...].astype(F32)[:, :e_half].reshape(9, 8, e_half)
    grads = {}
    for a in range(3):
        for b in range(3):
            places = [(u, v) for u in reach(a) for v in reach(b)]
            left_own = jnp.concatenate([own[3 * u + v] for u, v in places], axis=0).astype(BF16)
            left_peer = jnp.concatenate([peer[3 * u + v] for u, v in places], axis=0).astype(BF16)
            out = nt(left_own, w_own_ref[3 * a + b]) + nt(left_peer, w_peer_ref[3 * a + b])
            for n, (u, v) in enumerate(places):
                at = (2 * u + a - 1) * half + 2 * v + b - 1
                piece = out[8 * n : 8 * n + 8]
                grads[at] = grads[at] + piece if at in grads else piece
    dfeat = jnp.concatenate([grads[at] for at in range(half * half)], axis=0) * scale
    dfeat = dfeat.astype(BF16)

    hat2 = hat2_ref[...]
    ds_acc[...] += tn(dfeat, patch_ref[...])
    back = nn(dfeat, ds_ref[...])
    for di in range(2):
        for dj in range(2):
            at = (2 * di + dj) * channels
            dlow_ref[:, di, :, dj] = back[:, at : at + channels].reshape(half, half, 8, channels)
    dhat2 = dlow_ref[...].reshape(PIX * 8, channels) * ds_gain_ref[...]
    mean_a = jnp.mean(dhat2, axis=-1, keepdims=True)
    mean_b = jnp.mean(dhat2 * hat2, axis=-1, keepdims=True)
    dmixed = rstd2_ref[...] * (dhat2 - mean_a - hat2 * mean_b)
    dbranch = (dmixed * scale_ref[...]).astype(BF16)
    proj_acc[...] += tn(dbranch, hidden_ref[...])
    dhidden = nn(dbranch, proj_ref[...])
    dbefore = (dhidden * slope_ref[...]).astype(BF16)
    hat1 = hat1_ref[...]
    normed = (hat1 * gain_ref[...]).astype(BF16)
    up_acc[...] += tn(normed, dbefore)
    dhat1 = nt(dbefore, up_ref[...]) * gain_ref[...]
    mean_a = jnp.mean(dhat1, axis=-1, keepdims=True)
    mean_b = jnp.mean(dhat1 * hat1, axis=-1, keepdims=True)
    dspatial = rstd1_ref[...] * (dhat1 - mean_a - hat1 * mean_b)
    dspatial_ref[...] = dspatial.reshape(SIDE, SIDE, 8, channels)
    fill_padded(padded_ref, got_ref, wide_ref, pixels_ref, channels)

    def tap_step(a, carry):
        totals = [jnp.zeros((8, channels), F32) for _ in range(7)]
        for i in range(SIDE):
            grad = dspatial_ref[i]
            for b in range(7):
                product = padded_ref[i + a, b : b + SIDE] * grad
                totals[b] = totals[b] + jnp.sum(product, axis=0)
        for b in range(7):
            dw_ref[a, b] += totals[b]
        return carry

    lax.fori_loop(0, 7, tap_step, 0)

    @pl.when(step == pl.num_programs(0) - 1)
    def _():
        pack_ref[...] = jnp.zeros_like(pack_ref)
        for n in range(3):
            lanes = slice(128 * n, 128 * n + 128)
            pack_ref[192 * n : 192 * n + 192, :] = ds_acc[:, lanes]
            pack_ref[576 + 96 * n : 672 + 96 * n, :] = up_acc[:, lanes]
            pack_ref[864 + 96 * n : 960 + 96 * n, :] = proj_acc[:, lanes]
        pack_ref[1152:1201, 0:channels] = jnp.sum(dw_ref[...], axis=2).reshape(49, channels)
        mine = pl.multiple_of(chan_ref[0] * HALF_ROWS, 8)
        other = pl.multiple_of((1 - chan_ref[0]) * HALF_ROWS, 8)
        keep_ref[...] = pack_ref[pl.ds(mine, HALF_ROWS), :]
        send_ref[...] = pack_ref[pl.ds(other, HALF_ROWS), :].astype(BF16)


def unpack_kernel(chan_ref, own_ref, peer_ref, dw_ref, up_ref, proj_ref, ds_ref, pack_ref):
    channels = dw_ref.shape[1]
    mine = pl.multiple_of(chan_ref[0] * HALF_ROWS, 8)
    other = pl.multiple_of((1 - chan_ref[0]) * HALF_ROWS, 8)
    pack_ref[pl.ds(mine, HALF_ROWS), :] = own_ref[...].astype(F32)
    pack_ref[pl.ds(other, HALF_ROWS), :] = peer_ref[...].astype(F32)
    for n in range(3):
        lanes = slice(128 * n, 128 * n + 128)
        ds_ref[:, lanes] = pack_ref[192 * n : 192 * n + 192, :]
        up_ref[:, lanes] = pack_ref[576 + 96 * n : 672 + 96 * n, :]
        proj_ref[:, lanes] = pack_ref[864 + 96 * n : 960 + 96 * n, :]
    dw_ref[...] = pack_ref[1152:1201, 0:channels]


def spread_kernel(feat_ref, w_ref, key_ref, y_ref, below_ref, *, last):
    width = w_ref.shape[1]
    feats = unfold(feat_ref[...].astype(F32)).reshape(16, 8, width)
    outs = {}
    for a in range(3):
        for b in range(3):
            places = [(u, v) for u in reach(a) for v in reach(b)]
            left = jnp.concatenate(
                [feats[(2 * u + a - 1) * 4 + 2 * v + b - 1] for u, v in places], axis=0
            ).astype(BF16)
            out = nn(left, w_ref[3 * a + b])
            for n, (u, v) in enumerate(places):
                piece = out[8 * n : 8 * n + 8]
                at = 3 * u + v
                outs[at] = outs[at] + piece if at in outs else piece
    total = jnp.concatenate([outs[at] for at in range(9)], axis=0)
    y_ref[...] = total
    pick = (key_ref[...] == float(last)).astype(F32).astype(BF16)
    high = total.astype(BF16)
    rest = (total - high.astype(F32)).astype(BF16)

    @pl.when(pl.program_id(0) == 0)
    def _():
        below_ref[...] = jnp.zeros_like(below_ref)

    below_ref[...] += tn(high, pick) + tn(rest, pick)


def map_kernel(y_ref, key_ref, above_ref, out_ref):
    out_rows, width, _ = out_ref.shape
    turned = y_ref[...].T
    high = turned.astype(BF16)
    rest = (turned - high.astype(F32)).astype(BF16)
    key = key_ref[...]

    def row_of(o):
        pick = (key == o).astype(F32).astype(BF16)
        return nn(high, pick) + nn(rest, pick)

    out_ref[0] = (row_of(0.0) + above_ref[...]).astype(BF16)

    def step(o, carry):
        out_ref[o] = row_of(o.astype(F32)).astype(BF16)
        return carry

    lax.fori_loop(1, out_rows, step, 0)


def weight_kernel(
    place_ref, near_ref, far_ref, keep_ref, send_ref, feat_ref, cot_ref, send_acc, *, scale
):
    near = near_ref.shape[0]
    members = feat_ref.shape[1] // 8
    width, e_half = keep_ref.shape[1:]
    step = pl.program_id(0)

    @pl.when(step == 0)
    def _():
        keep_ref[...] = jnp.zeros_like(keep_ref)
        send_acc[...] = jnp.zeros_like(send_acc)

    def take(member, block):
        block = block.astype(F32)
        feat_ref[:, 8 * member : 8 * member + 8] = unfold(block[:FEAT_ROWS]).reshape(16, 8, width)
        own = block[FEAT_ROWS : FEAT_ROWS + COT_ROWS].reshape(9, 8, 128)
        peer = block[FEAT_ROWS + COT_ROWS :].reshape(9, 8, 128)
        cot_ref[:, 8 * member : 8 * member + 8, 0:128] = own
        cot_ref[:, 8 * member : 8 * member + 8, 128:256] = peer

    for member in range(members):
        at = place_ref[0] ^ member

        @pl.when(at < near)
        def _():
            take(member, near_ref[jnp.minimum(at, near - 1)])

        if members > near:

            @pl.when(at >= near)
            def _():
                take(member, far_ref[jnp.maximum(at - near, 0)])

    for a in range(3):
        for b in range(3):
            places = [(u, v) for u in reach(a) for v in reach(b)]
            left = jnp.concatenate(
                [feat_ref[(2 * u + a - 1) * 4 + 2 * v + b - 1] for u, v in places], axis=0
            ).astype(BF16)
            right = jnp.concatenate([cot_ref[3 * u + v] for u, v in places], axis=0).astype(BF16)
            total = tn(left, right) * scale
            keep_ref[3 * a + b] += total[:, :e_half]
            send_acc[3 * a + b] += total[:, 128 : 128 + e_half]

    @pl.when(step == pl.num_programs(0) - 1)
    def _():
        send_ref[...] = send_acc[...].astype(BF16)


def whole(shape):
    return pl.BlockSpec(shape, lambda g: (0,) * len(shape))


def on_device(
    tile_pixels, tile_cell, agg_cot, dw_weight, norm_gain, up_weight, proj_weight,
    layer_scale, ds_gain, ds_weight, agg_weight,
):
    channels = dw_weight.shape[1]
    hid = up_weight.shape[1]
    width = ds_weight.shape[1]
    bands = lax.axis_size("slide")
    sources = bands * lax.axis_size("chan")
    chunks = sources // 8
    pixch = tile_pixels.shape[2]
    out_rows = agg_cot.shape[1]
    e_half = agg_weight.shape[2]
    cols = agg_cot.shape[3]
    blocks = CAP * chunks
    total_rows = out_rows * bands * lax.axis_size("rep") * cols
    loss_scale = 1.0 / math.sqrt(total_rows)
    chan = lax.axis_index("chan").astype(jnp.int32)[None]
    gain = norm_gain[None]
    scale = layer_scale[None]
    low_gain = ds_gain[None]
    proj_turned = proj_weight.T
    ds_turned = ds_weight.T

    packed, top_cot = pl.pallas_call(
        pack_kernel,
        grid=(1,),
        out_shape=(
            jax.ShapeDtypeStruct((sources, WIRE_ROWS, 128), BF16),
            jax.ShapeDtypeStruct((e_half, cols), BF16),
        ),
        in_specs=[
            SMEM,
            pl.BlockSpec((None,) + tile_pixels.shape[1:], lambda i: (0, 0, 0)),
            pl.BlockSpec((None, None, e_half, cols), lambda i: (0, 0, 0, 0)),
        ],
        out_specs=(whole((sources, WIRE_ROWS, 128)), whole((e_half, cols))),
        scratch_shapes=[pltpu.VMEM((sources, WIRE_ROWS, 128), F32)],
        cost_estimate=takes(1.5),
        name="pack",
    )(tile_cell, tile_pixels, agg_cot)
    below_cot = shifted(top_cot, "slide", -1)
    packed, own_weight = lax.optimization_barrier((packed, agg_weight))
    peer_weight = swapped(own_weight, "chan", 1)
    got = lax.all_to_all(packed, ("slide", "chan"), split_axis=0, concat_axis=0, tiled=True)

    key, cots_own, cots_send = pl.pallas_call(
        patch_kernel,
        out_shape=(
            jax.ShapeDtypeStruct((blocks * COT_ROWS, cols), F32),
            jax.ShapeDtypeStruct((chunks * COT_ROWS, 128), BF16),
            jax.ShapeDtypeStruct((chunks * COT_ROWS, 128), BF16),
        ),
        in_specs=[
            SMEM,
            pl.BlockSpec((sources, 8, 128), lambda i: (0, pixch // 1024, 0)),
            pl.BlockSpec((None, out_rows, e_half, cols), lambda i: (0, 0, 0, 0)),
            whole((e_half, cols)),
        ],
        out_specs=(
            whole((blocks * COT_ROWS, cols)),
            whole((chunks * COT_ROWS, 128)),
            whole((chunks * COT_ROWS, 128)),
        ),
        grid=(1,),
        scratch_shapes=[pltpu.VMEM((sources, 8, 128), F32)],
        compiler_params=params_of(),
        cost_estimate=takes(1.2),
        name="patch",
    )(chan, got, agg_cot, below_cot)
    cots_peer = swapped(cots_send, "chan", 1)
    cots_own = cots_own.reshape(chunks, COT_ROWS, 128)
    cots_peer = cots_peer.reshape(chunks, COT_ROWS, 128)

    rows = PIX * 8
    pixel_spec = pl.BlockSpec((8, WIRE_ROWS, 128), lambda g: (g, 0, 0))
    pixel_scratch = [pltpu.VMEM((8, WIRE_ROWS, 128), F32), pltpu.VMEM((8, pixch), F32)]

    def chunk(*shape):
        return pl.BlockSpec((None,) + shape, lambda g: (g,) + (0,) * len(shape))

    feats, hat1, rstd1, hat2, rstd2, hidden, slope, patches = pl.pallas_call(
        stem_kernel,
        grid=(chunks,),
        out_shape=(
            jax.ShapeDtypeStruct((chunks, FEAT_ROWS, 128), BF16),
            jax.ShapeDtypeStruct((chunks, rows, channels), F32),
            jax.ShapeDtypeStruct((chunks, rows, 1), F32),
            jax.ShapeDtypeStruct((chunks, rows, channels), F32),
            jax.ShapeDtypeStruct((chunks, rows, 1), F32),
            jax.ShapeDtypeStruct((chunks, rows, hid), BF16),
            jax.ShapeDtypeStruct((chunks, rows, hid), F32),
            jax.ShapeDtypeStruct((chunks, 128, 4 * channels), BF16),
        ),
        in_specs=[
            pixel_spec,
            whole(dw_weight.shape), whole((1, channels)), whole(up_weight.shape),
            whole(proj_turned.shape), whole((1, channels)), whole((1, channels)),
            whole(ds_turned.shape),
        ],
        out_specs=(
            chunk(FEAT_ROWS, 128), chunk(rows, channels), chunk(rows, 1), chunk(rows, channels),
            chunk(rows, 1), chunk(rows, hid), chunk(rows, hid), chunk(128, 4 * channels),
        ),
        scratch_shapes=[
            pltpu.VMEM((SIDE + 6, SIDE + 6, 8, channels), F32),
            pltpu.VMEM((SIDE, SIDE, 8, channels), F32),
            pltpu.VMEM((SIDE // 2, 2, SIDE // 2, 2, 8, channels), F32),
            pltpu.VMEM((128, 4 * channels), F32),
            *pixel_scratch,
        ],
        compiler_params=params_of(),
        cost_estimate=takes(2.7),
        name="stem",
    )(got, dw_weight, gain, up_weight, proj_turned, scale, low_gain, ds_turned)

    feats_band = jnp.concatenate([feats, swapped(feats, "chan", 1)], axis=0)
    spread, below = pl.pallas_call(
        lambda *refs: spread_kernel(*refs, last=out_rows),
        grid=(blocks,),
        out_shape=(
            jax.ShapeDtypeStruct((blocks * 72, e_half), F32),
            jax.ShapeDtypeStruct((e_half, cols), F32),
        ),
        in_specs=[
            chunk(FEAT_ROWS, 128), whole(agg_weight.shape),
            pl.BlockSpec((72, cols), lambda g: (g, 0)),
        ],
        out_specs=(pl.BlockSpec((72, e_half), lambda g: (g, 0)), whole((e_half, cols))),
        compiler_params=params_of(),
        cost_estimate=takes(1.0),
        name="spread",
    )(feats_band, agg_weight, key)
    tile_blocks = jnp.concatenate([feats, cots_own, cots_peer], axis=1)
    gather = chunks == 1
    near = far = tile_blocks
    place = jnp.zeros((1,), jnp.int32)
    spans = [("slide", 1 << n) for n in reversed(range(bands.bit_length() - 1))]
    spans += [("rep", 1 << n) for n in range(lax.axis_size("rep").bit_length() - 1)]

    def widen(n, near, place):
        axis, step = spans[n]
        bit = (lax.axis_index(axis).astype(jnp.int32) // step) % 2
        return swapped(near, axis, step), place + bit * (1 << n)

    if gather:
        far, place = widen(0, near, place)
        near = jnp.concatenate([near, far], axis=0)

    keep, send = pl.pallas_call(
        lambda *refs: back_kernel(*refs, scale=loss_scale),
        grid=(chunks,),
        out_shape=(
            jax.ShapeDtypeStruct((HALF_ROWS, 128), F32),
            jax.ShapeDtypeStruct((HALF_ROWS, 128), BF16),
        ),
        in_specs=[
            SMEM, chunk(COT_ROWS, 128), chunk(COT_ROWS, 128),
            whole(agg_weight.shape), whole(agg_weight.shape), pixel_spec,
            chunk(rows, channels), chunk(rows, 1), chunk(rows, channels), chunk(rows, 1),
            chunk(rows, hid), chunk(rows, hid), chunk(128, 4 * channels),
            whole((1, channels)), whole(up_weight.shape), whole(proj_turned.shape),
            whole((1, channels)), whole((1, channels)), whole(ds_turned.shape),
        ],
        out_specs=(whole((HALF_ROWS, 128)), whole((HALF_ROWS, 128))),
        scratch_shapes=[
            pltpu.VMEM((SIDE + 6, SIDE + 6, 8, channels), F32),
            pltpu.VMEM((SIDE // 2, 2, SIDE // 2, 2, 8, channels), F32),
            pltpu.VMEM((SIDE, SIDE, 8, channels), F32),
            pltpu.VMEM((7, 7, 8, channels), F32),
            pltpu.VMEM(ds_turned.shape, F32),
            pltpu.VMEM(up_weight.shape, F32),
            pltpu.VMEM(proj_turned.shape, F32),
            pltpu.VMEM((2 * HALF_ROWS, 128), F32),
            *pixel_scratch,
        ],
        compiler_params=params_of(),
        cost_estimate=takes(3.7),
        name="stem_back",
    )(
        chan, cots_own, cots_peer, agg_weight, peer_weight, got,
        hat1, rstd1, hat2, rstd2, hidden, slope, patches,
        gain, up_weight, proj_turned, scale, low_gain, ds_turned,
    )

    part = keep + swapped(send, "chan", 1).astype(F32)
    if gather:
        part, near, spread, below = lax.optimization_barrier((part, near, spread, below))
    steps = []
    for axis in ("rep", "slide"):
        step = 1
        while step < lax.axis_size(axis):
            steps.append((axis, step))
            step *= 2
    for n, (axis, step) in enumerate(steps):
        wire = part.astype(BF16)
        if n == 1:
            wire, below = lax.optimization_barrier((wire, below))
        part = wire.astype(F32) + swapped(wire, axis, step).astype(F32)
    above = shifted(below, "slide", 1)
    map_call = pl.pallas_call(
        map_kernel,
        out_shape=jax.ShapeDtypeStruct((out_rows, e_half, cols), BF16),
        in_specs=[VMEM, VMEM, VMEM],
        out_specs=VMEM,
        compiler_params=pltpu.CompilerParams(vmem_limit_bytes=24 << 20),
        cost_estimate=takes(3.5),
        name="agg_map",
    )
    agg_map = map_call(spread, key, above)

    for n in range(1, len(spans) if gather else 0):
        far, place = widen(n, near, place)
        if n < len(spans) - 1:
            near = jnp.concatenate([near, far], axis=0)

    if gather:
        far, agg_map = lax.optimization_barrier((far, agg_map))
    count = 2 * near.shape[0] if gather else chunks
    per = count if gather else 1
    near_count = near.shape[0] if gather else 1
    agg_keep, agg_send = pl.pallas_call(
        lambda *refs: weight_kernel(*refs, scale=loss_scale),
        grid=(count // per,),
        out_shape=(
            jax.ShapeDtypeStruct((9, width, e_half), F32),
            jax.ShapeDtypeStruct((9, width, e_half), BF16),
        ),
        in_specs=[
            SMEM,
            pl.BlockSpec((near_count, BLOCK_ROWS, 128), lambda g: (g, 0, 0)),
            pl.BlockSpec((near_count, BLOCK_ROWS, 128), lambda g: (g, 0, 0)),
        ],
        out_specs=(whole((9, width, e_half)), whole((9, width, e_half))),
        scratch_shapes=[
            pltpu.VMEM((16, per * 8, width), F32),
            pltpu.VMEM((9, per * 8, 256), F32),
            pltpu.VMEM((9, width, e_half), F32),
        ],
        compiler_params=params_of(),
        cost_estimate=takes(1.4),
        name="agg_weight_grad",
    )(place, near, far)
    agg_grad = agg_keep + swapped(agg_send, "chan", 1).astype(F32)
    if not gather:
        agg_grad = lax.psum(agg_grad, ("slide", "rep"))

    part = part.astype(BF16)
    peer_part = swapped(part, "chan", 1)
    part, agg_grad = lax.optimization_barrier((part, agg_grad))
    dw_grad, up_grad, proj_grad, ds_grad = pl.pallas_call(
        unpack_kernel,
        out_shape=(
            jax.ShapeDtypeStruct(dw_weight.shape, F32),
            jax.ShapeDtypeStruct(up_weight.shape, F32),
            jax.ShapeDtypeStruct(proj_turned.shape, F32),
            jax.ShapeDtypeStruct(ds_turned.shape, F32),
        ),
        in_specs=[SMEM, VMEM, VMEM],
        out_specs=(VMEM, VMEM, VMEM, VMEM),
        scratch_shapes=[pltpu.VMEM((2 * HALF_ROWS, 128), F32)],
        compiler_params=pltpu.CompilerParams(vmem_limit_bytes=24 << 20),
        cost_estimate=takes(1.5),
        name="unpack",
    )(chan, part, peer_part)
    proj_grad = proj_grad.T
    ds_grad = ds_grad.T
    return (agg_map[None], agg_grad, dw_grad, up_grad, proj_grad, ds_grad)


def solution(mesh):
    in_specs = (
        P(("groups", "rep"), ("slide", "chan"), None),
        P(("groups", "rep"), ("slide", "chan")),
        P(("groups", "rep"), "slide", "chan", None),
        P(), P(), P(), P(), P(), P(), P(),
        P(None, None, "chan"),
    )
    out_specs = (
        P(("groups", "rep"), "slide", "chan", None),
        P("groups", None, "chan"),
        P("groups", None),
        P("groups", None),
        P("groups", None),
        P("groups", None),
    )
    return jax.shard_map(
        on_device, mesh=mesh, in_specs=in_specs, out_specs=out_specs, check_vma=False
    )
```

```python
import math

import jax
import jax.numpy as jnp
from jax import lax
from jax.experimental import pallas as pl
from jax.experimental.pallas import tpu as pltpu
from jax.sharding import PartitionSpec as P

SIDE = 8
CAP = 2
GW = 64
BAND_CELLS = 512
PIX = SIDE * SIDE
HALF_ROWS = 608
FEAT_ROWS = 192
COT_ROWS = 72
WIRE_ROWS = 56
BLOCK_ROWS = FEAT_ROWS + 2 * COT_ROWS
F32 = jnp.float32
BF16 = jnp.bfloat16
VMEM = pl.BlockSpec(memory_space=pltpu.VMEM)
SMEM = pl.BlockSpec(memory_space=pltpu.SMEM)


def params_of(steps=1):
    return pltpu.CompilerParams(
        dimension_semantics=("arbitrary",) * steps, vmem_limit_bytes=24 << 20
    )


def takes(microseconds):
    return pl.CostEstimate(
        flops=0, transcendentals=0, bytes_accessed=int(microseconds * 3.69e6)
    )


def nn(left, right):
    return lax.dot_general(left, right, (((1,), (0,)), ((), ())), preferred_element_type=F32)


def nt(left, right):
    return lax.dot_general(left, right, (((1,), (1,)), ((), ())), preferred_element_type=F32)


def tn(left, right):
    return lax.dot_general(left, right, (((0,), (0,)), ((), ())), preferred_element_type=F32)


def shifted(value, axis, steps):
    count = lax.axis_size(axis)
    first, last = (max(0, -steps), min(count, count - steps))
    return lax.ppermute(value, axis, [(source, source + steps) for source in range(first, last)])


def swapped(value, axis, step):
    count = lax.axis_size(axis)
    return lax.ppermute(value, axis, [(place, place ^ step) for place in range(count)])


def reach(tap):
    return (1, 2) if tap == 0 else (0, 1)


def pack_kernel(cells_ref, pixels_ref, row_ref, out_ref, below_ref, wide_ref):
    slots = pixels_ref.shape[0]
    rows = out_ref.shape[0]
    pixch = pixels_ref.shape[1]
    cells = [cells_ref[0, t] for t in range(slots)]
    live = [cell >= 0 for cell in cells]
    bands = [cell // BAND_CELLS for cell in cells]
    places = []
    for t in range(slots):
        rank = jnp.int32(0)
        for s in range(t):
            rank = rank + ((bands[s] == bands[t]) & live[s]).astype(jnp.int32)
        places.append(jnp.where(live[t], bands[t] * CAP + rank, -1))
    dest = lax.broadcasted_iota(jnp.int32, (rows, slots), 0)
    slot = lax.broadcasted_iota(jnp.int32, (rows, slots), 1)
    place = jnp.full((rows, slots), -1, jnp.int32)
    for t in range(slots):
        place = jnp.where(slot == t, places[t], place)
    route = (place == dest).astype(F32).astype(BF16)
    below_ref[...] = row_ref[...].astype(BF16)
    routed = nn(route, pixels_ref[...])
    wide_ref[...] = jnp.zeros_like(wide_ref)
    for n in range(pixch // 128):
        wide_ref[:, n, :] = routed[:, 128 * n : 128 * n + 128]
    lane = lax.broadcasted_iota(jnp.int32, (rows, 128), 1)
    base = (lax.broadcasted_iota(jnp.int32, (rows, 128), 0) // CAP) * CAP
    notes = jnp.zeros((rows, 128), F32)
    for t in range(slots):
        within = cells[t] % BAND_CELLS
        own_row = (within // GW).astype(F32)
        own_col = (within % GW).astype(F32)
        for rank in range(CAP):
            hit = base + rank == places[t]
            for at, value in enumerate((own_row, own_col, jnp.float32(1.0))):
                notes = jnp.where(hit & (lane == 3 * rank + at), value, notes)
    wide_ref[:, pixch // 128, :] = notes
    out_ref[...] = wide_ref[...].astype(BF16)


def patch_kernel(chan_ref, meta_ref, cot_ref, below_ref, key_ref, own_ref, send_ref, meta_f32):
    sources = meta_ref.shape[0]
    chunks = sources // 8
    out_rows, e_half, _ = cot_ref.shape
    meta_f32[...] = meta_ref[...].astype(F32)
    meta = meta_f32[:, 0, :]
    first = chan_ref[0] == 0
    lane = lax.broadcasted_iota(jnp.int32, (8, 128), 1).astype(F32)
    blocks = []
    for mine in (True, False):
        for chunk in range(chunks):
            part = meta[chunk * 8 : chunk * 8 + 8]
            low = [jnp.broadcast_to(part[:, n : n + 1], (8, 128)) for n in range(3)]
            high = [jnp.broadcast_to(part[:, n : n + 1], (8, 128)) for n in range(3, 6)]
            row, col, valid = (
                jnp.where(first == mine, one, two) for one, two in zip(low, high)
            )
            for u in range(3):
                for v in range(3):
                    hit = (lane == 2.0 * col + v) & (valid > 0.5)
                    blocks.append(jnp.where(hit, 2.0 * row + u, -1.0))
    key = jnp.concatenate(blocks, axis=0)
    key_ref[...] = key

    def step(o, total):
        pick = (key == o.astype(F32)).astype(F32).astype(BF16)
        return total + nt(pick, cot_ref[o].astype(BF16))

    total = lax.fori_loop(
        0, out_rows, step, jnp.zeros((key.shape[0], e_half), F32), unroll=4
    )
    pick = (key == float(out_rows)).astype(F32).astype(BF16)
    total = total + nt(pick, below_ref[...])
    half = total.shape[0] // 2
    own_ref[...] = jnp.zeros_like(own_ref)
    send_ref[...] = jnp.zeros_like(send_ref)
    own_ref[:, :e_half] = total[:half].astype(BF16)
    send_ref[:, :e_half] = total[half:].astype(BF16)


def center_of(values):
    center = values - jnp.mean(values, axis=-1, keepdims=True)
    rstd = lax.rsqrt(jnp.mean(center * center, axis=-1, keepdims=True) + 1e-06)
    return center * rstd, rstd


def fill_padded(padded_ref, got_ref, wide_ref, pixels_ref, channels):
    wide_ref[...] = got_ref[...].astype(F32)
    for n in range(pixels_ref.shape[1] // 128):
        pixels_ref[:, 128 * n : 128 * n + 128] = wide_ref[:, n, :]
    padded_ref[...] = jnp.zeros_like(padded_ref)
    for i in range(SIDE):
        for j in range(SIDE):
            at = (i * SIDE + j) * channels
            padded_ref[i + 3, j + 3] = pixels_ref[:, at : at + channels]


def stem_kernel(
    got_ref, dw_ref, gain_ref, up_ref, proj_ref, scale_ref, ds_gain_ref, ds_ref,
    feat_ref, hat1_ref, rstd1_ref, hat2_ref, rstd2_ref, hidden_ref, slope_ref, patch_ref,
    padded_ref, spatial_ref, low_ref, patch_f32, wide_ref, pixels_ref,
):
    channels = dw_ref.shape[1]
    fill_padded(padded_ref, got_ref, wide_ref, pixels_ref, channels)

    def row_step(i, carry):
        total = jnp.zeros((SIDE, 8, channels), F32)
        for a in range(7):
            for b in range(7):
                weight = dw_ref[pl.ds(7 * a + b, 1), :].reshape(1, 1, channels)
                total = total + weight * padded_ref[i + a, b : b + SIDE]
        spatial_ref[i] = total
        return carry

    lax.fori_loop(0, SIDE, row_step, 0)
    hat1, rstd1 = center_of(spatial_ref[...].reshape(PIX * 8, channels))
    hat1_ref[...] = hat1
    rstd1_ref[...] = rstd1
    normed = (hat1 * gain_ref[...]).astype(BF16)
    before = nn(normed, up_ref[...])
    cdf = 0.5 * (1.0 + lax.erf(before * math.sqrt(0.5)))
    pdf = jnp.exp(-0.5 * before * before) * (1.0 / math.sqrt(2.0 * math.pi))
    hidden = (before * cdf).astype(BF16)
    hidden_ref[...] = hidden
    slope_ref[...] = cdf + before * pdf
    branch = nt(hidden, proj_ref[...])
    inputs = padded_ref[3 : 3 + SIDE, 3 : 3 + SIDE].reshape(PIX * 8, channels)
    hat2, rstd2 = center_of(inputs + scale_ref[...] * branch)
    hat2_ref[...] = hat2
    rstd2_ref[...] = rstd2
    low_ref[...] = (hat2 * ds_gain_ref[...]).reshape(low_ref.shape)
    half = SIDE // 2
    for di in range(2):
        for dj in range(2):
            at = (2 * di + dj) * channels
            patch_f32[:, at : at + channels] = low_ref[:, di, :, dj].reshape(-1, channels)
    patches = patch_f32[...].astype(BF16)
    patch_ref[...] = patches
    total = nt(patches, ds_ref[...])
    rows = total.shape[0]
    feat_ref[0:rows] = total[:, 0:128].astype(BF16)
    rest = jnp.concatenate([total[: rows // 2, 128:192], total[rows // 2 :, 128:192]], axis=1)
    feat_ref[rows:] = rest.astype(BF16)


def unfold(block):
    rest = block[128:]
    return jnp.concatenate(
        [block[:128], jnp.concatenate([rest[:, :64], rest[:, 64:]], axis=0)], axis=1
    )


def back_kernel(
    chan_ref, own_ref, peer_ref, w_own_ref, w_peer_ref, got_ref,
    hat1_ref, rstd1_ref, hat2_ref, rstd2_ref, hidden_ref, slope_ref, patch_ref,
    gain_ref, up_ref, proj_ref, scale_ref, ds_gain_ref, ds_ref,
    keep_ref, send_ref,
    padded_ref, dlow_ref, dspatial_ref, dw_ref, ds_acc, up_acc, proj_acc, pack_ref,
    wide_ref, pixels_ref,
    *, scale,
):
    channels = gain_ref.shape[1]
    e_half = w_own_ref.shape[2]
    half = SIDE // 2
    step = pl.program_id(0)

    @pl.when(step == 0)
    def _():
        dw_ref[...] = jnp.zeros_like(dw_ref)
        ds_acc[...] = jnp.zeros_like(ds_acc)
        up_acc[...] = jnp.zeros_like(up_acc)
        proj_acc[...] = jnp.zeros_like(proj_acc)

    own = own_ref[...].astype(F32)[:, :e_half].reshape(9, 8, e_half)
    peer = peer_ref[...].astype(F32)[:, :e_half].reshape(9, 8, e_half)
    grads = {}
    for a in range(3):
        for b in range(3):
            places = [(u, v) for u in reach(a) for v in reach(b)]
            left_own = jnp.concatenate([own[3 * u + v] for u, v in places], axis=0).astype(BF16)
            left_peer = jnp.concatenate([peer[3 * u + v] for u, v in places], axis=0).astype(BF16)
            out = nt(left_own, w_own_ref[3 * a + b]) + nt(left_peer, w_peer_ref[3 * a + b])
            for n, (u, v) in enumerate(places):
                at = (2 * u + a - 1) * half + 2 * v + b - 1
                piece = out[8 * n : 8 * n + 8]
                grads[at] = grads[at] + piece if at in grads else piece
    dfeat = jnp.concatenate([grads[at] for at in range(half * half)], axis=0) * scale
    dfeat = dfeat.astype(BF16)

    hat2 = hat2_ref[...]
    ds_acc[...] += tn(dfeat, patch_ref[...])
    back = nn(dfeat, ds_ref[...])
    for di in range(2):
        for dj in range(2):
            at = (2 * di + dj) * channels
            dlow_ref[:, di, :, dj] = back[:, at : at + channels].reshape(half, half, 8, channels)
    dhat2 = dlow_ref[...].reshape(PIX * 8, channels) * ds_gain_ref[...]
    mean_a = jnp.mean(dhat2, axis=-1, keepdims=True)
    mean_b = jnp.mean(dhat2 * hat2, axis=-1, keepdims=True)
    dmixed = rstd2_ref[...] * (dhat2 - mean_a - hat2 * mean_b)
    dbranch = (dmixed * scale_ref[...]).astype(BF16)
    proj_acc[...] += tn(dbranch, hidden_ref[...])
    dhidden = nn(dbranch, proj_ref[...])
    dbefore = (dhidden * slope_ref[...]).astype(BF16)
    hat1 = hat1_ref[...]
    normed = (hat1 * gain_ref[...]).astype(BF16)
    up_acc[...] += tn(normed, dbefore)
    dhat1 = nt(dbefore, up_ref[...]) * gain_ref[...]
    mean_a = jnp.mean(dhat1, axis=-1, keepdims=True)
    mean_b = jnp.mean(dhat1 * hat1, axis=-1, keepdims=True)
    dspatial = rstd1_ref[...] * (dhat1 - mean_a - hat1 * mean_b)
    dspatial_ref[...] = dspatial.reshape(SIDE, SIDE, 8, channels)
    fill_padded(padded_ref, got_ref, wide_ref, pixels_ref, channels)

    def tap_step(a, carry):
        totals = [jnp.zeros((8, channels), F32) for _ in range(7)]
        for i in range(SIDE):
            grad = dspatial_ref[i]
            for b in range(7):
                product = padded_ref[i + a, b : b + SIDE] * grad
                totals[b] = totals[b] + jnp.sum(product, axis=0)
        for b in range(7):
            dw_ref[a, b] += totals[b]
        return carry

    lax.fori_loop(0, 7, tap_step, 0)

    @pl.when(step == pl.num_programs(0) - 1)
    def _():
        pack_ref[...] = jnp.zeros_like(pack_ref)
        for n in range(3):
            lanes = slice(128 * n, 128 * n + 128)
            pack_ref[192 * n : 192 * n + 192, :] = ds_acc[:, lanes]
            pack_ref[576 + 96 * n : 672 + 96 * n, :] = up_acc[:, lanes]
            pack_ref[864 + 96 * n : 960 + 96 * n, :] = proj_acc[:, lanes]
        pack_ref[1152:1201, 0:channels] = jnp.sum(dw_ref[...], axis=2).reshape(49, channels)
        mine = pl.multiple_of(chan_ref[0] * HALF_ROWS, 8)
        other = pl.multiple_of((1 - chan_ref[0]) * HALF_ROWS, 8)
        keep_ref[...] = pack_ref[pl.ds(mine, HALF_ROWS), :]
        send_ref[...] = pack_ref[pl.ds(other, HALF_ROWS), :].astype(BF16)


def unpack_kernel(chan_ref, own_ref, peer_ref, dw_ref, up_ref, proj_ref, ds_ref, pack_ref):
    channels = dw_ref.shape[1]
    mine = pl.multiple_of(chan_ref[0] * HALF_ROWS, 8)
    other = pl.multiple_of((1 - chan_ref[0]) * HALF_ROWS, 8)
    pack_ref[pl.ds(mine, HALF_ROWS), :] = own_ref[...].astype(F32)
    pack_ref[pl.ds(other, HALF_ROWS), :] = peer_ref[...].astype(F32)
    for n in range(3):
        lanes = slice(128 * n, 128 * n + 128)
        ds_ref[:, lanes] = pack_ref[192 * n : 192 * n + 192, :]
        up_ref[:, lanes] = pack_ref[576 + 96 * n : 672 + 96 * n, :]
        proj_ref[:, lanes] = pack_ref[864 + 96 * n : 960 + 96 * n, :]
    dw_ref[...] = pack_ref[1152:1201, 0:channels]


def spread_kernel(feat_ref, w_ref, key_ref, y_ref, below_ref, *, last):
    width = w_ref.shape[1]
    feats = unfold(feat_ref[...].astype(F32)).reshape(16, 8, width)
    outs = {}
    for a in range(3):
        for b in range(3):
            places = [(u, v) for u in reach(a) for v in reach(b)]
            left = jnp.concatenate(
                [feats[(2 * u + a - 1) * 4 + 2 * v + b - 1] for u, v in places], axis=0
            ).astype(BF16)
            out = nn(left, w_ref[3 * a + b])
            for n, (u, v) in enumerate(places):
                piece = out[8 * n : 8 * n + 8]
                at = 3 * u + v
                outs[at] = outs[at] + piece if at in outs else piece
    total = jnp.concatenate([outs[at] for at in range(9)], axis=0)
    y_ref[...] = total
    pick = (key_ref[...] == float(last)).astype(F32).astype(BF16)
    high = total.astype(BF16)
    rest = (total - high.astype(F32)).astype(BF16)

    @pl.when(pl.program_id(0) == 0)
    def _():
        below_ref[...] = jnp.zeros_like(below_ref)

    below_ref[...] += tn(high, pick) + tn(rest, pick)


def map_kernel(y_ref, key_ref, above_ref, out_ref):
    out_rows, width, _ = out_ref.shape
    turned = y_ref[...].T
    high = turned.astype(BF16)
    rest = (turned - high.astype(F32)).astype(BF16)
    key = key_ref[...]

    def row_of(o):
        pick = (key == o).astype(F32).astype(BF16)
        return nn(high, pick) + nn(rest, pick)

    out_ref[0] = (row_of(0.0) + above_ref[...]).astype(BF16)

    def step(o, carry):
        out_ref[o] = row_of(o.astype(F32)).astype(BF16)
        return carry

    lax.fori_loop(1, out_rows, step, 0)


def weight_kernel(
    place_ref, near_ref, far_ref, keep_ref, send_ref, feat_ref, cot_ref, send_acc, *, scale
):
    near = near_ref.shape[0]
    members = feat_ref.shape[1] // 8
    width, e_half = keep_ref.shape[1:]
    step = pl.program_id(0)

    @pl.when(step == 0)
    def _():
        keep_ref[...] = jnp.zeros_like(keep_ref)
        send_acc[...] = jnp.zeros_like(send_acc)

    def take(member, block):
        block = block.astype(F32)
        feat_ref[:, 8 * member : 8 * member + 8] = unfold(block[:FEAT_ROWS]).reshape(16, 8, width)
        own = block[FEAT_ROWS : FEAT_ROWS + COT_ROWS].reshape(9, 8, 128)
        peer = block[FEAT_ROWS + COT_ROWS :].reshape(9, 8, 128)
        cot_ref[:, 8 * member : 8 * member + 8, 0:128] = own
        cot_ref[:, 8 * member : 8 * member + 8, 128:256] = peer

    for member in range(members):
        at = place_ref[0] ^ member

        @pl.when(at < near)
        def _():
            take(member, near_ref[jnp.minimum(at, near - 1)])

        if members > near:

            @pl.when(at >= near)
            def _():
                take(member, far_ref[jnp.maximum(at - near, 0)])

    for a in range(3):
        for b in range(3):
            places = [(u, v) for u in reach(a) for v in reach(b)]
            left = jnp.concatenate(
                [feat_ref[(2 * u + a - 1) * 4 + 2 * v + b - 1] for u, v in places], axis=0
            ).astype(BF16)
            right = jnp.concatenate([cot_ref[3 * u + v] for u, v in places], axis=0).astype(BF16)
            total = tn(left, right) * scale
            keep_ref[3 * a + b] += total[:, :e_half]
            send_acc[3 * a + b] += total[:, 128 : 128 + e_half]

    @pl.when(step == pl.num_programs(0) - 1)
    def _():
        send_ref[...] = send_acc[...].astype(BF16)


def whole(shape):
    return pl.BlockSpec(shape, lambda g: (0,) * len(shape))


def on_device(
    tile_pixels, tile_cell, agg_cot, dw_weight, norm_gain, up_weight, proj_weight,
    layer_scale, ds_gain, ds_weight, agg_weight,
):
    channels = dw_weight.shape[1]
    hid = up_weight.shape[1]
    width = ds_weight.shape[1]
    bands = lax.axis_size("slide")
    sources = bands * lax.axis_size("chan")
    chunks = sources // 8
    pixch = tile_pixels.shape[2]
    out_rows = agg_cot.shape[1]
    e_half = agg_weight.shape[2]
    cols = agg_cot.shape[3]
    blocks = CAP * chunks
    total_rows = out_rows * bands * lax.axis_size("rep") * cols
    loss_scale = 1.0 / math.sqrt(total_rows)
    chan = lax.axis_index("chan").astype(jnp.int32)[None]
    gain = norm_gain[None]
    scale = layer_scale[None]
    low_gain = ds_gain[None]
    proj_turned = proj_weight.T
    ds_turned = ds_weight.T

    packed, top_cot = pl.pallas_call(
        pack_kernel,
        grid=(1,),
        out_shape=(
            jax.ShapeDtypeStruct((sources, WIRE_ROWS, 128), BF16),
            jax.ShapeDtypeStruct((e_half, cols), BF16),
        ),
        in_specs=[
            SMEM,
            pl.BlockSpec((None,) + tile_pixels.shape[1:], lambda i: (0, 0, 0)),
            pl.BlockSpec((None, None, e_half, cols), lambda i: (0, 0, 0, 0)),
        ],
        out_specs=(whole((sources, WIRE_ROWS, 128)), whole((e_half, cols))),
        scratch_shapes=[pltpu.VMEM((sources, WIRE_ROWS, 128), F32)],
        cost_estimate=takes(1.5),
        name="pack",
    )(tile_cell, tile_pixels, agg_cot)
    below_cot = shifted(top_cot, "slide", -1)
    packed, own_weight = lax.optimization_barrier((packed, agg_weight))
    peer_weight = swapped(own_weight, "chan", 1)
    got = lax.all_to_all(packed, ("slide", "chan"), split_axis=0, concat_axis=0, tiled=True)

    key, cots_own, cots_send = pl.pallas_call(
        patch_kernel,
        out_shape=(
            jax.ShapeDtypeStruct((blocks * COT_ROWS, cols), F32),
            jax.ShapeDtypeStruct((chunks * COT_ROWS, 128), BF16),
            jax.ShapeDtypeStruct((chunks * COT_ROWS, 128), BF16),
        ),
        in_specs=[
            SMEM,
            pl.BlockSpec((sources, 8, 128), lambda i: (0, pixch // 1024, 0)),
            pl.BlockSpec((None, out_rows, e_half, cols), lambda i: (0, 0, 0, 0)),
            whole((e_half, cols)),
        ],
        out_specs=(
            whole((blocks * COT_ROWS, cols)),
            whole((chunks * COT_ROWS, 128)),
            whole((chunks * COT_ROWS, 128)),
        ),
        grid=(1,),
        scratch_shapes=[pltpu.VMEM((sources, 8, 128), F32)],
        compiler_params=params_of(),
        cost_estimate=takes(1.2),
        name="patch",
    )(chan, got, agg_cot, below_cot)
    cots_peer = swapped(cots_send, "chan", 1)
    cots_own = cots_own.reshape(chunks, COT_ROWS, 128)
    cots_peer = cots_peer.reshape(chunks, COT_ROWS, 128)

    rows = PIX * 8
    pixel_spec = pl.BlockSpec((8, WIRE_ROWS, 128), lambda g: (g, 0, 0))
    pixel_scratch = [pltpu.VMEM((8, WIRE_ROWS, 128), F32), pltpu.VMEM((8, pixch), F32)]

    def chunk(*shape):
        return pl.BlockSpec((None,) + shape, lambda g: (g,) + (0,) * len(shape))

    feats, hat1, rstd1, hat2, rstd2, hidden, slope, patches = pl.pallas_call(
        stem_kernel,
        grid=(chunks,),
        out_shape=(
            jax.ShapeDtypeStruct((chunks, FEAT_ROWS, 128), BF16),
            jax.ShapeDtypeStruct((chunks, rows, channels), F32),
            jax.ShapeDtypeStruct((chunks, rows, 1), F32),
            jax.ShapeDtypeStruct((chunks, rows, channels), F32),
            jax.ShapeDtypeStruct((chunks, rows, 1), F32),
            jax.ShapeDtypeStruct((chunks, rows, hid), BF16),
            jax.ShapeDtypeStruct((chunks, rows, hid), F32),
            jax.ShapeDtypeStruct((chunks, 128, 4 * channels), BF16),
        ),
        in_specs=[
            pixel_spec,
            whole(dw_weight.shape), whole((1, channels)), whole(up_weight.shape),
            whole(proj_turned.shape), whole((1, channels)), whole((1, channels)),
            whole(ds_turned.shape),
        ],
        out_specs=(
            chunk(FEAT_ROWS, 128), chunk(rows, channels), chunk(rows, 1), chunk(rows, channels),
            chunk(rows, 1), chunk(rows, hid), chunk(rows, hid), chunk(128, 4 * channels),
        ),
        scratch_shapes=[
            pltpu.VMEM((SIDE + 6, SIDE + 6, 8, channels), F32),
            pltpu.VMEM((SIDE, SIDE, 8, channels), F32),
            pltpu.VMEM((SIDE // 2, 2, SIDE // 2, 2, 8, channels), F32),
            pltpu.VMEM((128, 4 * channels), F32),
            *pixel_scratch,
        ],
        compiler_params=params_of(),
        cost_estimate=takes(2.7),
        name="stem",
    )(got, dw_weight, gain, up_weight, proj_turned, scale, low_gain, ds_turned)

    feats_band = jnp.concatenate([feats, swapped(feats, "chan", 1)], axis=0)
    spread, below = pl.pallas_call(
        lambda *refs: spread_kernel(*refs, last=out_rows),
        grid=(blocks,),
        out_shape=(
            jax.ShapeDtypeStruct((blocks * 72, e_half), F32),
            jax.ShapeDtypeStruct((e_half, cols), F32),
        ),
        in_specs=[
            chunk(FEAT_ROWS, 128), whole(agg_weight.shape),
            pl.BlockSpec((72, cols), lambda g: (g, 0)),
        ],
        out_specs=(pl.BlockSpec((72, e_half), lambda g: (g, 0)), whole((e_half, cols))),
        compiler_params=params_of(),
        cost_estimate=takes(1.0),
        name="spread",
    )(feats_band, agg_weight, key)
    tile_blocks = jnp.concatenate([feats, cots_own, cots_peer], axis=1)
    gather = chunks == 1
    near = far = tile_blocks
    place = jnp.zeros((1,), jnp.int32)
    spans = [("slide", 1 << n) for n in reversed(range(bands.bit_length() - 1))]
    spans += [("rep", 1 << n) for n in range(lax.axis_size("rep").bit_length() - 1)]

    def widen(n, near, place):
        axis, step = spans[n]
        bit = (lax.axis_index(axis).astype(jnp.int32) // step) % 2
        return swapped(near, axis, step), place + bit * (1 << n)

    if gather:
        far, place = widen(0, near, place)
        near = jnp.concatenate([near, far], axis=0)

    keep, send = pl.pallas_call(
        lambda *refs: back_kernel(*refs, scale=loss_scale),
        grid=(chunks,),
        out_shape=(
            jax.ShapeDtypeStruct((HALF_ROWS, 128), F32),
            jax.ShapeDtypeStruct((HALF_ROWS, 128), BF16),
        ),
        in_specs=[
            SMEM, chunk(COT_ROWS, 128), chunk(COT_ROWS, 128),
            whole(agg_weight.shape), whole(agg_weight.shape), pixel_spec,
            chunk(rows, channels), chunk(rows, 1), chunk(rows, channels), chunk(rows, 1),
            chunk(rows, hid), chunk(rows, hid), chunk(128, 4 * channels),
            whole((1, channels)), whole(up_weight.shape), whole(proj_turned.shape),
            whole((1, channels)), whole((1, channels)), whole(ds_turned.shape),
        ],
        out_specs=(whole((HALF_ROWS, 128)), whole((HALF_ROWS, 128))),
        scratch_shapes=[
            pltpu.VMEM((SIDE + 6, SIDE + 6, 8, channels), F32),
            pltpu.VMEM((SIDE // 2, 2, SIDE // 2, 2, 8, channels), F32),
            pltpu.VMEM((SIDE, SIDE, 8, channels), F32),
            pltpu.VMEM((7, 7, 8, channels), F32),
            pltpu.VMEM(ds_turned.shape, F32),
            pltpu.VMEM(up_weight.shape, F32),
            pltpu.VMEM(proj_turned.shape, F32),
            pltpu.VMEM((2 * HALF_ROWS, 128), F32),
            *pixel_scratch,
        ],
        compiler_params=params_of(),
        cost_estimate=takes(3.7),
        name="stem_back",
    )(
        chan, cots_own, cots_peer, agg_weight, peer_weight, got,
        hat1, rstd1, hat2, rstd2, hidden, slope, patches,
        gain, up_weight, proj_turned, scale, low_gain, ds_turned,
    )

    part = keep + swapped(send, "chan", 1).astype(F32)
    if gather:
        part, near, spread, below = lax.optimization_barrier((part, near, spread, below))
    above = shifted(below, "slide", 1)
    steps = []
    for axis in ("rep", "slide"):
        step = 1
        while step < lax.axis_size(axis):
            steps.append((axis, step))
            step *= 2
    for n, (axis, step) in enumerate(steps):
        wire = part.astype(BF16)
        if n == 1:
            wire, above = lax.optimization_barrier((wire, above))
        part = wire.astype(F32) + swapped(wire, axis, step).astype(F32)
    map_call = pl.pallas_call(
        map_kernel,
        out_shape=jax.ShapeDtypeStruct((out_rows, e_half, cols), BF16),
        in_specs=[VMEM, VMEM, VMEM],
        out_specs=VMEM,
        compiler_params=pltpu.CompilerParams(vmem_limit_bytes=24 << 20),
        cost_estimate=takes(3.5),
        name="agg_map",
    )
    agg_map = map_call(spread, key, above)

    for n in range(1, len(spans) if gather else 0):
        far, place = widen(n, near, place)
        if n < len(spans) - 1:
            near = jnp.concatenate([near, far], axis=0)

    if gather:
        far, agg_map = lax.optimization_barrier((far, agg_map))
    count = 2 * near.shape[0] if gather else chunks
    per = count if gather else 1
    near_count = near.shape[0] if gather else 1
    agg_keep, agg_send = pl.pallas_call(
        lambda *refs: weight_kernel(*refs, scale=loss_scale),
        grid=(count // per,),
        out_shape=(
            jax.ShapeDtypeStruct((9, width, e_half), F32),
            jax.ShapeDtypeStruct((9, width, e_half), BF16),
        ),
        in_specs=[
            SMEM,
            pl.BlockSpec((near_count, BLOCK_ROWS, 128), lambda g: (g, 0, 0)),
            pl.BlockSpec((near_count, BLOCK_ROWS, 128), lambda g: (g, 0, 0)),
        ],
        out_specs=(whole((9, width, e_half)), whole((9, width, e_half))),
        scratch_shapes=[
            pltpu.VMEM((16, per * 8, width), F32),
            pltpu.VMEM((9, per * 8, 256), F32),
            pltpu.VMEM((9, width, e_half), F32),
        ],
        compiler_params=params_of(),
        cost_estimate=takes(1.4),
        name="agg_weight_grad",
    )(place, near, far)
    agg_grad = agg_keep + swapped(agg_send, "chan", 1).astype(F32)
    if not gather:
        agg_grad = lax.psum(agg_grad, ("slide", "rep"))

    part = part.astype(BF16)
    peer_part = swapped(part, "chan", 1)
    part, agg_grad = lax.optimization_barrier((part, agg_grad))
    dw_grad, up_grad, proj_grad, ds_grad = pl.pallas_call(
        unpack_kernel,
        out_shape=(
            jax.ShapeDtypeStruct(dw_weight.shape, F32),
            jax.ShapeDtypeStruct(up_weight.shape, F32),
            jax.ShapeDtypeStruct(proj_turned.shape, F32),
            jax.ShapeDtypeStruct(ds_turned.shape, F32),
        ),
        in_specs=[SMEM, VMEM, VMEM],
        out_specs=(VMEM, VMEM, VMEM, VMEM),
        scratch_shapes=[pltpu.VMEM((2 * HALF_ROWS, 128), F32)],
        compiler_params=pltpu.CompilerParams(vmem_limit_bytes=24 << 20),
        cost_estimate=takes(1.5),
        name="unpack",
    )(chan, part, peer_part)
    proj_grad = proj_grad.T
    ds_grad = ds_grad.T
    return (agg_map[None], agg_grad, dw_grad, up_grad, proj_grad, ds_grad)


def solution(mesh):
    in_specs = (
        P(("groups", "rep"), ("slide", "chan"), None),
        P(("groups", "rep"), ("slide", "chan")),
        P(("groups", "rep"), "slide", "chan", None),
        P(), P(), P(), P(), P(), P(), P(),
        P(None, None, "chan"),
    )
    out_specs = (
        P(("groups", "rep"), "slide", "chan", None),
        P("groups", None, "chan"),
        P("groups", None),
        P("groups", None),
        P("groups", None),
        P("groups", None),
    )
    return jax.shard_map(
        on_device, mesh=mesh, in_specs=in_specs, out_specs=out_specs, check_vma=False
    )
```

```python
import math

import jax
import jax.numpy as jnp
from jax import lax
from jax.experimental import pallas as pl
from jax.experimental.pallas import tpu as pltpu
from jax.sharding import PartitionSpec as P

SIDE = 8
CAP = 2
GW = 64
BAND_CELLS = 512
PIX = SIDE * SIDE
HALF_ROWS = 608
FEAT_ROWS = 192
COT_ROWS = 72
WIRE_ROWS = 56
BLOCK_ROWS = FEAT_ROWS + 2 * COT_ROWS
F32 = jnp.float32
BF16 = jnp.bfloat16
VMEM = pl.BlockSpec(memory_space=pltpu.VMEM)
SMEM = pl.BlockSpec(memory_space=pltpu.SMEM)


def params_of(steps=1):
    return pltpu.CompilerParams(
        dimension_semantics=("arbitrary",) * steps, vmem_limit_bytes=24 << 20
    )


def takes(microseconds):
    return pl.CostEstimate(
        flops=0, transcendentals=0, bytes_accessed=int(microseconds * 3.69e6)
    )


def nn(left, right):
    return lax.dot_general(left, right, (((1,), (0,)), ((), ())), preferred_element_type=F32)


def nt(left, right):
    return lax.dot_general(left, right, (((1,), (1,)), ((), ())), preferred_element_type=F32)


def tn(left, right):
    return lax.dot_general(left, right, (((0,), (0,)), ((), ())), preferred_element_type=F32)


def shifted(value, axis, steps):
    count = lax.axis_size(axis)
    first, last = (max(0, -steps), min(count, count - steps))
    return lax.ppermute(value, axis, [(source, source + steps) for source in range(first, last)])


def swapped(value, axis, step):
    count = lax.axis_size(axis)
    return lax.ppermute(value, axis, [(place, place ^ step) for place in range(count)])


def reach(tap):
    return (1, 2) if tap == 0 else (0, 1)


def pack_kernel(cells_ref, pixels_ref, row_ref, out_ref, below_ref, wide_ref, note_ref):
    slots = pixels_ref.shape[0]
    rows = out_ref.shape[0]
    pixch = pixels_ref.shape[1]
    cells = [cells_ref[0, t] for t in range(slots)]
    live = [cell >= 0 for cell in cells]
    bands = [cell // BAND_CELLS for cell in cells]
    places = []
    for t in range(slots):
        rank = jnp.int32(0)
        for s in range(t):
            rank = rank + ((bands[s] == bands[t]) & live[s]).astype(jnp.int32)
        places.append(jnp.where(live[t], bands[t] * CAP + rank, -1))
    below_ref[...] = row_ref[...].astype(BF16)
    pixels = pixels_ref[...].astype(F32)
    for n in range(pixch // 128):
        wide_ref[:, n, :] = pixels[:, 128 * n : 128 * n + 128]
    wide_ref[:, pixch // 128 :, :] = jnp.zeros_like(wide_ref[:, pixch // 128 :, :])
    out_ref[...] = jnp.zeros_like(out_ref)
    for t in range(slots):

        @pl.when(live[t])
        def _():
            out_ref[jnp.maximum(places[t], 0)] = wide_ref[t].astype(BF16)

    lane = lax.broadcasted_iota(jnp.int32, (rows, 128), 1)
    base = (lax.broadcasted_iota(jnp.int32, (rows, 128), 0) // CAP) * CAP
    notes = jnp.zeros((rows, 128), F32)
    for t in range(slots):
        within = cells[t] % BAND_CELLS
        own_row = (within // GW).astype(F32)
        own_col = (within % GW).astype(F32)
        for rank in range(CAP):
            hit = base + rank == places[t]
            for at, value in enumerate((own_row, own_col, jnp.float32(1.0))):
                notes = jnp.where(hit & (lane == 3 * rank + at), value, notes)
    note_ref[...] = jnp.zeros_like(note_ref)
    note_ref[:, 0, :] = notes
    out_ref[:, pixch // 128 :, :] = note_ref[...].astype(BF16)


def patch_kernel(chan_ref, meta_ref, cot_ref, below_ref, key_ref, own_ref, send_ref, meta_f32):
    sources = meta_ref.shape[0]
    chunks = sources // 8
    out_rows, e_half, _ = cot_ref.shape
    meta_f32[...] = meta_ref[...].astype(F32)
    meta = meta_f32[:, 0, :]
    first = chan_ref[0] == 0
    lane = lax.broadcasted_iota(jnp.int32, (8, 128), 1).astype(F32)
    blocks = []
    for mine in (True, False):
        for chunk in range(chunks):
            part = meta[chunk * 8 : chunk * 8 + 8]
            low = [jnp.broadcast_to(part[:, n : n + 1], (8, 128)) for n in range(3)]
            high = [jnp.broadcast_to(part[:, n : n + 1], (8, 128)) for n in range(3, 6)]
            row, col, valid = (
                jnp.where(first == mine, one, two) for one, two in zip(low, high)
            )
            for u in range(3):
                for v in range(3):
                    hit = (lane == 2.0 * col + v) & (valid > 0.5)
                    blocks.append(jnp.where(hit, 2.0 * row + u, -1.0))
    key = jnp.concatenate(blocks, axis=0)
    key_ref[...] = key

    def step(o, total):
        pick = (key == o.astype(F32)).astype(F32).astype(BF16)
        return total + nt(pick, cot_ref[o].astype(BF16))

    total = lax.fori_loop(
        0, out_rows, step, jnp.zeros((key.shape[0], e_half), F32), unroll=4
    )
    pick = (key == float(out_rows)).astype(F32).astype(BF16)
    total = total + nt(pick, below_ref[...])
    half = total.shape[0] // 2
    own_ref[...] = jnp.zeros_like(own_ref)
    send_ref[...] = jnp.zeros_like(send_ref)
    own_ref[:, :e_half] = total[:half].astype(BF16)
    send_ref[:, :e_half] = total[half:].astype(BF16)


def center_of(values):
    center = values - jnp.mean(values, axis=-1, keepdims=True)
    rstd = lax.rsqrt(jnp.mean(center * center, axis=-1, keepdims=True) + 1e-06)
    return center * rstd, rstd


def fill_padded(padded_ref, got_ref, wide_ref, pixels_ref, channels):
    wide_ref[...] = got_ref[...].astype(F32)
    for n in range(pixels_ref.shape[1] // 128):
        pixels_ref[:, 128 * n : 128 * n + 128] = wide_ref[:, n, :]
    padded_ref[...] = jnp.zeros_like(padded_ref)
    for i in range(SIDE):
        for j in range(SIDE):
            at = (i * SIDE + j) * channels
            padded_ref[i + 3, j + 3] = pixels_ref[:, at : at + channels]


def stem_kernel(
    got_ref, dw_ref, gain_ref, up_ref, proj_ref, scale_ref, ds_gain_ref, ds_ref,
    feat_ref, hat1_ref, rstd1_ref, hat2_ref, rstd2_ref, hidden_ref, slope_ref, patch_ref,
    padded_ref, spatial_ref, low_ref, patch_f32, wide_ref, pixels_ref,
):
    channels = dw_ref.shape[1]
    fill_padded(padded_ref, got_ref, wide_ref, pixels_ref, channels)

    for i in range(SIDE):
        total = jnp.zeros((SIDE, 8, channels), F32)
        for a in range(max(0, 3 - i), min(7, SIDE + 3 - i)):
            for b in range(7):
                weight = dw_ref[7 * a + b : 7 * a + b + 1, :].reshape(1, 1, channels)
                total = total + weight * padded_ref[i + a, b : b + SIDE]
        spatial_ref[i] = total
    hat1, rstd1 = center_of(spatial_ref[...].reshape(PIX * 8, channels))
    hat1_ref[...] = hat1
    rstd1_ref[...] = rstd1
    normed = (hat1 * gain_ref[...]).astype(BF16)
    before = nn(normed, up_ref[...])
    cdf = 0.5 * (1.0 + lax.erf(before * math.sqrt(0.5)))
    pdf = jnp.exp(-0.5 * before * before) * (1.0 / math.sqrt(2.0 * math.pi))
    hidden = (before * cdf).astype(BF16)
    hidden_ref[...] = hidden
    slope_ref[...] = cdf + before * pdf
    branch = nt(hidden, proj_ref[...])
    inputs = padded_ref[3 : 3 + SIDE, 3 : 3 + SIDE].reshape(PIX * 8, channels)
    hat2, rstd2 = center_of(inputs + scale_ref[...] * branch)
    hat2_ref[...] = hat2
    rstd2_ref[...] = rstd2
    low_ref[...] = (hat2 * ds_gain_ref[...]).reshape(low_ref.shape)
    half = SIDE // 2
    for di in range(2):
        for dj in range(2):
            at = (2 * di + dj) * channels
            patch_f32[:, at : at + channels] = low_ref[:, di, :, dj].reshape(-1, channels)
    patches = patch_f32[...].astype(BF16)
    patch_ref[...] = patches
    total = nt(patches, ds_ref[...])
    rows = total.shape[0]
    feat_ref[0:rows] = total[:, 0:128].astype(BF16)
    rest = jnp.concatenate([total[: rows // 2, 128:192], total[rows // 2 :, 128:192]], axis=1)
    feat_ref[rows:] = rest.astype(BF16)


def unfold(block):
    rest = block[128:]
    return jnp.concatenate(
        [block[:128], jnp.concatenate([rest[:, :64], rest[:, 64:]], axis=0)], axis=1
    )


def back_kernel(
    chan_ref, own_ref, peer_ref, w_own_ref, w_peer_ref, got_ref,
    hat1_ref, rstd1_ref, hat2_ref, rstd2_ref, hidden_ref, slope_ref, patch_ref,
    gain_ref, up_ref, proj_ref, scale_ref, ds_gain_ref, ds_ref,
    keep_ref, send_ref,
    padded_ref, dlow_ref, dspatial_ref, dw_ref, ds_acc, up_acc, proj_acc, pack_ref,
    wide_ref, pixels_ref, w_ref,
    *, scale,
):
    channels = gain_ref.shape[1]
    half = SIDE // 2
    step = pl.program_id(0)

    @pl.when(step == 0)
    def _():
        dw_ref[...] = jnp.zeros_like(dw_ref)
        ds_acc[...] = jnp.zeros_like(ds_acc)
        up_acc[...] = jnp.zeros_like(up_acc)
        proj_acc[...] = jnp.zeros_like(proj_acc)

    e_half = w_own_ref.shape[2]
    w_ref[...] = jnp.zeros_like(w_ref)
    w_ref[:, :, 0:e_half] = w_own_ref[...]
    w_ref[:, :, 128 : 128 + e_half] = w_peer_ref[...]
    cots = jnp.concatenate([own_ref[...], peer_ref[...]], axis=1)
    grads = {}
    for a in range(3):
        for b in range(3):
            out = nt(cots, w_ref[3 * a + b])
            for u in reach(a):
                for v in reach(b):
                    at = (2 * u + a - 1) * half + 2 * v + b - 1
                    row = 8 * (3 * u + v)
                    piece = out[row : row + 8]
                    grads[at] = grads[at] + piece if at in grads else piece
    dfeat = jnp.concatenate([grads[at] for at in range(half * half)], axis=0) * scale
    dfeat = dfeat.astype(BF16)

    hat2 = hat2_ref[...]
    ds_acc[...] += tn(dfeat, patch_ref[...])
    back = nn(dfeat, ds_ref[...])
    for di in range(2):
        for dj in range(2):
            at = (2 * di + dj) * channels
            dlow_ref[:, di, :, dj] = back[:, at : at + channels].reshape(half, half, 8, channels)
    dhat2 = dlow_ref[...].reshape(PIX * 8, channels) * ds_gain_ref[...]
    mean_a = jnp.mean(dhat2, axis=-1, keepdims=True)
    mean_b = jnp.mean(dhat2 * hat2, axis=-1, keepdims=True)
    dmixed = rstd2_ref[...] * (dhat2 - mean_a - hat2 * mean_b)
    dbranch = (dmixed * scale_ref[...]).astype(BF16)
    proj_acc[...] += tn(dbranch, hidden_ref[...])
    dhidden = nn(dbranch, proj_ref[...])
    dbefore = (dhidden * slope_ref[...]).astype(BF16)
    hat1 = hat1_ref[...]
    normed = (hat1 * gain_ref[...]).astype(BF16)
    up_acc[...] += tn(normed, dbefore)
    dhat1 = nt(dbefore, up_ref[...]) * gain_ref[...]
    mean_a = jnp.mean(dhat1, axis=-1, keepdims=True)
    mean_b = jnp.mean(dhat1 * hat1, axis=-1, keepdims=True)
    dspatial = rstd1_ref[...] * (dhat1 - mean_a - hat1 * mean_b)
    dspatial_ref[...] = dspatial.reshape(SIDE, SIDE, 8, channels)
    fill_padded(padded_ref, got_ref, wide_ref, pixels_ref, channels)

    for a in range(7):
        totals = [jnp.zeros((8, channels), F32) for _ in range(7)]
        for i in range(max(0, 3 - a), min(SIDE, SIDE + 3 - a)):
            for b in range(7):
                low, high = max(0, 3 - b), min(SIDE, SIDE + 3 - b)
                product = padded_ref[i + a, b + low : b + high] * dspatial_ref[i, low:high]
                totals[b] = totals[b] + jnp.sum(product, axis=0)
        for b in range(7):
            dw_ref[a, b] += totals[b]

    @pl.when(step == pl.num_programs(0) - 1)
    def _():
        pack_ref[...] = jnp.zeros_like(pack_ref)
        for n in range(3):
            lanes = slice(128 * n, 128 * n + 128)
            pack_ref[192 * n : 192 * n + 192, :] = ds_acc[:, lanes]
            pack_ref[576 + 96 * n : 672 + 96 * n, :] = up_acc[:, lanes]
            pack_ref[864 + 96 * n : 960 + 96 * n, :] = proj_acc[:, lanes]
        pack_ref[1152:1201, 0:channels] = jnp.sum(dw_ref[...], axis=2).reshape(49, channels)
        mine = pl.multiple_of(chan_ref[0] * HALF_ROWS, 8)
        other = pl.multiple_of((1 - chan_ref[0]) * HALF_ROWS, 8)
        keep_ref[...] = pack_ref[pl.ds(mine, HALF_ROWS), :]
        send_ref[...] = pack_ref[pl.ds(other, HALF_ROWS), :].astype(BF16)


def unpack_kernel(chan_ref, own_ref, peer_ref, dw_ref, up_ref, proj_ref, ds_ref, pack_ref):
    channels = dw_ref.shape[1]
    mine = pl.multiple_of(chan_ref[0] * HALF_ROWS, 8)
    other = pl.multiple_of((1 - chan_ref[0]) * HALF_ROWS, 8)
    pack_ref[pl.ds(mine, HALF_ROWS), :] = own_ref[...].astype(F32)
    pack_ref[pl.ds(other, HALF_ROWS), :] = peer_ref[...].astype(F32)
    for n in range(3):
        lanes = slice(128 * n, 128 * n + 128)
        ds_ref[:, lanes] = pack_ref[192 * n : 192 * n + 192, :]
        up_ref[:, lanes] = pack_ref[576 + 96 * n : 672 + 96 * n, :]
        proj_ref[:, lanes] = pack_ref[864 + 96 * n : 960 + 96 * n, :]
    dw_ref[...] = pack_ref[1152:1201, 0:channels]


def spread_kernel(feat_ref, w_ref, key_ref, y_ref, below_ref, *, last):
    width = w_ref.shape[1]
    feats = unfold(feat_ref[...].astype(F32)).reshape(16, 8, width)
    outs = {}
    for a in range(3):
        for b in range(3):
            places = [(u, v) for u in reach(a) for v in reach(b)]
            left = jnp.concatenate(
                [feats[(2 * u + a - 1) * 4 + 2 * v + b - 1] for u, v in places], axis=0
            ).astype(BF16)
            out = nn(left, w_ref[3 * a + b])
            for n, (u, v) in enumerate(places):
                piece = out[8 * n : 8 * n + 8]
                at = 3 * u + v
                outs[at] = outs[at] + piece if at in outs else piece
    total = jnp.concatenate([outs[at] for at in range(9)], axis=0)
    y_ref[...] = total
    pick = (key_ref[...] == float(last)).astype(F32).astype(BF16)
    high = total.astype(BF16)
    rest = (total - high.astype(F32)).astype(BF16)

    @pl.when(pl.program_id(0) == 0)
    def _():
        below_ref[...] = jnp.zeros_like(below_ref)

    below_ref[...] += tn(high, pick) + tn(rest, pick)


def map_kernel(y_ref, key_ref, above_ref, out_ref):
    out_rows, width, _ = out_ref.shape
    turned = y_ref[...].T
    high = turned.astype(BF16)
    rest = (turned - high.astype(F32)).astype(BF16)
    key = key_ref[...]

    def row_of(o):
        pick = (key == o).astype(F32).astype(BF16)
        return nn(high, pick) + nn(rest, pick)

    out_ref[0] = (row_of(0.0) + above_ref[...]).astype(BF16)

    def step(o, carry):
        out_ref[o] = row_of(o.astype(F32)).astype(BF16)
        return carry

    lax.fori_loop(1, out_rows, step, 0)


def weight_kernel(
    place_ref, near_ref, far_ref, keep_ref, send_ref, feat_ref, cot_ref, send_acc, *, scale
):
    near = near_ref.shape[0]
    members = feat_ref.shape[1] // 8
    width, e_half = keep_ref.shape[1:]
    step = pl.program_id(0)

    @pl.when(step == 0)
    def _():
        keep_ref[...] = jnp.zeros_like(keep_ref)
        send_acc[...] = jnp.zeros_like(send_acc)

    def take(member, block):
        block = block.astype(F32)
        feat_ref[:, 8 * member : 8 * member + 8] = unfold(block[:FEAT_ROWS]).reshape(16, 8, width)
        own = block[FEAT_ROWS : FEAT_ROWS + COT_ROWS].reshape(9, 8, 128)
        peer = block[FEAT_ROWS + COT_ROWS :].reshape(9, 8, 128)
        cot_ref[:, 8 * member : 8 * member + 8, 0:128] = own
        cot_ref[:, 8 * member : 8 * member + 8, 128:256] = peer

    for member in range(members):
        at = place_ref[0] ^ member

        @pl.when(at < near)
        def _():
            take(member, near_ref[jnp.minimum(at, near - 1)])

        if members > near:

            @pl.when(at >= near)
            def _():
                take(member, far_ref[jnp.maximum(at - near, 0)])

    for a in range(3):
        for b in range(3):
            places = [(u, v) for u in reach(a) for v in reach(b)]
            left = jnp.concatenate(
                [feat_ref[(2 * u + a - 1) * 4 + 2 * v + b - 1] for u, v in places], axis=0
            ).astype(BF16)
            right = jnp.concatenate([cot_ref[3 * u + v] for u, v in places], axis=0).astype(BF16)
            total = tn(left, right) * scale
            keep_ref[3 * a + b] += total[:, :e_half]
            send_acc[3 * a + b] += total[:, 128 : 128 + e_half]

    @pl.when(step == pl.num_programs(0) - 1)
    def _():
        send_ref[...] = send_acc[...].astype(BF16)


def whole(shape):
    return pl.BlockSpec(shape, lambda g: (0,) * len(shape))


def on_device(
    tile_pixels, tile_cell, agg_cot, dw_weight, norm_gain, up_weight, proj_weight,
    layer_scale, ds_gain, ds_weight, agg_weight,
):
    channels = dw_weight.shape[1]
    hid = up_weight.shape[1]
    width = ds_weight.shape[1]
    bands = lax.axis_size("slide")
    sources = bands * lax.axis_size("chan")
    chunks = sources // 8
    pixch = tile_pixels.shape[2]
    out_rows = agg_cot.shape[1]
    e_half = agg_weight.shape[2]
    cols = agg_cot.shape[3]
    blocks = CAP * chunks
    total_rows = out_rows * bands * lax.axis_size("rep") * cols
    loss_scale = 1.0 / math.sqrt(total_rows)
    chan = lax.axis_index("chan").astype(jnp.int32)[None]
    gain = norm_gain[None]
    scale = layer_scale[None]
    low_gain = ds_gain[None]
    proj_turned = proj_weight.T
    ds_turned = ds_weight.T

    packed, top_cot = pl.pallas_call(
        pack_kernel,
        grid=(1,),
        out_shape=(
            jax.ShapeDtypeStruct((sources, WIRE_ROWS, 128), BF16),
            jax.ShapeDtypeStruct((e_half, cols), BF16),
        ),
        in_specs=[
            SMEM,
            pl.BlockSpec((None,) + tile_pixels.shape[1:], lambda i: (0, 0, 0)),
            pl.BlockSpec((None, None, e_half, cols), lambda i: (0, 0, 0, 0)),
        ],
        out_specs=(whole((sources, WIRE_ROWS, 128)), whole((e_half, cols))),
        scratch_shapes=[
            pltpu.VMEM((tile_pixels.shape[1], WIRE_ROWS, 128), F32),
            pltpu.VMEM((sources, 8, 128), F32),
        ],
        cost_estimate=takes(1.5),
        name="pack",
    )(tile_cell, tile_pixels, agg_cot)
    below_cot = shifted(top_cot, "slide", -1)
    packed, own_weight = lax.optimization_barrier((packed, agg_weight))
    peer_weight = swapped(own_weight, "chan", 1)
    got = lax.all_to_all(packed, ("slide", "chan"), split_axis=0, concat_axis=0, tiled=True)

    key, cots_own, cots_send = pl.pallas_call(
        patch_kernel,
        out_shape=(
            jax.ShapeDtypeStruct((blocks * COT_ROWS, cols), F32),
            jax.ShapeDtypeStruct((chunks * COT_ROWS, 128), BF16),
            jax.ShapeDtypeStruct((chunks * COT_ROWS, 128), BF16),
        ),
        in_specs=[
            SMEM,
            pl.BlockSpec((sources, 8, 128), lambda i: (0, pixch // 1024, 0)),
            pl.BlockSpec((None, out_rows, e_half, cols), lambda i: (0, 0, 0, 0)),
            whole((e_half, cols)),
        ],
        out_specs=(
            whole((blocks * COT_ROWS, cols)),
            whole((chunks * COT_ROWS, 128)),
            whole((chunks * COT_ROWS, 128)),
        ),
        grid=(1,),
        scratch_shapes=[pltpu.VMEM((sources, 8, 128), F32)],
        compiler_params=params_of(),
        cost_estimate=takes(1.2),
        name="patch",
    )(chan, got, agg_cot, below_cot)
    cots_peer = swapped(cots_send, "chan", 1)
    cots_own = cots_own.reshape(chunks, COT_ROWS, 128)
    cots_peer = cots_peer.reshape(chunks, COT_ROWS, 128)

    rows = PIX * 8
    pixel_spec = pl.BlockSpec((8, WIRE_ROWS, 128), lambda g: (g, 0, 0))
    pixel_scratch = [pltpu.VMEM((8, WIRE_ROWS, 128), F32), pltpu.VMEM((8, pixch), F32)]

    def chunk(*shape):
        return pl.BlockSpec((None,) + shape, lambda g: (g,) + (0,) * len(shape))

    feats, hat1, rstd1, hat2, rstd2, hidden, slope, patches = pl.pallas_call(
        stem_kernel,
        grid=(chunks,),
        out_shape=(
            jax.ShapeDtypeStruct((chunks, FEAT_ROWS, 128), BF16),
            jax.ShapeDtypeStruct((chunks, rows, channels), F32),
            jax.ShapeDtypeStruct((chunks, rows, 1), F32),
            jax.ShapeDtypeStruct((chunks, rows, channels), F32),
            jax.ShapeDtypeStruct((chunks, rows, 1), F32),
            jax.ShapeDtypeStruct((chunks, rows, hid), BF16),
            jax.ShapeDtypeStruct((chunks, rows, hid), F32),
            jax.ShapeDtypeStruct((chunks, 128, 4 * channels), BF16),
        ),
        in_specs=[
            pixel_spec,
            whole(dw_weight.shape), whole((1, channels)), whole(up_weight.shape),
            whole(proj_turned.shape), whole((1, channels)), whole((1, channels)),
            whole(ds_turned.shape),
        ],
        out_specs=(
            chunk(FEAT_ROWS, 128), chunk(rows, channels), chunk(rows, 1), chunk(rows, channels),
            chunk(rows, 1), chunk(rows, hid), chunk(rows, hid), chunk(128, 4 * channels),
        ),
        scratch_shapes=[
            pltpu.VMEM((SIDE + 6, SIDE + 6, 8, channels), F32),
            pltpu.VMEM((SIDE, SIDE, 8, channels), F32),
            pltpu.VMEM((SIDE // 2, 2, SIDE // 2, 2, 8, channels), F32),
            pltpu.VMEM((128, 4 * channels), F32),
            *pixel_scratch,
        ],
        compiler_params=params_of(),
        cost_estimate=takes(2.7),
        name="stem",
    )(got, dw_weight, gain, up_weight, proj_turned, scale, low_gain, ds_turned)

    feats_band = jnp.concatenate([feats, swapped(feats, "chan", 1)], axis=0)
    spread, below = pl.pallas_call(
        lambda *refs: spread_kernel(*refs, last=out_rows),
        grid=(blocks,),
        out_shape=(
            jax.ShapeDtypeStruct((blocks * 72, e_half), F32),
            jax.ShapeDtypeStruct((e_half, cols), F32),
        ),
        in_specs=[
            chunk(FEAT_ROWS, 128), whole(agg_weight.shape),
            pl.BlockSpec((72, cols), lambda g: (g, 0)),
        ],
        out_specs=(pl.BlockSpec((72, e_half), lambda g: (g, 0)), whole((e_half, cols))),
        compiler_params=params_of(),
        cost_estimate=takes(1.0),
        name="spread",
    )(feats_band, agg_weight, key)
    tile_blocks = jnp.concatenate([feats, cots_own, cots_peer], axis=1)
    gather = chunks == 1
    near = far = tile_blocks
    place = jnp.zeros((1,), jnp.int32)
    spans = [("slide", 1 << n) for n in reversed(range(bands.bit_length() - 1))]
    spans += [("rep", 1 << n) for n in range(lax.axis_size("rep").bit_length() - 1)]

    def widen(n, near, place):
        axis, step = spans[n]
        bit = (lax.axis_index(axis).astype(jnp.int32) // step) % 2
        return swapped(near, axis, step), place + bit * (1 << n)

    if gather:
        far, place = widen(0, near, place)
        near = jnp.concatenate([near, far], axis=0)

    keep, send = pl.pallas_call(
        lambda *refs: back_kernel(*refs, scale=loss_scale),
        grid=(chunks,),
        out_shape=(
            jax.ShapeDtypeStruct((HALF_ROWS, 128), F32),
            jax.ShapeDtypeStruct((HALF_ROWS, 128), BF16),
        ),
        in_specs=[
            SMEM, chunk(COT_ROWS, 128), chunk(COT_ROWS, 128),
            whole(agg_weight.shape), whole(agg_weight.shape), pixel_spec,
            chunk(rows, channels), chunk(rows, 1), chunk(rows, channels), chunk(rows, 1),
            chunk(rows, hid), chunk(rows, hid), chunk(128, 4 * channels),
            whole((1, channels)), whole(up_weight.shape), whole(proj_turned.shape),
            whole((1, channels)), whole((1, channels)), whole(ds_turned.shape),
        ],
        out_specs=(whole((HALF_ROWS, 128)), whole((HALF_ROWS, 128))),
        scratch_shapes=[
            pltpu.VMEM((SIDE + 6, SIDE + 6, 8, channels), F32),
            pltpu.VMEM((SIDE // 2, 2, SIDE // 2, 2, 8, channels), F32),
            pltpu.VMEM((SIDE, SIDE, 8, channels), F32),
            pltpu.VMEM((7, 7, 8, channels), F32),
            pltpu.VMEM(ds_turned.shape, F32),
            pltpu.VMEM(up_weight.shape, F32),
            pltpu.VMEM(proj_turned.shape, F32),
            pltpu.VMEM((2 * HALF_ROWS, 128), F32),
            *pixel_scratch,
            pltpu.VMEM((9, width, 256), BF16),
        ],
        compiler_params=params_of(),
        cost_estimate=takes(3.7),
        name="stem_back",
    )(
        chan, cots_own, cots_peer, agg_weight, peer_weight, got,
        hat1, rstd1, hat2, rstd2, hidden, slope, patches,
        gain, up_weight, proj_turned, scale, low_gain, ds_turned,
    )

    part = keep + swapped(send, "chan", 1).astype(F32)
    if gather:
        part, near, spread, below = lax.optimization_barrier((part, near, spread, below))
    above = shifted(below, "slide", 1)
    steps = []
    for axis in ("rep", "slide"):
        step = 1
        while step < lax.axis_size(axis):
            steps.append((axis, step))
            step *= 2
    for n, (axis, step) in enumerate(steps):
        wire = part.astype(BF16)
        if n == 1:
            wire, above = lax.optimization_barrier((wire, above))
        part = wire.astype(F32) + swapped(wire, axis, step).astype(F32)
    map_call = pl.pallas_call(
        map_kernel,
        out_shape=jax.ShapeDtypeStruct((out_rows, e_half, cols), BF16),
        in_specs=[VMEM, VMEM, VMEM],
        out_specs=VMEM,
        compiler_params=pltpu.CompilerParams(vmem_limit_bytes=24 << 20),
        cost_estimate=takes(3.5),
        name="agg_map",
    )
    agg_map = map_call(spread, key, above)

    for n in range(1, len(spans) if gather else 0):
        far, place = widen(n, near, place)
        if n < len(spans) - 1:
            near = jnp.concatenate([near, far], axis=0)

    if gather:
        far, agg_map = lax.optimization_barrier((far, agg_map))
    count = 2 * near.shape[0] if gather else chunks
    per = count if gather else 1
    near_count = near.shape[0] if gather else 1
    agg_keep, agg_send = pl.pallas_call(
        lambda *refs: weight_kernel(*refs, scale=loss_scale),
        grid=(count // per,),
        out_shape=(
            jax.ShapeDtypeStruct((9, width, e_half), F32),
            jax.ShapeDtypeStruct((9, width, e_half), BF16),
        ),
        in_specs=[
            SMEM,
            pl.BlockSpec((near_count, BLOCK_ROWS, 128), lambda g: (g, 0, 0)),
            pl.BlockSpec((near_count, BLOCK_ROWS, 128), lambda g: (g, 0, 0)),
        ],
        out_specs=(whole((9, width, e_half)), whole((9, width, e_half))),
        scratch_shapes=[
            pltpu.VMEM((16, per * 8, width), F32),
            pltpu.VMEM((9, per * 8, 256), F32),
            pltpu.VMEM((9, width, e_half), F32),
        ],
        compiler_params=params_of(),
        cost_estimate=takes(1.4),
        name="agg_weight_grad",
    )(place, near, far)
    agg_grad = agg_keep + swapped(agg_send, "chan", 1).astype(F32)
    if not gather:
        agg_grad = lax.psum(agg_grad, ("slide", "rep"))

    part = part.astype(BF16)
    peer_part = swapped(part, "chan", 1)
    part, agg_grad = lax.optimization_barrier((part, agg_grad))
    dw_grad, up_grad, proj_grad, ds_grad = pl.pallas_call(
        unpack_kernel,
        out_shape=(
            jax.ShapeDtypeStruct(dw_weight.shape, F32),
            jax.ShapeDtypeStruct(up_weight.shape, F32),
            jax.ShapeDtypeStruct(proj_turned.shape, F32),
            jax.ShapeDtypeStruct(ds_turned.shape, F32),
        ),
        in_specs=[SMEM, VMEM, VMEM],
        out_specs=(VMEM, VMEM, VMEM, VMEM),
        scratch_shapes=[pltpu.VMEM((2 * HALF_ROWS, 128), F32)],
        compiler_params=pltpu.CompilerParams(vmem_limit_bytes=24 << 20),
        cost_estimate=takes(1.5),
        name="unpack",
    )(chan, part, peer_part)
    proj_grad = proj_grad.T
    ds_grad = ds_grad.T
    return (agg_map[None], agg_grad, dw_grad, up_grad, proj_grad, ds_grad)


def solution(mesh):
    in_specs = (
        P(("groups", "rep"), ("slide", "chan"), None),
        P(("groups", "rep"), ("slide", "chan")),
        P(("groups", "rep"), "slide", "chan", None),
        P(), P(), P(), P(), P(), P(), P(),
        P(None, None, "chan"),
    )
    out_specs = (
        P(("groups", "rep"), "slide", "chan", None),
        P("groups", None, "chan"),
        P("groups", None),
        P("groups", None),
        P("groups", None),
        P("groups", None),
    )
    return jax.shard_map(
        on_device, mesh=mesh, in_specs=in_specs, out_specs=out_specs, check_vma=False
    )
```

```python
import math

import jax
import jax.numpy as jnp
from jax import lax
from jax.experimental import pallas as pl
from jax.experimental.pallas import tpu as pltpu
from jax.sharding import PartitionSpec as P

SIDE = 8
CAP = 2
GW = 64
BAND_CELLS = 512
PIX = SIDE * SIDE
HALF_ROWS = 608
FEAT_ROWS = 192
COT_ROWS = 72
WIRE_ROWS = 56
BLOCK_ROWS = FEAT_ROWS + 2 * COT_ROWS
F32 = jnp.float32
BF16 = jnp.bfloat16
VMEM = pl.BlockSpec(memory_space=pltpu.VMEM)
SMEM = pl.BlockSpec(memory_space=pltpu.SMEM)


def params_of(steps=1):
    return pltpu.CompilerParams(
        dimension_semantics=("arbitrary",) * steps, vmem_limit_bytes=24 << 20
    )


def takes(microseconds):
    return pl.CostEstimate(
        flops=0, transcendentals=0, bytes_accessed=int(microseconds * 3.69e6)
    )


def nn(left, right):
    return lax.dot_general(left, right, (((1,), (0,)), ((), ())), preferred_element_type=F32)


def nt(left, right):
    return lax.dot_general(left, right, (((1,), (1,)), ((), ())), preferred_element_type=F32)


def tn(left, right):
    return lax.dot_general(left, right, (((0,), (0,)), ((), ())), preferred_element_type=F32)


def shifted(value, axis, steps):
    count = lax.axis_size(axis)
    first, last = (max(0, -steps), min(count, count - steps))
    return lax.ppermute(value, axis, [(source, source + steps) for source in range(first, last)])


def swapped(value, axis, step):
    count = lax.axis_size(axis)
    return lax.ppermute(value, axis, [(place, place ^ step) for place in range(count)])


def reach(tap):
    return (1, 2) if tap == 0 else (0, 1)


def pack_kernel(slide_ref, chan_ref, cells_ref, pixels_ref, row_ref, *refs):
    out_refs, below_ref, packed_ref, wide_ref, note_ref = refs[:-4], *refs[-4:]
    slots, pixch = pixels_ref.shape
    rows = packed_ref.shape[0]
    slide, chan = slide_ref[0], chan_ref[0]
    cells = [cells_ref[0, t] for t in range(slots)]
    live = [cell >= 0 for cell in cells]
    bands = [cell // BAND_CELLS for cell in cells]
    below_ref[...] = row_ref[...].astype(BF16)
    pixels = pixels_ref[...].astype(F32)
    for n in range(pixch // 128):
        wide_ref[:, n, :] = pixels[:, 128 * n : 128 * n + 128]
    wide_ref[:, pixch // 128 :, :] = jnp.zeros_like(wide_ref[:, pixch // 128 :, :])
    packed_ref[...] = jnp.zeros_like(packed_ref)
    lane = lax.broadcasted_iota(jnp.int32, (rows, 128), 1)
    base = ((lax.broadcasted_iota(jnp.int32, (rows, 128), 0) // CAP) ^ slide) * CAP
    notes = jnp.zeros((rows, 128), F32)
    for t in range(slots):
        order = jnp.int32(0)
        for s in range(t):
            order = order + ((bands[s] == bands[t]) & live[s]).astype(jnp.int32)
        band = jnp.maximum(bands[t], 0)
        place = (band ^ slide) * CAP + (order ^ chan)
        known = jnp.where(live[t], bands[t] * CAP + order, -1)

        @pl.when(live[t])
        def _():
            packed_ref[place] = wide_ref[t].astype(BF16)

        within = cells[t] % BAND_CELLS
        own_row = (within // GW).astype(F32)
        own_col = (within % GW).astype(F32)
        for rank in range(CAP):
            hit = base + rank == known
            for at, value in enumerate((own_row, own_col, jnp.float32(1.0))):
                notes = jnp.where(hit & (lane == 3 * rank + at), value, notes)
    note_ref[...] = jnp.zeros_like(note_ref)
    note_ref[:, 0, :] = notes
    packed_ref[:, pixch // 128 :, :] = note_ref[...].astype(BF16)
    count = rows // len(out_refs)
    for n, out_ref in enumerate(out_refs):
        out_ref[...] = packed_ref[count * n : count * n + count]


def stack_kernel(*refs):
    for n, part_ref in enumerate(refs[:-1]):
        refs[-1][n] = part_ref[0]


def gathered(target_ref, refs, other=False):
    if len(refs) == 1:
        target_ref[...] = refs[0][...].astype(F32)
        return
    half = len(refs) - 1
    first, second = (half, 0) if other else (0, half)
    for n in range(half):
        target_ref[first + n] = refs[n][0].astype(F32)
    target_ref[second : second + half] = refs[half][...].astype(F32)


def patch_kernel(chan_ref, cot_ref, bottom_ref, *refs):
    meta_refs, (key_ref, own_ref, send_ref, meta_f32, other_f32) = refs[:-5], refs[-5:]
    sources = meta_f32.shape[0]
    chunks = sources // 8
    out_rows, e_half, _ = cot_ref.shape
    gathered(meta_f32, meta_refs)
    gathered(other_f32, meta_refs, other=True)
    metas = {True: meta_f32[:, 0, :], False: other_f32[:, 0, :]}
    first = chan_ref[0] == 0
    lane = lax.broadcasted_iota(jnp.int32, (8, 128), 1).astype(F32)
    blocks = []
    for mine in (True, False):
        for chunk in range(chunks):
            part = metas[mine][chunk * 8 : chunk * 8 + 8]
            low = [jnp.broadcast_to(part[:, n : n + 1], (8, 128)) for n in range(3)]
            high = [jnp.broadcast_to(part[:, n : n + 1], (8, 128)) for n in range(3, 6)]
            row, col, valid = (
                jnp.where(first == mine, one, two) for one, two in zip(low, high)
            )
            for u in range(3):
                for v in range(3):
                    hit = (lane == 2.0 * col + v) & (valid > 0.5)
                    blocks.append(jnp.where(hit, 2.0 * row + u, -1.0))
    key = jnp.concatenate(blocks, axis=0)
    key_ref[...] = key

    def step(o, total):
        pick = (key == o.astype(F32)).astype(F32).astype(BF16)
        return total + nt(pick, cot_ref[o].astype(BF16))

    total = lax.fori_loop(
        0, out_rows, step, jnp.zeros((key.shape[0], e_half), F32), unroll=4
    )
    pick = (key == float(out_rows)).astype(F32).astype(BF16)
    total = total + nt(pick, bottom_ref[...])
    half = total.shape[0] // 2
    own_ref[...] = jnp.zeros_like(own_ref)
    send_ref[...] = jnp.zeros_like(send_ref)
    own_ref[:, :e_half] = total[:half].astype(BF16)
    send_ref[:, :e_half] = total[half:].astype(BF16)


def center_of(values):
    center = values - jnp.mean(values, axis=-1, keepdims=True)
    rstd = lax.rsqrt(jnp.mean(center * center, axis=-1, keepdims=True) + 1e-06)
    return center * rstd, rstd


def fill_padded(padded_ref, got_refs, wide_ref, pixels_ref, channels):
    gathered(wide_ref, got_refs)
    for n in range(pixels_ref.shape[1] // 128):
        pixels_ref[:, 128 * n : 128 * n + 128] = wide_ref[:, n, :]
    padded_ref[...] = jnp.zeros_like(padded_ref)
    for i in range(SIDE):
        for j in range(SIDE):
            at = (i * SIDE + j) * channels
            padded_ref[i + 3, j + 3] = pixels_ref[:, at : at + channels]


def stem_kernel(
    *refs, parts
):
    got_refs = refs[:parts]
    (
    dw_ref, gain_ref, up_ref, proj_ref, scale_ref, ds_gain_ref, ds_ref,
    feat_ref, hat1_ref, rstd1_ref, hat2_ref, rstd2_ref, hidden_ref, slope_ref, patch_ref,
    padded_ref, spatial_ref, low_ref, patch_f32, wide_ref, pixels_ref,
    ) = refs[parts:]
    channels = dw_ref.shape[1]
    fill_padded(padded_ref, got_refs, wide_ref, pixels_ref, channels)

    for i in range(SIDE):
        total = jnp.zeros((SIDE, 8, channels), F32)
        for a in range(max(0, 3 - i), min(7, SIDE + 3 - i)):
            for b in range(7):
                weight = dw_ref[7 * a + b : 7 * a + b + 1, :].reshape(1, 1, channels)
                total = total + weight * padded_ref[i + a, b : b + SIDE]
        spatial_ref[i] = total
    hat1, rstd1 = center_of(spatial_ref[...].reshape(PIX * 8, channels))
    hat1_ref[...] = hat1
    rstd1_ref[...] = rstd1
    normed = (hat1 * gain_ref[...]).astype(BF16)
    before = nn(normed, up_ref[...])
    cdf = 0.5 * (1.0 + lax.erf(before * math.sqrt(0.5)))
    pdf = jnp.exp(-0.5 * before * before) * (1.0 / math.sqrt(2.0 * math.pi))
    hidden = (before * cdf).astype(BF16)
    hidden_ref[...] = hidden
    slope_ref[...] = cdf + before * pdf
    branch = nt(hidden, proj_ref[...])
    inputs = padded_ref[3 : 3 + SIDE, 3 : 3 + SIDE].reshape(PIX * 8, channels)
    hat2, rstd2 = center_of(inputs + scale_ref[...] * branch)
    hat2_ref[...] = hat2
    rstd2_ref[...] = rstd2
    low_ref[...] = (hat2 * ds_gain_ref[...]).reshape(low_ref.shape)
    half = SIDE // 2
    for di in range(2):
        for dj in range(2):
            at = (2 * di + dj) * channels
            patch_f32[:, at : at + channels] = low_ref[:, di, :, dj].reshape(-1, channels)
    patches = patch_f32[...].astype(BF16)
    patch_ref[...] = patches
    total = nt(patches, ds_ref[...])
    rows = total.shape[0]
    feat_ref[0:rows] = total[:, 0:128].astype(BF16)
    rest = jnp.concatenate([total[: rows // 2, 128:192], total[rows // 2 :, 128:192]], axis=1)
    feat_ref[rows:] = rest.astype(BF16)


def unfold(block):
    rest = block[128:]
    return jnp.concatenate(
        [block[:128], jnp.concatenate([rest[:, :64], rest[:, 64:]], axis=0)], axis=1
    )


def back_kernel(*refs, parts, scale):
    got_refs = refs[:parts]
    (
    chan_ref, own_ref, peer_ref, w_own_ref, w_peer_ref,
    hat1_ref, rstd1_ref, hat2_ref, rstd2_ref, hidden_ref, slope_ref, patch_ref,
    gain_ref, up_ref, proj_ref, scale_ref, ds_gain_ref, ds_ref,
    keep_ref, send_ref,
    padded_ref, dlow_ref, dspatial_ref, dw_ref, ds_acc, up_acc, proj_acc, pack_ref,
    wide_ref, pixels_ref, w_ref,
    ) = refs[parts:]
    channels = gain_ref.shape[1]
    half = SIDE // 2
    step = pl.program_id(0)

    @pl.when(step == 0)
    def _():
        dw_ref[...] = jnp.zeros_like(dw_ref)
        ds_acc[...] = jnp.zeros_like(ds_acc)
        up_acc[...] = jnp.zeros_like(up_acc)
        proj_acc[...] = jnp.zeros_like(proj_acc)

    e_half = w_own_ref.shape[2]
    w_ref[...] = jnp.zeros_like(w_ref)
    w_ref[:, :, 0:e_half] = w_own_ref[...]
    w_ref[:, :, 128 : 128 + e_half] = w_peer_ref[...]
    cots = jnp.concatenate([own_ref[...], peer_ref[...]], axis=1)
    grads = {}
    for a in range(3):
        for b in range(3):
            out = nt(cots, w_ref[3 * a + b])
            for u in reach(a):
                for v in reach(b):
                    at = (2 * u + a - 1) * half + 2 * v + b - 1
                    row = 8 * (3 * u + v)
                    piece = out[row : row + 8]
                    grads[at] = grads[at] + piece if at in grads else piece
    dfeat = jnp.concatenate([grads[at] for at in range(half * half)], axis=0) * scale
    dfeat = dfeat.astype(BF16)

    hat2 = hat2_ref[...]
    ds_acc[...] += tn(dfeat, patch_ref[...])
    back = nn(dfeat, ds_ref[...])
    for di in range(2):
        for dj in range(2):
            at = (2 * di + dj) * channels
            dlow_ref[:, di, :, dj] = back[:, at : at + channels].reshape(half, half, 8, channels)
    dhat2 = dlow_ref[...].reshape(PIX * 8, channels) * ds_gain_ref[...]
    mean_a = jnp.mean(dhat2, axis=-1, keepdims=True)
    mean_b = jnp.mean(dhat2 * hat2, axis=-1, keepdims=True)
    dmixed = rstd2_ref[...] * (dhat2 - mean_a - hat2 * mean_b)
    dbranch = (dmixed * scale_ref[...]).astype(BF16)
    proj_acc[...] += tn(dbranch, hidden_ref[...])
    dhidden = nn(dbranch, proj_ref[...])
    dbefore = (dhidden * slope_ref[...]).astype(BF16)
    hat1 = hat1_ref[...]
    normed = (hat1 * gain_ref[...]).astype(BF16)
    up_acc[...] += tn(normed, dbefore)
    dhat1 = nt(dbefore, up_ref[...]) * gain_ref[...]
    mean_a = jnp.mean(dhat1, axis=-1, keepdims=True)
    mean_b = jnp.mean(dhat1 * hat1, axis=-1, keepdims=True)
    dspatial = rstd1_ref[...] * (dhat1 - mean_a - hat1 * mean_b)
    dspatial_ref[...] = dspatial.reshape(SIDE, SIDE, 8, channels)
    fill_padded(padded_ref, got_refs, wide_ref, pixels_ref, channels)

    for a in range(7):
        totals = [jnp.zeros((8, channels), F32) for _ in range(7)]
        for i in range(max(0, 3 - a), min(SIDE, SIDE + 3 - a)):
            for b in range(7):
                low, high = max(0, 3 - b), min(SIDE, SIDE + 3 - b)
                product = padded_ref[i + a, b + low : b + high] * dspatial_ref[i, low:high]
                totals[b] = totals[b] + jnp.sum(product, axis=0)
        for b in range(7):
            dw_ref[a, b] += totals[b]

    @pl.when(step == pl.num_programs(0) - 1)
    def _():
        pack_ref[...] = jnp.zeros_like(pack_ref)
        for n in range(3):
            lanes = slice(128 * n, 128 * n + 128)
            pack_ref[192 * n : 192 * n + 192, :] = ds_acc[:, lanes]
            pack_ref[576 + 96 * n : 672 + 96 * n, :] = up_acc[:, lanes]
            pack_ref[864 + 96 * n : 960 + 96 * n, :] = proj_acc[:, lanes]
        pack_ref[1152:1201, 0:channels] = jnp.sum(dw_ref[...], axis=2).reshape(49, channels)
        mine = pl.multiple_of(chan_ref[0] * HALF_ROWS, 8)
        other = pl.multiple_of((1 - chan_ref[0]) * HALF_ROWS, 8)
        keep_ref[...] = pack_ref[pl.ds(mine, HALF_ROWS), :]
        send_ref[...] = pack_ref[pl.ds(other, HALF_ROWS), :].astype(BF16)


def unpack_kernel(chan_ref, own_ref, peer_ref, dw_ref, up_ref, proj_ref, ds_ref, pack_ref):
    channels = dw_ref.shape[1]
    mine = pl.multiple_of(chan_ref[0] * HALF_ROWS, 8)
    other = pl.multiple_of((1 - chan_ref[0]) * HALF_ROWS, 8)
    pack_ref[pl.ds(mine, HALF_ROWS), :] = own_ref[...].astype(F32)
    pack_ref[pl.ds(other, HALF_ROWS), :] = peer_ref[...].astype(F32)
    for n in range(3):
        lanes = slice(128 * n, 128 * n + 128)
        ds_ref[:, lanes] = pack_ref[192 * n : 192 * n + 192, :]
        up_ref[:, lanes] = pack_ref[576 + 96 * n : 672 + 96 * n, :]
        proj_ref[:, lanes] = pack_ref[864 + 96 * n : 960 + 96 * n, :]
    dw_ref[...] = pack_ref[1152:1201, 0:channels]


def spread_kernel(feat_ref, w_ref, key_ref, y_ref, below_ref, *, last):
    width = w_ref.shape[1]
    feats = unfold(feat_ref[...].astype(F32)).reshape(16, 8, width)
    outs = {}
    for a in range(3):
        for b in range(3):
            places = [(u, v) for u in reach(a) for v in reach(b)]
            left = jnp.concatenate(
                [feats[(2 * u + a - 1) * 4 + 2 * v + b - 1] for u, v in places], axis=0
            ).astype(BF16)
            out = nn(left, w_ref[3 * a + b])
            for n, (u, v) in enumerate(places):
                piece = out[8 * n : 8 * n + 8]
                at = 3 * u + v
                outs[at] = outs[at] + piece if at in outs else piece
    total = jnp.concatenate([outs[at] for at in range(9)], axis=0)
    y_ref[...] = total
    pick = (key_ref[...] == float(last)).astype(F32).astype(BF16)
    high = total.astype(BF16)
    rest = (total - high.astype(F32)).astype(BF16)

    @pl.when(pl.program_id(0) == 0)
    def _():
        below_ref[...] = jnp.zeros_like(below_ref)

    below_ref[...] += tn(high, pick) + tn(rest, pick)


def map_kernel(y_ref, key_ref, above_ref, out_ref):
    out_rows, width, _ = out_ref.shape
    turned = y_ref[...].T
    high = turned.astype(BF16)
    rest = (turned - high.astype(F32)).astype(BF16)
    key = key_ref[...]

    def row_of(o):
        pick = (key == o).astype(F32).astype(BF16)
        return nn(high, pick) + nn(rest, pick)

    out_ref[0] = (row_of(0.0) + above_ref[...]).astype(BF16)

    def step(o, carry):
        out_ref[o] = row_of(o.astype(F32)).astype(BF16)
        return carry

    lax.fori_loop(1, out_rows, step, 0)


def weight_kernel(
    place_ref, near_ref, far_ref, keep_ref, send_ref, feat_ref, cot_ref, send_acc, *, scale
):
    near = near_ref.shape[0]
    members = feat_ref.shape[1] // 8
    width, e_half = keep_ref.shape[1:]
    step = pl.program_id(0)

    @pl.when(step == 0)
    def _():
        keep_ref[...] = jnp.zeros_like(keep_ref)
        send_acc[...] = jnp.zeros_like(send_acc)

    def take(member, block):
        block = block.astype(F32)
        feat_ref[:, 8 * member : 8 * member + 8] = unfold(block[:FEAT_ROWS]).reshape(16, 8, width)
        own = block[FEAT_ROWS : FEAT_ROWS + COT_ROWS].reshape(9, 8, 128)
        peer = block[FEAT_ROWS + COT_ROWS :].reshape(9, 8, 128)
        cot_ref[:, 8 * member : 8 * member + 8, 0:128] = own
        cot_ref[:, 8 * member : 8 * member + 8, 128:256] = peer

    for member in range(members):
        at = place_ref[0] ^ member

        @pl.when(at < near)
        def _():
            take(member, near_ref[jnp.minimum(at, near - 1)])

        if members > near:

            @pl.when(at >= near)
            def _():
                take(member, far_ref[jnp.maximum(at - near, 0)])

    for a in range(3):
        for b in range(3):
            places = [(u, v) for u in reach(a) for v in reach(b)]
            left = jnp.concatenate(
                [feat_ref[(2 * u + a - 1) * 4 + 2 * v + b - 1] for u, v in places], axis=0
            ).astype(BF16)
            right = jnp.concatenate([cot_ref[3 * u + v] for u, v in places], axis=0).astype(BF16)
            total = tn(left, right) * scale
            keep_ref[3 * a + b] += total[:, :e_half]
            send_acc[3 * a + b] += total[:, 128 : 128 + e_half]

    @pl.when(step == pl.num_programs(0) - 1)
    def _():
        send_ref[...] = send_acc[...].astype(BF16)


def whole(shape):
    return pl.BlockSpec(shape, lambda g: (0,) * len(shape))


def on_device(
    tile_pixels, tile_cell, agg_cot, dw_weight, norm_gain, up_weight, proj_weight,
    layer_scale, ds_gain, ds_weight, agg_weight,
):
    channels = dw_weight.shape[1]
    hid = up_weight.shape[1]
    width = ds_weight.shape[1]
    bands = lax.axis_size("slide")
    sources = bands * lax.axis_size("chan")
    chunks = sources // 8
    pixch = tile_pixels.shape[2]
    out_rows = agg_cot.shape[1]
    e_half = agg_weight.shape[2]
    cols = agg_cot.shape[3]
    blocks = CAP * chunks
    total_rows = out_rows * bands * lax.axis_size("rep") * cols
    loss_scale = 1.0 / math.sqrt(total_rows)
    chan = lax.axis_index("chan").astype(jnp.int32)[None]
    gain = norm_gain[None]
    scale = layer_scale[None]
    low_gain = ds_gain[None]
    proj_turned = proj_weight.T
    ds_turned = ds_weight.T

    paired = 1 < bands <= 4
    pieces = bands if paired else 1
    spot = (jnp.zeros((1,), jnp.int32),) * 2
    if paired:
        spot = (lax.axis_index("slide").astype(jnp.int32)[None], chan)
    *packed, top_cot = pl.pallas_call(
        pack_kernel,
        grid=(1,),
        out_shape=(
            *[jax.ShapeDtypeStruct((sources // pieces, WIRE_ROWS, 128), BF16)] * pieces,
            jax.ShapeDtypeStruct((e_half, cols), BF16),
        ),
        in_specs=[
            SMEM,
            SMEM,
            SMEM,
            pl.BlockSpec((None,) + tile_pixels.shape[1:], lambda i: (0, 0, 0)),
            pl.BlockSpec((None, None, e_half, cols), lambda i: (0, 0, 0, 0)),
        ],
        out_specs=(*[whole((sources // pieces, WIRE_ROWS, 128))] * pieces, whole((e_half, cols))),
        scratch_shapes=[
            pltpu.VMEM((sources, WIRE_ROWS, 128), BF16),
            pltpu.VMEM((tile_pixels.shape[1], WIRE_ROWS, 128), F32),
            pltpu.VMEM((sources, 8, 128), F32),
        ],
        cost_estimate=takes(1.5),
        name="pack",
    )(*spot, tile_cell, tile_pixels, agg_cot)
    below_cot = shifted(top_cot, "slide", -1)
    packed[0], own_weight = lax.optimization_barrier((packed[0], agg_weight))
    peer_weight = swapped(own_weight, "chan", 1)
    if paired:
        got = [packed[0]] + [None] * (bands - 1)
        for step in reversed(range(1, bands)):
            got[step] = swapped(packed[step], "slide", step)
        got[1], below_cot = lax.optimization_barrier((got[1], below_cot))
        others = pl.pallas_call(
            stack_kernel,
            grid=(1,),
            out_shape=jax.ShapeDtypeStruct((bands, WIRE_ROWS, 128), BF16),
            in_specs=[pl.BlockSpec((1, WIRE_ROWS, 128), lambda i: (1, 0, 0))] * bands,
            out_specs=whole((bands, WIRE_ROWS, 128)),
            compiler_params=params_of(),
            cost_estimate=takes(0.5),
            name="stack",
        )(*got)
        got.append(swapped(others, "chan", 1))
    else:
        got = [
            lax.all_to_all(packed[0], ("slide", "chan"), split_axis=0, concat_axis=0, tiled=True)
        ]

    key, cots_own, cots_send = pl.pallas_call(
        patch_kernel,
        out_shape=(
            jax.ShapeDtypeStruct((blocks * COT_ROWS, cols), F32),
            jax.ShapeDtypeStruct((chunks * COT_ROWS, 128), BF16),
            jax.ShapeDtypeStruct((chunks * COT_ROWS, 128), BF16),
        ),
        in_specs=[
            SMEM,
            pl.BlockSpec((None, out_rows, e_half, cols), lambda i: (0, 0, 0, 0)),
            whole((e_half, cols)),
            *[
                pl.BlockSpec((part.shape[0], 8, 128), lambda i: (0, pixch // 1024, 0))
                for part in got
            ],
        ],
        out_specs=(
            whole((blocks * COT_ROWS, cols)),
            whole((chunks * COT_ROWS, 128)),
            whole((chunks * COT_ROWS, 128)),
        ),
        grid=(1,),
        scratch_shapes=[pltpu.VMEM((sources, 8, 128), F32)] * 2,
        compiler_params=params_of(),
        cost_estimate=takes(1.2),
        name="patch",
    )(chan, agg_cot, below_cot, *got)
    cots_peer = swapped(cots_send, "chan", 1)
    cots_own = cots_own.reshape(chunks, COT_ROWS, 128)
    cots_peer = cots_peer.reshape(chunks, COT_ROWS, 128)

    rows = PIX * 8
    pixel_specs = [pl.BlockSpec((8, WIRE_ROWS, 128), lambda g: (g, 0, 0))]
    if paired:
        pixel_specs = [whole(part.shape) for part in got]
    pixel_scratch = [pltpu.VMEM((8, WIRE_ROWS, 128), F32), pltpu.VMEM((8, pixch), F32)]

    def chunk(*shape):
        return pl.BlockSpec((None,) + shape, lambda g: (g,) + (0,) * len(shape))

    feats, hat1, rstd1, hat2, rstd2, hidden, slope, patches = pl.pallas_call(
        lambda *refs: stem_kernel(*refs, parts=len(got)),
        grid=(chunks,),
        out_shape=(
            jax.ShapeDtypeStruct((chunks, FEAT_ROWS, 128), BF16),
            jax.ShapeDtypeStruct((chunks, rows, channels), F32),
            jax.ShapeDtypeStruct((chunks, rows, 1), F32),
            jax.ShapeDtypeStruct((chunks, rows, channels), F32),
            jax.ShapeDtypeStruct((chunks, rows, 1), F32),
            jax.ShapeDtypeStruct((chunks, rows, hid), BF16),
            jax.ShapeDtypeStruct((chunks, rows, hid), F32),
            jax.ShapeDtypeStruct((chunks, 128, 4 * channels), BF16),
        ),
        in_specs=[
            *pixel_specs,
            whole(dw_weight.shape), whole((1, channels)), whole(up_weight.shape),
            whole(proj_turned.shape), whole((1, channels)), whole((1, channels)),
            whole(ds_turned.shape),
        ],
        out_specs=(
            chunk(FEAT_ROWS, 128), chunk(rows, channels), chunk(rows, 1), chunk(rows, channels),
            chunk(rows, 1), chunk(rows, hid), chunk(rows, hid), chunk(128, 4 * channels),
        ),
        scratch_shapes=[
            pltpu.VMEM((SIDE + 6, SIDE + 6, 8, channels), F32),
            pltpu.VMEM((SIDE, SIDE, 8, channels), F32),
            pltpu.VMEM((SIDE // 2, 2, SIDE // 2, 2, 8, channels), F32),
            pltpu.VMEM((128, 4 * channels), F32),
            *pixel_scratch,
        ],
        compiler_params=params_of(),
        cost_estimate=takes(2.7),
        name="stem",
    )(*got, dw_weight, gain, up_weight, proj_turned, scale, low_gain, ds_turned)

    feats_band = jnp.concatenate([feats, swapped(feats, "chan", 1)], axis=0)
    spread, below = pl.pallas_call(
        lambda *refs: spread_kernel(*refs, last=out_rows),
        grid=(blocks,),
        out_shape=(
            jax.ShapeDtypeStruct((blocks * 72, e_half), F32),
            jax.ShapeDtypeStruct((e_half, cols), F32),
        ),
        in_specs=[
            chunk(FEAT_ROWS, 128), whole(agg_weight.shape),
            pl.BlockSpec((72, cols), lambda g: (g, 0)),
        ],
        out_specs=(pl.BlockSpec((72, e_half), lambda g: (g, 0)), whole((e_half, cols))),
        compiler_params=params_of(),
        cost_estimate=takes(1.0),
        name="spread",
    )(feats_band, agg_weight, key)
    tile_blocks = jnp.concatenate([feats, cots_own, cots_peer], axis=1)
    gather = chunks == 1
    near = far = tile_blocks
    place = jnp.zeros((1,), jnp.int32)
    spans = [("slide", 1 << n) for n in reversed(range(bands.bit_length() - 1))]
    spans += [("rep", 1 << n) for n in range(lax.axis_size("rep").bit_length() - 1)]

    def widen(n, near, place):
        axis, step = spans[n]
        bit = (lax.axis_index(axis).astype(jnp.int32) // step) % 2
        return swapped(near, axis, step), place + bit * (1 << n)

    if gather:
        far, place = widen(0, near, place)
        near = jnp.concatenate([near, far], axis=0)

    keep, send = pl.pallas_call(
        lambda *refs: back_kernel(*refs, parts=len(got), scale=loss_scale),
        grid=(chunks,),
        out_shape=(
            jax.ShapeDtypeStruct((HALF_ROWS, 128), F32),
            jax.ShapeDtypeStruct((HALF_ROWS, 128), BF16),
        ),
        in_specs=[
            *pixel_specs,
            SMEM, chunk(COT_ROWS, 128), chunk(COT_ROWS, 128),
            whole(agg_weight.shape), whole(agg_weight.shape),
            chunk(rows, channels), chunk(rows, 1), chunk(rows, channels), chunk(rows, 1),
            chunk(rows, hid), chunk(rows, hid), chunk(128, 4 * channels),
            whole((1, channels)), whole(up_weight.shape), whole(proj_turned.shape),
            whole((1, channels)), whole((1, channels)), whole(ds_turned.shape),
        ],
        out_specs=(whole((HALF_ROWS, 128)), whole((HALF_ROWS, 128))),
        scratch_shapes=[
            pltpu.VMEM((SIDE + 6, SIDE + 6, 8, channels), F32),
            pltpu.VMEM((SIDE // 2, 2, SIDE // 2, 2, 8, channels), F32),
            pltpu.VMEM((SIDE, SIDE, 8, channels), F32),
            pltpu.VMEM((7, 7, 8, channels), F32),
            pltpu.VMEM(ds_turned.shape, F32),
            pltpu.VMEM(up_weight.shape, F32),
            pltpu.VMEM(proj_turned.shape, F32),
            pltpu.VMEM((2 * HALF_ROWS, 128), F32),
            *pixel_scratch,
            pltpu.VMEM((9, width, 256), BF16),
        ],
        compiler_params=params_of(),
        cost_estimate=takes(3.7),
        name="stem_back",
    )(
        *got, chan, cots_own, cots_peer, agg_weight, peer_weight,
        hat1, rstd1, hat2, rstd2, hidden, slope, patches,
        gain, up_weight, proj_turned, scale, low_gain, ds_turned,
    )

    part = keep + swapped(send, "chan", 1).astype(F32)
    if gather:
        part, near, spread, below = lax.optimization_barrier((part, near, spread, below))
    above = shifted(below, "slide", 1)
    steps = []
    for axis in ("rep", "slide"):
        step = 1
        while step < lax.axis_size(axis):
            steps.append((axis, step))
            step *= 2
    for n, (axis, step) in enumerate(steps):
        wire = part.astype(BF16)
        if n == 1:
            wire, above = lax.optimization_barrier((wire, above))
        part = wire.astype(F32) + swapped(wire, axis, step).astype(F32)
    map_call = pl.pallas_call(
        map_kernel,
        out_shape=jax.ShapeDtypeStruct((out_rows, e_half, cols), BF16),
        in_specs=[VMEM, VMEM, VMEM],
        out_specs=VMEM,
        compiler_params=pltpu.CompilerParams(vmem_limit_bytes=24 << 20),
        cost_estimate=takes(3.5),
        name="agg_map",
    )
    agg_map = map_call(spread, key, above)

    for n in range(1, len(spans) if gather else 0):
        far, place = widen(n, near, place)
        if n < len(spans) - 1:
            near = jnp.concatenate([near, far], axis=0)

    if gather:
        far, agg_map = lax.optimization_barrier((far, agg_map))
    count = 2 * near.shape[0] if gather else chunks
    per = count if gather else 1
    near_count = near.shape[0] if gather else 1
    agg_keep, agg_send = pl.pallas_call(
        lambda *refs: weight_kernel(*refs, scale=loss_scale),
        grid=(count // per,),
        out_shape=(
            jax.ShapeDtypeStruct((9, width, e_half), F32),
            jax.ShapeDtypeStruct((9, width, e_half), BF16),
        ),
        in_specs=[
            SMEM,
            pl.BlockSpec((near_count, BLOCK_ROWS, 128), lambda g: (g, 0, 0)),
            pl.BlockSpec((near_count, BLOCK_ROWS, 128), lambda g: (g, 0, 0)),
        ],
        out_specs=(whole((9, width, e_half)), whole((9, width, e_half))),
        scratch_shapes=[
            pltpu.VMEM((16, per * 8, width), F32),
            pltpu.VMEM((9, per * 8, 256), F32),
            pltpu.VMEM((9, width, e_half), F32),
        ],
        compiler_params=params_of(),
        cost_estimate=takes(1.4),
        name="agg_weight_grad",
    )(place, near, far)
    agg_grad = agg_keep + swapped(agg_send, "chan", 1).astype(F32)
    if not gather:
        agg_grad = lax.psum(agg_grad, ("slide", "rep"))

    part = part.astype(BF16)
    peer_part = swapped(part, "chan", 1)
    part, agg_grad = lax.optimization_barrier((part, agg_grad))
    dw_grad, up_grad, proj_grad, ds_grad = pl.pallas_call(
        unpack_kernel,
        out_shape=(
            jax.ShapeDtypeStruct(dw_weight.shape, F32),
            jax.ShapeDtypeStruct(up_weight.shape, F32),
            jax.ShapeDtypeStruct(proj_turned.shape, F32),
            jax.ShapeDtypeStruct(ds_turned.shape, F32),
        ),
        in_specs=[SMEM, VMEM, VMEM],
        out_specs=(VMEM, VMEM, VMEM, VMEM),
        scratch_shapes=[pltpu.VMEM((2 * HALF_ROWS, 128), F32)],
        compiler_params=pltpu.CompilerParams(vmem_limit_bytes=24 << 20),
        cost_estimate=takes(1.5),
        name="unpack",
    )(chan, part, peer_part)
    proj_grad = proj_grad.T
    ds_grad = ds_grad.T
    return (agg_map[None], agg_grad, dw_grad, up_grad, proj_grad, ds_grad)


def solution(mesh):
    in_specs = (
        P(("groups", "rep"), ("slide", "chan"), None),
        P(("groups", "rep"), ("slide", "chan")),
        P(("groups", "rep"), "slide", "chan", None),
        P(), P(), P(), P(), P(), P(), P(),
        P(None, None, "chan"),
    )
    out_specs = (
        P(("groups", "rep"), "slide", "chan", None),
        P("groups", None, "chan"),
        P("groups", None),
        P("groups", None),
        P("groups", None),
        P("groups", None),
    )
    return jax.shard_map(
        on_device, mesh=mesh, in_specs=in_specs, out_specs=out_specs, check_vma=False
    )
```

```python
import math

import jax
import jax.numpy as jnp
from jax import lax
from jax.experimental import pallas as pl
from jax.experimental.pallas import tpu as pltpu
from jax.sharding import PartitionSpec as P

SIDE = 8
CAP = 2
PIX = SIDE * SIDE
HALF_ROWS = 608
FEAT_ROWS = 192
COT_ROWS = 72
WIRE_ROWS = 56
BLOCK_ROWS = FEAT_ROWS + 2 * COT_ROWS
F32 = jnp.float32
BF16 = jnp.bfloat16
VMEM = pl.BlockSpec(memory_space=pltpu.VMEM)
SMEM = pl.BlockSpec(memory_space=pltpu.SMEM)


def params_of(steps=1):
    return pltpu.CompilerParams(
        dimension_semantics=("arbitrary",) * steps, vmem_limit_bytes=24 << 20
    )


def takes(microseconds):
    return pl.CostEstimate(
        flops=0, transcendentals=0, bytes_accessed=int(microseconds * 3.69e6)
    )


def nn(left, right):
    return lax.dot_general(left, right, (((1,), (0,)), ((), ())), preferred_element_type=F32)


def nt(left, right):
    return lax.dot_general(left, right, (((1,), (1,)), ((), ())), preferred_element_type=F32)


def tn(left, right):
    return lax.dot_general(left, right, (((0,), (0,)), ((), ())), preferred_element_type=F32)


def shifted(value, axis, steps):
    count = lax.axis_size(axis)
    first, last = (max(0, -steps), min(count, count - steps))
    return lax.ppermute(value, axis, [(source, source + steps) for source in range(first, last)])


def swapped(value, axis, step):
    count = lax.axis_size(axis)
    return lax.ppermute(value, axis, [(place, place ^ step) for place in range(count)])


def reach(tap):
    return (1, 2) if tap == 0 else (0, 1)


def pack_kernel(cells_ref, pixels_ref, row_ref, out_ref, below_ref, wide_ref, note_ref):
    slots = pixels_ref.shape[0]
    rows = out_ref.shape[0]
    pixch = pixels_ref.shape[1]
    cells = [cells_ref[0, t] for t in range(slots)]
    live = [cell >= 0 for cell in cells]
    bands = [cell >> 9 for cell in cells]
    places = []
    for t in range(slots):
        rank = jnp.int32(0)
        for s in range(t):
            rank = rank + ((bands[s] == bands[t]) & live[s]).astype(jnp.int32)
        places.append(jnp.where(live[t], bands[t] * CAP + rank, -1))
    below_ref[...] = row_ref[...].astype(BF16)
    pixels = pixels_ref[...].astype(F32)
    for n in range(pixch // 128):
        wide_ref[:, n, :] = pixels[:, 128 * n : 128 * n + 128]
    wide_ref[:, pixch // 128 :, :] = jnp.zeros_like(wide_ref[:, pixch // 128 :, :])
    out_ref[...] = jnp.zeros_like(out_ref)
    for t in range(slots):

        @pl.when(live[t])
        def _():
            out_ref[jnp.maximum(places[t], 0)] = wide_ref[t].astype(BF16)

    lane = lax.broadcasted_iota(jnp.int32, (rows, 128), 1)
    base = (lax.broadcasted_iota(jnp.int32, (rows, 128), 0) // CAP) * CAP
    notes = jnp.zeros((rows, 128), F32)
    for t in range(slots):
        own_row = ((cells[t] >> 6) & 7).astype(F32)
        own_col = (cells[t] & 63).astype(F32)
        for rank in range(CAP):
            hit = base + rank == places[t]
            for at, value in enumerate((own_row, own_col, jnp.float32(1.0))):
                notes = jnp.where(hit & (lane == 3 * rank + at), value, notes)
    note_ref[...] = jnp.zeros_like(note_ref)
    note_ref[:, 0, :] = notes
    out_ref[:, pixch // 128 :, :] = note_ref[...].astype(BF16)


def patch_kernel(chan_ref, meta_ref, cot_ref, below_ref, key_ref, own_ref, send_ref, meta_f32):
    sources = meta_ref.shape[0]
    chunks = sources // 8
    out_rows, e_half, _ = cot_ref.shape
    meta_f32[...] = meta_ref[...].astype(F32)
    meta = meta_f32[:, 0, :]
    first = chan_ref[0] == 0
    lane = lax.broadcasted_iota(jnp.int32, (8, 128), 1).astype(F32)
    blocks = []
    for mine in (True, False):
        for chunk in range(chunks):
            part = meta[chunk * 8 : chunk * 8 + 8]
            low = [jnp.broadcast_to(part[:, n : n + 1], (8, 128)) for n in range(3)]
            high = [jnp.broadcast_to(part[:, n : n + 1], (8, 128)) for n in range(3, 6)]
            row, col, valid = (
                jnp.where(first == mine, one, two) for one, two in zip(low, high)
            )
            for u in range(3):
                for v in range(3):
                    hit = (lane == 2.0 * col + v) & (valid > 0.5)
                    blocks.append(jnp.where(hit, 2.0 * row + u, -1.0))
    key = jnp.concatenate(blocks, axis=0)
    key_ref[...] = key

    total = jnp.zeros((key.shape[0], e_half), F32)
    for first_row in range(0, out_rows, 4):
        rows = range(first_row, first_row + 4)
        picks = [(key == float(o)).astype(F32).astype(BF16) for o in rows]
        cots = [cot_ref[o].astype(BF16) for o in rows]
        total = total + nt(jnp.concatenate(picks, axis=1), jnp.concatenate(cots, axis=1))
    pick = (key == float(out_rows)).astype(F32).astype(BF16)
    total = total + nt(pick, below_ref[...])
    half = total.shape[0] // 2
    own_ref[...] = jnp.zeros_like(own_ref)
    send_ref[...] = jnp.zeros_like(send_ref)
    own_ref[:, :e_half] = total[:half].astype(BF16)
    send_ref[:, :e_half] = total[half:].astype(BF16)


def center_of(values):
    center = values - jnp.mean(values, axis=-1, keepdims=True)
    rstd = lax.rsqrt(jnp.mean(center * center, axis=-1, keepdims=True) + 1e-06)
    return center * rstd, rstd


def fill_padded(padded_ref, got_ref, wide_ref, pixels_ref, channels):
    wide_ref[...] = got_ref[...].astype(F32)
    for n in range(pixels_ref.shape[1] // 128):
        pixels_ref[:, 128 * n : 128 * n + 128] = wide_ref[:, n, :]
    padded_ref[...] = jnp.zeros_like(padded_ref)
    for i in range(SIDE):
        for j in range(SIDE):
            at = (i * SIDE + j) * channels
            padded_ref[i + 3, j + 3] = pixels_ref[:, at : at + channels]


def stem_kernel(
    got_ref, dw_ref, gain_ref, up_ref, proj_ref, scale_ref, ds_gain_ref, ds_ref,
    feat_ref, hat1_ref, rstd1_ref, hat2_ref, rstd2_ref, hidden_ref, slope_ref, patch_ref,
    padded_ref, spatial_ref, low_ref, patch_f32, wide_ref, pixels_ref,
):
    channels = dw_ref.shape[1]
    fill_padded(padded_ref, got_ref, wide_ref, pixels_ref, channels)

    for i in range(SIDE):
        total = jnp.zeros((SIDE, 8, channels), F32)
        for a in range(max(0, 3 - i), min(7, SIDE + 3 - i)):
            for b in range(7):
                weight = dw_ref[7 * a + b : 7 * a + b + 1, :].reshape(1, 1, channels)
                total = total + weight * padded_ref[i + a, b : b + SIDE]
        spatial_ref[i] = total
    hat1, rstd1 = center_of(spatial_ref[...].reshape(PIX * 8, channels))
    hat1_ref[...] = hat1
    rstd1_ref[...] = rstd1
    normed = (hat1 * gain_ref[...]).astype(BF16)
    before = nn(normed, up_ref[...])
    cdf = 0.5 * (1.0 + lax.erf(before * math.sqrt(0.5)))
    pdf = jnp.exp(-0.5 * before * before) * (1.0 / math.sqrt(2.0 * math.pi))
    hidden = (before * cdf).astype(BF16)
    hidden_ref[...] = hidden
    slope_ref[...] = cdf + before * pdf
    branch = nt(hidden, proj_ref[...])
    inputs = padded_ref[3 : 3 + SIDE, 3 : 3 + SIDE].reshape(PIX * 8, channels)
    hat2, rstd2 = center_of(inputs + scale_ref[...] * branch)
    hat2_ref[...] = hat2
    rstd2_ref[...] = rstd2
    low_ref[...] = (hat2 * ds_gain_ref[...]).reshape(low_ref.shape)
    half = SIDE // 2
    for di in range(2):
        for dj in range(2):
            at = (2 * di + dj) * channels
            patch_f32[:, at : at + channels] = low_ref[:, di, :, dj].reshape(-1, channels)
    patches = patch_f32[...].astype(BF16)
    patch_ref[...] = patches
    total = nt(patches, ds_ref[...])
    rows = total.shape[0]
    feat_ref[0:rows] = total[:, 0:128].astype(BF16)
    rest = jnp.concatenate([total[: rows // 2, 128:192], total[rows // 2 :, 128:192]], axis=1)
    feat_ref[rows:] = rest.astype(BF16)


def unfold(block):
    rest = block[128:]
    return jnp.concatenate(
        [block[:128], jnp.concatenate([rest[:, :64], rest[:, 64:]], axis=0)], axis=1
    )


def back_kernel(
    chan_ref, own_ref, peer_ref, w_own_ref, w_peer_ref, got_ref,
    hat1_ref, rstd1_ref, hat2_ref, rstd2_ref, hidden_ref, slope_ref, patch_ref,
    gain_ref, up_ref, proj_ref, scale_ref, ds_gain_ref, ds_ref,
    keep_ref, send_ref,
    padded_ref, dlow_ref, dspatial_ref, dw_ref, ds_acc, up_acc, proj_acc, pack_ref,
    wide_ref, pixels_ref, w_ref,
    *, scale,
):
    channels = gain_ref.shape[1]
    half = SIDE // 2
    step = pl.program_id(0)

    @pl.when(step == 0)
    def _():
        dw_ref[...] = jnp.zeros_like(dw_ref)
        ds_acc[...] = jnp.zeros_like(ds_acc)
        up_acc[...] = jnp.zeros_like(up_acc)
        proj_acc[...] = jnp.zeros_like(proj_acc)

    e_half = w_own_ref.shape[2]
    w_ref[...] = jnp.zeros_like(w_ref)
    w_ref[:, :, 0:e_half] = w_own_ref[...]
    w_ref[:, :, 128 : 128 + e_half] = w_peer_ref[...]
    cots = jnp.concatenate([own_ref[...], peer_ref[...]], axis=1)
    grads = {}
    for a in range(3):
        for b in range(3):
            out = nt(cots, w_ref[3 * a + b])
            for u in reach(a):
                for v in reach(b):
                    at = (2 * u + a - 1) * half + 2 * v + b - 1
                    row = 8 * (3 * u + v)
                    piece = out[row : row + 8]
                    grads[at] = grads[at] + piece if at in grads else piece
    dfeat = jnp.concatenate([grads[at] for at in range(half * half)], axis=0) * scale
    dfeat = dfeat.astype(BF16)

    hat2 = hat2_ref[...]
    ds_acc[...] += tn(dfeat, patch_ref[...])
    back = nn(dfeat, ds_ref[...])
    for di in range(2):
        for dj in range(2):
            at = (2 * di + dj) * channels
            dlow_ref[:, di, :, dj] = back[:, at : at + channels].reshape(half, half, 8, channels)
    dhat2 = dlow_ref[...].reshape(PIX * 8, channels) * ds_gain_ref[...]
    mean_a = jnp.mean(dhat2, axis=-1, keepdims=True)
    mean_b = jnp.mean(dhat2 * hat2, axis=-1, keepdims=True)
    dmixed = rstd2_ref[...] * (dhat2 - mean_a - hat2 * mean_b)
    dbranch = (dmixed * scale_ref[...]).astype(BF16)
    proj_acc[...] += tn(dbranch, hidden_ref[...])
    dhidden = nn(dbranch, proj_ref[...])
    dbefore = (dhidden * slope_ref[...]).astype(BF16)
    hat1 = hat1_ref[...]
    normed = (hat1 * gain_ref[...]).astype(BF16)
    up_acc[...] += tn(normed, dbefore)
    dhat1 = nt(dbefore, up_ref[...]) * gain_ref[...]
    mean_a = jnp.mean(dhat1, axis=-1, keepdims=True)
    mean_b = jnp.mean(dhat1 * hat1, axis=-1, keepdims=True)
    dspatial = rstd1_ref[...] * (dhat1 - mean_a - hat1 * mean_b)
    dspatial_ref[...] = dspatial.reshape(SIDE, SIDE, 8, channels)
    fill_padded(padded_ref, got_ref, wide_ref, pixels_ref, channels)

    for a in range(7):
        totals = [jnp.zeros((8, channels), F32) for _ in range(7)]
        for i in range(max(0, 3 - a), min(SIDE, SIDE + 3 - a)):
            for b in range(7):
                low, high = max(0, 3 - b), min(SIDE, SIDE + 3 - b)
                product = padded_ref[i + a, b + low : b + high] * dspatial_ref[i, low:high]
                totals[b] = totals[b] + jnp.sum(product, axis=0)
        for b in range(7):
            dw_ref[a, b] += totals[b]

    @pl.when(step == pl.num_programs(0) - 1)
    def _():
        pack_ref[...] = jnp.zeros_like(pack_ref)
        for n in range(3):
            lanes = slice(128 * n, 128 * n + 128)
            pack_ref[192 * n : 192 * n + 192, :] = ds_acc[:, lanes]
            pack_ref[576 + 96 * n : 672 + 96 * n, :] = up_acc[:, lanes]
            pack_ref[864 + 96 * n : 960 + 96 * n, :] = proj_acc[:, lanes]
        pack_ref[1152:1201, 0:channels] = jnp.sum(dw_ref[...], axis=2).reshape(49, channels)
        mine = pl.multiple_of(chan_ref[0] * HALF_ROWS, 8)
        other = pl.multiple_of((1 - chan_ref[0]) * HALF_ROWS, 8)
        keep_ref[...] = pack_ref[pl.ds(mine, HALF_ROWS), :]
        send_ref[...] = pack_ref[pl.ds(other, HALF_ROWS), :].astype(BF16)


def unpack_kernel(chan_ref, own_ref, peer_ref, dw_ref, up_ref, proj_ref, ds_ref, pack_ref):
    channels = dw_ref.shape[1]
    mine = pl.multiple_of(chan_ref[0] * HALF_ROWS, 8)
    other = pl.multiple_of((1 - chan_ref[0]) * HALF_ROWS, 8)
    pack_ref[pl.ds(mine, HALF_ROWS), :] = own_ref[...].astype(F32)
    pack_ref[pl.ds(other, HALF_ROWS), :] = peer_ref[...].astype(F32)
    for n in range(3):
        lanes = slice(128 * n, 128 * n + 128)
        ds_ref[:, lanes] = pack_ref[192 * n : 192 * n + 192, :]
        up_ref[:, lanes] = pack_ref[576 + 96 * n : 672 + 96 * n, :]
        proj_ref[:, lanes] = pack_ref[864 + 96 * n : 960 + 96 * n, :]
    dw_ref[...] = pack_ref[1152:1201, 0:channels]


def spread_kernel(feat_ref, w_ref, key_ref, y_ref, below_ref, *, last):
    width = w_ref.shape[1]
    feats = unfold(feat_ref[...].astype(F32)).reshape(16, 8, width)
    outs = {}
    for a in range(3):
        for b in range(3):
            places = [(u, v) for u in reach(a) for v in reach(b)]
            left = jnp.concatenate(
                [feats[(2 * u + a - 1) * 4 + 2 * v + b - 1] for u, v in places], axis=0
            ).astype(BF16)
            out = nn(left, w_ref[3 * a + b])
            for n, (u, v) in enumerate(places):
                piece = out[8 * n : 8 * n + 8]
                at = 3 * u + v
                outs[at] = outs[at] + piece if at in outs else piece
    total = jnp.concatenate([outs[at] for at in range(9)], axis=0)
    y_ref[...] = total
    pick = (key_ref[...] == float(last)).astype(F32).astype(BF16)
    high = total.astype(BF16)
    rest = (total - high.astype(F32)).astype(BF16)

    @pl.when(pl.program_id(0) == 0)
    def _():
        below_ref[...] = jnp.zeros_like(below_ref)

    below_ref[...] += tn(high, pick) + tn(rest, pick)


def map_kernel(y_ref, key_ref, above_ref, out_ref):
    out_rows, width, _ = out_ref.shape
    turned = y_ref[...].T
    high = turned.astype(BF16)
    rest = (turned - high.astype(F32)).astype(BF16)
    key = key_ref[...]

    def row_of(o):
        pick = (key == o).astype(F32).astype(BF16)
        return nn(high, pick) + nn(rest, pick)

    out_ref[0] = (row_of(0.0) + above_ref[...]).astype(BF16)

    def step(o, carry):
        out_ref[o] = row_of(o.astype(F32)).astype(BF16)
        return carry

    lax.fori_loop(1, out_rows, step, 0)


def weight_kernel(
    place_ref, near_ref, far_ref, keep_ref, send_ref, feat_ref, cot_ref, send_acc, *, scale
):
    near = near_ref.shape[0]
    members = feat_ref.shape[1] // 8
    width, e_half = keep_ref.shape[1:]
    step = pl.program_id(0)

    @pl.when(step == 0)
    def _():
        keep_ref[...] = jnp.zeros_like(keep_ref)
        send_acc[...] = jnp.zeros_like(send_acc)

    def take(member, block):
        block = block.astype(F32)
        feat_ref[:, 8 * member : 8 * member + 8] = unfold(block[:FEAT_ROWS]).reshape(16, 8, width)
        own = block[FEAT_ROWS : FEAT_ROWS + COT_ROWS].reshape(9, 8, 128)
        peer = block[FEAT_ROWS + COT_ROWS :].reshape(9, 8, 128)
        cot_ref[:, 8 * member : 8 * member + 8, 0:128] = own
        cot_ref[:, 8 * member : 8 * member + 8, 128:256] = peer

    for member in range(members):
        at = place_ref[0] ^ member

        @pl.when(at < near)
        def _():
            take(member, near_ref[jnp.minimum(at, near - 1)])

        if members > near:

            @pl.when(at >= near)
            def _():
                take(member, far_ref[jnp.maximum(at - near, 0)])

    for a in range(3):
        for b in range(3):
            places = [(u, v) for u in reach(a) for v in reach(b)]
            left = jnp.concatenate(
                [feat_ref[(2 * u + a - 1) * 4 + 2 * v + b - 1] for u, v in places], axis=0
            ).astype(BF16)
            right = jnp.concatenate([cot_ref[3 * u + v] for u, v in places], axis=0).astype(BF16)
            total = tn(left, right) * scale
            keep_ref[3 * a + b] += total[:, :e_half]
            send_acc[3 * a + b] += total[:, 128 : 128 + e_half]

    @pl.when(step == pl.num_programs(0) - 1)
    def _():
        send_ref[...] = send_acc[...].astype(BF16)


def whole(shape):
    return pl.BlockSpec(shape, lambda g: (0,) * len(shape))


def on_device(
    tile_pixels, tile_cell, agg_cot, dw_weight, norm_gain, up_weight, proj_weight,
    layer_scale, ds_gain, ds_weight, agg_weight,
):
    channels = dw_weight.shape[1]
    hid = up_weight.shape[1]
    width = ds_weight.shape[1]
    bands = lax.axis_size("slide")
    sources = bands * lax.axis_size("chan")
    chunks = sources // 8
    pixch = tile_pixels.shape[2]
    out_rows = agg_cot.shape[1]
    e_half = agg_weight.shape[2]
    cols = agg_cot.shape[3]
    blocks = CAP * chunks
    total_rows = out_rows * bands * lax.axis_size("rep") * cols
    loss_scale = 1.0 / math.sqrt(total_rows)
    chan = lax.axis_index("chan").astype(jnp.int32)[None]
    gain = norm_gain[None]
    scale = layer_scale[None]
    low_gain = ds_gain[None]
    proj_turned = proj_weight.T
    ds_turned = ds_weight.T

    packed, top_cot = pl.pallas_call(
        pack_kernel,
        grid=(1,),
        out_shape=(
            jax.ShapeDtypeStruct((sources, WIRE_ROWS, 128), BF16),
            jax.ShapeDtypeStruct((e_half, cols), BF16),
        ),
        in_specs=[
            SMEM,
            pl.BlockSpec((None,) + tile_pixels.shape[1:], lambda i: (0, 0, 0)),
            pl.BlockSpec((None, None, e_half, cols), lambda i: (0, 0, 0, 0)),
        ],
        out_specs=(whole((sources, WIRE_ROWS, 128)), whole((e_half, cols))),
        scratch_shapes=[
            pltpu.VMEM((tile_pixels.shape[1], WIRE_ROWS, 128), F32),
            pltpu.VMEM((sources, 8, 128), F32),
        ],
        cost_estimate=takes(1.5),
        name="pack",
    )(tile_cell, tile_pixels, agg_cot)
    below_cot = shifted(top_cot, "slide", -1)
    packed, own_weight = lax.optimization_barrier((packed, agg_weight))
    peer_weight = swapped(own_weight, "chan", 1)
    got = lax.all_to_all(packed, ("slide", "chan"), split_axis=0, concat_axis=0, tiled=True)

    key, cots_own, cots_send = pl.pallas_call(
        patch_kernel,
        out_shape=(
            jax.ShapeDtypeStruct((blocks * COT_ROWS, cols), F32),
            jax.ShapeDtypeStruct((chunks * COT_ROWS, 128), BF16),
            jax.ShapeDtypeStruct((chunks * COT_ROWS, 128), BF16),
        ),
        in_specs=[
            SMEM,
            pl.BlockSpec((sources, 8, 128), lambda i: (0, pixch // 1024, 0)),
            pl.BlockSpec((None, out_rows, e_half, cols), lambda i: (0, 0, 0, 0)),
            whole((e_half, cols)),
        ],
        out_specs=(
            whole((blocks * COT_ROWS, cols)),
            whole((chunks * COT_ROWS, 128)),
            whole((chunks * COT_ROWS, 128)),
        ),
        grid=(1,),
        scratch_shapes=[pltpu.VMEM((sources, 8, 128), F32)],
        compiler_params=params_of(),
        cost_estimate=takes(1.2),
        name="patch",
    )(chan, got, agg_cot, below_cot)
    cots_peer = swapped(cots_send, "chan", 1)
    cots_own = cots_own.reshape(chunks, COT_ROWS, 128)
    cots_peer = cots_peer.reshape(chunks, COT_ROWS, 128)

    rows = PIX * 8
    pixel_spec = pl.BlockSpec((8, WIRE_ROWS, 128), lambda g: (g, 0, 0))
    pixel_scratch = [pltpu.VMEM((8, WIRE_ROWS, 128), F32), pltpu.VMEM((8, pixch), F32)]

    def chunk(*shape):
        return pl.BlockSpec((None,) + shape, lambda g: (g,) + (0,) * len(shape))

    feats, hat1, rstd1, hat2, rstd2, hidden, slope, patches = pl.pallas_call(
        stem_kernel,
        grid=(chunks,),
        out_shape=(
            jax.ShapeDtypeStruct((chunks, FEAT_ROWS, 128), BF16),
            jax.ShapeDtypeStruct((chunks, rows, channels), F32),
            jax.ShapeDtypeStruct((chunks, rows, 1), F32),
            jax.ShapeDtypeStruct((chunks, rows, channels), F32),
            jax.ShapeDtypeStruct((chunks, rows, 1), F32),
            jax.ShapeDtypeStruct((chunks, rows, hid), BF16),
            jax.ShapeDtypeStruct((chunks, rows, hid), F32),
            jax.ShapeDtypeStruct((chunks, 128, 4 * channels), BF16),
        ),
        in_specs=[
            pixel_spec,
            whole(dw_weight.shape), whole((1, channels)), whole(up_weight.shape),
            whole(proj_turned.shape), whole((1, channels)), whole((1, channels)),
            whole(ds_turned.shape),
        ],
        out_specs=(
            chunk(FEAT_ROWS, 128), chunk(rows, channels), chunk(rows, 1), chunk(rows, channels),
            chunk(rows, 1), chunk(rows, hid), chunk(rows, hid), chunk(128, 4 * channels),
        ),
        scratch_shapes=[
            pltpu.VMEM((SIDE + 6, SIDE + 6, 8, channels), F32),
            pltpu.VMEM((SIDE, SIDE, 8, channels), F32),
            pltpu.VMEM((SIDE // 2, 2, SIDE // 2, 2, 8, channels), F32),
            pltpu.VMEM((128, 4 * channels), F32),
            *pixel_scratch,
        ],
        compiler_params=params_of(),
        cost_estimate=takes(2.7),
        name="stem",
    )(got, dw_weight, gain, up_weight, proj_turned, scale, low_gain, ds_turned)

    feats_band = jnp.concatenate([feats, swapped(feats, "chan", 1)], axis=0)
    spread, below = pl.pallas_call(
        lambda *refs: spread_kernel(*refs, last=out_rows),
        grid=(blocks,),
        out_shape=(
            jax.ShapeDtypeStruct((blocks * 72, e_half), F32),
            jax.ShapeDtypeStruct((e_half, cols), F32),
        ),
        in_specs=[
            chunk(FEAT_ROWS, 128), whole(agg_weight.shape),
            pl.BlockSpec((72, cols), lambda g: (g, 0)),
        ],
        out_specs=(pl.BlockSpec((72, e_half), lambda g: (g, 0)), whole((e_half, cols))),
        compiler_params=params_of(),
        cost_estimate=takes(1.0),
        name="spread",
    )(feats_band, agg_weight, key)
    tile_blocks = jnp.concatenate([feats, cots_own, cots_peer], axis=1)
    gather = chunks == 1
    near = far = tile_blocks
    place = jnp.zeros((1,), jnp.int32)
    spans = [("slide", 1 << n) for n in reversed(range(bands.bit_length() - 1))]
    spans += [("rep", 1 << n) for n in range(lax.axis_size("rep").bit_length() - 1)]

    def widen(n, near, place):
        axis, step = spans[n]
        bit = (lax.axis_index(axis).astype(jnp.int32) // step) % 2
        return swapped(near, axis, step), place + bit * (1 << n)

    if gather:
        far, place = widen(0, near, place)
        near = jnp.concatenate([near, far], axis=0)

    keep, send = pl.pallas_call(
        lambda *refs: back_kernel(*refs, scale=loss_scale),
        grid=(chunks,),
        out_shape=(
            jax.ShapeDtypeStruct((HALF_ROWS, 128), F32),
            jax.ShapeDtypeStruct((HALF_ROWS, 128), BF16),
        ),
        in_specs=[
            SMEM, chunk(COT_ROWS, 128), chunk(COT_ROWS, 128),
            whole(agg_weight.shape), whole(agg_weight.shape), pixel_spec,
            chunk(rows, channels), chunk(rows, 1), chunk(rows, channels), chunk(rows, 1),
            chunk(rows, hid), chunk(rows, hid), chunk(128, 4 * channels),
            whole((1, channels)), whole(up_weight.shape), whole(proj_turned.shape),
            whole((1, channels)), whole((1, channels)), whole(ds_turned.shape),
        ],
        out_specs=(whole((HALF_ROWS, 128)), whole((HALF_ROWS, 128))),
        scratch_shapes=[
            pltpu.VMEM((SIDE + 6, SIDE + 6, 8, channels), F32),
            pltpu.VMEM((SIDE // 2, 2, SIDE // 2, 2, 8, channels), F32),
            pltpu.VMEM((SIDE, SIDE, 8, channels), F32),
            pltpu.VMEM((7, 7, 8, channels), F32),
            pltpu.VMEM(ds_turned.shape, F32),
            pltpu.VMEM(up_weight.shape, F32),
            pltpu.VMEM(proj_turned.shape, F32),
            pltpu.VMEM((2 * HALF_ROWS, 128), F32),
            *pixel_scratch,
            pltpu.VMEM((9, width, 256), BF16),
        ],
        compiler_params=params_of(),
        cost_estimate=takes(3.7),
        name="stem_back",
    )(
        chan, cots_own, cots_peer, agg_weight, peer_weight, got,
        hat1, rstd1, hat2, rstd2, hidden, slope, patches,
        gain, up_weight, proj_turned, scale, low_gain, ds_turned,
    )

    part = keep + swapped(send, "chan", 1).astype(F32)
    if gather:
        part, near, spread, below = lax.optimization_barrier((part, near, spread, below))
    above = shifted(below, "slide", 1)
    steps = []
    for axis in ("rep", "slide"):
        step = 1
        while step < lax.axis_size(axis):
            steps.append((axis, step))
            step *= 2
    for n, (axis, step) in enumerate(steps):
        wire = part.astype(BF16)
        if n == 1:
            wire, above = lax.optimization_barrier((wire, above))
        part = wire.astype(F32) + swapped(wire, axis, step).astype(F32)
    map_call = pl.pallas_call(
        map_kernel,
        out_shape=jax.ShapeDtypeStruct((out_rows, e_half, cols), BF16),
        in_specs=[VMEM, VMEM, VMEM],
        out_specs=VMEM,
        compiler_params=pltpu.CompilerParams(vmem_limit_bytes=24 << 20),
        cost_estimate=takes(3.5),
        name="agg_map",
    )
    agg_map = map_call(spread, key, above)

    for n in range(1, len(spans) if gather else 0):
        far, place = widen(n, near, place)
        if n < len(spans) - 1:
            near = jnp.concatenate([near, far], axis=0)

    if gather:
        far, agg_map = lax.optimization_barrier((far, agg_map))
    count = 2 * near.shape[0] if gather else chunks
    per = count if gather else 1
    near_count = near.shape[0] if gather else 1
    agg_keep, agg_send = pl.pallas_call(
        lambda *refs: weight_kernel(*refs, scale=loss_scale),
        grid=(count // per,),
        out_shape=(
            jax.ShapeDtypeStruct((9, width, e_half), F32),
            jax.ShapeDtypeStruct((9, width, e_half), BF16),
        ),
        in_specs=[
            SMEM,
            pl.BlockSpec((near_count, BLOCK_ROWS, 128), lambda g: (g, 0, 0)),
            pl.BlockSpec((near_count, BLOCK_ROWS, 128), lambda g: (g, 0, 0)),
        ],
        out_specs=(whole((9, width, e_half)), whole((9, width, e_half))),
        scratch_shapes=[
            pltpu.VMEM((16, per * 8, width), F32),
            pltpu.VMEM((9, per * 8, 256), F32),
            pltpu.VMEM((9, width, e_half), F32),
        ],
        compiler_params=params_of(),
        cost_estimate=takes(1.4),
        name="agg_weight_grad",
    )(place, near, far)
    agg_grad = agg_keep + swapped(agg_send, "chan", 1).astype(F32)
    if not gather:
        agg_grad = lax.psum(agg_grad, ("slide", "rep"))

    part = part.astype(BF16)
    peer_part = swapped(part, "chan", 1)
    part, agg_grad = lax.optimization_barrier((part, agg_grad))
    dw_grad, up_grad, proj_grad, ds_grad = pl.pallas_call(
        unpack_kernel,
        out_shape=(
            jax.ShapeDtypeStruct(dw_weight.shape, F32),
            jax.ShapeDtypeStruct(up_weight.shape, F32),
            jax.ShapeDtypeStruct(proj_turned.shape, F32),
            jax.ShapeDtypeStruct(ds_turned.shape, F32),
        ),
        in_specs=[SMEM, VMEM, VMEM],
        out_specs=(VMEM, VMEM, VMEM, VMEM),
        scratch_shapes=[pltpu.VMEM((2 * HALF_ROWS, 128), F32)],
        compiler_params=pltpu.CompilerParams(vmem_limit_bytes=24 << 20),
        cost_estimate=takes(1.5),
        name="unpack",
    )(chan, part, peer_part)
    proj_grad = proj_grad.T
    ds_grad = ds_grad.T
    return (agg_map[None], agg_grad, dw_grad, up_grad, proj_grad, ds_grad)


def solution(mesh):
    in_specs = (
        P(("groups", "rep"), ("slide", "chan"), None),
        P(("groups", "rep"), ("slide", "chan")),
        P(("groups", "rep"), "slide", "chan", None),
        P(), P(), P(), P(), P(), P(), P(),
        P(None, None, "chan"),
    )
    out_specs = (
        P(("groups", "rep"), "slide", "chan", None),
        P("groups", None, "chan"),
        P("groups", None),
        P("groups", None),
        P("groups", None),
        P("groups", None),
    )
    return jax.shard_map(
        on_device, mesh=mesh, in_specs=in_specs, out_specs=out_specs, check_vma=False
    )
```

```python
import math

import jax
import jax.numpy as jnp
from jax import lax
from jax.experimental import pallas as pl
from jax.experimental.pallas import tpu as pltpu
from jax.sharding import PartitionSpec as P

SIDE = 8
CAP = 2
PIX = SIDE * SIDE
HALF_ROWS = 608
FEAT_ROWS = 192
COT_ROWS = 72
WIRE_ROWS = 56
BLOCK_ROWS = FEAT_ROWS + 2 * COT_ROWS
F32 = jnp.float32
BF16 = jnp.bfloat16
VMEM = pl.BlockSpec(memory_space=pltpu.VMEM)
SMEM = pl.BlockSpec(memory_space=pltpu.SMEM)


def params_of(steps=1):
    return pltpu.CompilerParams(
        dimension_semantics=("arbitrary",) * steps, vmem_limit_bytes=24 << 20
    )


def takes(microseconds):
    return pl.CostEstimate(
        flops=0, transcendentals=0, bytes_accessed=int(microseconds * 3.69e6)
    )


def nn(left, right):
    return lax.dot_general(left, right, (((1,), (0,)), ((), ())), preferred_element_type=F32)


def nt(left, right):
    return lax.dot_general(left, right, (((1,), (1,)), ((), ())), preferred_element_type=F32)


def tn(left, right):
    return lax.dot_general(left, right, (((0,), (0,)), ((), ())), preferred_element_type=F32)


def shifted(value, axis, steps):
    count = lax.axis_size(axis)
    first, last = (max(0, -steps), min(count, count - steps))
    return lax.ppermute(value, axis, [(source, source + steps) for source in range(first, last)])


def swapped(value, axis, step):
    count = lax.axis_size(axis)
    return lax.ppermute(value, axis, [(place, place ^ step) for place in range(count)])


def reach(tap):
    return (1, 2) if tap == 0 else (0, 1)


def pack_kernel(cells_ref, pixels_ref, row_ref, out_ref, below_ref, wide_ref, note_ref):
    slots = pixels_ref.shape[0]
    rows = out_ref.shape[0]
    pixch = pixels_ref.shape[1]
    cells = [cells_ref[0, t] for t in range(slots)]
    live = [cell >= 0 for cell in cells]
    bands = [cell >> 9 for cell in cells]
    places = []
    for t in range(slots):
        rank = jnp.int32(0)
        for s in range(t):
            rank = rank + ((bands[s] == bands[t]) & live[s]).astype(jnp.int32)
        places.append(jnp.where(live[t], bands[t] * CAP + rank, -1))
    below_ref[...] = row_ref[...].astype(BF16)
    pixels = pixels_ref[...].astype(F32)
    for n in range(pixch // 128):
        wide_ref[:, n, :] = pixels[:, 128 * n : 128 * n + 128]
    wide_ref[:, pixch // 128 :, :] = jnp.zeros_like(wide_ref[:, pixch // 128 :, :])
    out_ref[...] = jnp.zeros_like(out_ref)
    for t in range(slots):

        @pl.when(live[t])
        def _():
            out_ref[jnp.maximum(places[t], 0)] = wide_ref[t].astype(BF16)

    lane = lax.broadcasted_iota(jnp.int32, (rows, 128), 1)
    base = (lax.broadcasted_iota(jnp.int32, (rows, 128), 0) // CAP) * CAP
    notes = jnp.zeros((rows, 128), F32)
    for t in range(slots):
        own_row = ((cells[t] >> 6) & 7).astype(F32)
        own_col = (cells[t] & 63).astype(F32)
        for rank in range(CAP):
            hit = base + rank == places[t]
            for at, value in enumerate((own_row, own_col, jnp.float32(1.0))):
                notes = jnp.where(hit & (lane == 3 * rank + at), value, notes)
    note_ref[...] = jnp.zeros_like(note_ref)
    note_ref[:, 0, :] = notes
    out_ref[:, pixch // 128 :, :] = note_ref[...].astype(BF16)


def patch_kernel(chan_ref, meta_ref, cot_ref, below_ref, key_ref, own_ref, send_ref, meta_f32):
    sources = meta_ref.shape[0]
    chunks = sources // 8
    out_rows, e_half, _ = cot_ref.shape
    meta_f32[...] = meta_ref[...].astype(F32)
    meta = meta_f32[:, 0, :]
    first = chan_ref[0] == 0
    lane = lax.broadcasted_iota(jnp.int32, (8, 128), 1).astype(F32)
    blocks = []
    for mine in (True, False):
        for chunk in range(chunks):
            part = meta[chunk * 8 : chunk * 8 + 8]
            low = [jnp.broadcast_to(part[:, n : n + 1], (8, 128)) for n in range(3)]
            high = [jnp.broadcast_to(part[:, n : n + 1], (8, 128)) for n in range(3, 6)]
            row, col, valid = (
                jnp.where(first == mine, one, two) for one, two in zip(low, high)
            )
            for u in range(3):
                for v in range(3):
                    hit = (lane == 2.0 * col + v) & (valid > 0.5)
                    blocks.append(jnp.where(hit, 2.0 * row + u, -1.0))
    key = jnp.concatenate(blocks, axis=0)
    key_ref[...] = key

    total = jnp.zeros((key.shape[0], e_half), F32)
    for first_row in range(0, out_rows, 4):
        rows = range(first_row, first_row + 4)
        picks = [(key == float(o)).astype(F32).astype(BF16) for o in rows]
        cots = [cot_ref[o].astype(BF16) for o in rows]
        total = total + nt(jnp.concatenate(picks, axis=1), jnp.concatenate(cots, axis=1))
    pick = (key == float(out_rows)).astype(F32).astype(BF16)
    total = total + nt(pick, below_ref[...])
    half = total.shape[0] // 2
    own_ref[...] = jnp.zeros_like(own_ref)
    send_ref[...] = jnp.zeros_like(send_ref)
    own_ref[:, :e_half] = total[:half].astype(BF16)
    send_ref[:, :e_half] = total[half:].astype(BF16)


def center_of(values):
    center = values - jnp.mean(values, axis=-1, keepdims=True)
    rstd = lax.rsqrt(jnp.mean(center * center, axis=-1, keepdims=True) + 1e-06)
    return center * rstd, rstd


def fill_padded(padded_ref, got_ref, wide_ref, pixels_ref, channels):
    wide_ref[...] = got_ref[...].astype(F32)
    for n in range(pixels_ref.shape[1] // 128):
        pixels_ref[:, 128 * n : 128 * n + 128] = wide_ref[:, n, :]
    padded_ref[...] = jnp.zeros_like(padded_ref)
    for i in range(SIDE):
        for j in range(SIDE):
            at = (i * SIDE + j) * channels
            padded_ref[i + 3, j + 3] = pixels_ref[:, at : at + channels]


def stem_kernel(
    got_ref, dw_ref, gain_ref, up_ref, proj_ref, scale_ref, ds_gain_ref, ds_ref,
    feat_ref, hat1_ref, rstd1_ref, hat2_ref, rstd2_ref, hidden_ref, slope_ref, patch_ref,
    padded_ref, spatial_ref, low_ref, patch_f32, wide_ref, pixels_ref,
):
    channels = dw_ref.shape[1]
    fill_padded(padded_ref, got_ref, wide_ref, pixels_ref, channels)

    for i in range(SIDE):
        total = jnp.zeros((SIDE, 8, channels), F32)
        for a in range(max(0, 3 - i), min(7, SIDE + 3 - i)):
            for b in range(7):
                weight = dw_ref[7 * a + b : 7 * a + b + 1, :].reshape(1, 1, channels)
                total = total + weight * padded_ref[i + a, b : b + SIDE]
        spatial_ref[i] = total
    hat1, rstd1 = center_of(spatial_ref[...].reshape(PIX * 8, channels))
    hat1_ref[...] = hat1
    rstd1_ref[...] = rstd1
    normed = (hat1 * gain_ref[...]).astype(BF16)
    before = nn(normed, up_ref[...])
    cdf = 0.5 * (1.0 + lax.erf(before * math.sqrt(0.5)))
    pdf = jnp.exp(-0.5 * before * before) * (1.0 / math.sqrt(2.0 * math.pi))
    hidden = (before * cdf).astype(BF16)
    hidden_ref[...] = hidden
    slope_ref[...] = cdf + before * pdf
    branch = nt(hidden, proj_ref[...])
    inputs = padded_ref[3 : 3 + SIDE, 3 : 3 + SIDE].reshape(PIX * 8, channels)
    hat2, rstd2 = center_of(inputs + scale_ref[...] * branch)
    hat2_ref[...] = hat2
    rstd2_ref[...] = rstd2
    low_ref[...] = (hat2 * ds_gain_ref[...]).reshape(low_ref.shape)
    half = SIDE // 2
    for di in range(2):
        for dj in range(2):
            at = (2 * di + dj) * channels
            patch_f32[:, at : at + channels] = low_ref[:, di, :, dj].reshape(-1, channels)
    patches = patch_f32[...].astype(BF16)
    patch_ref[...] = patches
    total = nt(patches, ds_ref[...])
    rows = total.shape[0]
    feat_ref[0:rows] = total[:, 0:128].astype(BF16)
    rest = jnp.concatenate([total[: rows // 2, 128:192], total[rows // 2 :, 128:192]], axis=1)
    feat_ref[rows:] = rest.astype(BF16)


def unfold(block):
    rest = block[128:]
    return jnp.concatenate(
        [block[:128], jnp.concatenate([rest[:, :64], rest[:, 64:]], axis=0)], axis=1
    )


def back_kernel(
    chan_ref, own_ref, peer_ref, w_own_ref, w_peer_ref, got_ref,
    hat1_ref, rstd1_ref, hat2_ref, rstd2_ref, hidden_ref, slope_ref, patch_ref,
    gain_ref, up_ref, proj_ref, scale_ref, ds_gain_ref, ds_ref,
    keep_ref, send_ref,
    padded_ref, dlow_ref, dspatial_ref, dw_ref, ds_acc, up_acc, proj_acc, pack_ref,
    wide_ref, pixels_ref, w_ref,
    *, scale,
):
    channels = gain_ref.shape[1]
    half = SIDE // 2
    step = pl.program_id(0)

    @pl.when(step == 0)
    def _():
        dw_ref[...] = jnp.zeros_like(dw_ref)
        ds_acc[...] = jnp.zeros_like(ds_acc)
        up_acc[...] = jnp.zeros_like(up_acc)
        proj_acc[...] = jnp.zeros_like(proj_acc)

    e_half = w_own_ref.shape[2]
    w_ref[...] = jnp.zeros_like(w_ref)
    w_ref[:, :, 0:e_half] = w_own_ref[...]
    w_ref[:, :, 128 : 128 + e_half] = w_peer_ref[...]
    cots = jnp.concatenate([own_ref[...], peer_ref[...]], axis=1)
    grads = {}
    for a in range(3):
        for b in range(3):
            out = nt(cots, w_ref[3 * a + b])
            for u in reach(a):
                for v in reach(b):
                    at = (2 * u + a - 1) * half + 2 * v + b - 1
                    row = 8 * (3 * u + v)
                    piece = out[row : row + 8]
                    grads[at] = grads[at] + piece if at in grads else piece
    dfeat = jnp.concatenate([grads[at] for at in range(half * half)], axis=0) * scale
    dfeat = dfeat.astype(BF16)

    hat2 = hat2_ref[...]
    ds_acc[...] += tn(dfeat, patch_ref[...])
    back = nn(dfeat, ds_ref[...])
    for di in range(2):
        for dj in range(2):
            at = (2 * di + dj) * channels
            dlow_ref[:, di, :, dj] = back[:, at : at + channels].reshape(half, half, 8, channels)
    dhat2 = dlow_ref[...].reshape(PIX * 8, channels) * ds_gain_ref[...]
    mean_a = jnp.mean(dhat2, axis=-1, keepdims=True)
    mean_b = jnp.mean(dhat2 * hat2, axis=-1, keepdims=True)
    dmixed = rstd2_ref[...] * (dhat2 - mean_a - hat2 * mean_b)
    dbranch = (dmixed * scale_ref[...]).astype(BF16)
    proj_acc[...] += tn(dbranch, hidden_ref[...])
    dhidden = nn(dbranch, proj_ref[...])
    dbefore = (dhidden * slope_ref[...]).astype(BF16)
    hat1 = hat1_ref[...]
    normed = (hat1 * gain_ref[...]).astype(BF16)
    up_acc[...] += tn(normed, dbefore)
    dhat1 = nt(dbefore, up_ref[...]) * gain_ref[...]
    mean_a = jnp.mean(dhat1, axis=-1, keepdims=True)
    mean_b = jnp.mean(dhat1 * hat1, axis=-1, keepdims=True)
    dspatial = rstd1_ref[...] * (dhat1 - mean_a - hat1 * mean_b)
    dspatial_ref[...] = dspatial.reshape(SIDE, SIDE, 8, channels)
    fill_padded(padded_ref, got_ref, wide_ref, pixels_ref, channels)

    for a in range(7):
        totals = [jnp.zeros((8, channels), F32) for _ in range(7)]
        for i in range(max(0, 3 - a), min(SIDE, SIDE + 3 - a)):
            for b in range(7):
                low, high = max(0, 3 - b), min(SIDE, SIDE + 3 - b)
                product = padded_ref[i + a, b + low : b + high] * dspatial_ref[i, low:high]
                totals[b] = totals[b] + jnp.sum(product, axis=0)
        for b in range(7):
            dw_ref[a, b] += totals[b]

    @pl.when(step == pl.num_programs(0) - 1)
    def _():
        pack_ref[...] = jnp.zeros_like(pack_ref)
        for n in range(3):
            lanes = slice(128 * n, 128 * n + 128)
            pack_ref[192 * n : 192 * n + 192, :] = ds_acc[:, lanes]
            pack_ref[576 + 96 * n : 672 + 96 * n, :] = up_acc[:, lanes]
            pack_ref[864 + 96 * n : 960 + 96 * n, :] = proj_acc[:, lanes]
        pack_ref[1152:1201, 0:channels] = jnp.sum(dw_ref[...], axis=2).reshape(49, channels)
        mine = pl.multiple_of(chan_ref[0] * HALF_ROWS, 8)
        other = pl.multiple_of((1 - chan_ref[0]) * HALF_ROWS, 8)
        keep_ref[...] = pack_ref[pl.ds(mine, HALF_ROWS), :]
        send_ref[...] = pack_ref[pl.ds(other, HALF_ROWS), :].astype(BF16)


def unpack_kernel(chan_ref, own_ref, peer_ref, dw_ref, up_ref, proj_ref, ds_ref, pack_ref):
    channels = dw_ref.shape[1]
    mine = pl.multiple_of(chan_ref[0] * HALF_ROWS, 8)
    other = pl.multiple_of((1 - chan_ref[0]) * HALF_ROWS, 8)
    pack_ref[pl.ds(mine, HALF_ROWS), :] = own_ref[...].astype(F32)
    pack_ref[pl.ds(other, HALF_ROWS), :] = peer_ref[...].astype(F32)
    for n in range(3):
        lanes = slice(128 * n, 128 * n + 128)
        ds_ref[:, lanes] = pack_ref[192 * n : 192 * n + 192, :]
        up_ref[:, lanes] = pack_ref[576 + 96 * n : 672 + 96 * n, :]
        proj_ref[:, lanes] = pack_ref[864 + 96 * n : 960 + 96 * n, :]
    dw_ref[...] = pack_ref[1152:1201, 0:channels]


def spread_kernel(feat_ref, w_ref, key_ref, y_ref, below_ref, *, last):
    width = w_ref.shape[1]
    feats = unfold(feat_ref[...].astype(F32)).reshape(16, 8, width)
    outs = {}
    for a in range(3):
        for b in range(3):
            places = [(u, v) for u in reach(a) for v in reach(b)]
            left = jnp.concatenate(
                [feats[(2 * u + a - 1) * 4 + 2 * v + b - 1] for u, v in places], axis=0
            ).astype(BF16)
            out = nn(left, w_ref[3 * a + b])
            for n, (u, v) in enumerate(places):
                piece = out[8 * n : 8 * n + 8]
                at = 3 * u + v
                outs[at] = outs[at] + piece if at in outs else piece
    total = jnp.concatenate([outs[at] for at in range(9)], axis=0)
    y_ref[...] = total
    pick = (key_ref[...] == float(last)).astype(F32).astype(BF16)
    high = total.astype(BF16)
    rest = (total - high.astype(F32)).astype(BF16)

    @pl.when(pl.program_id(0) == 0)
    def _():
        below_ref[...] = jnp.zeros_like(below_ref)

    below_ref[...] += tn(high, pick) + tn(rest, pick)


def map_kernel(y_ref, key_ref, above_ref, out_ref):
    out_rows, width, _ = out_ref.shape
    turned = y_ref[...].T
    high = turned.astype(BF16)
    rest = (turned - high.astype(F32)).astype(BF16)
    key = key_ref[...]

    def row_of(o):
        pick = (key == o).astype(F32).astype(BF16)
        return nn(high, pick) + nn(rest, pick)

    out_ref[0] = (row_of(0.0) + above_ref[...]).astype(BF16)

    def step(o, carry):
        out_ref[o] = row_of(o.astype(F32)).astype(BF16)
        return carry

    lax.fori_loop(1, out_rows, step, 0)


def weight_kernel(
    place_ref, near_ref, far_ref, keep_ref, send_ref, feat_ref, cot_ref, send_acc, *, scale
):
    near = near_ref.shape[0]
    members = feat_ref.shape[1] // 8
    width, e_half = keep_ref.shape[1:]
    step = pl.program_id(0)

    @pl.when(step == 0)
    def _():
        keep_ref[...] = jnp.zeros_like(keep_ref)
        send_acc[...] = jnp.zeros_like(send_acc)

    def take(member, block):
        block = block.astype(F32)
        feat_ref[:, 8 * member : 8 * member + 8] = unfold(block[:FEAT_ROWS]).reshape(16, 8, width)
        own = block[FEAT_ROWS : FEAT_ROWS + COT_ROWS].reshape(9, 8, 128)
        peer = block[FEAT_ROWS + COT_ROWS :].reshape(9, 8, 128)
        cot_ref[:, 8 * member : 8 * member + 8, 0:128] = own
        cot_ref[:, 8 * member : 8 * member + 8, 128:256] = peer

    for member in range(members):
        at = place_ref[0] ^ member

        @pl.when(at < near)
        def _():
            take(member, near_ref[jnp.minimum(at, near - 1)])

        if members > near:

            @pl.when(at >= near)
            def _():
                take(member, far_ref[jnp.maximum(at - near, 0)])

    for a in range(3):
        for b in range(3):
            places = [(u, v) for u in reach(a) for v in reach(b)]
            left = jnp.concatenate(
                [feat_ref[(2 * u + a - 1) * 4 + 2 * v + b - 1] for u, v in places], axis=0
            ).astype(BF16)
            right = jnp.concatenate([cot_ref[3 * u + v] for u, v in places], axis=0).astype(BF16)
            total = tn(left, right) * scale
            keep_ref[3 * a + b] += total[:, :e_half]
            send_acc[3 * a + b] += total[:, 128 : 128 + e_half]

    @pl.when(step == pl.num_programs(0) - 1)
    def _():
        send_ref[...] = send_acc[...].astype(BF16)


def whole(shape):
    return pl.BlockSpec(shape, lambda g: (0,) * len(shape))


def on_device(
    tile_pixels, tile_cell, agg_cot, dw_weight, norm_gain, up_weight, proj_weight,
    layer_scale, ds_gain, ds_weight, agg_weight,
):
    channels = dw_weight.shape[1]
    hid = up_weight.shape[1]
    width = ds_weight.shape[1]
    bands = lax.axis_size("slide")
    sources = bands * lax.axis_size("chan")
    chunks = sources // 8
    pixch = tile_pixels.shape[2]
    out_rows = agg_cot.shape[1]
    e_half = agg_weight.shape[2]
    cols = agg_cot.shape[3]
    blocks = CAP * chunks
    total_rows = out_rows * bands * lax.axis_size("rep") * cols
    loss_scale = 1.0 / math.sqrt(total_rows)
    chan = lax.axis_index("chan").astype(jnp.int32)[None]
    gain = norm_gain[None]
    scale = layer_scale[None]
    low_gain = ds_gain[None]
    proj_turned = proj_weight.T
    ds_turned = ds_weight.T

    packed, top_cot = pl.pallas_call(
        pack_kernel,
        grid=(1,),
        out_shape=(
            jax.ShapeDtypeStruct((sources, WIRE_ROWS, 128), BF16),
            jax.ShapeDtypeStruct((e_half, cols), BF16),
        ),
        in_specs=[
            SMEM,
            pl.BlockSpec((None,) + tile_pixels.shape[1:], lambda i: (0, 0, 0)),
            pl.BlockSpec((None, None, e_half, cols), lambda i: (0, 0, 0, 0)),
        ],
        out_specs=(whole((sources, WIRE_ROWS, 128)), whole((e_half, cols))),
        scratch_shapes=[
            pltpu.VMEM((tile_pixels.shape[1], WIRE_ROWS, 128), F32),
            pltpu.VMEM((sources, 8, 128), F32),
        ],
        cost_estimate=takes(1.5),
        name="pack",
    )(tile_cell, tile_pixels, agg_cot)
    below_cot = shifted(top_cot, "slide", -1)
    packed, own_weight = lax.optimization_barrier((packed, agg_weight))
    peer_weight = swapped(own_weight, "chan", 1)
    got = lax.all_to_all(packed, ("slide", "chan"), split_axis=0, concat_axis=0, tiled=True)

    key, cots_own, cots_send = pl.pallas_call(
        patch_kernel,
        out_shape=(
            jax.ShapeDtypeStruct((blocks * COT_ROWS, cols), F32),
            jax.ShapeDtypeStruct((chunks * COT_ROWS, 128), BF16),
            jax.ShapeDtypeStruct((chunks * COT_ROWS, 128), BF16),
        ),
        in_specs=[
            SMEM,
            pl.BlockSpec((sources, 8, 128), lambda i: (0, pixch // 1024, 0)),
            pl.BlockSpec((None, out_rows, e_half, cols), lambda i: (0, 0, 0, 0)),
            whole((e_half, cols)),
        ],
        out_specs=(
            whole((blocks * COT_ROWS, cols)),
            whole((chunks * COT_ROWS, 128)),
            whole((chunks * COT_ROWS, 128)),
        ),
        grid=(1,),
        scratch_shapes=[pltpu.VMEM((sources, 8, 128), F32)],
        compiler_params=params_of(),
        cost_estimate=takes(1.2),
        name="patch",
    )(chan, got, agg_cot, below_cot)
    cots_peer = swapped(cots_send, "chan", 1)
    cots_own = cots_own.reshape(chunks, COT_ROWS, 128)
    cots_peer = cots_peer.reshape(chunks, COT_ROWS, 128)

    rows = PIX * 8
    pixel_spec = pl.BlockSpec((8, WIRE_ROWS, 128), lambda g: (g, 0, 0))
    pixel_scratch = [pltpu.VMEM((8, WIRE_ROWS, 128), F32), pltpu.VMEM((8, pixch), F32)]

    def chunk(*shape):
        return pl.BlockSpec((None,) + shape, lambda g: (g,) + (0,) * len(shape))

    feats, hat1, rstd1, hat2, rstd2, hidden, slope, patches = pl.pallas_call(
        stem_kernel,
        grid=(chunks,),
        out_shape=(
            jax.ShapeDtypeStruct((chunks, FEAT_ROWS, 128), BF16),
            jax.ShapeDtypeStruct((chunks, rows, channels), F32),
            jax.ShapeDtypeStruct((chunks, rows, 1), F32),
            jax.ShapeDtypeStruct((chunks, rows, channels), F32),
            jax.ShapeDtypeStruct((chunks, rows, 1), F32),
            jax.ShapeDtypeStruct((chunks, rows, hid), BF16),
            jax.ShapeDtypeStruct((chunks, rows, hid), F32),
            jax.ShapeDtypeStruct((chunks, 128, 4 * channels), BF16),
        ),
        in_specs=[
            pixel_spec,
            whole(dw_weight.shape), whole((1, channels)), whole(up_weight.shape),
            whole(proj_turned.shape), whole((1, channels)), whole((1, channels)),
            whole(ds_turned.shape),
        ],
        out_specs=(
            chunk(FEAT_ROWS, 128), chunk(rows, channels), chunk(rows, 1), chunk(rows, channels),
            chunk(rows, 1), chunk(rows, hid), chunk(rows, hid), chunk(128, 4 * channels),
        ),
        scratch_shapes=[
            pltpu.VMEM((SIDE + 6, SIDE + 6, 8, channels), F32),
            pltpu.VMEM((SIDE, SIDE, 8, channels), F32),
            pltpu.VMEM((SIDE // 2, 2, SIDE // 2, 2, 8, channels), F32),
            pltpu.VMEM((128, 4 * channels), F32),
            *pixel_scratch,
        ],
        compiler_params=params_of(),
        cost_estimate=takes(2.7),
        name="stem",
    )(got, dw_weight, gain, up_weight, proj_turned, scale, low_gain, ds_turned)

    feats_band = jnp.concatenate([feats, swapped(feats, "chan", 1)], axis=0)
    spread, below = pl.pallas_call(
        lambda *refs: spread_kernel(*refs, last=out_rows),
        grid=(blocks,),
        out_shape=(
            jax.ShapeDtypeStruct((blocks * 72, e_half), F32),
            jax.ShapeDtypeStruct((e_half, cols), F32),
        ),
        in_specs=[
            chunk(FEAT_ROWS, 128), whole(agg_weight.shape),
            pl.BlockSpec((72, cols), lambda g: (g, 0)),
        ],
        out_specs=(pl.BlockSpec((72, e_half), lambda g: (g, 0)), whole((e_half, cols))),
        compiler_params=params_of(),
        cost_estimate=takes(1.0),
        name="spread",
    )(feats_band, agg_weight, key)
    tile_blocks = jnp.concatenate([feats, cots_own, cots_peer], axis=1)
    gather = chunks == 1
    near = far = tile_blocks
    place = jnp.zeros((1,), jnp.int32)
    spans = [("slide", 1 << n) for n in reversed(range(bands.bit_length() - 1))]
    spans += [("rep", 1 << n) for n in range(lax.axis_size("rep").bit_length() - 1)]

    def widen(n, near, place):
        axis, step = spans[n]
        bit = (lax.axis_index(axis).astype(jnp.int32) // step) % 2
        return swapped(near, axis, step), place + bit * (1 << n)

    if gather:
        far, place = widen(0, near, place)
        near = jnp.concatenate([near, far], axis=0)

    keep, send = pl.pallas_call(
        lambda *refs: back_kernel(*refs, scale=loss_scale),
        grid=(chunks,),
        out_shape=(
            jax.ShapeDtypeStruct((HALF_ROWS, 128), F32),
            jax.ShapeDtypeStruct((HALF_ROWS, 128), BF16),
        ),
        in_specs=[
            SMEM, chunk(COT_ROWS, 128), chunk(COT_ROWS, 128),
            whole(agg_weight.shape), whole(agg_weight.shape), pixel_spec,
            chunk(rows, channels), chunk(rows, 1), chunk(rows, channels), chunk(rows, 1),
            chunk(rows, hid), chunk(rows, hid), chunk(128, 4 * channels),
            whole((1, channels)), whole(up_weight.shape), whole(proj_turned.shape),
            whole((1, channels)), whole((1, channels)), whole(ds_turned.shape),
        ],
        out_specs=(whole((HALF_ROWS, 128)), whole((HALF_ROWS, 128))),
        scratch_shapes=[
            pltpu.VMEM((SIDE + 6, SIDE + 6, 8, channels), F32),
            pltpu.VMEM((SIDE // 2, 2, SIDE // 2, 2, 8, channels), F32),
            pltpu.VMEM((SIDE, SIDE, 8, channels), F32),
            pltpu.VMEM((7, 7, 8, channels), F32),
            pltpu.VMEM(ds_turned.shape, F32),
            pltpu.VMEM(up_weight.shape, F32),
            pltpu.VMEM(proj_turned.shape, F32),
            pltpu.VMEM((2 * HALF_ROWS, 128), F32),
            *pixel_scratch,
            pltpu.VMEM((9, width, 256), BF16),
        ],
        compiler_params=params_of(),
        cost_estimate=takes(3.7),
        name="stem_back",
    )(
        chan, cots_own, cots_peer, agg_weight, peer_weight, got,
        hat1, rstd1, hat2, rstd2, hidden, slope, patches,
        gain, up_weight, proj_turned, scale, low_gain, ds_turned,
    )

    part = keep + swapped(send, "chan", 1).astype(F32)
    if gather:
        part, near, spread, below = lax.optimization_barrier((part, near, spread, below))
    above = shifted(below, "slide", 1)
    steps = []
    for axis in ("rep", "slide"):
        step = 1
        while step < lax.axis_size(axis):
            steps.append((axis, step))
            step *= 2
    for n, (axis, step) in enumerate(steps):
        wire = part.astype(BF16)
        part = wire.astype(F32) + swapped(wire, axis, step).astype(F32)
    map_call = pl.pallas_call(
        map_kernel,
        out_shape=jax.ShapeDtypeStruct((out_rows, e_half, cols), BF16),
        in_specs=[VMEM, VMEM, VMEM],
        out_specs=VMEM,
        compiler_params=pltpu.CompilerParams(vmem_limit_bytes=24 << 20),
        cost_estimate=takes(3.5),
        name="agg_map",
    )

    for n in range(1, len(spans) if gather else 0):
        if n == len(spans) - 1:
            near, above = lax.optimization_barrier((near, above))
        far, place = widen(n, near, place)
        if n < len(spans) - 1:
            near = jnp.concatenate([near, far], axis=0)

    agg_map = map_call(spread, key, above)
    if gather:
        far, agg_map = lax.optimization_barrier((far, agg_map))
    count = 2 * near.shape[0] if gather else chunks
    per = count if gather else 1
    near_count = near.shape[0] if gather else 1
    agg_keep, agg_send = pl.pallas_call(
        lambda *refs: weight_kernel(*refs, scale=loss_scale),
        grid=(count // per,),
        out_shape=(
            jax.ShapeDtypeStruct((9, width, e_half), F32),
            jax.ShapeDtypeStruct((9, width, e_half), BF16),
        ),
        in_specs=[
            SMEM,
            pl.BlockSpec((near_count, BLOCK_ROWS, 128), lambda g: (g, 0, 0)),
            pl.BlockSpec((near_count, BLOCK_ROWS, 128), lambda g: (g, 0, 0)),
        ],
        out_specs=(whole((9, width, e_half)), whole((9, width, e_half))),
        scratch_shapes=[
            pltpu.VMEM((16, per * 8, width), F32),
            pltpu.VMEM((9, per * 8, 256), F32),
            pltpu.VMEM((9, width, e_half), F32),
        ],
        compiler_params=params_of(),
        cost_estimate=takes(1.4),
        name="agg_weight_grad",
    )(place, near, far)
    agg_grad = agg_keep + swapped(agg_send, "chan", 1).astype(F32)
    if not gather:
        agg_grad = lax.psum(agg_grad, ("slide", "rep"))

    part = part.astype(BF16)
    peer_part = swapped(part, "chan", 1)
    part, agg_grad = lax.optimization_barrier((part, agg_grad))
    dw_grad, up_grad, proj_grad, ds_grad = pl.pallas_call(
        unpack_kernel,
        out_shape=(
            jax.ShapeDtypeStruct(dw_weight.shape, F32),
            jax.ShapeDtypeStruct(up_weight.shape, F32),
            jax.ShapeDtypeStruct(proj_turned.shape, F32),
            jax.ShapeDtypeStruct(ds_turned.shape, F32),
        ),
        in_specs=[SMEM, VMEM, VMEM],
        out_specs=(VMEM, VMEM, VMEM, VMEM),
        scratch_shapes=[pltpu.VMEM((2 * HALF_ROWS, 128), F32)],
        compiler_params=pltpu.CompilerParams(vmem_limit_bytes=24 << 20),
        cost_estimate=takes(1.5),
        name="unpack",
    )(chan, part, peer_part)
    proj_grad = proj_grad.T
    ds_grad = ds_grad.T
    return (agg_map[None], agg_grad, dw_grad, up_grad, proj_grad, ds_grad)


def solution(mesh):
    in_specs = (
        P(("groups", "rep"), ("slide", "chan"), None),
        P(("groups", "rep"), ("slide", "chan")),
        P(("groups", "rep"), "slide", "chan", None),
        P(), P(), P(), P(), P(), P(), P(),
        P(None, None, "chan"),
    )
    out_specs = (
        P(("groups", "rep"), "slide", "chan", None),
        P("groups", None, "chan"),
        P("groups", None),
        P("groups", None),
        P("groups", None),
        P("groups", None),
    )
    return jax.shard_map(
        on_device, mesh=mesh, in_specs=in_specs, out_specs=out_specs, check_vma=False
    )
```

```python
import math

import jax
import jax.numpy as jnp
from jax import lax
from jax.experimental import pallas as pl
from jax.experimental.pallas import tpu as pltpu
from jax.sharding import PartitionSpec as P

SIDE = 8
CAP = 2
PIX = SIDE * SIDE
HALF_ROWS = 608
FEAT_ROWS = 192
COT_ROWS = 72
WIRE_ROWS = 56
BLOCK_ROWS = FEAT_ROWS + 2 * COT_ROWS
F32 = jnp.float32
BF16 = jnp.bfloat16
VMEM = pl.BlockSpec(memory_space=pltpu.VMEM)
SMEM = pl.BlockSpec(memory_space=pltpu.SMEM)


def params_of(steps=1):
    return pltpu.CompilerParams(
        dimension_semantics=("arbitrary",) * steps, vmem_limit_bytes=24 << 20
    )


def takes(microseconds):
    return pl.CostEstimate(
        flops=0, transcendentals=0, bytes_accessed=int(microseconds * 3.69e6)
    )


def nn(left, right):
    return lax.dot_general(left, right, (((1,), (0,)), ((), ())), preferred_element_type=F32)


def nt(left, right):
    return lax.dot_general(left, right, (((1,), (1,)), ((), ())), preferred_element_type=F32)


def tn(left, right):
    return lax.dot_general(left, right, (((0,), (0,)), ((), ())), preferred_element_type=F32)


def shifted(value, axis, steps):
    count = lax.axis_size(axis)
    first, last = (max(0, -steps), min(count, count - steps))
    return lax.ppermute(value, axis, [(source, source + steps) for source in range(first, last)])


def swapped(value, axis, step):
    count = lax.axis_size(axis)
    return lax.ppermute(value, axis, [(place, place ^ step) for place in range(count)])


def reach(tap):
    return (1, 2) if tap == 0 else (0, 1)


def pack_kernel(cells_ref, pixels_ref, row_ref, out_ref, below_ref, wide_ref, note_ref):
    slots = pixels_ref.shape[0]
    rows = out_ref.shape[0]
    pixch = pixels_ref.shape[1]
    cells = [cells_ref[0, t] for t in range(slots)]
    live = [cell >= 0 for cell in cells]
    bands = [cell >> 9 for cell in cells]
    places = []
    for t in range(slots):
        rank = jnp.int32(0)
        for s in range(t):
            rank = rank + ((bands[s] == bands[t]) & live[s]).astype(jnp.int32)
        places.append(jnp.where(live[t], bands[t] * CAP + rank, -1))
    below_ref[...] = row_ref[...].astype(BF16)
    pixels = pixels_ref[...].astype(F32)
    for n in range(pixch // 128):
        wide_ref[:, n, :] = pixels[:, 128 * n : 128 * n + 128]
    wide_ref[:, pixch // 128 :, :] = jnp.zeros_like(wide_ref[:, pixch // 128 :, :])
    out_ref[...] = jnp.zeros_like(out_ref)
    for t in range(slots):

        @pl.when(live[t])
        def _():
            out_ref[jnp.maximum(places[t], 0)] = wide_ref[t].astype(BF16)

    lane = lax.broadcasted_iota(jnp.int32, (rows, 128), 1)
    base = (lax.broadcasted_iota(jnp.int32, (rows, 128), 0) // CAP) * CAP
    notes = jnp.zeros((rows, 128), F32)
    for t in range(slots):
        own_row = ((cells[t] >> 6) & 7).astype(F32)
        own_col = (cells[t] & 63).astype(F32)
        for rank in range(CAP):
            hit = base + rank == places[t]
            for at, value in enumerate((own_row, own_col, jnp.float32(1.0))):
                notes = jnp.where(hit & (lane == 3 * rank + at), value, notes)
    note_ref[...] = jnp.zeros_like(note_ref)
    note_ref[:, 0, :] = notes
    out_ref[:, pixch // 128 :, :] = note_ref[...].astype(BF16)


def patch_kernel(chan_ref, meta_ref, cot_ref, below_ref, key_ref, own_ref, send_ref, meta_f32):
    sources = meta_ref.shape[0]
    chunks = sources // 8
    out_rows, e_half, _ = cot_ref.shape
    meta_f32[...] = meta_ref[...].astype(F32)
    meta = meta_f32[:, 0, :]
    first = chan_ref[0] == 0
    lane = lax.broadcasted_iota(jnp.int32, (8, 128), 1).astype(F32)
    blocks = []
    for mine in (True, False):
        for chunk in range(chunks):
            part = meta[chunk * 8 : chunk * 8 + 8]
            low = [jnp.broadcast_to(part[:, n : n + 1], (8, 128)) for n in range(3)]
            high = [jnp.broadcast_to(part[:, n : n + 1], (8, 128)) for n in range(3, 6)]
            row, col, valid = (
                jnp.where(first == mine, one, two) for one, two in zip(low, high)
            )
            for u in range(3):
                for v in range(3):
                    hit = (lane == 2.0 * col + v) & (valid > 0.5)
                    blocks.append(jnp.where(hit, 2.0 * row + u, -1.0))
    key = jnp.concatenate(blocks, axis=0)
    key_ref[...] = key

    total = jnp.zeros((key.shape[0], e_half), F32)
    for first_row in range(0, out_rows, 4):
        rows = range(first_row, first_row + 4)
        picks = [(key == float(o)).astype(F32).astype(BF16) for o in rows]
        cots = [cot_ref[o].astype(BF16) for o in rows]
        total = total + nt(jnp.concatenate(picks, axis=1), jnp.concatenate(cots, axis=1))
    pick = (key == float(out_rows)).astype(F32).astype(BF16)
    total = total + nt(pick, below_ref[...])
    half = total.shape[0] // 2
    own_ref[...] = jnp.zeros_like(own_ref)
    send_ref[...] = jnp.zeros_like(send_ref)
    own_ref[:, :e_half] = total[:half].astype(BF16)
    send_ref[:, :e_half] = total[half:].astype(BF16)


def center_of(values):
    center = values - jnp.mean(values, axis=-1, keepdims=True)
    rstd = lax.rsqrt(jnp.mean(center * center, axis=-1, keepdims=True) + 1e-06)
    return center * rstd, rstd


def fill_padded(padded_ref, got_ref, wide_ref, pixels_ref, channels):
    wide_ref[...] = got_ref[...].astype(F32)
    for n in range(pixels_ref.shape[1] // 128):
        pixels_ref[:, 128 * n : 128 * n + 128] = wide_ref[:, n, :]
    padded_ref[...] = jnp.zeros_like(padded_ref)
    for i in range(SIDE):
        for j in range(SIDE):
            at = (i * SIDE + j) * channels
            padded_ref[i + 3, j + 3] = pixels_ref[:, at : at + channels]


def stem_kernel(
    got_ref, dw_ref, gain_ref, up_ref, proj_ref, scale_ref, ds_gain_ref, ds_ref,
    feat_ref, hat1_ref, rstd1_ref, hat2_ref, rstd2_ref, hidden_ref, slope_ref, patch_ref,
    padded_ref, spatial_ref, low_ref, patch_f32, wide_ref, pixels_ref,
):
    channels = dw_ref.shape[1]
    fill_padded(padded_ref, got_ref, wide_ref, pixels_ref, channels)

    for i in range(SIDE):
        total = jnp.zeros((SIDE, 8, channels), F32)
        for a in range(max(0, 3 - i), min(7, SIDE + 3 - i)):
            for b in range(7):
                weight = dw_ref[7 * a + b : 7 * a + b + 1, :].reshape(1, 1, channels)
                total = total + weight * padded_ref[i + a, b : b + SIDE]
        spatial_ref[i] = total
    hat1, rstd1 = center_of(spatial_ref[...].reshape(PIX * 8, channels))
    hat1_ref[...] = hat1
    rstd1_ref[...] = rstd1
    normed = (hat1 * gain_ref[...]).astype(BF16)
    before = nn(normed, up_ref[...])
    cdf = 0.5 * (1.0 + lax.erf(before * math.sqrt(0.5)))
    pdf = jnp.exp(-0.5 * before * before) * (1.0 / math.sqrt(2.0 * math.pi))
    hidden = (before * cdf).astype(BF16)
    hidden_ref[...] = hidden
    slope_ref[...] = cdf + before * pdf
    branch = nt(hidden, proj_ref[...])
    inputs = padded_ref[3 : 3 + SIDE, 3 : 3 + SIDE].reshape(PIX * 8, channels)
    hat2, rstd2 = center_of(inputs + scale_ref[...] * branch)
    hat2_ref[...] = hat2
    rstd2_ref[...] = rstd2
    low_ref[...] = (hat2 * ds_gain_ref[...]).reshape(low_ref.shape)
    half = SIDE // 2
    for di in range(2):
        for dj in range(2):
            at = (2 * di + dj) * channels
            patch_f32[:, at : at + channels] = low_ref[:, di, :, dj].reshape(-1, channels)
    patches = patch_f32[...].astype(BF16)
    patch_ref[...] = patches
    total = nt(patches, ds_ref[...])
    rows = total.shape[0]
    feat_ref[0:rows] = total[:, 0:128].astype(BF16)
    rest = jnp.concatenate([total[: rows // 2, 128:192], total[rows // 2 :, 128:192]], axis=1)
    feat_ref[rows:] = rest.astype(BF16)


def unfold(block):
    rest = block[128:]
    return jnp.concatenate(
        [block[:128], jnp.concatenate([rest[:, :64], rest[:, 64:]], axis=0)], axis=1
    )


def back_kernel(
    chan_ref, own_ref, peer_ref, w_own_ref, w_peer_ref, got_ref,
    hat1_ref, rstd1_ref, hat2_ref, rstd2_ref, hidden_ref, slope_ref, patch_ref,
    gain_ref, up_ref, proj_ref, scale_ref, ds_gain_ref, ds_ref,
    keep_ref, send_ref,
    padded_ref, dlow_ref, dspatial_ref, dw_ref, ds_acc, up_acc, proj_acc, pack_ref,
    wide_ref, pixels_ref, w_ref,
    *, scale,
):
    channels = gain_ref.shape[1]
    half = SIDE // 2
    step = pl.program_id(0)

    @pl.when(step == 0)
    def _():
        dw_ref[...] = jnp.zeros_like(dw_ref)
        ds_acc[...] = jnp.zeros_like(ds_acc)
        up_acc[...] = jnp.zeros_like(up_acc)
        proj_acc[...] = jnp.zeros_like(proj_acc)

    e_half = w_own_ref.shape[2]
    w_ref[...] = jnp.zeros_like(w_ref)
    w_ref[:, :, 0:e_half] = w_own_ref[...]
    w_ref[:, :, 128 : 128 + e_half] = w_peer_ref[...]
    cots = jnp.concatenate([own_ref[...], peer_ref[...]], axis=1)
    grads = {}
    for a in range(3):
        for b in range(3):
            out = nt(cots, w_ref[3 * a + b])
            for u in reach(a):
                for v in reach(b):
                    at = (2 * u + a - 1) * half + 2 * v + b - 1
                    row = 8 * (3 * u + v)
                    piece = out[row : row + 8]
                    grads[at] = grads[at] + piece if at in grads else piece
    dfeat = jnp.concatenate([grads[at] for at in range(half * half)], axis=0) * scale
    dfeat = dfeat.astype(BF16)

    hat2 = hat2_ref[...]
    ds_acc[...] += tn(dfeat, patch_ref[...])
    back = nn(dfeat, ds_ref[...])
    for di in range(2):
        for dj in range(2):
            at = (2 * di + dj) * channels
            dlow_ref[:, di, :, dj] = back[:, at : at + channels].reshape(half, half, 8, channels)
    dhat2 = dlow_ref[...].reshape(PIX * 8, channels) * ds_gain_ref[...]
    mean_a = jnp.mean(dhat2, axis=-1, keepdims=True)
    mean_b = jnp.mean(dhat2 * hat2, axis=-1, keepdims=True)
    dmixed = rstd2_ref[...] * (dhat2 - mean_a - hat2 * mean_b)
    dbranch = (dmixed * scale_ref[...]).astype(BF16)
    proj_acc[...] += tn(dbranch, hidden_ref[...])
    dhidden = nn(dbranch, proj_ref[...])
    dbefore = (dhidden * slope_ref[...]).astype(BF16)
    hat1 = hat1_ref[...]
    normed = (hat1 * gain_ref[...]).astype(BF16)
    up_acc[...] += tn(normed, dbefore)
    dhat1 = nt(dbefore, up_ref[...]) * gain_ref[...]
    mean_a = jnp.mean(dhat1, axis=-1, keepdims=True)
    mean_b = jnp.mean(dhat1 * hat1, axis=-1, keepdims=True)
    dspatial = rstd1_ref[...] * (dhat1 - mean_a - hat1 * mean_b)
    dspatial_ref[...] = dspatial.reshape(SIDE, SIDE, 8, channels)
    fill_padded(padded_ref, got_ref, wide_ref, pixels_ref, channels)

    for a in range(7):
        totals = [jnp.zeros((8, channels), F32) for _ in range(7)]
        for i in range(max(0, 3 - a), min(SIDE, SIDE + 3 - a)):
            for b in range(7):
                low, high = max(0, 3 - b), min(SIDE, SIDE + 3 - b)
                product = padded_ref[i + a, b + low : b + high] * dspatial_ref[i, low:high]
                totals[b] = totals[b] + jnp.sum(product, axis=0)
        for b in range(7):
            dw_ref[a, b] += totals[b]

    @pl.when(step == pl.num_programs(0) - 1)
    def _():
        pack_ref[...] = jnp.zeros_like(pack_ref)
        for n in range(3):
            lanes = slice(128 * n, 128 * n + 128)
            pack_ref[192 * n : 192 * n + 192, :] = ds_acc[:, lanes]
            pack_ref[576 + 96 * n : 672 + 96 * n, :] = up_acc[:, lanes]
            pack_ref[864 + 96 * n : 960 + 96 * n, :] = proj_acc[:, lanes]
        pack_ref[1152:1201, 0:channels] = jnp.sum(dw_ref[...], axis=2).reshape(49, channels)
        mine = pl.multiple_of(chan_ref[0] * HALF_ROWS, 8)
        other = pl.multiple_of((1 - chan_ref[0]) * HALF_ROWS, 8)
        keep_ref[...] = pack_ref[pl.ds(mine, HALF_ROWS), :]
        send_ref[...] = pack_ref[pl.ds(other, HALF_ROWS), :].astype(BF16)


def unpack_kernel(chan_ref, own_ref, peer_ref, dw_ref, up_ref, proj_ref, ds_ref, pack_ref):
    channels = dw_ref.shape[1]
    mine = pl.multiple_of(chan_ref[0] * HALF_ROWS, 8)
    other = pl.multiple_of((1 - chan_ref[0]) * HALF_ROWS, 8)
    pack_ref[pl.ds(mine, HALF_ROWS), :] = own_ref[...].astype(F32)
    pack_ref[pl.ds(other, HALF_ROWS), :] = peer_ref[...].astype(F32)
    for n in range(3):
        lanes = slice(128 * n, 128 * n + 128)
        ds_ref[:, lanes] = pack_ref[192 * n : 192 * n + 192, :]
        up_ref[:, lanes] = pack_ref[576 + 96 * n : 672 + 96 * n, :]
        proj_ref[:, lanes] = pack_ref[864 + 96 * n : 960 + 96 * n, :]
    dw_ref[...] = pack_ref[1152:1201, 0:channels]


def spread_kernel(feat_ref, w_ref, key_ref, y_ref, below_ref, *, last):
    width = w_ref.shape[1]
    feats = unfold(feat_ref[...].astype(F32)).reshape(16, 8, width)
    outs = {}
    for a in range(3):
        for b in range(3):
            places = [(u, v) for u in reach(a) for v in reach(b)]
            left = jnp.concatenate(
                [feats[(2 * u + a - 1) * 4 + 2 * v + b - 1] for u, v in places], axis=0
            ).astype(BF16)
            out = nn(left, w_ref[3 * a + b])
            for n, (u, v) in enumerate(places):
                piece = out[8 * n : 8 * n + 8]
                at = 3 * u + v
                outs[at] = outs[at] + piece if at in outs else piece
    total = jnp.concatenate([outs[at] for at in range(9)], axis=0)
    y_ref[...] = total
    pick = (key_ref[...] == float(last)).astype(F32).astype(BF16)
    high = total.astype(BF16)
    rest = (total - high.astype(F32)).astype(BF16)

    @pl.when(pl.program_id(0) == 0)
    def _():
        below_ref[...] = jnp.zeros_like(below_ref)

    below_ref[...] += tn(high, pick) + tn(rest, pick)


def map_kernel(y_ref, key_ref, above_ref, out_ref):
    out_rows, width, _ = out_ref.shape
    turned = y_ref[...].T
    high = turned.astype(BF16)
    rest = (turned - high.astype(F32)).astype(BF16)
    key = key_ref[...]

    def row_of(o):
        pick = (key == o).astype(F32).astype(BF16)
        return nn(high, pick) + nn(rest, pick)

    out_ref[0] = (row_of(0.0) + above_ref[...]).astype(BF16)

    def step(o, carry):
        out_ref[o] = row_of(o.astype(F32)).astype(BF16)
        return carry

    lax.fori_loop(1, out_rows, step, 0)


def weight_kernel(
    place_ref, near_ref, far_ref, keep_ref, send_ref, feat_ref, cot_ref, send_acc, *, scale
):
    near = near_ref.shape[0]
    members = feat_ref.shape[1] // 8
    width, e_half = keep_ref.shape[1:]
    step = pl.program_id(0)

    @pl.when(step == 0)
    def _():
        keep_ref[...] = jnp.zeros_like(keep_ref)
        send_acc[...] = jnp.zeros_like(send_acc)

    def take(member, block):
        block = block.astype(F32)
        feat_ref[:, 8 * member : 8 * member + 8] = unfold(block[:FEAT_ROWS]).reshape(16, 8, width)
        own = block[FEAT_ROWS : FEAT_ROWS + COT_ROWS].reshape(9, 8, 128)
        peer = block[FEAT_ROWS + COT_ROWS :].reshape(9, 8, 128)
        cot_ref[:, 8 * member : 8 * member + 8, 0:128] = own
        cot_ref[:, 8 * member : 8 * member + 8, 128:256] = peer

    for member in range(members):
        at = place_ref[0] ^ member

        @pl.when(at < near)
        def _():
            take(member, near_ref[jnp.minimum(at, near - 1)])

        if members > near:

            @pl.when(at >= near)
            def _():
                take(member, far_ref[jnp.maximum(at - near, 0)])

    for a in range(3):
        for b in range(3):
            places = [(u, v) for u in reach(a) for v in reach(b)]
            left = jnp.concatenate(
                [feat_ref[(2 * u + a - 1) * 4 + 2 * v + b - 1] for u, v in places], axis=0
            ).astype(BF16)
            right = jnp.concatenate([cot_ref[3 * u + v] for u, v in places], axis=0).astype(BF16)
            total = tn(left, right) * scale
            keep_ref[3 * a + b] += total[:, :e_half]
            send_acc[3 * a + b] += total[:, 128 : 128 + e_half]

    @pl.when(step == pl.num_programs(0) - 1)
    def _():
        send_ref[...] = send_acc[...].astype(BF16)


def whole(shape):
    return pl.BlockSpec(shape, lambda g: (0,) * len(shape))


def on_device(
    tile_pixels, tile_cell, agg_cot, dw_weight, norm_gain, up_weight, proj_weight,
    layer_scale, ds_gain, ds_weight, agg_weight,
):
    channels = dw_weight.shape[1]
    hid = up_weight.shape[1]
    width = ds_weight.shape[1]
    bands = lax.axis_size("slide")
    sources = bands * lax.axis_size("chan")
    chunks = sources // 8
    pixch = tile_pixels.shape[2]
    out_rows = agg_cot.shape[1]
    e_half = agg_weight.shape[2]
    cols = agg_cot.shape[3]
    blocks = CAP * chunks
    total_rows = out_rows * bands * lax.axis_size("rep") * cols
    loss_scale = 1.0 / math.sqrt(total_rows)
    chan = lax.axis_index("chan").astype(jnp.int32)[None]
    gain = norm_gain[None]
    scale = layer_scale[None]
    low_gain = ds_gain[None]
    proj_turned = proj_weight.T
    ds_turned = ds_weight.T

    packed, top_cot = pl.pallas_call(
        pack_kernel,
        grid=(1,),
        out_shape=(
            jax.ShapeDtypeStruct((sources, WIRE_ROWS, 128), BF16),
            jax.ShapeDtypeStruct((e_half, cols), BF16),
        ),
        in_specs=[
            SMEM,
            pl.BlockSpec((None,) + tile_pixels.shape[1:], lambda i: (0, 0, 0)),
            pl.BlockSpec((None, None, e_half, cols), lambda i: (0, 0, 0, 0)),
        ],
        out_specs=(whole((sources, WIRE_ROWS, 128)), whole((e_half, cols))),
        scratch_shapes=[
            pltpu.VMEM((tile_pixels.shape[1], WIRE_ROWS, 128), F32),
            pltpu.VMEM((sources, 8, 128), F32),
        ],
        cost_estimate=takes(1.5),
        name="pack",
    )(tile_cell, tile_pixels, agg_cot)
    below_cot = shifted(top_cot, "slide", -1)
    packed, own_weight = lax.optimization_barrier((packed, agg_weight))
    peer_weight = swapped(own_weight, "chan", 1)
    got = lax.all_to_all(packed, ("slide", "chan"), split_axis=0, concat_axis=0, tiled=True)

    key, cots_own, cots_send = pl.pallas_call(
        patch_kernel,
        out_shape=(
            jax.ShapeDtypeStruct((blocks * COT_ROWS, cols), F32),
            jax.ShapeDtypeStruct((chunks * COT_ROWS, 128), BF16),
            jax.ShapeDtypeStruct((chunks * COT_ROWS, 128), BF16),
        ),
        in_specs=[
            SMEM,
            pl.BlockSpec((sources, 8, 128), lambda i: (0, pixch // 1024, 0)),
            pl.BlockSpec((None, out_rows, e_half, cols), lambda i: (0, 0, 0, 0)),
            whole((e_half, cols)),
        ],
        out_specs=(
            whole((blocks * COT_ROWS, cols)),
            whole((chunks * COT_ROWS, 128)),
            whole((chunks * COT_ROWS, 128)),
        ),
        grid=(1,),
        scratch_shapes=[pltpu.VMEM((sources, 8, 128), F32)],
        compiler_params=params_of(),
        cost_estimate=takes(1.2),
        name="patch",
    )(chan, got, agg_cot, below_cot)
    cots_peer = swapped(cots_send, "chan", 1)
    cots_own = cots_own.reshape(chunks, COT_ROWS, 128)
    cots_peer = cots_peer.reshape(chunks, COT_ROWS, 128)

    rows = PIX * 8
    pixel_spec = pl.BlockSpec((8, WIRE_ROWS, 128), lambda g: (g, 0, 0))
    pixel_scratch = [pltpu.VMEM((8, WIRE_ROWS, 128), F32), pltpu.VMEM((8, pixch), F32)]

    def chunk(*shape):
        return pl.BlockSpec((None,) + shape, lambda g: (g,) + (0,) * len(shape))

    feats, hat1, rstd1, hat2, rstd2, hidden, slope, patches = pl.pallas_call(
        stem_kernel,
        grid=(chunks,),
        out_shape=(
            jax.ShapeDtypeStruct((chunks, FEAT_ROWS, 128), BF16),
            jax.ShapeDtypeStruct((chunks, rows, channels), F32),
            jax.ShapeDtypeStruct((chunks, rows, 1), F32),
            jax.ShapeDtypeStruct((chunks, rows, channels), F32),
            jax.ShapeDtypeStruct((chunks, rows, 1), F32),
            jax.ShapeDtypeStruct((chunks, rows, hid), BF16),
            jax.ShapeDtypeStruct((chunks, rows, hid), F32),
            jax.ShapeDtypeStruct((chunks, 128, 4 * channels), BF16),
        ),
        in_specs=[
            pixel_spec,
            whole(dw_weight.shape), whole((1, channels)), whole(up_weight.shape),
            whole(proj_turned.shape), whole((1, channels)), whole((1, channels)),
            whole(ds_turned.shape),
        ],
        out_specs=(
            chunk(FEAT_ROWS, 128), chunk(rows, channels), chunk(rows, 1), chunk(rows, channels),
            chunk(rows, 1), chunk(rows, hid), chunk(rows, hid), chunk(128, 4 * channels),
        ),
        scratch_shapes=[
            pltpu.VMEM((SIDE + 6, SIDE + 6, 8, channels), F32),
            pltpu.VMEM((SIDE, SIDE, 8, channels), F32),
            pltpu.VMEM((SIDE // 2, 2, SIDE // 2, 2, 8, channels), F32),
            pltpu.VMEM((128, 4 * channels), F32),
            *pixel_scratch,
        ],
        compiler_params=params_of(),
        cost_estimate=takes(2.7),
        name="stem",
    )(got, dw_weight, gain, up_weight, proj_turned, scale, low_gain, ds_turned)

    feats_band = jnp.concatenate([feats, swapped(feats, "chan", 1)], axis=0)
    spread, below = pl.pallas_call(
        lambda *refs: spread_kernel(*refs, last=out_rows),
        grid=(blocks,),
        out_shape=(
            jax.ShapeDtypeStruct((blocks * 72, e_half), F32),
            jax.ShapeDtypeStruct((e_half, cols), F32),
        ),
        in_specs=[
            chunk(FEAT_ROWS, 128), whole(agg_weight.shape),
            pl.BlockSpec((72, cols), lambda g: (g, 0)),
        ],
        out_specs=(pl.BlockSpec((72, e_half), lambda g: (g, 0)), whole((e_half, cols))),
        compiler_params=params_of(),
        cost_estimate=takes(1.0),
        name="spread",
    )(feats_band, agg_weight, key)
    tile_blocks = jnp.concatenate([feats, cots_own, cots_peer], axis=1)
    gather = chunks == 1
    near = far = tile_blocks
    place = jnp.zeros((1,), jnp.int32)
    spans = [("slide", 1 << n) for n in reversed(range(bands.bit_length() - 1))]
    spans += [("rep", 1 << n) for n in range(lax.axis_size("rep").bit_length() - 1)]

    def widen(n, near, place):
        axis, step = spans[n]
        bit = (lax.axis_index(axis).astype(jnp.int32) // step) % 2
        return swapped(near, axis, step), place + bit * (1 << n)

    if gather:
        far, place = widen(0, near, place)
        near = jnp.concatenate([near, far], axis=0)

    keep, send = pl.pallas_call(
        lambda *refs: back_kernel(*refs, scale=loss_scale),
        grid=(chunks,),
        out_shape=(
            jax.ShapeDtypeStruct((HALF_ROWS, 128), F32),
            jax.ShapeDtypeStruct((HALF_ROWS, 128), BF16),
        ),
        in_specs=[
            SMEM, chunk(COT_ROWS, 128), chunk(COT_ROWS, 128),
            whole(agg_weight.shape), whole(agg_weight.shape), pixel_spec,
            chunk(rows, channels), chunk(rows, 1), chunk(rows, channels), chunk(rows, 1),
            chunk(rows, hid), chunk(rows, hid), chunk(128, 4 * channels),
            whole((1, channels)), whole(up_weight.shape), whole(proj_turned.shape),
            whole((1, channels)), whole((1, channels)), whole(ds_turned.shape),
        ],
        out_specs=(whole((HALF_ROWS, 128)), whole((HALF_ROWS, 128))),
        scratch_shapes=[
            pltpu.VMEM((SIDE + 6, SIDE + 6, 8, channels), F32),
            pltpu.VMEM((SIDE // 2, 2, SIDE // 2, 2, 8, channels), F32),
            pltpu.VMEM((SIDE, SIDE, 8, channels), F32),
            pltpu.VMEM((7, 7, 8, channels), F32),
            pltpu.VMEM(ds_turned.shape, F32),
            pltpu.VMEM(up_weight.shape, F32),
            pltpu.VMEM(proj_turned.shape, F32),
            pltpu.VMEM((2 * HALF_ROWS, 128), F32),
            *pixel_scratch,
            pltpu.VMEM((9, width, 256), BF16),
        ],
        compiler_params=params_of(),
        cost_estimate=takes(3.7),
        name="stem_back",
    )(
        chan, cots_own, cots_peer, agg_weight, peer_weight, got,
        hat1, rstd1, hat2, rstd2, hidden, slope, patches,
        gain, up_weight, proj_turned, scale, low_gain, ds_turned,
    )

    part = keep + swapped(send, "chan", 1).astype(F32)
    if gather:
        part, near, spread, below = lax.optimization_barrier((part, near, spread, below))
    above = shifted(below, "slide", 1)
    steps = []
    for axis in ("rep", "slide"):
        for n in reversed(range(lax.axis_size(axis).bit_length() - 1)):
            steps.append((axis, 1 << n))
    for n, (axis, step) in enumerate(steps):
        wire = part.astype(BF16)
        part = wire.astype(F32) + swapped(wire, axis, step).astype(F32)
    map_call = pl.pallas_call(
        map_kernel,
        out_shape=jax.ShapeDtypeStruct((out_rows, e_half, cols), BF16),
        in_specs=[VMEM, VMEM, VMEM],
        out_specs=VMEM,
        compiler_params=pltpu.CompilerParams(vmem_limit_bytes=24 << 20),
        cost_estimate=takes(3.5),
        name="agg_map",
    )

    for n in range(1, len(spans) if gather else 0):
        if n == len(spans) - 1:
            near, above = lax.optimization_barrier((near, above))
        far, place = widen(n, near, place)
        if n < len(spans) - 1:
            near = jnp.concatenate([near, far], axis=0)

    agg_map = map_call(spread, key, above)
    if gather:
        far, agg_map = lax.optimization_barrier((far, agg_map))
    count = 2 * near.shape[0] if gather else chunks
    per = count if gather else 1
    near_count = near.shape[0] if gather else 1
    agg_keep, agg_send = pl.pallas_call(
        lambda *refs: weight_kernel(*refs, scale=loss_scale),
        grid=(count // per,),
        out_shape=(
            jax.ShapeDtypeStruct((9, width, e_half), F32),
            jax.ShapeDtypeStruct((9, width, e_half), BF16),
        ),
        in_specs=[
            SMEM,
            pl.BlockSpec((near_count, BLOCK_ROWS, 128), lambda g: (g, 0, 0)),
            pl.BlockSpec((near_count, BLOCK_ROWS, 128), lambda g: (g, 0, 0)),
        ],
        out_specs=(whole((9, width, e_half)), whole((9, width, e_half))),
        scratch_shapes=[
            pltpu.VMEM((16, per * 8, width), F32),
            pltpu.VMEM((9, per * 8, 256), F32),
            pltpu.VMEM((9, width, e_half), F32),
        ],
        compiler_params=params_of(),
        cost_estimate=takes(1.4),
        name="agg_weight_grad",
    )(place, near, far)
    agg_grad = agg_keep + swapped(agg_send, "chan", 1).astype(F32)
    if not gather:
        agg_grad = lax.psum(agg_grad, ("slide", "rep"))

    part = part.astype(BF16)
    peer_part = swapped(part, "chan", 1)
    part, agg_grad = lax.optimization_barrier((part, agg_grad))
    dw_grad, up_grad, proj_grad, ds_grad = pl.pallas_call(
        unpack_kernel,
        out_shape=(
            jax.ShapeDtypeStruct(dw_weight.shape, F32),
            jax.ShapeDtypeStruct(up_weight.shape, F32),
            jax.ShapeDtypeStruct(proj_turned.shape, F32),
            jax.ShapeDtypeStruct(ds_turned.shape, F32),
        ),
        in_specs=[SMEM, VMEM, VMEM],
        out_specs=(VMEM, VMEM, VMEM, VMEM),
        scratch_shapes=[pltpu.VMEM((2 * HALF_ROWS, 128), F32)],
        compiler_params=pltpu.CompilerParams(vmem_limit_bytes=24 << 20),
        cost_estimate=takes(1.5),
        name="unpack",
    )(chan, part, peer_part)
    proj_grad = proj_grad.T
    ds_grad = ds_grad.T
    return (agg_map[None], agg_grad, dw_grad, up_grad, proj_grad, ds_grad)


def solution(mesh):
    in_specs = (
        P(("groups", "rep"), ("slide", "chan"), None),
        P(("groups", "rep"), ("slide", "chan")),
        P(("groups", "rep"), "slide", "chan", None),
        P(), P(), P(), P(), P(), P(), P(),
        P(None, None, "chan"),
    )
    out_specs = (
        P(("groups", "rep"), "slide", "chan", None),
        P("groups", None, "chan"),
        P("groups", None),
        P("groups", None),
        P("groups", None),
        P("groups", None),
    )
    return jax.shard_map(
        on_device, mesh=mesh, in_specs=in_specs, out_specs=out_specs, check_vma=False
    )
```

```python
import math

import jax
import jax.numpy as jnp
from jax import lax
from jax.experimental import pallas as pl
from jax.experimental.pallas import tpu as pltpu
from jax.sharding import PartitionSpec as P

SIDE = 8
CAP = 2
PIX = SIDE * SIDE
HALF_ROWS = 608
FEAT_ROWS = 192
COT_ROWS = 72
WIRE_ROWS = 56
BLOCK_ROWS = FEAT_ROWS + 2 * COT_ROWS
F32 = jnp.float32
BF16 = jnp.bfloat16
VMEM = pl.BlockSpec(memory_space=pltpu.VMEM)
SMEM = pl.BlockSpec(memory_space=pltpu.SMEM)


def params_of(steps=1):
    return pltpu.CompilerParams(
        dimension_semantics=("arbitrary",) * steps, vmem_limit_bytes=24 << 20
    )


def takes(microseconds):
    return pl.CostEstimate(
        flops=0, transcendentals=0, bytes_accessed=int(microseconds * 3.69e6)
    )


def nn(left, right):
    return lax.dot_general(left, right, (((1,), (0,)), ((), ())), preferred_element_type=F32)


def nt(left, right):
    return lax.dot_general(left, right, (((1,), (1,)), ((), ())), preferred_element_type=F32)


def tn(left, right):
    return lax.dot_general(left, right, (((0,), (0,)), ((), ())), preferred_element_type=F32)


def shifted(value, axis, steps):
    count = lax.axis_size(axis)
    first, last = (max(0, -steps), min(count, count - steps))
    return lax.ppermute(value, axis, [(source, source + steps) for source in range(first, last)])


def swapped(value, axis, step):
    count = lax.axis_size(axis)
    return lax.ppermute(value, axis, [(place, place ^ step) for place in range(count)])


def reach(tap):
    return (1, 2) if tap == 0 else (0, 1)


def pack_kernel(cells_ref, pixels_ref, row_ref, out_ref, below_ref, wide_ref, note_ref):
    slots = pixels_ref.shape[0]
    rows = out_ref.shape[0]
    pixch = pixels_ref.shape[1]
    cells = [cells_ref[0, t] for t in range(slots)]
    live = [cell >= 0 for cell in cells]
    bands = [cell >> 9 for cell in cells]
    places = []
    for t in range(slots):
        rank = jnp.int32(0)
        for s in range(t):
            rank = rank + ((bands[s] == bands[t]) & live[s]).astype(jnp.int32)
        places.append(jnp.where(live[t], bands[t] * CAP + rank, -1))
    below_ref[...] = row_ref[...].astype(BF16)
    pixels = pixels_ref[...].astype(F32)
    for n in range(pixch // 128):
        wide_ref[:, n, :] = pixels[:, 128 * n : 128 * n + 128]
    wide_ref[:, pixch // 128 :, :] = jnp.zeros_like(wide_ref[:, pixch // 128 :, :])
    out_ref[...] = jnp.zeros_like(out_ref)
    for t in range(slots):

        @pl.when(live[t])
        def _():
            out_ref[jnp.maximum(places[t], 0)] = wide_ref[t].astype(BF16)

    lane = lax.broadcasted_iota(jnp.int32, (rows, 128), 1)
    base = (lax.broadcasted_iota(jnp.int32, (rows, 128), 0) // CAP) * CAP
    notes = jnp.zeros((rows, 128), F32)
    for t in range(slots):
        own_row = ((cells[t] >> 6) & 7).astype(F32)
        own_col = (cells[t] & 63).astype(F32)
        for rank in range(CAP):
            hit = base + rank == places[t]
            for at, value in enumerate((own_row, own_col, jnp.float32(1.0))):
                notes = jnp.where(hit & (lane == 3 * rank + at), value, notes)
    note_ref[...] = jnp.zeros_like(note_ref)
    note_ref[:, 0, :] = notes
    out_ref[:, pixch // 128 :, :] = note_ref[...].astype(BF16)


def patch_kernel(chan_ref, meta_ref, cot_ref, below_ref, key_ref, own_ref, send_ref, meta_f32):
    sources = meta_ref.shape[0]
    chunks = sources // 8
    out_rows, e_half, _ = cot_ref.shape
    meta_f32[...] = meta_ref[...].astype(F32)
    meta = meta_f32[:, 0, :]
    first = chan_ref[0] == 0
    lane = lax.broadcasted_iota(jnp.int32, (8, 128), 1).astype(F32)
    blocks = []
    for mine in (True, False):
        for chunk in range(chunks):
            part = meta[chunk * 8 : chunk * 8 + 8]
            low = [jnp.broadcast_to(part[:, n : n + 1], (8, 128)) for n in range(3)]
            high = [jnp.broadcast_to(part[:, n : n + 1], (8, 128)) for n in range(3, 6)]
            row, col, valid = (
                jnp.where(first == mine, one, two) for one, two in zip(low, high)
            )
            for u in range(3):
                for v in range(3):
                    hit = (lane == 2.0 * col + v) & (valid > 0.5)
                    blocks.append(jnp.where(hit, 2.0 * row + u, -1.0))
    key = jnp.concatenate(blocks, axis=0)
    key_ref[...] = key

    total = jnp.zeros((key.shape[0], e_half), F32)
    for first_row in range(0, out_rows, 4):
        rows = range(first_row, first_row + 4)
        picks = [(key == float(o)).astype(F32).astype(BF16) for o in rows]
        cots = [cot_ref[o].astype(BF16) for o in rows]
        total = total + nt(jnp.concatenate(picks, axis=1), jnp.concatenate(cots, axis=1))
    pick = (key == float(out_rows)).astype(F32).astype(BF16)
    total = total + nt(pick, below_ref[...])
    half = total.shape[0] // 2
    own_ref[...] = jnp.zeros_like(own_ref)
    send_ref[...] = jnp.zeros_like(send_ref)
    own_ref[:, :e_half] = total[:half].astype(BF16)
    send_ref[:, :e_half] = total[half:].astype(BF16)


def center_of(values):
    center = values - jnp.mean(values, axis=-1, keepdims=True)
    rstd = lax.rsqrt(jnp.mean(center * center, axis=-1, keepdims=True) + 1e-06)
    return center * rstd, rstd


def fill_padded(padded_ref, got_ref, wide_ref, pixels_ref, channels):
    wide_ref[...] = got_ref[...].astype(F32)
    for n in range(pixels_ref.shape[1] // 128):
        pixels_ref[:, 128 * n : 128 * n + 128] = wide_ref[:, n, :]
    padded_ref[...] = jnp.zeros_like(padded_ref)
    for i in range(SIDE):
        for j in range(SIDE):
            at = (i * SIDE + j) * channels
            padded_ref[i + 3, j + 3] = pixels_ref[:, at : at + channels]


def stem_kernel(
    got_ref, dw_ref, gain_ref, up_ref, proj_ref, scale_ref, ds_gain_ref, ds_ref,
    feat_ref, hat1_ref, rstd1_ref, hat2_ref, rstd2_ref, hidden_ref, slope_ref, patch_ref,
    padded_ref, spatial_ref, low_ref, patch_f32, wide_ref, pixels_ref,
):
    channels = dw_ref.shape[1]
    fill_padded(padded_ref, got_ref, wide_ref, pixels_ref, channels)

    for i in range(SIDE):
        total = jnp.zeros((SIDE, 8, channels), F32)
        for a in range(max(0, 3 - i), min(7, SIDE + 3 - i)):
            for b in range(7):
                weight = dw_ref[7 * a + b : 7 * a + b + 1, :].reshape(1, 1, channels)
                total = total + weight * padded_ref[i + a, b : b + SIDE]
        spatial_ref[i] = total
    hat1, rstd1 = center_of(spatial_ref[...].reshape(PIX * 8, channels))
    hat1_ref[...] = hat1
    rstd1_ref[...] = rstd1
    normed = (hat1 * gain_ref[...]).astype(BF16)
    before = nn(normed, up_ref[...])
    cdf = 0.5 * (1.0 + lax.erf(before * math.sqrt(0.5)))
    pdf = jnp.exp(-0.5 * before * before) * (1.0 / math.sqrt(2.0 * math.pi))
    hidden = (before * cdf).astype(BF16)
    hidden_ref[...] = hidden
    slope_ref[...] = cdf + before * pdf
    branch = nt(hidden, proj_ref[...])
    inputs = padded_ref[3 : 3 + SIDE, 3 : 3 + SIDE].reshape(PIX * 8, channels)
    hat2, rstd2 = center_of(inputs + scale_ref[...] * branch)
    hat2_ref[...] = hat2
    rstd2_ref[...] = rstd2
    low_ref[...] = (hat2 * ds_gain_ref[...]).reshape(low_ref.shape)
    half = SIDE // 2
    for di in range(2):
        for dj in range(2):
            at = (2 * di + dj) * channels
            patch_f32[:, at : at + channels] = low_ref[:, di, :, dj].reshape(-1, channels)
    patches = patch_f32[...].astype(BF16)
    patch_ref[...] = patches
    total = nt(patches, ds_ref[...])
    rows = total.shape[0]
    feat_ref[0:rows] = total[:, 0:128].astype(BF16)
    rest = jnp.concatenate([total[: rows // 2, 128:192], total[rows // 2 :, 128:192]], axis=1)
    feat_ref[rows:] = rest.astype(BF16)


def unfold(block):
    rest = block[128:]
    return jnp.concatenate(
        [block[:128], jnp.concatenate([rest[:, :64], rest[:, 64:]], axis=0)], axis=1
    )


def back_kernel(
    chan_ref, own_ref, peer_ref, w_own_ref, w_peer_ref, got_ref,
    hat1_ref, rstd1_ref, hat2_ref, rstd2_ref, hidden_ref, slope_ref, patch_ref,
    gain_ref, up_ref, proj_ref, scale_ref, ds_gain_ref, ds_ref,
    keep_ref, send_ref,
    padded_ref, dlow_ref, dspatial_ref, dw_ref, ds_acc, up_acc, proj_acc, pack_ref,
    wide_ref, pixels_ref, w_ref,
    *, scale,
):
    channels = gain_ref.shape[1]
    half = SIDE // 2
    step = pl.program_id(0)

    @pl.when(step == 0)
    def _():
        dw_ref[...] = jnp.zeros_like(dw_ref)
        ds_acc[...] = jnp.zeros_like(ds_acc)
        up_acc[...] = jnp.zeros_like(up_acc)
        proj_acc[...] = jnp.zeros_like(proj_acc)

    e_half = w_own_ref.shape[2]
    w_ref[...] = jnp.zeros_like(w_ref)
    w_ref[:, :, 0:e_half] = w_own_ref[...]
    w_ref[:, :, 128 : 128 + e_half] = w_peer_ref[...]
    cots = jnp.concatenate([own_ref[...], peer_ref[...]], axis=1)
    grads = {}
    for a in range(3):
        for b in range(3):
            out = nt(cots, w_ref[3 * a + b])
            for u in reach(a):
                for v in reach(b):
                    at = (2 * u + a - 1) * half + 2 * v + b - 1
                    row = 8 * (3 * u + v)
                    piece = out[row : row + 8]
                    grads[at] = grads[at] + piece if at in grads else piece
    dfeat = jnp.concatenate([grads[at] for at in range(half * half)], axis=0) * scale
    dfeat = dfeat.astype(BF16)

    hat2 = hat2_ref[...]
    ds_acc[...] += tn(dfeat, patch_ref[...])
    back = nn(dfeat, ds_ref[...])
    for di in range(2):
        for dj in range(2):
            at = (2 * di + dj) * channels
            dlow_ref[:, di, :, dj] = back[:, at : at + channels].reshape(half, half, 8, channels)
    dhat2 = dlow_ref[...].reshape(PIX * 8, channels) * ds_gain_ref[...]
    mean_a = jnp.mean(dhat2, axis=-1, keepdims=True)
    mean_b = jnp.mean(dhat2 * hat2, axis=-1, keepdims=True)
    dmixed = rstd2_ref[...] * (dhat2 - mean_a - hat2 * mean_b)
    dbranch = (dmixed * scale_ref[...]).astype(BF16)
    proj_acc[...] += tn(dbranch, hidden_ref[...])
    dhidden = nn(dbranch, proj_ref[...])
    dbefore = (dhidden * slope_ref[...]).astype(BF16)
    hat1 = hat1_ref[...]
    normed = (hat1 * gain_ref[...]).astype(BF16)
    up_acc[...] += tn(normed, dbefore)
    dhat1 = nt(dbefore, up_ref[...]) * gain_ref[...]
    mean_a = jnp.mean(dhat1, axis=-1, keepdims=True)
    mean_b = jnp.mean(dhat1 * hat1, axis=-1, keepdims=True)
    dspatial = rstd1_ref[...] * (dhat1 - mean_a - hat1 * mean_b)
    dspatial_ref[...] = dspatial.reshape(SIDE, SIDE, 8, channels)
    fill_padded(padded_ref, got_ref, wide_ref, pixels_ref, channels)

    for a in range(7):
        totals = [jnp.zeros((8, channels), F32) for _ in range(7)]
        for i in range(max(0, 3 - a), min(SIDE, SIDE + 3 - a)):
            for b in range(7):
                low, high = max(0, 3 - b), min(SIDE, SIDE + 3 - b)
                product = padded_ref[i + a, b + low : b + high] * dspatial_ref[i, low:high]
                totals[b] = totals[b] + jnp.sum(product, axis=0)
        for b in range(7):
            dw_ref[a, b] += totals[b]

    @pl.when(step == pl.num_programs(0) - 1)
    def _():
        pack_ref[...] = jnp.zeros_like(pack_ref)
        for n in range(3):
            lanes = slice(128 * n, 128 * n + 128)
            pack_ref[192 * n : 192 * n + 192, :] = ds_acc[:, lanes]
            pack_ref[576 + 96 * n : 672 + 96 * n, :] = up_acc[:, lanes]
            pack_ref[864 + 96 * n : 960 + 96 * n, :] = proj_acc[:, lanes]
        pack_ref[1152:1201, 0:channels] = jnp.sum(dw_ref[...], axis=2).reshape(49, channels)
        mine = pl.multiple_of(chan_ref[0] * HALF_ROWS, 8)
        other = pl.multiple_of((1 - chan_ref[0]) * HALF_ROWS, 8)
        keep_ref[...] = pack_ref[pl.ds(mine, HALF_ROWS), :]
        send_ref[...] = pack_ref[pl.ds(other, HALF_ROWS), :].astype(BF16)


def unpack_kernel(chan_ref, own_ref, peer_ref, dw_ref, up_ref, proj_ref, ds_ref, pack_ref):
    channels = dw_ref.shape[1]
    mine = pl.multiple_of(chan_ref[0] * HALF_ROWS, 8)
    other = pl.multiple_of((1 - chan_ref[0]) * HALF_ROWS, 8)
    pack_ref[pl.ds(mine, HALF_ROWS), :] = own_ref[...].astype(F32)
    pack_ref[pl.ds(other, HALF_ROWS), :] = peer_ref[...].astype(F32)
    for n in range(3):
        lanes = slice(128 * n, 128 * n + 128)
        ds_ref[:, lanes] = pack_ref[192 * n : 192 * n + 192, :]
        up_ref[:, lanes] = pack_ref[576 + 96 * n : 672 + 96 * n, :]
        proj_ref[:, lanes] = pack_ref[864 + 96 * n : 960 + 96 * n, :]
    dw_ref[...] = pack_ref[1152:1201, 0:channels]


def spread_kernel(feat_ref, w_ref, key_ref, y_ref, below_ref, *, last):
    width = w_ref.shape[1]
    feats = unfold(feat_ref[...].astype(F32)).reshape(16, 8, width)
    outs = {}
    for a in range(3):
        for b in range(3):
            places = [(u, v) for u in reach(a) for v in reach(b)]
            left = jnp.concatenate(
                [feats[(2 * u + a - 1) * 4 + 2 * v + b - 1] for u, v in places], axis=0
            ).astype(BF16)
            out = nn(left, w_ref[3 * a + b])
            for n, (u, v) in enumerate(places):
                piece = out[8 * n : 8 * n + 8]
                at = 3 * u + v
                outs[at] = outs[at] + piece if at in outs else piece
    total = jnp.concatenate([outs[at] for at in range(9)], axis=0)
    y_ref[...] = total
    pick = (key_ref[...] == float(last)).astype(F32).astype(BF16)
    high = total.astype(BF16)
    rest = (total - high.astype(F32)).astype(BF16)

    @pl.when(pl.program_id(0) == 0)
    def _():
        below_ref[...] = jnp.zeros_like(below_ref)

    below_ref[...] += tn(high, pick) + tn(rest, pick)


def map_kernel(y_ref, key_ref, above_ref, out_ref):
    out_rows, width, _ = out_ref.shape
    turned = y_ref[...].T
    high = turned.astype(BF16)
    rest = (turned - high.astype(F32)).astype(BF16)
    key = key_ref[...]

    def row_of(o):
        pick = (key == o).astype(F32).astype(BF16)
        return nn(high, pick) + nn(rest, pick)

    out_ref[0] = (row_of(0.0) + above_ref[...]).astype(BF16)

    def step(o, carry):
        out_ref[o] = row_of(o.astype(F32)).astype(BF16)
        return carry

    lax.fori_loop(1, out_rows, step, 0)


def weight_kernel(
    place_ref, near_ref, far_ref, keep_ref, send_ref, feat_ref, cot_ref, send_acc, *, scale
):
    near = near_ref.shape[0]
    members = feat_ref.shape[1] // 8
    width, e_half = keep_ref.shape[1:]
    step = pl.program_id(0)

    @pl.when(step == 0)
    def _():
        keep_ref[...] = jnp.zeros_like(keep_ref)
        send_acc[...] = jnp.zeros_like(send_acc)

    def take(member, block):
        block = block.astype(F32)
        feat_ref[:, 8 * member : 8 * member + 8] = unfold(block[:FEAT_ROWS]).reshape(16, 8, width)
        own = block[FEAT_ROWS : FEAT_ROWS + COT_ROWS].reshape(9, 8, 128)
        peer = block[FEAT_ROWS + COT_ROWS :].reshape(9, 8, 128)
        cot_ref[:, 8 * member : 8 * member + 8, 0:128] = own
        cot_ref[:, 8 * member : 8 * member + 8, 128:256] = peer

    for member in range(members):
        at = place_ref[0] ^ member

        @pl.when(at < near)
        def _():
            take(member, near_ref[jnp.minimum(at, near - 1)])

        if members > near:

            @pl.when(at >= near)
            def _():
                take(member, far_ref[jnp.maximum(at - near, 0)])

    for a in range(3):
        for b in range(3):
            places = [(u, v) for u in reach(a) for v in reach(b)]
            left = jnp.concatenate(
                [feat_ref[(2 * u + a - 1) * 4 + 2 * v + b - 1] for u, v in places], axis=0
            ).astype(BF16)
            right = jnp.concatenate([cot_ref[3 * u + v] for u, v in places], axis=0).astype(BF16)
            total = tn(left, right) * scale
            keep_ref[3 * a + b] += total[:, :e_half]
            send_acc[3 * a + b] += total[:, 128 : 128 + e_half]

    @pl.when(step == pl.num_programs(0) - 1)
    def _():
        send_ref[...] = send_acc[...].astype(BF16)


def whole(shape):
    return pl.BlockSpec(shape, lambda g: (0,) * len(shape))


def on_device(
    tile_pixels, tile_cell, agg_cot, dw_weight, norm_gain, up_weight, proj_weight,
    layer_scale, ds_gain, ds_weight, agg_weight,
):
    channels = dw_weight.shape[1]
    hid = up_weight.shape[1]
    width = ds_weight.shape[1]
    bands = lax.axis_size("slide")
    sources = bands * lax.axis_size("chan")
    chunks = sources // 8
    pixch = tile_pixels.shape[2]
    out_rows = agg_cot.shape[1]
    e_half = agg_weight.shape[2]
    cols = agg_cot.shape[3]
    blocks = CAP * chunks
    total_rows = out_rows * bands * lax.axis_size("rep") * cols
    loss_scale = 1.0 / math.sqrt(total_rows)
    chan = lax.axis_index("chan").astype(jnp.int32)[None]
    gain = norm_gain[None]
    scale = layer_scale[None]
    low_gain = ds_gain[None]
    proj_turned = proj_weight.T
    ds_turned = ds_weight.T

    packed, top_cot = pl.pallas_call(
        pack_kernel,
        grid=(1,),
        out_shape=(
            jax.ShapeDtypeStruct((sources, WIRE_ROWS, 128), BF16),
            jax.ShapeDtypeStruct((e_half, cols), BF16),
        ),
        in_specs=[
            SMEM,
            pl.BlockSpec((None,) + tile_pixels.shape[1:], lambda i: (0, 0, 0)),
            pl.BlockSpec((None, None, e_half, cols), lambda i: (0, 0, 0, 0)),
        ],
        out_specs=(whole((sources, WIRE_ROWS, 128)), whole((e_half, cols))),
        scratch_shapes=[
            pltpu.VMEM((tile_pixels.shape[1], WIRE_ROWS, 128), F32),
            pltpu.VMEM((sources, 8, 128), F32),
        ],
        cost_estimate=takes(1.5),
        name="pack",
    )(tile_cell, tile_pixels, agg_cot)
    below_cot = shifted(top_cot, "slide", -1)
    packed, own_weight = lax.optimization_barrier((packed, agg_weight))
    peer_weight = swapped(own_weight, "chan", 1)
    got = lax.all_to_all(packed, ("slide", "chan"), split_axis=0, concat_axis=0, tiled=True)

    key, cots_own, cots_send = pl.pallas_call(
        patch_kernel,
        out_shape=(
            jax.ShapeDtypeStruct((blocks * COT_ROWS, cols), F32),
            jax.ShapeDtypeStruct((chunks * COT_ROWS, 128), BF16),
            jax.ShapeDtypeStruct((chunks * COT_ROWS, 128), BF16),
        ),
        in_specs=[
            SMEM,
            pl.BlockSpec((sources, 8, 128), lambda i: (0, pixch // 1024, 0)),
            pl.BlockSpec((None, out_rows, e_half, cols), lambda i: (0, 0, 0, 0)),
            whole((e_half, cols)),
        ],
        out_specs=(
            whole((blocks * COT_ROWS, cols)),
            whole((chunks * COT_ROWS, 128)),
            whole((chunks * COT_ROWS, 128)),
        ),
        grid=(1,),
        scratch_shapes=[pltpu.VMEM((sources, 8, 128), F32)],
        compiler_params=params_of(),
        cost_estimate=takes(1.2),
        name="patch",
    )(chan, got, agg_cot, below_cot)
    cots_peer = swapped(cots_send, "chan", 1)
    cots_own = cots_own.reshape(chunks, COT_ROWS, 128)
    cots_peer = cots_peer.reshape(chunks, COT_ROWS, 128)

    rows = PIX * 8
    pixel_spec = pl.BlockSpec((8, WIRE_ROWS, 128), lambda g: (g, 0, 0))
    pixel_scratch = [pltpu.VMEM((8, WIRE_ROWS, 128), F32), pltpu.VMEM((8, pixch), F32)]

    def chunk(*shape):
        return pl.BlockSpec((None,) + shape, lambda g: (g,) + (0,) * len(shape))

    feats, hat1, rstd1, hat2, rstd2, hidden, slope, patches = pl.pallas_call(
        stem_kernel,
        grid=(chunks,),
        out_shape=(
            jax.ShapeDtypeStruct((chunks, FEAT_ROWS, 128), BF16),
            jax.ShapeDtypeStruct((chunks, rows, channels), F32),
            jax.ShapeDtypeStruct((chunks, rows, 1), F32),
            jax.ShapeDtypeStruct((chunks, rows, channels), F32),
            jax.ShapeDtypeStruct((chunks, rows, 1), F32),
            jax.ShapeDtypeStruct((chunks, rows, hid), BF16),
            jax.ShapeDtypeStruct((chunks, rows, hid), F32),
            jax.ShapeDtypeStruct((chunks, 128, 4 * channels), BF16),
        ),
        in_specs=[
            pixel_spec,
            whole(dw_weight.shape), whole((1, channels)), whole(up_weight.shape),
            whole(proj_turned.shape), whole((1, channels)), whole((1, channels)),
            whole(ds_turned.shape),
        ],
        out_specs=(
            chunk(FEAT_ROWS, 128), chunk(rows, channels), chunk(rows, 1), chunk(rows, channels),
            chunk(rows, 1), chunk(rows, hid), chunk(rows, hid), chunk(128, 4 * channels),
        ),
        scratch_shapes=[
            pltpu.VMEM((SIDE + 6, SIDE + 6, 8, channels), F32),
            pltpu.VMEM((SIDE, SIDE, 8, channels), F32),
            pltpu.VMEM((SIDE // 2, 2, SIDE // 2, 2, 8, channels), F32),
            pltpu.VMEM((128, 4 * channels), F32),
            *pixel_scratch,
        ],
        compiler_params=params_of(),
        cost_estimate=takes(2.7),
        name="stem",
    )(got, dw_weight, gain, up_weight, proj_turned, scale, low_gain, ds_turned)

    feats_band = jnp.concatenate([feats, swapped(feats, "chan", 1)], axis=0)
    spread, below = pl.pallas_call(
        lambda *refs: spread_kernel(*refs, last=out_rows),
        grid=(blocks,),
        out_shape=(
            jax.ShapeDtypeStruct((blocks * 72, e_half), F32),
            jax.ShapeDtypeStruct((e_half, cols), F32),
        ),
        in_specs=[
            chunk(FEAT_ROWS, 128), whole(agg_weight.shape),
            pl.BlockSpec((72, cols), lambda g: (g, 0)),
        ],
        out_specs=(pl.BlockSpec((72, e_half), lambda g: (g, 0)), whole((e_half, cols))),
        compiler_params=params_of(),
        cost_estimate=takes(1.0),
        name="spread",
    )(feats_band, agg_weight, key)
    tile_blocks = jnp.concatenate([feats, cots_own, cots_peer], axis=1)
    gather = chunks == 1
    near = far = tile_blocks
    place = jnp.zeros((1,), jnp.int32)
    spans = [("slide", 1 << n) for n in reversed(range(bands.bit_length() - 1))]
    spans += [("rep", 1 << n) for n in range(lax.axis_size("rep").bit_length() - 1)]

    def widen(n, near, place):
        axis, step = spans[n]
        bit = (lax.axis_index(axis).astype(jnp.int32) // step) % 2
        return swapped(near, axis, step), place + bit * (1 << n)

    if gather:
        far, place = widen(0, near, place)
        near = jnp.concatenate([near, far], axis=0)

    keep, send = pl.pallas_call(
        lambda *refs: back_kernel(*refs, scale=loss_scale),
        grid=(chunks,),
        out_shape=(
            jax.ShapeDtypeStruct((HALF_ROWS, 128), F32),
            jax.ShapeDtypeStruct((HALF_ROWS, 128), BF16),
        ),
        in_specs=[
            SMEM, chunk(COT_ROWS, 128), chunk(COT_ROWS, 128),
            whole(agg_weight.shape), whole(agg_weight.shape), pixel_spec,
            chunk(rows, channels), chunk(rows, 1), chunk(rows, channels), chunk(rows, 1),
            chunk(rows, hid), chunk(rows, hid), chunk(128, 4 * channels),
            whole((1, channels)), whole(up_weight.shape), whole(proj_turned.shape),
            whole((1, channels)), whole((1, channels)), whole(ds_turned.shape),
        ],
        out_specs=(whole((HALF_ROWS, 128)), whole((HALF_ROWS, 128))),
        scratch_shapes=[
            pltpu.VMEM((SIDE + 6, SIDE + 6, 8, channels), F32),
            pltpu.VMEM((SIDE // 2, 2, SIDE // 2, 2, 8, channels), F32),
            pltpu.VMEM((SIDE, SIDE, 8, channels), F32),
            pltpu.VMEM((7, 7, 8, channels), F32),
            pltpu.VMEM(ds_turned.shape, F32),
            pltpu.VMEM(up_weight.shape, F32),
            pltpu.VMEM(proj_turned.shape, F32),
            pltpu.VMEM((2 * HALF_ROWS, 128), F32),
            *pixel_scratch,
            pltpu.VMEM((9, width, 256), BF16),
        ],
        compiler_params=params_of(),
        cost_estimate=takes(3.7),
        name="stem_back",
    )(
        chan, cots_own, cots_peer, agg_weight, peer_weight, got,
        hat1, rstd1, hat2, rstd2, hidden, slope, patches,
        gain, up_weight, proj_turned, scale, low_gain, ds_turned,
    )

    part = keep + swapped(send, "chan", 1).astype(F32)
    if gather:
        part, near, spread, below = lax.optimization_barrier((part, near, spread, below))
    above = shifted(below, "slide", 1)
    for n in range(1, len(spans) if gather else 0):
        if n == len(spans) - 1:
            near, above = lax.optimization_barrier((near, above))
        far, place = widen(n, near, place)
        if n < len(spans) - 1:
            near = jnp.concatenate([near, far], axis=0)
    map_call = pl.pallas_call(
        map_kernel,
        out_shape=jax.ShapeDtypeStruct((out_rows, e_half, cols), BF16),
        in_specs=[VMEM, VMEM, VMEM],
        out_specs=VMEM,
        compiler_params=pltpu.CompilerParams(vmem_limit_bytes=24 << 20),
        cost_estimate=takes(3.5),
        name="agg_map",
    )
    agg_map = map_call(spread, key, above)

    steps = []
    for axis in ("rep", "slide"):
        for n in reversed(range(lax.axis_size(axis).bit_length() - 1)):
            steps.append((axis, 1 << n))
    for n, (axis, step) in enumerate(steps):
        wire = part.astype(BF16)
        if n == len(steps) - 1:
            wire, agg_map = lax.optimization_barrier((wire, agg_map))
        part = wire.astype(F32) + swapped(wire, axis, step).astype(F32)

    count = 2 * near.shape[0] if gather else chunks
    per = count if gather else 1
    near_count = near.shape[0] if gather else 1
    agg_keep, agg_send = pl.pallas_call(
        lambda *refs: weight_kernel(*refs, scale=loss_scale),
        grid=(count // per,),
        out_shape=(
            jax.ShapeDtypeStruct((9, width, e_half), F32),
            jax.ShapeDtypeStruct((9, width, e_half), BF16),
        ),
        in_specs=[
            SMEM,
            pl.BlockSpec((near_count, BLOCK_ROWS, 128), lambda g: (g, 0, 0)),
            pl.BlockSpec((near_count, BLOCK_ROWS, 128), lambda g: (g, 0, 0)),
        ],
        out_specs=(whole((9, width, e_half)), whole((9, width, e_half))),
        scratch_shapes=[
            pltpu.VMEM((16, per * 8, width), F32),
            pltpu.VMEM((9, per * 8, 256), F32),
            pltpu.VMEM((9, width, e_half), F32),
        ],
        compiler_params=params_of(),
        cost_estimate=takes(1.4),
        name="agg_weight_grad",
    )(place, near, far)
    agg_grad = agg_keep + swapped(agg_send, "chan", 1).astype(F32)
    if not gather:
        agg_grad = lax.psum(agg_grad, ("slide", "rep"))

    part = part.astype(BF16)
    peer_part = swapped(part, "chan", 1)
    part, agg_grad = lax.optimization_barrier((part, agg_grad))
    dw_grad, up_grad, proj_grad, ds_grad = pl.pallas_call(
        unpack_kernel,
        out_shape=(
            jax.ShapeDtypeStruct(dw_weight.shape, F32),
            jax.ShapeDtypeStruct(up_weight.shape, F32),
            jax.ShapeDtypeStruct(proj_turned.shape, F32),
            jax.ShapeDtypeStruct(ds_turned.shape, F32),
        ),
        in_specs=[SMEM, VMEM, VMEM],
        out_specs=(VMEM, VMEM, VMEM, VMEM),
        scratch_shapes=[pltpu.VMEM((2 * HALF_ROWS, 128), F32)],
        compiler_params=pltpu.CompilerParams(vmem_limit_bytes=24 << 20),
        cost_estimate=takes(1.5),
        name="unpack",
    )(chan, part, peer_part)
    proj_grad = proj_grad.T
    ds_grad = ds_grad.T
    return (agg_map[None], agg_grad, dw_grad, up_grad, proj_grad, ds_grad)


def solution(mesh):
    in_specs = (
        P(("groups", "rep"), ("slide", "chan"), None),
        P(("groups", "rep"), ("slide", "chan")),
        P(("groups", "rep"), "slide", "chan", None),
        P(), P(), P(), P(), P(), P(), P(),
        P(None, None, "chan"),
    )
    out_specs = (
        P(("groups", "rep"), "slide", "chan", None),
        P("groups", None, "chan"),
        P("groups", None),
        P("groups", None),
        P("groups", None),
        P("groups", None),
    )
    return jax.shard_map(
        on_device, mesh=mesh, in_specs=in_specs, out_specs=out_specs, check_vma=False
    )
```

```python
import math

import jax
import jax.numpy as jnp
from jax import lax
from jax.experimental import pallas as pl
from jax.experimental.pallas import tpu as pltpu
from jax.sharding import PartitionSpec as P

SIDE = 8
CAP = 2
PIX = SIDE * SIDE
HALF_ROWS = 608
FEAT_ROWS = 192
COT_ROWS = 72
WIRE_ROWS = 56
BLOCK_ROWS = FEAT_ROWS + 2 * COT_ROWS
F32 = jnp.float32
BF16 = jnp.bfloat16
VMEM = pl.BlockSpec(memory_space=pltpu.VMEM)
SMEM = pl.BlockSpec(memory_space=pltpu.SMEM)


def params_of(steps=1):
    return pltpu.CompilerParams(
        dimension_semantics=("arbitrary",) * steps, vmem_limit_bytes=24 << 20
    )


def takes(microseconds):
    return pl.CostEstimate(
        flops=0, transcendentals=0, bytes_accessed=int(microseconds * 3.69e6)
    )


def nn(left, right):
    return lax.dot_general(left, right, (((1,), (0,)), ((), ())), preferred_element_type=F32)


def nt(left, right):
    return lax.dot_general(left, right, (((1,), (1,)), ((), ())), preferred_element_type=F32)


def tn(left, right):
    return lax.dot_general(left, right, (((0,), (0,)), ((), ())), preferred_element_type=F32)


def shifted(value, axis, steps):
    count = lax.axis_size(axis)
    first, last = (max(0, -steps), min(count, count - steps))
    return lax.ppermute(value, axis, [(source, source + steps) for source in range(first, last)])


def swapped(value, axis, step):
    count = lax.axis_size(axis)
    return lax.ppermute(value, axis, [(place, place ^ step) for place in range(count)])


def reach(tap):
    return (1, 2) if tap == 0 else (0, 1)


def pack_kernel(cells_ref, pixels_ref, row_ref, out_ref, below_ref, wide_ref, note_ref):
    slots = pixels_ref.shape[0]
    rows = out_ref.shape[0]
    pixch = pixels_ref.shape[1]
    cells = [cells_ref[0, t] for t in range(slots)]
    live = [cell >= 0 for cell in cells]
    bands = [cell >> 9 for cell in cells]
    places = []
    for t in range(slots):
        rank = jnp.int32(0)
        for s in range(t):
            rank = rank + ((bands[s] == bands[t]) & live[s]).astype(jnp.int32)
        places.append(jnp.where(live[t], bands[t] * CAP + rank, -1))
    below_ref[...] = row_ref[...].astype(BF16)
    pixels = pixels_ref[...].astype(F32)
    for n in range(pixch // 128):
        wide_ref[:, n, :] = pixels[:, 128 * n : 128 * n + 128]
    wide_ref[:, pixch // 128 :, :] = jnp.zeros_like(wide_ref[:, pixch // 128 :, :])
    out_ref[...] = jnp.zeros_like(out_ref)
    for t in range(slots):

        @pl.when(live[t])
        def _():
            out_ref[jnp.maximum(places[t], 0)] = wide_ref[t].astype(BF16)

    lane = lax.broadcasted_iota(jnp.int32, (rows, 128), 1)
    base = (lax.broadcasted_iota(jnp.int32, (rows, 128), 0) // CAP) * CAP
    notes = jnp.zeros((rows, 128), F32)
    for t in range(slots):
        own_row = ((cells[t] >> 6) & 7).astype(F32)
        own_col = (cells[t] & 63).astype(F32)
        for rank in range(CAP):
            hit = base + rank == places[t]
            for at, value in enumerate((own_row, own_col, jnp.float32(1.0))):
                notes = jnp.where(hit & (lane == 3 * rank + at), value, notes)
    note_ref[...] = jnp.zeros_like(note_ref)
    note_ref[:, 0, :] = notes
    out_ref[:, pixch // 128 :, :] = note_ref[...].astype(BF16)


def patch_kernel(chan_ref, meta_ref, cot_ref, below_ref, key_ref, own_ref, send_ref, meta_f32):
    sources = meta_ref.shape[0]
    chunks = sources // 8
    out_rows, e_half, _ = cot_ref.shape
    meta_f32[...] = meta_ref[...].astype(F32)
    meta = meta_f32[:, 0, :]
    first = chan_ref[0] == 0
    lane = lax.broadcasted_iota(jnp.int32, (8, 128), 1).astype(F32)
    blocks = []
    for mine in (True, False):
        for chunk in range(chunks):
            part = meta[chunk * 8 : chunk * 8 + 8]
            low = [jnp.broadcast_to(part[:, n : n + 1], (8, 128)) for n in range(3)]
            high = [jnp.broadcast_to(part[:, n : n + 1], (8, 128)) for n in range(3, 6)]
            row, col, valid = (
                jnp.where(first == mine, one, two) for one, two in zip(low, high)
            )
            for u in range(3):
                for v in range(3):
                    hit = (lane == 2.0 * col + v) & (valid > 0.5)
                    blocks.append(jnp.where(hit, 2.0 * row + u, -1.0))
    key = jnp.concatenate(blocks, axis=0)
    key_ref[...] = key

    total = jnp.zeros((key.shape[0], e_half), F32)
    for first_row in range(0, out_rows, 4):
        rows = range(first_row, first_row + 4)
        picks = [(key == float(o)).astype(F32).astype(BF16) for o in rows]
        cots = [cot_ref[o].astype(BF16) for o in rows]
        total = total + nt(jnp.concatenate(picks, axis=1), jnp.concatenate(cots, axis=1))
    pick = (key == float(out_rows)).astype(F32).astype(BF16)
    total = total + nt(pick, below_ref[...])
    half = total.shape[0] // 2
    own_ref[...] = jnp.zeros_like(own_ref)
    send_ref[...] = jnp.zeros_like(send_ref)
    own_ref[:, :e_half] = total[:half].astype(BF16)
    send_ref[:, :e_half] = total[half:].astype(BF16)


def center_of(values):
    center = values - jnp.mean(values, axis=-1, keepdims=True)
    rstd = lax.rsqrt(jnp.mean(center * center, axis=-1, keepdims=True) + 1e-06)
    return center * rstd, rstd


def fill_padded(padded_ref, got_ref, wide_ref, pixels_ref, channels):
    wide_ref[...] = got_ref[...].astype(F32)
    for n in range(pixels_ref.shape[1] // 128):
        pixels_ref[:, 128 * n : 128 * n + 128] = wide_ref[:, n, :]
    padded_ref[...] = jnp.zeros_like(padded_ref)
    for i in range(SIDE):
        for j in range(SIDE):
            at = (i * SIDE + j) * channels
            padded_ref[i + 3, j + 3] = pixels_ref[:, at : at + channels]


def stem_kernel(
    got_ref, dw_ref, gain_ref, up_ref, proj_ref, scale_ref, ds_gain_ref, ds_ref,
    feat_ref, hat1_ref, rstd1_ref, hat2_ref, rstd2_ref, hidden_ref, slope_ref, patch_ref,
    padded_ref, spatial_ref, low_ref, patch_f32, wide_ref, pixels_ref,
):
    channels = dw_ref.shape[1]
    fill_padded(padded_ref, got_ref, wide_ref, pixels_ref, channels)

    for i in range(SIDE):
        total = jnp.zeros((SIDE, 8, channels), F32)
        for a in range(max(0, 3 - i), min(7, SIDE + 3 - i)):
            for b in range(7):
                weight = dw_ref[7 * a + b : 7 * a + b + 1, :].reshape(1, 1, channels)
                total = total + weight * padded_ref[i + a, b : b + SIDE]
        spatial_ref[i] = total
    hat1, rstd1 = center_of(spatial_ref[...].reshape(PIX * 8, channels))
    hat1_ref[...] = hat1
    rstd1_ref[...] = rstd1
    normed = (hat1 * gain_ref[...]).astype(BF16)
    before = nn(normed, up_ref[...])
    cdf = 0.5 * (1.0 + lax.erf(before * math.sqrt(0.5)))
    pdf = jnp.exp(-0.5 * before * before) * (1.0 / math.sqrt(2.0 * math.pi))
    hidden = (before * cdf).astype(BF16)
    hidden_ref[...] = hidden
    slope_ref[...] = cdf + before * pdf
    branch = nt(hidden, proj_ref[...])
    inputs = padded_ref[3 : 3 + SIDE, 3 : 3 + SIDE].reshape(PIX * 8, channels)
    hat2, rstd2 = center_of(inputs + scale_ref[...] * branch)
    hat2_ref[...] = hat2
    rstd2_ref[...] = rstd2
    low_ref[...] = (hat2 * ds_gain_ref[...]).reshape(low_ref.shape)
    half = SIDE // 2
    for di in range(2):
        for dj in range(2):
            at = (2 * di + dj) * channels
            patch_f32[:, at : at + channels] = low_ref[:, di, :, dj].reshape(-1, channels)
    patches = patch_f32[...].astype(BF16)
    patch_ref[...] = patches
    total = nt(patches, ds_ref[...])
    rows = total.shape[0]
    feat_ref[0:rows] = total[:, 0:128].astype(BF16)
    rest = jnp.concatenate([total[: rows // 2, 128:192], total[rows // 2 :, 128:192]], axis=1)
    feat_ref[rows:] = rest.astype(BF16)


def unfold(block):
    rest = block[128:]
    return jnp.concatenate(
        [block[:128], jnp.concatenate([rest[:, :64], rest[:, 64:]], axis=0)], axis=1
    )


def back_kernel(
    chan_ref, own_ref, peer_ref, w_own_ref, w_peer_ref, got_ref,
    hat1_ref, rstd1_ref, hat2_ref, rstd2_ref, hidden_ref, slope_ref, patch_ref,
    gain_ref, up_ref, proj_ref, scale_ref, ds_gain_ref, ds_ref,
    keep_ref, send_ref,
    padded_ref, dlow_ref, dspatial_ref, dw_ref, ds_acc, up_acc, proj_acc, pack_ref,
    wide_ref, pixels_ref, w_ref,
    *, scale,
):
    channels = gain_ref.shape[1]
    half = SIDE // 2
    step = pl.program_id(0)

    @pl.when(step == 0)
    def _():
        dw_ref[...] = jnp.zeros_like(dw_ref)
        ds_acc[...] = jnp.zeros_like(ds_acc)
        up_acc[...] = jnp.zeros_like(up_acc)
        proj_acc[...] = jnp.zeros_like(proj_acc)

    e_half = w_own_ref.shape[2]
    w_ref[...] = jnp.zeros_like(w_ref)
    w_ref[:, :, 0:e_half] = w_own_ref[...]
    w_ref[:, :, 128 : 128 + e_half] = w_peer_ref[...]
    cots = jnp.concatenate([own_ref[...], peer_ref[...]], axis=1)
    grads = {}
    for a in range(3):
        for b in range(3):
            out = nt(cots, w_ref[3 * a + b])
            for u in reach(a):
                for v in reach(b):
                    at = (2 * u + a - 1) * half + 2 * v + b - 1
                    row = 8 * (3 * u + v)
                    piece = out[row : row + 8]
                    grads[at] = grads[at] + piece if at in grads else piece
    dfeat = jnp.concatenate([grads[at] for at in range(half * half)], axis=0) * scale
    dfeat = dfeat.astype(BF16)

    hat2 = hat2_ref[...]
    ds_acc[...] += tn(dfeat, patch_ref[...])
    back = nn(dfeat, ds_ref[...])
    for di in range(2):
        for dj in range(2):
            at = (2 * di + dj) * channels
            dlow_ref[:, di, :, dj] = back[:, at : at + channels].reshape(half, half, 8, channels)
    dhat2 = dlow_ref[...].reshape(PIX * 8, channels) * ds_gain_ref[...]
    mean_a = jnp.mean(dhat2, axis=-1, keepdims=True)
    mean_b = jnp.mean(dhat2 * hat2, axis=-1, keepdims=True)
    dmixed = rstd2_ref[...] * (dhat2 - mean_a - hat2 * mean_b)
    dbranch = (dmixed * scale_ref[...]).astype(BF16)
    proj_acc[...] += tn(dbranch, hidden_ref[...])
    dhidden = nn(dbranch, proj_ref[...])
    dbefore = (dhidden * slope_ref[...]).astype(BF16)
    hat1 = hat1_ref[...]
    normed = (hat1 * gain_ref[...]).astype(BF16)
    up_acc[...] += tn(normed, dbefore)
    dhat1 = nt(dbefore, up_ref[...]) * gain_ref[...]
    mean_a = jnp.mean(dhat1, axis=-1, keepdims=True)
    mean_b = jnp.mean(dhat1 * hat1, axis=-1, keepdims=True)
    dspatial = rstd1_ref[...] * (dhat1 - mean_a - hat1 * mean_b)
    dspatial_ref[...] = dspatial.reshape(SIDE, SIDE, 8, channels)
    fill_padded(padded_ref, got_ref, wide_ref, pixels_ref, channels)

    for a in range(7):
        totals = [jnp.zeros((8, channels), F32) for _ in range(7)]
        for i in range(max(0, 3 - a), min(SIDE, SIDE + 3 - a)):
            for b in range(7):
                low, high = max(0, 3 - b), min(SIDE, SIDE + 3 - b)
                product = padded_ref[i + a, b + low : b + high] * dspatial_ref[i, low:high]
                totals[b] = totals[b] + jnp.sum(product, axis=0)
        for b in range(7):
            dw_ref[a, b] += totals[b]

    @pl.when(step == pl.num_programs(0) - 1)
    def _():
        pack_ref[...] = jnp.zeros_like(pack_ref)
        for n in range(3):
            lanes = slice(128 * n, 128 * n + 128)
            pack_ref[192 * n : 192 * n + 192, :] = ds_acc[:, lanes]
            pack_ref[576 + 96 * n : 672 + 96 * n, :] = up_acc[:, lanes]
            pack_ref[864 + 96 * n : 960 + 96 * n, :] = proj_acc[:, lanes]
        pack_ref[1152:1201, 0:channels] = jnp.sum(dw_ref[...], axis=2).reshape(49, channels)
        mine = pl.multiple_of(chan_ref[0] * HALF_ROWS, 8)
        other = pl.multiple_of((1 - chan_ref[0]) * HALF_ROWS, 8)
        keep_ref[...] = pack_ref[pl.ds(mine, HALF_ROWS), :]
        send_ref[...] = pack_ref[pl.ds(other, HALF_ROWS), :].astype(BF16)


def unpack_kernel(chan_ref, own_ref, peer_ref, dw_ref, up_ref, proj_ref, ds_ref, pack_ref):
    channels = dw_ref.shape[1]
    mine = pl.multiple_of(chan_ref[0] * HALF_ROWS, 8)
    other = pl.multiple_of((1 - chan_ref[0]) * HALF_ROWS, 8)
    pack_ref[pl.ds(mine, HALF_ROWS), :] = own_ref[...].astype(F32)
    pack_ref[pl.ds(other, HALF_ROWS), :] = peer_ref[...].astype(F32)
    for n in range(3):
        lanes = slice(128 * n, 128 * n + 128)
        ds_ref[:, lanes] = pack_ref[192 * n : 192 * n + 192, :]
        up_ref[:, lanes] = pack_ref[576 + 96 * n : 672 + 96 * n, :]
        proj_ref[:, lanes] = pack_ref[864 + 96 * n : 960 + 96 * n, :]
    dw_ref[...] = pack_ref[1152:1201, 0:channels]


def spread_kernel(feat_ref, w_ref, key_ref, y_ref, below_ref, *, last):
    width = w_ref.shape[1]
    feats = unfold(feat_ref[...].astype(F32)).reshape(16, 8, width)
    outs = {}
    for a in range(3):
        for b in range(3):
            places = [(u, v) for u in reach(a) for v in reach(b)]
            left = jnp.concatenate(
                [feats[(2 * u + a - 1) * 4 + 2 * v + b - 1] for u, v in places], axis=0
            ).astype(BF16)
            out = nn(left, w_ref[3 * a + b])
            for n, (u, v) in enumerate(places):
                piece = out[8 * n : 8 * n + 8]
                at = 3 * u + v
                outs[at] = outs[at] + piece if at in outs else piece
    total = jnp.concatenate([outs[at] for at in range(9)], axis=0)
    y_ref[...] = total
    pick = (key_ref[...] == float(last)).astype(F32).astype(BF16)
    high = total.astype(BF16)
    rest = (total - high.astype(F32)).astype(BF16)

    @pl.when(pl.program_id(0) == 0)
    def _():
        below_ref[...] = jnp.zeros_like(below_ref)

    below_ref[...] += tn(high, pick) + tn(rest, pick)


def map_kernel(y_ref, key_ref, above_ref, out_ref):
    out_rows, width, _ = out_ref.shape
    turned = y_ref[...].T
    high = turned.astype(BF16)
    rest = (turned - high.astype(F32)).astype(BF16)
    key = key_ref[...]

    def row_of(o):
        pick = (key == o).astype(F32).astype(BF16)
        return nn(high, pick) + nn(rest, pick)

    out_ref[0] = (row_of(0.0) + above_ref[...]).astype(BF16)

    def step(o, carry):
        out_ref[o] = row_of(o.astype(F32)).astype(BF16)
        return carry

    lax.fori_loop(1, out_rows, step, 0)


def weight_kernel(
    place_ref, near_ref, far_ref, keep_ref, send_ref, feat_ref, cot_ref, send_acc, *, scale
):
    near = near_ref.shape[0]
    members = feat_ref.shape[1] // 8
    width, e_half = keep_ref.shape[1:]
    step = pl.program_id(0)

    @pl.when(step == 0)
    def _():
        keep_ref[...] = jnp.zeros_like(keep_ref)
        send_acc[...] = jnp.zeros_like(send_acc)

    def take(member, block):
        block = block.astype(F32)
        feat_ref[:, 8 * member : 8 * member + 8] = unfold(block[:FEAT_ROWS]).reshape(16, 8, width)
        own = block[FEAT_ROWS : FEAT_ROWS + COT_ROWS].reshape(9, 8, 128)
        peer = block[FEAT_ROWS + COT_ROWS :].reshape(9, 8, 128)
        cot_ref[:, 8 * member : 8 * member + 8, 0:128] = own
        cot_ref[:, 8 * member : 8 * member + 8, 128:256] = peer

    for member in range(members):
        at = place_ref[0] ^ member

        @pl.when(at < near)
        def _():
            take(member, near_ref[jnp.minimum(at, near - 1)])

        if members > near:

            @pl.when(at >= near)
            def _():
                take(member, far_ref[jnp.maximum(at - near, 0)])

    for a in range(3):
        for b in range(3):
            places = [(u, v) for u in reach(a) for v in reach(b)]
            left = jnp.concatenate(
                [feat_ref[(2 * u + a - 1) * 4 + 2 * v + b - 1] for u, v in places], axis=0
            ).astype(BF16)
            right = jnp.concatenate([cot_ref[3 * u + v] for u, v in places], axis=0).astype(BF16)
            total = tn(left, right) * scale
            keep_ref[3 * a + b] += total[:, :e_half]
            send_acc[3 * a + b] += total[:, 128 : 128 + e_half]

    @pl.when(step == pl.num_programs(0) - 1)
    def _():
        send_ref[...] = send_acc[...].astype(BF16)


def whole(shape):
    return pl.BlockSpec(shape, lambda g: (0,) * len(shape))


def on_device(
    tile_pixels, tile_cell, agg_cot, dw_weight, norm_gain, up_weight, proj_weight,
    layer_scale, ds_gain, ds_weight, agg_weight,
):
    channels = dw_weight.shape[1]
    hid = up_weight.shape[1]
    width = ds_weight.shape[1]
    bands = lax.axis_size("slide")
    sources = bands * lax.axis_size("chan")
    chunks = sources // 8
    pixch = tile_pixels.shape[2]
    out_rows = agg_cot.shape[1]
    e_half = agg_weight.shape[2]
    cols = agg_cot.shape[3]
    blocks = CAP * chunks
    total_rows = out_rows * bands * lax.axis_size("rep") * cols
    loss_scale = 1.0 / math.sqrt(total_rows)
    chan = lax.axis_index("chan").astype(jnp.int32)[None]
    gain = norm_gain[None]
    scale = layer_scale[None]
    low_gain = ds_gain[None]
    proj_turned = proj_weight.T
    ds_turned = ds_weight.T

    packed, top_cot = pl.pallas_call(
        pack_kernel,
        grid=(1,),
        out_shape=(
            jax.ShapeDtypeStruct((sources, WIRE_ROWS, 128), BF16),
            jax.ShapeDtypeStruct((e_half, cols), BF16),
        ),
        in_specs=[
            SMEM,
            pl.BlockSpec((None,) + tile_pixels.shape[1:], lambda i: (0, 0, 0)),
            pl.BlockSpec((None, None, e_half, cols), lambda i: (0, 0, 0, 0)),
        ],
        out_specs=(whole((sources, WIRE_ROWS, 128)), whole((e_half, cols))),
        scratch_shapes=[
            pltpu.VMEM((tile_pixels.shape[1], WIRE_ROWS, 128), F32),
            pltpu.VMEM((sources, 8, 128), F32),
        ],
        cost_estimate=takes(1.5),
        name="pack",
    )(tile_cell, tile_pixels, agg_cot)
    below_cot = shifted(top_cot, "slide", -1)
    packed, own_weight = lax.optimization_barrier((packed, agg_weight))
    peer_weight = swapped(own_weight, "chan", 1)
    got = lax.all_to_all(packed, ("slide", "chan"), split_axis=0, concat_axis=0, tiled=True)

    key, cots_own, cots_send = pl.pallas_call(
        patch_kernel,
        out_shape=(
            jax.ShapeDtypeStruct((blocks * COT_ROWS, cols), F32),
            jax.ShapeDtypeStruct((chunks * COT_ROWS, 128), BF16),
            jax.ShapeDtypeStruct((chunks * COT_ROWS, 128), BF16),
        ),
        in_specs=[
            SMEM,
            pl.BlockSpec((sources, 8, 128), lambda i: (0, pixch // 1024, 0)),
            pl.BlockSpec((None, out_rows, e_half, cols), lambda i: (0, 0, 0, 0)),
            whole((e_half, cols)),
        ],
        out_specs=(
            whole((blocks * COT_ROWS, cols)),
            whole((chunks * COT_ROWS, 128)),
            whole((chunks * COT_ROWS, 128)),
        ),
        grid=(1,),
        scratch_shapes=[pltpu.VMEM((sources, 8, 128), F32)],
        compiler_params=params_of(),
        cost_estimate=takes(1.2),
        name="patch",
    )(chan, got, agg_cot, below_cot)
    cots_peer = swapped(cots_send, "chan", 1)
    cots_own = cots_own.reshape(chunks, COT_ROWS, 128)
    cots_peer = cots_peer.reshape(chunks, COT_ROWS, 128)

    rows = PIX * 8
    pixel_spec = pl.BlockSpec((8, WIRE_ROWS, 128), lambda g: (g, 0, 0))
    pixel_scratch = [pltpu.VMEM((8, WIRE_ROWS, 128), F32), pltpu.VMEM((8, pixch), F32)]

    def chunk(*shape):
        return pl.BlockSpec((None,) + shape, lambda g: (g,) + (0,) * len(shape))

    feats, hat1, rstd1, hat2, rstd2, hidden, slope, patches = pl.pallas_call(
        stem_kernel,
        grid=(chunks,),
        out_shape=(
            jax.ShapeDtypeStruct((chunks, FEAT_ROWS, 128), BF16),
            jax.ShapeDtypeStruct((chunks, rows, channels), F32),
            jax.ShapeDtypeStruct((chunks, rows, 1), F32),
            jax.ShapeDtypeStruct((chunks, rows, channels), F32),
            jax.ShapeDtypeStruct((chunks, rows, 1), F32),
            jax.ShapeDtypeStruct((chunks, rows, hid), BF16),
            jax.ShapeDtypeStruct((chunks, rows, hid), F32),
            jax.ShapeDtypeStruct((chunks, 128, 4 * channels), BF16),
        ),
        in_specs=[
            pixel_spec,
            whole(dw_weight.shape), whole((1, channels)), whole(up_weight.shape),
            whole(proj_turned.shape), whole((1, channels)), whole((1, channels)),
            whole(ds_turned.shape),
        ],
        out_specs=(
            chunk(FEAT_ROWS, 128), chunk(rows, channels), chunk(rows, 1), chunk(rows, channels),
            chunk(rows, 1), chunk(rows, hid), chunk(rows, hid), chunk(128, 4 * channels),
        ),
        scratch_shapes=[
            pltpu.VMEM((SIDE + 6, SIDE + 6, 8, channels), F32),
            pltpu.VMEM((SIDE, SIDE, 8, channels), F32),
            pltpu.VMEM((SIDE // 2, 2, SIDE // 2, 2, 8, channels), F32),
            pltpu.VMEM((128, 4 * channels), F32),
            *pixel_scratch,
        ],
        compiler_params=params_of(),
        cost_estimate=takes(2.7),
        name="stem",
    )(got, dw_weight, gain, up_weight, proj_turned, scale, low_gain, ds_turned)

    feats_band = jnp.concatenate([feats, swapped(feats, "chan", 1)], axis=0)
    spread, below = pl.pallas_call(
        lambda *refs: spread_kernel(*refs, last=out_rows),
        grid=(blocks,),
        out_shape=(
            jax.ShapeDtypeStruct((blocks * 72, e_half), F32),
            jax.ShapeDtypeStruct((e_half, cols), F32),
        ),
        in_specs=[
            chunk(FEAT_ROWS, 128), whole(agg_weight.shape),
            pl.BlockSpec((72, cols), lambda g: (g, 0)),
        ],
        out_specs=(pl.BlockSpec((72, e_half), lambda g: (g, 0)), whole((e_half, cols))),
        compiler_params=params_of(),
        cost_estimate=takes(1.0),
        name="spread",
    )(feats_band, agg_weight, key)
    tile_blocks = jnp.concatenate([feats, cots_own, cots_peer], axis=1)
    gather = chunks == 1
    near = far = tile_blocks
    place = jnp.zeros((1,), jnp.int32)
    spans = [("slide", 1 << n) for n in reversed(range(bands.bit_length() - 1))]
    spans += [("rep", 1 << n) for n in range(lax.axis_size("rep").bit_length() - 1)]

    def widen(n, near, place):
        axis, step = spans[n]
        bit = (lax.axis_index(axis).astype(jnp.int32) // step) % 2
        return swapped(near, axis, step), place + bit * (1 << n)

    if gather:
        far, place = widen(0, near, place)
        near = jnp.concatenate([near, far], axis=0)

    keep, send = pl.pallas_call(
        lambda *refs: back_kernel(*refs, scale=loss_scale),
        grid=(chunks,),
        out_shape=(
            jax.ShapeDtypeStruct((HALF_ROWS, 128), F32),
            jax.ShapeDtypeStruct((HALF_ROWS, 128), BF16),
        ),
        in_specs=[
            SMEM, chunk(COT_ROWS, 128), chunk(COT_ROWS, 128),
            whole(agg_weight.shape), whole(agg_weight.shape), pixel_spec,
            chunk(rows, channels), chunk(rows, 1), chunk(rows, channels), chunk(rows, 1),
            chunk(rows, hid), chunk(rows, hid), chunk(128, 4 * channels),
            whole((1, channels)), whole(up_weight.shape), whole(proj_turned.shape),
            whole((1, channels)), whole((1, channels)), whole(ds_turned.shape),
        ],
        out_specs=(whole((HALF_ROWS, 128)), whole((HALF_ROWS, 128))),
        scratch_shapes=[
            pltpu.VMEM((SIDE + 6, SIDE + 6, 8, channels), F32),
            pltpu.VMEM((SIDE // 2, 2, SIDE // 2, 2, 8, channels), F32),
            pltpu.VMEM((SIDE, SIDE, 8, channels), F32),
            pltpu.VMEM((7, 7, 8, channels), F32),
            pltpu.VMEM(ds_turned.shape, F32),
            pltpu.VMEM(up_weight.shape, F32),
            pltpu.VMEM(proj_turned.shape, F32),
            pltpu.VMEM((2 * HALF_ROWS, 128), F32),
            *pixel_scratch,
            pltpu.VMEM((9, width, 256), BF16),
        ],
        compiler_params=params_of(),
        cost_estimate=takes(3.7),
        name="stem_back",
    )(
        chan, cots_own, cots_peer, agg_weight, peer_weight, got,
        hat1, rstd1, hat2, rstd2, hidden, slope, patches,
        gain, up_weight, proj_turned, scale, low_gain, ds_turned,
    )

    part = keep + swapped(send, "chan", 1).astype(F32)
    if gather:
        part, near, spread, below = lax.optimization_barrier((part, near, spread, below))
    for n in range(1, len(spans) if gather else 0):
        far, place = widen(n, near, place)
        if n < len(spans) - 1:
            near = jnp.concatenate([near, far], axis=0)
    map_call = pl.pallas_call(
        map_kernel,
        out_shape=jax.ShapeDtypeStruct((out_rows, e_half, cols), BF16),
        in_specs=[VMEM, VMEM, VMEM],
        out_specs=VMEM,
        compiler_params=pltpu.CompilerParams(vmem_limit_bytes=24 << 20),
        cost_estimate=takes(3.5),
        name="agg_map",
    )

    steps = []
    for axis in ("rep", "slide"):
        for n in reversed(range(lax.axis_size(axis).bit_length() - 1)):
            steps.append((axis, 1 << n))
    for n, (axis, step) in enumerate(steps):
        wire = part.astype(BF16)
        if n == max(0, len(steps) - 2):
            wire, below = lax.optimization_barrier((wire, below))
            agg_map = map_call(spread, key, shifted(below, "slide", 1))
        if n == len(steps) - 1:
            wire, agg_map = lax.optimization_barrier((wire, agg_map))
        part = wire.astype(F32) + swapped(wire, axis, step).astype(F32)

    count = 2 * near.shape[0] if gather else chunks
    per = count if gather else 1
    near_count = near.shape[0] if gather else 1
    agg_keep, agg_send = pl.pallas_call(
        lambda *refs: weight_kernel(*refs, scale=loss_scale),
        grid=(count // per,),
        out_shape=(
            jax.ShapeDtypeStruct((9, width, e_half), F32),
            jax.ShapeDtypeStruct((9, width, e_half), BF16),
        ),
        in_specs=[
            SMEM,
            pl.BlockSpec((near_count, BLOCK_ROWS, 128), lambda g: (g, 0, 0)),
            pl.BlockSpec((near_count, BLOCK_ROWS, 128), lambda g: (g, 0, 0)),
        ],
        out_specs=(whole((9, width, e_half)), whole((9, width, e_half))),
        scratch_shapes=[
            pltpu.VMEM((16, per * 8, width), F32),
            pltpu.VMEM((9, per * 8, 256), F32),
            pltpu.VMEM((9, width, e_half), F32),
        ],
        compiler_params=params_of(),
        cost_estimate=takes(1.4),
        name="agg_weight_grad",
    )(place, near, far)
    agg_grad = agg_keep + swapped(agg_send, "chan", 1).astype(F32)
    if not gather:
        agg_grad = lax.psum(agg_grad, ("slide", "rep"))

    part = part.astype(BF16)
    peer_part = swapped(part, "chan", 1)
    part, agg_grad = lax.optimization_barrier((part, agg_grad))
    dw_grad, up_grad, proj_grad, ds_grad = pl.pallas_call(
        unpack_kernel,
        out_shape=(
            jax.ShapeDtypeStruct(dw_weight.shape, F32),
            jax.ShapeDtypeStruct(up_weight.shape, F32),
            jax.ShapeDtypeStruct(proj_turned.shape, F32),
            jax.ShapeDtypeStruct(ds_turned.shape, F32),
        ),
        in_specs=[SMEM, VMEM, VMEM],
        out_specs=(VMEM, VMEM, VMEM, VMEM),
        scratch_shapes=[pltpu.VMEM((2 * HALF_ROWS, 128), F32)],
        compiler_params=pltpu.CompilerParams(vmem_limit_bytes=24 << 20),
        cost_estimate=takes(1.5),
        name="unpack",
    )(chan, part, peer_part)
    proj_grad = proj_grad.T
    ds_grad = ds_grad.T
    return (agg_map[None], agg_grad, dw_grad, up_grad, proj_grad, ds_grad)


def solution(mesh):
    in_specs = (
        P(("groups", "rep"), ("slide", "chan"), None),
        P(("groups", "rep"), ("slide", "chan")),
        P(("groups", "rep"), "slide", "chan", None),
        P(), P(), P(), P(), P(), P(), P(),
        P(None, None, "chan"),
    )
    out_specs = (
        P(("groups", "rep"), "slide", "chan", None),
        P("groups", None, "chan"),
        P("groups", None),
        P("groups", None),
        P("groups", None),
        P("groups", None),
    )
    return jax.shard_map(
        on_device, mesh=mesh, in_specs=in_specs, out_specs=out_specs, check_vma=False
    )
```

```python
import math

import jax
import jax.numpy as jnp
from jax import lax
from jax.experimental import pallas as pl
from jax.experimental.pallas import tpu as pltpu
from jax.sharding import PartitionSpec as P

SIDE = 8
CAP = 2
PIX = SIDE * SIDE
HALF_ROWS = 608
FEAT_ROWS = 192
COT_ROWS = 72
WIRE_ROWS = 56
BLOCK_ROWS = FEAT_ROWS + 2 * COT_ROWS
F32 = jnp.float32
BF16 = jnp.bfloat16
VMEM = pl.BlockSpec(memory_space=pltpu.VMEM)
SMEM = pl.BlockSpec(memory_space=pltpu.SMEM)


def params_of(steps=1):
    return pltpu.CompilerParams(
        dimension_semantics=("arbitrary",) * steps, vmem_limit_bytes=24 << 20
    )


def takes(microseconds):
    return pl.CostEstimate(
        flops=0, transcendentals=0, bytes_accessed=int(microseconds * 3.69e6)
    )


def nn(left, right):
    return lax.dot_general(left, right, (((1,), (0,)), ((), ())), preferred_element_type=F32)


def nt(left, right):
    return lax.dot_general(left, right, (((1,), (1,)), ((), ())), preferred_element_type=F32)


def tn(left, right):
    return lax.dot_general(left, right, (((0,), (0,)), ((), ())), preferred_element_type=F32)


def shifted(value, axis, steps):
    count = lax.axis_size(axis)
    first, last = (max(0, -steps), min(count, count - steps))
    return lax.ppermute(value, axis, [(source, source + steps) for source in range(first, last)])


def swapped(value, axis, step):
    count = lax.axis_size(axis)
    return lax.ppermute(value, axis, [(place, place ^ step) for place in range(count)])


def reach(tap):
    return (1, 2) if tap == 0 else (0, 1)


def pack_kernel(cells_ref, pixels_ref, row_ref, out_ref, below_ref, wide_ref, note_ref):
    slots = pixels_ref.shape[0]
    rows = out_ref.shape[0]
    pixch = pixels_ref.shape[1]
    cells = [cells_ref[0, t] for t in range(slots)]
    live = [cell >= 0 for cell in cells]
    bands = [cell >> 9 for cell in cells]
    places = []
    for t in range(slots):
        rank = jnp.int32(0)
        for s in range(t):
            rank = rank + ((bands[s] == bands[t]) & live[s]).astype(jnp.int32)
        places.append(jnp.where(live[t], bands[t] * CAP + rank, -1))
    below_ref[...] = row_ref[...].astype(BF16)
    pixels = pixels_ref[...].astype(F32)
    for n in range(pixch // 128):
        wide_ref[:, n, :] = pixels[:, 128 * n : 128 * n + 128]
    wide_ref[:, pixch // 128 :, :] = jnp.zeros_like(wide_ref[:, pixch // 128 :, :])
    out_ref[...] = jnp.zeros_like(out_ref)
    for t in range(slots):

        @pl.when(live[t])
        def _():
            out_ref[jnp.maximum(places[t], 0)] = wide_ref[t].astype(BF16)

    lane = lax.broadcasted_iota(jnp.int32, (rows, 128), 1)
    base = (lax.broadcasted_iota(jnp.int32, (rows, 128), 0) // CAP) * CAP
    notes = jnp.zeros((rows, 128), F32)
    for t in range(slots):
        own_row = ((cells[t] >> 6) & 7).astype(F32)
        own_col = (cells[t] & 63).astype(F32)
        for rank in range(CAP):
            hit = base + rank == places[t]
            for at, value in enumerate((own_row, own_col, jnp.float32(1.0))):
                notes = jnp.where(hit & (lane == 3 * rank + at), value, notes)
    note_ref[...] = jnp.zeros_like(note_ref)
    note_ref[:, 0, :] = notes
    out_ref[:, pixch // 128 :, :] = note_ref[...].astype(BF16)


def patch_kernel(chan_ref, meta_ref, cot_ref, below_ref, key_ref, own_ref, send_ref, meta_f32):
    sources = meta_ref.shape[0]
    chunks = sources // 8
    out_rows, e_half, _ = cot_ref.shape
    meta_f32[...] = meta_ref[...].astype(F32)
    meta = meta_f32[:, 0, :]
    first = chan_ref[0] == 0
    lane = lax.broadcasted_iota(jnp.int32, (8, 128), 1).astype(F32)
    blocks = []
    for mine in (True, False):
        for chunk in range(chunks):
            part = meta[chunk * 8 : chunk * 8 + 8]
            low = [jnp.broadcast_to(part[:, n : n + 1], (8, 128)) for n in range(3)]
            high = [jnp.broadcast_to(part[:, n : n + 1], (8, 128)) for n in range(3, 6)]
            row, col, valid = (
                jnp.where(first == mine, one, two) for one, two in zip(low, high)
            )
            for u in range(3):
                for v in range(3):
                    hit = (lane == 2.0 * col + v) & (valid > 0.5)
                    blocks.append(jnp.where(hit, 2.0 * row + u, -1.0))
    key = jnp.concatenate(blocks, axis=0)
    key_ref[...] = key

    total = jnp.zeros((key.shape[0], e_half), F32)
    for first_row in range(0, out_rows, 4):
        rows = range(first_row, first_row + 4)
        picks = [(key == float(o)).astype(F32).astype(BF16) for o in rows]
        cots = [cot_ref[o].astype(BF16) for o in rows]
        total = total + nt(jnp.concatenate(picks, axis=1), jnp.concatenate(cots, axis=1))
    pick = (key == float(out_rows)).astype(F32).astype(BF16)
    total = total + nt(pick, below_ref[...])
    half = total.shape[0] // 2
    own_ref[...] = jnp.zeros_like(own_ref)
    send_ref[...] = jnp.zeros_like(send_ref)
    own_ref[:, :e_half] = total[:half].astype(BF16)
    send_ref[:, :e_half] = total[half:].astype(BF16)


def center_of(values):
    center = values - jnp.mean(values, axis=-1, keepdims=True)
    rstd = lax.rsqrt(jnp.mean(center * center, axis=-1, keepdims=True) + 1e-06)
    return center * rstd, rstd


def fill_padded(padded_ref, got_ref, wide_ref, pixels_ref, channels):
    wide_ref[...] = got_ref[...].astype(F32)
    for n in range(pixels_ref.shape[1] // 128):
        pixels_ref[:, 128 * n : 128 * n + 128] = wide_ref[:, n, :]
    padded_ref[...] = jnp.zeros_like(padded_ref)
    for i in range(SIDE):
        for j in range(SIDE):
            at = (i * SIDE + j) * channels
            padded_ref[i + 3, j + 3] = pixels_ref[:, at : at + channels]


def stem_kernel(
    got_ref, dw_ref, gain_ref, up_ref, proj_ref, scale_ref, ds_gain_ref, ds_ref,
    feat_ref, hat1_ref, rstd1_ref, hat2_ref, rstd2_ref, hidden_ref, slope_ref, patch_ref,
    padded_ref, spatial_ref, low_ref, patch_f32, wide_ref, pixels_ref,
):
    channels = dw_ref.shape[1]
    fill_padded(padded_ref, got_ref, wide_ref, pixels_ref, channels)

    for i in range(SIDE):
        total = jnp.zeros((SIDE, 8, channels), F32)
        for a in range(max(0, 3 - i), min(7, SIDE + 3 - i)):
            for b in range(7):
                weight = dw_ref[7 * a + b : 7 * a + b + 1, :].reshape(1, 1, channels)
                total = total + weight * padded_ref[i + a, b : b + SIDE]
        spatial_ref[i] = total
    hat1, rstd1 = center_of(spatial_ref[...].reshape(PIX * 8, channels))
    hat1_ref[...] = hat1
    rstd1_ref[...] = rstd1
    normed = (hat1 * gain_ref[...]).astype(BF16)
    before = nn(normed, up_ref[...])
    cdf = 0.5 * (1.0 + lax.erf(before * math.sqrt(0.5)))
    pdf = jnp.exp(-0.5 * before * before) * (1.0 / math.sqrt(2.0 * math.pi))
    hidden = (before * cdf).astype(BF16)
    hidden_ref[...] = hidden
    slope_ref[...] = cdf + before * pdf
    branch = nt(hidden, proj_ref[...])
    inputs = padded_ref[3 : 3 + SIDE, 3 : 3 + SIDE].reshape(PIX * 8, channels)
    hat2, rstd2 = center_of(inputs + scale_ref[...] * branch)
    hat2_ref[...] = hat2
    rstd2_ref[...] = rstd2
    low_ref[...] = (hat2 * ds_gain_ref[...]).reshape(low_ref.shape)
    half = SIDE // 2
    for di in range(2):
        for dj in range(2):
            at = (2 * di + dj) * channels
            patch_f32[:, at : at + channels] = low_ref[:, di, :, dj].reshape(-1, channels)
    patches = patch_f32[...].astype(BF16)
    patch_ref[...] = patches
    total = nt(patches, ds_ref[...])
    rows = total.shape[0]
    feat_ref[0:rows] = total[:, 0:128].astype(BF16)
    rest = jnp.concatenate([total[: rows // 2, 128:192], total[rows // 2 :, 128:192]], axis=1)
    feat_ref[rows:] = rest.astype(BF16)


def unfold(block):
    rest = block[128:]
    return jnp.concatenate(
        [block[:128], jnp.concatenate([rest[:, :64], rest[:, 64:]], axis=0)], axis=1
    )


def back_kernel(
    chan_ref, own_ref, peer_ref, w_own_ref, w_peer_ref, got_ref,
    hat1_ref, rstd1_ref, hat2_ref, rstd2_ref, hidden_ref, slope_ref, patch_ref,
    gain_ref, up_ref, proj_ref, scale_ref, ds_gain_ref, ds_ref,
    keep_ref, send_ref,
    padded_ref, dlow_ref, dspatial_ref, dw_ref, ds_acc, up_acc, proj_acc, pack_ref,
    wide_ref, pixels_ref, w_ref,
    *, scale,
):
    channels = gain_ref.shape[1]
    half = SIDE // 2
    step = pl.program_id(0)

    @pl.when(step == 0)
    def _():
        dw_ref[...] = jnp.zeros_like(dw_ref)
        ds_acc[...] = jnp.zeros_like(ds_acc)
        up_acc[...] = jnp.zeros_like(up_acc)
        proj_acc[...] = jnp.zeros_like(proj_acc)

    e_half = w_own_ref.shape[2]
    w_ref[...] = jnp.zeros_like(w_ref)
    w_ref[:, :, 0:e_half] = w_own_ref[...]
    w_ref[:, :, 128 : 128 + e_half] = w_peer_ref[...]
    cots = jnp.concatenate([own_ref[...], peer_ref[...]], axis=1)
    grads = {}
    for a in range(3):
        for b in range(3):
            out = nt(cots, w_ref[3 * a + b])
            for u in reach(a):
                for v in reach(b):
                    at = (2 * u + a - 1) * half + 2 * v + b - 1
                    row = 8 * (3 * u + v)
                    piece = out[row : row + 8]
                    grads[at] = grads[at] + piece if at in grads else piece
    dfeat = jnp.concatenate([grads[at] for at in range(half * half)], axis=0) * scale
    dfeat = dfeat.astype(BF16)

    hat2 = hat2_ref[...]
    ds_acc[...] += tn(dfeat, patch_ref[...])
    back = nn(dfeat, ds_ref[...])
    for di in range(2):
        for dj in range(2):
            at = (2 * di + dj) * channels
            dlow_ref[:, di, :, dj] = back[:, at : at + channels].reshape(half, half, 8, channels)
    dhat2 = dlow_ref[...].reshape(PIX * 8, channels) * ds_gain_ref[...]
    mean_a = jnp.mean(dhat2, axis=-1, keepdims=True)
    mean_b = jnp.mean(dhat2 * hat2, axis=-1, keepdims=True)
    dmixed = rstd2_ref[...] * (dhat2 - mean_a - hat2 * mean_b)
    dbranch = (dmixed * scale_ref[...]).astype(BF16)
    proj_acc[...] += tn(dbranch, hidden_ref[...])
    dhidden = nn(dbranch, proj_ref[...])
    dbefore = (dhidden * slope_ref[...]).astype(BF16)
    hat1 = hat1_ref[...]
    normed = (hat1 * gain_ref[...]).astype(BF16)
    up_acc[...] += tn(normed, dbefore)
    dhat1 = nt(dbefore, up_ref[...]) * gain_ref[...]
    mean_a = jnp.mean(dhat1, axis=-1, keepdims=True)
    mean_b = jnp.mean(dhat1 * hat1, axis=-1, keepdims=True)
    dspatial = rstd1_ref[...] * (dhat1 - mean_a - hat1 * mean_b)
    dspatial_ref[...] = dspatial.reshape(SIDE, SIDE, 8, channels)
    fill_padded(padded_ref, got_ref, wide_ref, pixels_ref, channels)

    for a in range(7):
        totals = [jnp.zeros((8, channels), F32) for _ in range(7)]
        for i in range(max(0, 3 - a), min(SIDE, SIDE + 3 - a)):
            for b in range(7):
                low, high = max(0, 3 - b), min(SIDE, SIDE + 3 - b)
                product = padded_ref[i + a, b + low : b + high] * dspatial_ref[i, low:high]
                totals[b] = totals[b] + jnp.sum(product, axis=0)
        for b in range(7):
            dw_ref[a, b] += totals[b]

    @pl.when(step == pl.num_programs(0) - 1)
    def _():
        pack_ref[...] = jnp.zeros_like(pack_ref)
        for n in range(3):
            lanes = slice(128 * n, 128 * n + 128)
            pack_ref[192 * n : 192 * n + 192, :] = ds_acc[:, lanes]
            pack_ref[576 + 96 * n : 672 + 96 * n, :] = up_acc[:, lanes]
            pack_ref[864 + 96 * n : 960 + 96 * n, :] = proj_acc[:, lanes]
        pack_ref[1152:1201, 0:channels] = jnp.sum(dw_ref[...], axis=2).reshape(49, channels)
        mine = pl.multiple_of(chan_ref[0] * HALF_ROWS, 8)
        other = pl.multiple_of((1 - chan_ref[0]) * HALF_ROWS, 8)
        keep_ref[...] = pack_ref[pl.ds(mine, HALF_ROWS), :]
        send_ref[...] = pack_ref[pl.ds(other, HALF_ROWS), :].astype(BF16)


def unpack_kernel(chan_ref, own_ref, peer_ref, dw_ref, up_ref, proj_ref, ds_ref, pack_ref):
    channels = dw_ref.shape[1]
    mine = pl.multiple_of(chan_ref[0] * HALF_ROWS, 8)
    other = pl.multiple_of((1 - chan_ref[0]) * HALF_ROWS, 8)
    pack_ref[pl.ds(mine, HALF_ROWS), :] = own_ref[...].astype(F32)
    pack_ref[pl.ds(other, HALF_ROWS), :] = peer_ref[...].astype(F32)
    for n in range(3):
        lanes = slice(128 * n, 128 * n + 128)
        ds_ref[:, lanes] = pack_ref[192 * n : 192 * n + 192, :]
        up_ref[:, lanes] = pack_ref[576 + 96 * n : 672 + 96 * n, :]
        proj_ref[:, lanes] = pack_ref[864 + 96 * n : 960 + 96 * n, :]
    dw_ref[...] = pack_ref[1152:1201, 0:channels]


def spread_kernel(feat_ref, w_ref, key_ref, y_ref, below_ref, *, last):
    width = w_ref.shape[1]
    feats = unfold(feat_ref[...].astype(F32)).reshape(16, 8, width)
    outs = {}
    for a in range(3):
        for b in range(3):
            places = [(u, v) for u in reach(a) for v in reach(b)]
            left = jnp.concatenate(
                [feats[(2 * u + a - 1) * 4 + 2 * v + b - 1] for u, v in places], axis=0
            ).astype(BF16)
            out = nn(left, w_ref[3 * a + b])
            for n, (u, v) in enumerate(places):
                piece = out[8 * n : 8 * n + 8]
                at = 3 * u + v
                outs[at] = outs[at] + piece if at in outs else piece
    total = jnp.concatenate([outs[at] for at in range(9)], axis=0)
    y_ref[...] = total
    pick = (key_ref[...] == float(last)).astype(F32).astype(BF16)
    high = total.astype(BF16)
    rest = (total - high.astype(F32)).astype(BF16)

    @pl.when(pl.program_id(0) == 0)
    def _():
        below_ref[...] = jnp.zeros_like(below_ref)

    below_ref[...] += tn(high, pick) + tn(rest, pick)


def map_kernel(y_ref, key_ref, above_ref, out_ref):
    out_rows, width, _ = out_ref.shape
    turned = y_ref[...].T
    high = turned.astype(BF16)
    rest = (turned - high.astype(F32)).astype(BF16)
    key = key_ref[...]

    def row_of(o):
        pick = (key == o).astype(F32).astype(BF16)
        return nn(high, pick) + nn(rest, pick)

    out_ref[0] = (row_of(0.0) + above_ref[...]).astype(BF16)

    def step(o, carry):
        out_ref[o] = row_of(o.astype(F32)).astype(BF16)
        return carry

    lax.fori_loop(1, out_rows, step, 0)


def weight_kernel(
    place_ref, near_ref, far_ref, keep_ref, send_ref, feat_ref, cot_ref, send_acc, *, scale
):
    near = near_ref.shape[0]
    members = feat_ref.shape[1] // 8
    width, e_half = keep_ref.shape[1:]
    step = pl.program_id(0)

    @pl.when(step == 0)
    def _():
        keep_ref[...] = jnp.zeros_like(keep_ref)
        send_acc[...] = jnp.zeros_like(send_acc)

    def take(member, block):
        block = block.astype(F32)
        feat_ref[:, 8 * member : 8 * member + 8] = unfold(block[:FEAT_ROWS]).reshape(16, 8, width)
        own = block[FEAT_ROWS : FEAT_ROWS + COT_ROWS].reshape(9, 8, 128)
        peer = block[FEAT_ROWS + COT_ROWS :].reshape(9, 8, 128)
        cot_ref[:, 8 * member : 8 * member + 8, 0:128] = own
        cot_ref[:, 8 * member : 8 * member + 8, 128:256] = peer

    for member in range(members):
        at = place_ref[0] ^ member

        @pl.when(at < near)
        def _():
            take(member, near_ref[jnp.minimum(at, near - 1)])

        if members > near:

            @pl.when(at >= near)
            def _():
                take(member, far_ref[jnp.maximum(at - near, 0)])

    for a in range(3):
        for b in range(3):
            places = [(u, v) for u in reach(a) for v in reach(b)]
            left = jnp.concatenate(
                [feat_ref[(2 * u + a - 1) * 4 + 2 * v + b - 1] for u, v in places], axis=0
            ).astype(BF16)
            right = jnp.concatenate([cot_ref[3 * u + v] for u, v in places], axis=0).astype(BF16)
            total = tn(left, right) * scale
            keep_ref[3 * a + b] += total[:, :e_half]
            send_acc[3 * a + b] += total[:, 128 : 128 + e_half]

    @pl.when(step == pl.num_programs(0) - 1)
    def _():
        send_ref[...] = send_acc[...].astype(BF16)


def whole(shape):
    return pl.BlockSpec(shape, lambda g: (0,) * len(shape))


def on_device(
    tile_pixels, tile_cell, agg_cot, dw_weight, norm_gain, up_weight, proj_weight,
    layer_scale, ds_gain, ds_weight, agg_weight,
):
    channels = dw_weight.shape[1]
    hid = up_weight.shape[1]
    width = ds_weight.shape[1]
    bands = lax.axis_size("slide")
    sources = bands * lax.axis_size("chan")
    chunks = sources // 8
    pixch = tile_pixels.shape[2]
    out_rows = agg_cot.shape[1]
    e_half = agg_weight.shape[2]
    cols = agg_cot.shape[3]
    blocks = CAP * chunks
    total_rows = out_rows * bands * lax.axis_size("rep") * cols
    loss_scale = 1.0 / math.sqrt(total_rows)
    chan = lax.axis_index("chan").astype(jnp.int32)[None]
    gain = norm_gain[None]
    scale = layer_scale[None]
    low_gain = ds_gain[None]
    proj_turned = proj_weight.T
    ds_turned = ds_weight.T

    packed, top_cot = pl.pallas_call(
        pack_kernel,
        grid=(1,),
        out_shape=(
            jax.ShapeDtypeStruct((sources, WIRE_ROWS, 128), BF16),
            jax.ShapeDtypeStruct((e_half, cols), BF16),
        ),
        in_specs=[
            SMEM,
            pl.BlockSpec((None,) + tile_pixels.shape[1:], lambda i: (0, 0, 0)),
            pl.BlockSpec((None, None, e_half, cols), lambda i: (0, 0, 0, 0)),
        ],
        out_specs=(whole((sources, WIRE_ROWS, 128)), whole((e_half, cols))),
        scratch_shapes=[
            pltpu.VMEM((tile_pixels.shape[1], WIRE_ROWS, 128), F32),
            pltpu.VMEM((sources, 8, 128), F32),
        ],
        cost_estimate=takes(1.5),
        name="pack",
    )(tile_cell, tile_pixels, agg_cot)
    below_cot = shifted(top_cot, "slide", -1)
    packed, own_weight = lax.optimization_barrier((packed, agg_weight))
    peer_weight = swapped(own_weight, "chan", 1)
    got = lax.all_to_all(packed, ("slide", "chan"), split_axis=0, concat_axis=0, tiled=True)

    key, cots_own, cots_send = pl.pallas_call(
        patch_kernel,
        out_shape=(
            jax.ShapeDtypeStruct((blocks * COT_ROWS, cols), F32),
            jax.ShapeDtypeStruct((chunks * COT_ROWS, 128), BF16),
            jax.ShapeDtypeStruct((chunks * COT_ROWS, 128), BF16),
        ),
        in_specs=[
            SMEM,
            pl.BlockSpec((sources, 8, 128), lambda i: (0, pixch // 1024, 0)),
            pl.BlockSpec((None, out_rows, e_half, cols), lambda i: (0, 0, 0, 0)),
            whole((e_half, cols)),
        ],
        out_specs=(
            whole((blocks * COT_ROWS, cols)),
            whole((chunks * COT_ROWS, 128)),
            whole((chunks * COT_ROWS, 128)),
        ),
        grid=(1,),
        scratch_shapes=[pltpu.VMEM((sources, 8, 128), F32)],
        compiler_params=params_of(),
        cost_estimate=takes(1.2),
        name="patch",
    )(chan, got, agg_cot, below_cot)
    cots_peer = swapped(cots_send, "chan", 1)
    cots_own = cots_own.reshape(chunks, COT_ROWS, 128)
    cots_peer = cots_peer.reshape(chunks, COT_ROWS, 128)

    rows = PIX * 8
    pixel_spec = pl.BlockSpec((8, WIRE_ROWS, 128), lambda g: (g, 0, 0))
    pixel_scratch = [pltpu.VMEM((8, WIRE_ROWS, 128), F32), pltpu.VMEM((8, pixch), F32)]

    def chunk(*shape):
        return pl.BlockSpec((None,) + shape, lambda g: (g,) + (0,) * len(shape))

    feats, hat1, rstd1, hat2, rstd2, hidden, slope, patches = pl.pallas_call(
        stem_kernel,
        grid=(chunks,),
        out_shape=(
            jax.ShapeDtypeStruct((chunks, FEAT_ROWS, 128), BF16),
            jax.ShapeDtypeStruct((chunks, rows, channels), F32),
            jax.ShapeDtypeStruct((chunks, rows, 1), F32),
            jax.ShapeDtypeStruct((chunks, rows, channels), F32),
            jax.ShapeDtypeStruct((chunks, rows, 1), F32),
            jax.ShapeDtypeStruct((chunks, rows, hid), BF16),
            jax.ShapeDtypeStruct((chunks, rows, hid), F32),
            jax.ShapeDtypeStruct((chunks, 128, 4 * channels), BF16),
        ),
        in_specs=[
            pixel_spec,
            whole(dw_weight.shape), whole((1, channels)), whole(up_weight.shape),
            whole(proj_turned.shape), whole((1, channels)), whole((1, channels)),
            whole(ds_turned.shape),
        ],
        out_specs=(
            chunk(FEAT_ROWS, 128), chunk(rows, channels), chunk(rows, 1), chunk(rows, channels),
            chunk(rows, 1), chunk(rows, hid), chunk(rows, hid), chunk(128, 4 * channels),
        ),
        scratch_shapes=[
            pltpu.VMEM((SIDE + 6, SIDE + 6, 8, channels), F32),
            pltpu.VMEM((SIDE, SIDE, 8, channels), F32),
            pltpu.VMEM((SIDE // 2, 2, SIDE // 2, 2, 8, channels), F32),
            pltpu.VMEM((128, 4 * channels), F32),
            *pixel_scratch,
        ],
        compiler_params=params_of(),
        cost_estimate=takes(2.7),
        name="stem",
    )(got, dw_weight, gain, up_weight, proj_turned, scale, low_gain, ds_turned)

    feats_band = jnp.concatenate([feats, swapped(feats, "chan", 1)], axis=0)
    spread, below = pl.pallas_call(
        lambda *refs: spread_kernel(*refs, last=out_rows),
        grid=(blocks,),
        out_shape=(
            jax.ShapeDtypeStruct((blocks * 72, e_half), F32),
            jax.ShapeDtypeStruct((e_half, cols), F32),
        ),
        in_specs=[
            chunk(FEAT_ROWS, 128), whole(agg_weight.shape),
            pl.BlockSpec((72, cols), lambda g: (g, 0)),
        ],
        out_specs=(pl.BlockSpec((72, e_half), lambda g: (g, 0)), whole((e_half, cols))),
        compiler_params=params_of(),
        cost_estimate=takes(1.0),
        name="spread",
    )(feats_band, agg_weight, key)
    tile_blocks = jnp.concatenate([feats, cots_own, cots_peer], axis=1)
    gather = chunks == 1
    near = far = tile_blocks
    place = jnp.zeros((1,), jnp.int32)
    spans = [("slide", 1 << n) for n in range(bands.bit_length() - 1)]
    spans += [("rep", 1 << n) for n in range(lax.axis_size("rep").bit_length() - 1)]

    def widen(n, near, place):
        axis, step = spans[n]
        bit = (lax.axis_index(axis).astype(jnp.int32) // step) % 2
        return swapped(near, axis, step), place + bit * (1 << n)

    if gather:
        far, place = widen(0, near, place)
        near = jnp.concatenate([near, far], axis=0)

    keep, send = pl.pallas_call(
        lambda *refs: back_kernel(*refs, scale=loss_scale),
        grid=(chunks,),
        out_shape=(
            jax.ShapeDtypeStruct((HALF_ROWS, 128), F32),
            jax.ShapeDtypeStruct((HALF_ROWS, 128), BF16),
        ),
        in_specs=[
            SMEM, chunk(COT_ROWS, 128), chunk(COT_ROWS, 128),
            whole(agg_weight.shape), whole(agg_weight.shape), pixel_spec,
            chunk(rows, channels), chunk(rows, 1), chunk(rows, channels), chunk(rows, 1),
            chunk(rows, hid), chunk(rows, hid), chunk(128, 4 * channels),
            whole((1, channels)), whole(up_weight.shape), whole(proj_turned.shape),
            whole((1, channels)), whole((1, channels)), whole(ds_turned.shape),
        ],
        out_specs=(whole((HALF_ROWS, 128)), whole((HALF_ROWS, 128))),
        scratch_shapes=[
            pltpu.VMEM((SIDE + 6, SIDE + 6, 8, channels), F32),
            pltpu.VMEM((SIDE // 2, 2, SIDE // 2, 2, 8, channels), F32),
            pltpu.VMEM((SIDE, SIDE, 8, channels), F32),
            pltpu.VMEM((7, 7, 8, channels), F32),
            pltpu.VMEM(ds_turned.shape, F32),
            pltpu.VMEM(up_weight.shape, F32),
            pltpu.VMEM(proj_turned.shape, F32),
            pltpu.VMEM((2 * HALF_ROWS, 128), F32),
            *pixel_scratch,
            pltpu.VMEM((9, width, 256), BF16),
        ],
        compiler_params=params_of(),
        cost_estimate=takes(3.7),
        name="stem_back",
    )(
        chan, cots_own, cots_peer, agg_weight, peer_weight, got,
        hat1, rstd1, hat2, rstd2, hidden, slope, patches,
        gain, up_weight, proj_turned, scale, low_gain, ds_turned,
    )

    part = keep + swapped(send, "chan", 1).astype(F32)
    if gather:
        part, near, spread, below = lax.optimization_barrier((part, near, spread, below))
    above = shifted(below, "slide", 1)
    steps = []
    for axis in ("rep", "slide"):
        step = 1
        while step < lax.axis_size(axis):
            steps.append((axis, step))
            step *= 2
    for n, (axis, step) in enumerate(steps):
        wire = part.astype(BF16)
        part = wire.astype(F32) + swapped(wire, axis, step).astype(F32)
    map_call = pl.pallas_call(
        map_kernel,
        out_shape=jax.ShapeDtypeStruct((out_rows, e_half, cols), BF16),
        in_specs=[VMEM, VMEM, VMEM],
        out_specs=VMEM,
        compiler_params=pltpu.CompilerParams(vmem_limit_bytes=24 << 20),
        cost_estimate=takes(3.5),
        name="agg_map",
    )

    for n in range(1, len(spans) if gather else 0):
        if n == len(spans) - 1:
            near, above = lax.optimization_barrier((near, above))
        far, place = widen(n, near, place)
        if n < len(spans) - 1:
            near = jnp.concatenate([near, far], axis=0)

    agg_map = map_call(spread, key, above)
    if gather:
        far, agg_map = lax.optimization_barrier((far, agg_map))
    count = 2 * near.shape[0] if gather else chunks
    per = count if gather else 1
    near_count = near.shape[0] if gather else 1
    agg_keep, agg_send = pl.pallas_call(
        lambda *refs: weight_kernel(*refs, scale=loss_scale),
        grid=(count // per,),
        out_shape=(
            jax.ShapeDtypeStruct((9, width, e_half), F32),
            jax.ShapeDtypeStruct((9, width, e_half), BF16),
        ),
        in_specs=[
            SMEM,
            pl.BlockSpec((near_count, BLOCK_ROWS, 128), lambda g: (g, 0, 0)),
            pl.BlockSpec((near_count, BLOCK_ROWS, 128), lambda g: (g, 0, 0)),
        ],
        out_specs=(whole((9, width, e_half)), whole((9, width, e_half))),
        scratch_shapes=[
            pltpu.VMEM((16, per * 8, width), F32),
            pltpu.VMEM((9, per * 8, 256), F32),
            pltpu.VMEM((9, width, e_half), F32),
        ],
        compiler_params=params_of(),
        cost_estimate=takes(1.4),
        name="agg_weight_grad",
    )(place, near, far)
    agg_grad = agg_keep + swapped(agg_send, "chan", 1).astype(F32)
    if not gather:
        agg_grad = lax.psum(agg_grad, ("slide", "rep"))

    part = part.astype(BF16)
    peer_part = swapped(part, "chan", 1)
    part, agg_grad = lax.optimization_barrier((part, agg_grad))
    dw_grad, up_grad, proj_grad, ds_grad = pl.pallas_call(
        unpack_kernel,
        out_shape=(
            jax.ShapeDtypeStruct(dw_weight.shape, F32),
            jax.ShapeDtypeStruct(up_weight.shape, F32),
            jax.ShapeDtypeStruct(proj_turned.shape, F32),
            jax.ShapeDtypeStruct(ds_turned.shape, F32),
        ),
        in_specs=[SMEM, VMEM, VMEM],
        out_specs=(VMEM, VMEM, VMEM, VMEM),
        scratch_shapes=[pltpu.VMEM((2 * HALF_ROWS, 128), F32)],
        compiler_params=pltpu.CompilerParams(vmem_limit_bytes=24 << 20),
        cost_estimate=takes(1.5),
        name="unpack",
    )(chan, part, peer_part)
    proj_grad = proj_grad.T
    ds_grad = ds_grad.T
    return (agg_map[None], agg_grad, dw_grad, up_grad, proj_grad, ds_grad)


def solution(mesh):
    in_specs = (
        P(("groups", "rep"), ("slide", "chan"), None),
        P(("groups", "rep"), ("slide", "chan")),
        P(("groups", "rep"), "slide", "chan", None),
        P(), P(), P(), P(), P(), P(), P(),
        P(None, None, "chan"),
    )
    out_specs = (
        P(("groups", "rep"), "slide", "chan", None),
        P("groups", None, "chan"),
        P("groups", None),
        P("groups", None),
        P("groups", None),
        P("groups", None),
    )
    return jax.shard_map(
        on_device, mesh=mesh, in_specs=in_specs, out_specs=out_specs, check_vma=False
    )
```

```python
import math

import jax
import jax.numpy as jnp
from jax import lax
from jax.experimental import pallas as pl
from jax.experimental.pallas import tpu as pltpu
from jax.sharding import PartitionSpec as P

SIDE = 8
CAP = 2
PIX = SIDE * SIDE
HALF_ROWS = 608
FEAT_ROWS = 192
COT_ROWS = 72
WIRE_ROWS = 56
BLOCK_ROWS = FEAT_ROWS + 2 * COT_ROWS
F32 = jnp.float32
BF16 = jnp.bfloat16
VMEM = pl.BlockSpec(memory_space=pltpu.VMEM)
SMEM = pl.BlockSpec(memory_space=pltpu.SMEM)


def params_of(steps=1):
    return pltpu.CompilerParams(
        dimension_semantics=("arbitrary",) * steps, vmem_limit_bytes=24 << 20
    )


def takes(microseconds):
    return pl.CostEstimate(
        flops=0, transcendentals=0, bytes_accessed=int(microseconds * 3.69e6)
    )


def nn(left, right):
    return lax.dot_general(left, right, (((1,), (0,)), ((), ())), preferred_element_type=F32)


def nt(left, right):
    return lax.dot_general(left, right, (((1,), (1,)), ((), ())), preferred_element_type=F32)


def tn(left, right):
    return lax.dot_general(left, right, (((0,), (0,)), ((), ())), preferred_element_type=F32)


def shifted(value, axis, steps):
    count = lax.axis_size(axis)
    first, last = (max(0, -steps), min(count, count - steps))
    return lax.ppermute(value, axis, [(source, source + steps) for source in range(first, last)])


def swapped(value, axis, step):
    count = lax.axis_size(axis)
    return lax.ppermute(value, axis, [(place, place ^ step) for place in range(count)])


def reach(tap):
    return (1, 2) if tap == 0 else (0, 1)


def pack_kernel(cells_ref, pixels_ref, row_ref, out_ref, below_ref, wide_ref, note_ref):
    slots = pixels_ref.shape[0]
    rows = out_ref.shape[0]
    pixch = pixels_ref.shape[1]
    cells = [cells_ref[0, t] for t in range(slots)]
    live = [cell >= 0 for cell in cells]
    bands = [cell >> 9 for cell in cells]
    places = []
    for t in range(slots):
        rank = jnp.int32(0)
        for s in range(t):
            rank = rank + ((bands[s] == bands[t]) & live[s]).astype(jnp.int32)
        places.append(jnp.where(live[t], bands[t] * CAP + rank, -1))
    below_ref[...] = row_ref[...].astype(BF16)
    pixels = pixels_ref[...].astype(F32)
    for n in range(pixch // 128):
        wide_ref[:, n, :] = pixels[:, 128 * n : 128 * n + 128]
    wide_ref[:, pixch // 128 :, :] = jnp.zeros_like(wide_ref[:, pixch // 128 :, :])
    out_ref[...] = jnp.zeros_like(out_ref)
    for t in range(slots):

        @pl.when(live[t])
        def _():
            out_ref[jnp.maximum(places[t], 0)] = wide_ref[t].astype(BF16)

    lane = lax.broadcasted_iota(jnp.int32, (rows, 128), 1)
    base = (lax.broadcasted_iota(jnp.int32, (rows, 128), 0) // CAP) * CAP
    notes = jnp.zeros((rows, 128), F32)
    for t in range(slots):
        own_row = ((cells[t] >> 6) & 7).astype(F32)
        own_col = (cells[t] & 63).astype(F32)
        for rank in range(CAP):
            hit = base + rank == places[t]
            for at, value in enumerate((own_row, own_col, jnp.float32(1.0))):
                notes = jnp.where(hit & (lane == 3 * rank + at), value, notes)
    note_ref[...] = jnp.zeros_like(note_ref)
    note_ref[:, 0, :] = notes
    out_ref[:, pixch // 128 :, :] = note_ref[...].astype(BF16)


def patch_kernel(chan_ref, meta_ref, cot_ref, below_ref, key_ref, own_ref, send_ref, meta_f32):
    sources = meta_ref.shape[0]
    chunks = sources // 8
    out_rows, e_half, _ = cot_ref.shape
    meta_f32[...] = meta_ref[...].astype(F32)
    meta = meta_f32[:, 0, :]
    first = chan_ref[0] == 0
    lane = lax.broadcasted_iota(jnp.int32, (8, 128), 1).astype(F32)
    blocks = []
    for mine in (True, False):
        for chunk in range(chunks):
            part = meta[chunk * 8 : chunk * 8 + 8]
            low = [jnp.broadcast_to(part[:, n : n + 1], (8, 128)) for n in range(3)]
            high = [jnp.broadcast_to(part[:, n : n + 1], (8, 128)) for n in range(3, 6)]
            row, col, valid = (
                jnp.where(first == mine, one, two) for one, two in zip(low, high)
            )
            for u in range(3):
                for v in range(3):
                    hit = (lane == 2.0 * col + v) & (valid > 0.5)
                    blocks.append(jnp.where(hit, 2.0 * row + u, -1.0))
    key = jnp.concatenate(blocks, axis=0)
    key_ref[...] = key

    total = jnp.zeros((key.shape[0], e_half), F32)
    for first_row in range(0, out_rows, 4):
        rows = range(first_row, first_row + 4)
        picks = [(key == float(o)).astype(F32).astype(BF16) for o in rows]
        cots = [cot_ref[o].astype(BF16) for o in rows]
        total = total + nt(jnp.concatenate(picks, axis=1), jnp.concatenate(cots, axis=1))
    pick = (key == float(out_rows)).astype(F32).astype(BF16)
    total = total + nt(pick, below_ref[...])
    half = total.shape[0] // 2
    own_ref[...] = jnp.zeros_like(own_ref)
    send_ref[...] = jnp.zeros_like(send_ref)
    own_ref[:, :e_half] = total[:half].astype(BF16)
    send_ref[:, :e_half] = total[half:].astype(BF16)


def center_of(values):
    center = values - jnp.mean(values, axis=-1, keepdims=True)
    rstd = lax.rsqrt(jnp.mean(center * center, axis=-1, keepdims=True) + 1e-06)
    return center * rstd, rstd


def fill_padded(padded_ref, got_ref, wide_ref, pixels_ref, channels):
    wide_ref[...] = got_ref[...].astype(F32)
    for n in range(pixels_ref.shape[1] // 128):
        pixels_ref[:, 128 * n : 128 * n + 128] = wide_ref[:, n, :]
    padded_ref[...] = jnp.zeros_like(padded_ref)
    for i in range(SIDE):
        for j in range(SIDE):
            at = (i * SIDE + j) * channels
            padded_ref[i + 3, j + 3] = pixels_ref[:, at : at + channels]


def stem_kernel(
    got_ref, dw_ref, gain_ref, up_ref, proj_ref, scale_ref, ds_gain_ref, ds_ref,
    feat_ref, hat1_ref, rstd1_ref, hat2_ref, rstd2_ref, hidden_ref, slope_ref, patch_ref,
    padded_ref, spatial_ref, low_ref, patch_f32, wide_ref, pixels_ref,
):
    channels = dw_ref.shape[1]
    fill_padded(padded_ref, got_ref, wide_ref, pixels_ref, channels)

    for i in range(SIDE):
        total = jnp.zeros((SIDE, 8, channels), F32)
        for a in range(max(0, 3 - i), min(7, SIDE + 3 - i)):
            for b in range(7):
                weight = dw_ref[7 * a + b : 7 * a + b + 1, :].reshape(1, 1, channels)
                total = total + weight * padded_ref[i + a, b : b + SIDE]
        spatial_ref[i] = total
    hat1, rstd1 = center_of(spatial_ref[...].reshape(PIX * 8, channels))
    hat1_ref[...] = hat1
    rstd1_ref[...] = rstd1
    normed = (hat1 * gain_ref[...]).astype(BF16)
    before = nn(normed, up_ref[...])
    cdf = 0.5 * (1.0 + lax.erf(before * math.sqrt(0.5)))
    pdf = jnp.exp(-0.5 * before * before) * (1.0 / math.sqrt(2.0 * math.pi))
    hidden = (before * cdf).astype(BF16)
    hidden_ref[...] = hidden
    slope_ref[...] = cdf + before * pdf
    branch = nt(hidden, proj_ref[...])
    inputs = padded_ref[3 : 3 + SIDE, 3 : 3 + SIDE].reshape(PIX * 8, channels)
    hat2, rstd2 = center_of(inputs + scale_ref[...] * branch)
    hat2_ref[...] = hat2
    rstd2_ref[...] = rstd2
    low_ref[...] = (hat2 * ds_gain_ref[...]).reshape(low_ref.shape)
    half = SIDE // 2
    for di in range(2):
        for dj in range(2):
            at = (2 * di + dj) * channels
            patch_f32[:, at : at + channels] = low_ref[:, di, :, dj].reshape(-1, channels)
    patches = patch_f32[...].astype(BF16)
    patch_ref[...] = patches
    total = nt(patches, ds_ref[...])
    rows = total.shape[0]
    feat_ref[0:rows] = total[:, 0:128].astype(BF16)
    rest = jnp.concatenate([total[: rows // 2, 128:192], total[rows // 2 :, 128:192]], axis=1)
    feat_ref[rows:] = rest.astype(BF16)


def unfold(block):
    rest = block[128:]
    return jnp.concatenate(
        [block[:128], jnp.concatenate([rest[:, :64], rest[:, 64:]], axis=0)], axis=1
    )


def back_kernel(
    chan_ref, own_ref, peer_ref, w_own_ref, w_peer_ref, got_ref,
    hat1_ref, rstd1_ref, hat2_ref, rstd2_ref, hidden_ref, slope_ref, patch_ref,
    gain_ref, up_ref, proj_ref, scale_ref, ds_gain_ref, ds_ref,
    keep_ref, send_ref,
    padded_ref, dlow_ref, dspatial_ref, dw_ref, ds_acc, up_acc, proj_acc, pack_ref,
    wide_ref, pixels_ref, w_ref,
    *, scale,
):
    channels = gain_ref.shape[1]
    half = SIDE // 2
    step = pl.program_id(0)

    @pl.when(step == 0)
    def _():
        dw_ref[...] = jnp.zeros_like(dw_ref)
        ds_acc[...] = jnp.zeros_like(ds_acc)
        up_acc[...] = jnp.zeros_like(up_acc)
        proj_acc[...] = jnp.zeros_like(proj_acc)

    e_half = w_own_ref.shape[2]
    w_ref[...] = jnp.zeros_like(w_ref)
    w_ref[:, :, 0:e_half] = w_own_ref[...]
    w_ref[:, :, 128 : 128 + e_half] = w_peer_ref[...]
    cots = jnp.concatenate([own_ref[...], peer_ref[...]], axis=1)
    grads = {}
    for a in range(3):
        for b in range(3):
            out = nt(cots, w_ref[3 * a + b])
            for u in reach(a):
                for v in reach(b):
                    at = (2 * u + a - 1) * half + 2 * v + b - 1
                    row = 8 * (3 * u + v)
                    piece = out[row : row + 8]
                    grads[at] = grads[at] + piece if at in grads else piece
    dfeat = jnp.concatenate([grads[at] for at in range(half * half)], axis=0) * scale
    dfeat = dfeat.astype(BF16)

    hat2 = hat2_ref[...]
    ds_acc[...] += tn(dfeat, patch_ref[...])
    back = nn(dfeat, ds_ref[...])
    for di in range(2):
        for dj in range(2):
            at = (2 * di + dj) * channels
            dlow_ref[:, di, :, dj] = back[:, at : at + channels].reshape(half, half, 8, channels)
    dhat2 = dlow_ref[...].reshape(PIX * 8, channels) * ds_gain_ref[...]
    mean_a = jnp.mean(dhat2, axis=-1, keepdims=True)
    mean_b = jnp.mean(dhat2 * hat2, axis=-1, keepdims=True)
    dmixed = rstd2_ref[...] * (dhat2 - mean_a - hat2 * mean_b)
    dbranch = (dmixed * scale_ref[...]).astype(BF16)
    proj_acc[...] += tn(dbranch, hidden_ref[...])
    dhidden = nn(dbranch, proj_ref[...])
    dbefore = (dhidden * slope_ref[...]).astype(BF16)
    hat1 = hat1_ref[...]
    normed = (hat1 * gain_ref[...]).astype(BF16)
    up_acc[...] += tn(normed, dbefore)
    dhat1 = nt(dbefore, up_ref[...]) * gain_ref[...]
    mean_a = jnp.mean(dhat1, axis=-1, keepdims=True)
    mean_b = jnp.mean(dhat1 * hat1, axis=-1, keepdims=True)
    dspatial = rstd1_ref[...] * (dhat1 - mean_a - hat1 * mean_b)
    dspatial_ref[...] = dspatial.reshape(SIDE, SIDE, 8, channels)
    fill_padded(padded_ref, got_ref, wide_ref, pixels_ref, channels)

    for a in range(7):
        totals = [jnp.zeros((8, channels), F32) for _ in range(7)]
        for i in range(max(0, 3 - a), min(SIDE, SIDE + 3 - a)):
            for b in range(7):
                low, high = max(0, 3 - b), min(SIDE, SIDE + 3 - b)
                product = padded_ref[i + a, b + low : b + high] * dspatial_ref[i, low:high]
                totals[b] = totals[b] + jnp.sum(product, axis=0)
        for b in range(7):
            dw_ref[a, b] += totals[b]

    @pl.when(step == pl.num_programs(0) - 1)
    def _():
        pack_ref[...] = jnp.zeros_like(pack_ref)
        for n in range(3):
            lanes = slice(128 * n, 128 * n + 128)
            pack_ref[192 * n : 192 * n + 192, :] = ds_acc[:, lanes]
            pack_ref[576 + 96 * n : 672 + 96 * n, :] = up_acc[:, lanes]
            pack_ref[864 + 96 * n : 960 + 96 * n, :] = proj_acc[:, lanes]
        pack_ref[1152:1201, 0:channels] = jnp.sum(dw_ref[...], axis=2).reshape(49, channels)
        mine = pl.multiple_of(chan_ref[0] * HALF_ROWS, 8)
        other = pl.multiple_of((1 - chan_ref[0]) * HALF_ROWS, 8)
        keep_ref[...] = pack_ref[pl.ds(mine, HALF_ROWS), :]
        send_ref[...] = pack_ref[pl.ds(other, HALF_ROWS), :].astype(BF16)


def unpack_kernel(chan_ref, own_ref, peer_ref, dw_ref, up_ref, proj_ref, ds_ref, pack_ref):
    channels = dw_ref.shape[1]
    mine = pl.multiple_of(chan_ref[0] * HALF_ROWS, 8)
    other = pl.multiple_of((1 - chan_ref[0]) * HALF_ROWS, 8)
    pack_ref[pl.ds(mine, HALF_ROWS), :] = own_ref[...].astype(F32)
    pack_ref[pl.ds(other, HALF_ROWS), :] = peer_ref[...].astype(F32)
    for n in range(3):
        lanes = slice(128 * n, 128 * n + 128)
        ds_ref[:, lanes] = pack_ref[192 * n : 192 * n + 192, :]
        up_ref[:, lanes] = pack_ref[576 + 96 * n : 672 + 96 * n, :]
        proj_ref[:, lanes] = pack_ref[864 + 96 * n : 960 + 96 * n, :]
    dw_ref[...] = pack_ref[1152:1201, 0:channels]


def spread_kernel(feat_ref, w_ref, key_ref, y_ref, below_ref, *, last):
    width = w_ref.shape[1]
    feats = unfold(feat_ref[...].astype(F32)).reshape(16, 8, width)
    outs = {}
    for a in range(3):
        for b in range(3):
            places = [(u, v) for u in reach(a) for v in reach(b)]
            left = jnp.concatenate(
                [feats[(2 * u + a - 1) * 4 + 2 * v + b - 1] for u, v in places], axis=0
            ).astype(BF16)
            out = nn(left, w_ref[3 * a + b])
            for n, (u, v) in enumerate(places):
                piece = out[8 * n : 8 * n + 8]
                at = 3 * u + v
                outs[at] = outs[at] + piece if at in outs else piece
    total = jnp.concatenate([outs[at] for at in range(9)], axis=0)
    y_ref[...] = total
    pick = (key_ref[...] == float(last)).astype(F32).astype(BF16)
    high = total.astype(BF16)
    rest = (total - high.astype(F32)).astype(BF16)

    @pl.when(pl.program_id(0) == 0)
    def _():
        below_ref[...] = jnp.zeros_like(below_ref)

    below_ref[...] += tn(high, pick) + tn(rest, pick)


def map_kernel(y_ref, key_ref, above_ref, out_ref):
    out_rows, width, _ = out_ref.shape
    turned = y_ref[...].T
    high = turned.astype(BF16)
    rest = (turned - high.astype(F32)).astype(BF16)
    key = key_ref[...]

    def row_of(o):
        pick = (key == o).astype(F32).astype(BF16)
        return nn(high, pick) + nn(rest, pick)

    out_ref[0] = (row_of(0.0) + above_ref[...]).astype(BF16)

    def step(o, carry):
        out_ref[o] = row_of(o.astype(F32)).astype(BF16)
        return carry

    lax.fori_loop(1, out_rows, step, 0)


def weight_kernel(
    place_ref, near_ref, far_ref, keep_ref, send_ref, feat_ref, cot_ref, send_acc, *, scale
):
    near = near_ref.shape[0]
    members = feat_ref.shape[1] // 8
    width, e_half = keep_ref.shape[1:]
    step = pl.program_id(0)

    @pl.when(step == 0)
    def _():
        keep_ref[...] = jnp.zeros_like(keep_ref)
        send_acc[...] = jnp.zeros_like(send_acc)

    def take(member, block):
        block = block.astype(F32)
        feat_ref[:, 8 * member : 8 * member + 8] = unfold(block[:FEAT_ROWS]).reshape(16, 8, width)
        own = block[FEAT_ROWS : FEAT_ROWS + COT_ROWS].reshape(9, 8, 128)
        peer = block[FEAT_ROWS + COT_ROWS :].reshape(9, 8, 128)
        cot_ref[:, 8 * member : 8 * member + 8, 0:128] = own
        cot_ref[:, 8 * member : 8 * member + 8, 128:256] = peer

    for member in range(members):
        at = place_ref[0] ^ member

        @pl.when(at < near)
        def _():
            take(member, near_ref[jnp.minimum(at, near - 1)])

        if members > near:

            @pl.when(at >= near)
            def _():
                take(member, far_ref[jnp.maximum(at - near, 0)])

    for a in range(3):
        for b in range(3):
            places = [(u, v) for u in reach(a) for v in reach(b)]
            left = jnp.concatenate(
                [feat_ref[(2 * u + a - 1) * 4 + 2 * v + b - 1] for u, v in places], axis=0
            ).astype(BF16)
            right = jnp.concatenate([cot_ref[3 * u + v] for u, v in places], axis=0).astype(BF16)
            total = tn(left, right) * scale
            keep_ref[3 * a + b] += total[:, :e_half]
            send_acc[3 * a + b] += total[:, 128 : 128 + e_half]

    @pl.when(step == pl.num_programs(0) - 1)
    def _():
        send_ref[...] = send_acc[...].astype(BF16)


def whole(shape):
    return pl.BlockSpec(shape, lambda g: (0,) * len(shape))


def on_device(
    tile_pixels, tile_cell, agg_cot, dw_weight, norm_gain, up_weight, proj_weight,
    layer_scale, ds_gain, ds_weight, agg_weight,
):
    channels = dw_weight.shape[1]
    hid = up_weight.shape[1]
    width = ds_weight.shape[1]
    bands = lax.axis_size("slide")
    sources = bands * lax.axis_size("chan")
    chunks = sources // 8
    pixch = tile_pixels.shape[2]
    out_rows = agg_cot.shape[1]
    e_half = agg_weight.shape[2]
    cols = agg_cot.shape[3]
    blocks = CAP * chunks
    total_rows = out_rows * bands * lax.axis_size("rep") * cols
    loss_scale = 1.0 / math.sqrt(total_rows)
    chan = lax.axis_index("chan").astype(jnp.int32)[None]
    gain = norm_gain[None]
    scale = layer_scale[None]
    low_gain = ds_gain[None]
    proj_turned = proj_weight.T
    ds_turned = ds_weight.T

    packed, top_cot = pl.pallas_call(
        pack_kernel,
        grid=(1,),
        out_shape=(
            jax.ShapeDtypeStruct((sources, WIRE_ROWS, 128), BF16),
            jax.ShapeDtypeStruct((e_half, cols), BF16),
        ),
        in_specs=[
            SMEM,
            pl.BlockSpec((None,) + tile_pixels.shape[1:], lambda i: (0, 0, 0)),
            pl.BlockSpec((None, None, e_half, cols), lambda i: (0, 0, 0, 0)),
        ],
        out_specs=(whole((sources, WIRE_ROWS, 128)), whole((e_half, cols))),
        scratch_shapes=[
            pltpu.VMEM((tile_pixels.shape[1], WIRE_ROWS, 128), F32),
            pltpu.VMEM((sources, 8, 128), F32),
        ],
        cost_estimate=takes(1.5),
        name="pack",
    )(tile_cell, tile_pixels, agg_cot)
    below_cot = shifted(top_cot, "slide", -1)
    packed, own_weight = lax.optimization_barrier((packed, agg_weight))
    peer_weight = swapped(own_weight, "chan", 1)
    got = lax.all_to_all(packed, ("slide", "chan"), split_axis=0, concat_axis=0, tiled=True)

    key, cots_own, cots_send = pl.pallas_call(
        patch_kernel,
        out_shape=(
            jax.ShapeDtypeStruct((blocks * COT_ROWS, cols), F32),
            jax.ShapeDtypeStruct((chunks * COT_ROWS, 128), BF16),
            jax.ShapeDtypeStruct((chunks * COT_ROWS, 128), BF16),
        ),
        in_specs=[
            SMEM,
            pl.BlockSpec((sources, 8, 128), lambda i: (0, pixch // 1024, 0)),
            pl.BlockSpec((None, out_rows, e_half, cols), lambda i: (0, 0, 0, 0)),
            whole((e_half, cols)),
        ],
        out_specs=(
            whole((blocks * COT_ROWS, cols)),
            whole((chunks * COT_ROWS, 128)),
            whole((chunks * COT_ROWS, 128)),
        ),
        grid=(1,),
        scratch_shapes=[pltpu.VMEM((sources, 8, 128), F32)],
        compiler_params=params_of(),
        cost_estimate=takes(1.2),
        name="patch",
    )(chan, got, agg_cot, below_cot)
    cots_peer = swapped(cots_send, "chan", 1)
    cots_own = cots_own.reshape(chunks, COT_ROWS, 128)
    cots_peer = cots_peer.reshape(chunks, COT_ROWS, 128)

    rows = PIX * 8
    pixel_spec = pl.BlockSpec((8, WIRE_ROWS, 128), lambda g: (g, 0, 0))
    pixel_scratch = [pltpu.VMEM((8, WIRE_ROWS, 128), F32), pltpu.VMEM((8, pixch), F32)]

    def chunk(*shape):
        return pl.BlockSpec((None,) + shape, lambda g: (g,) + (0,) * len(shape))

    feats, hat1, rstd1, hat2, rstd2, hidden, slope, patches = pl.pallas_call(
        stem_kernel,
        grid=(chunks,),
        out_shape=(
            jax.ShapeDtypeStruct((chunks, FEAT_ROWS, 128), BF16),
            jax.ShapeDtypeStruct((chunks, rows, channels), F32),
            jax.ShapeDtypeStruct((chunks, rows, 1), F32),
            jax.ShapeDtypeStruct((chunks, rows, channels), F32),
            jax.ShapeDtypeStruct((chunks, rows, 1), F32),
            jax.ShapeDtypeStruct((chunks, rows, hid), BF16),
            jax.ShapeDtypeStruct((chunks, rows, hid), F32),
            jax.ShapeDtypeStruct((chunks, 128, 4 * channels), BF16),
        ),
        in_specs=[
            pixel_spec,
            whole(dw_weight.shape), whole((1, channels)), whole(up_weight.shape),
            whole(proj_turned.shape), whole((1, channels)), whole((1, channels)),
            whole(ds_turned.shape),
        ],
        out_specs=(
            chunk(FEAT_ROWS, 128), chunk(rows, channels), chunk(rows, 1), chunk(rows, channels),
            chunk(rows, 1), chunk(rows, hid), chunk(rows, hid), chunk(128, 4 * channels),
        ),
        scratch_shapes=[
            pltpu.VMEM((SIDE + 6, SIDE + 6, 8, channels), F32),
            pltpu.VMEM((SIDE, SIDE, 8, channels), F32),
            pltpu.VMEM((SIDE // 2, 2, SIDE // 2, 2, 8, channels), F32),
            pltpu.VMEM((128, 4 * channels), F32),
            *pixel_scratch,
        ],
        compiler_params=params_of(),
        cost_estimate=takes(2.7),
        name="stem",
    )(got, dw_weight, gain, up_weight, proj_turned, scale, low_gain, ds_turned)

    feats_band = jnp.concatenate([feats, swapped(feats, "chan", 1)], axis=0)
    spread, below = pl.pallas_call(
        lambda *refs: spread_kernel(*refs, last=out_rows),
        grid=(blocks,),
        out_shape=(
            jax.ShapeDtypeStruct((blocks * 72, e_half), F32),
            jax.ShapeDtypeStruct((e_half, cols), F32),
        ),
        in_specs=[
            chunk(FEAT_ROWS, 128), whole(agg_weight.shape),
            pl.BlockSpec((72, cols), lambda g: (g, 0)),
        ],
        out_specs=(pl.BlockSpec((72, e_half), lambda g: (g, 0)), whole((e_half, cols))),
        compiler_params=params_of(),
        cost_estimate=takes(1.0),
        name="spread",
    )(feats_band, agg_weight, key)
    tile_blocks = jnp.concatenate([feats, cots_own, cots_peer], axis=1)
    gather = chunks == 1
    near = far = tile_blocks
    place = jnp.zeros((1,), jnp.int32)
    spans = [("slide", 1 << n) for n in reversed(range(bands.bit_length() - 1))]
    spans += [("rep", 1 << n) for n in range(lax.axis_size("rep").bit_length() - 1)]

    def widen(n, near, place):
        axis, step = spans[n]
        bit = (lax.axis_index(axis).astype(jnp.int32) // step) % 2
        return swapped(near, axis, step), place + bit * (1 << n)

    if gather:
        far, place = widen(0, near, place)
        near = jnp.concatenate([near, far], axis=0)

    keep, send = pl.pallas_call(
        lambda *refs: back_kernel(*refs, scale=loss_scale),
        grid=(chunks,),
        out_shape=(
            jax.ShapeDtypeStruct((HALF_ROWS, 128), F32),
            jax.ShapeDtypeStruct((HALF_ROWS, 128), BF16),
        ),
        in_specs=[
            SMEM, chunk(COT_ROWS, 128), chunk(COT_ROWS, 128),
            whole(agg_weight.shape), whole(agg_weight.shape), pixel_spec,
            chunk(rows, channels), chunk(rows, 1), chunk(rows, channels), chunk(rows, 1),
            chunk(rows, hid), chunk(rows, hid), chunk(128, 4 * channels),
            whole((1, channels)), whole(up_weight.shape), whole(proj_turned.shape),
            whole((1, channels)), whole((1, channels)), whole(ds_turned.shape),
        ],
        out_specs=(whole((HALF_ROWS, 128)), whole((HALF_ROWS, 128))),
        scratch_shapes=[
            pltpu.VMEM((SIDE + 6, SIDE + 6, 8, channels), F32),
            pltpu.VMEM((SIDE // 2, 2, SIDE // 2, 2, 8, channels), F32),
            pltpu.VMEM((SIDE, SIDE, 8, channels), F32),
            pltpu.VMEM((7, 7, 8, channels), F32),
            pltpu.VMEM(ds_turned.shape, F32),
            pltpu.VMEM(up_weight.shape, F32),
            pltpu.VMEM(proj_turned.shape, F32),
            pltpu.VMEM((2 * HALF_ROWS, 128), F32),
            *pixel_scratch,
            pltpu.VMEM((9, width, 256), BF16),
        ],
        compiler_params=params_of(),
        cost_estimate=takes(3.7),
        name="stem_back",
    )(
        chan, cots_own, cots_peer, agg_weight, peer_weight, got,
        hat1, rstd1, hat2, rstd2, hidden, slope, patches,
        gain, up_weight, proj_turned, scale, low_gain, ds_turned,
    )

    part = keep + swapped(send, "chan", 1).astype(F32)
    if gather:
        part, near, spread, below = lax.optimization_barrier((part, near, spread, below))
    above = shifted(below, "slide", 1)
    for n in range(1, len(spans) if gather else 0):
        far, place = widen(n, near, place)
        if n < len(spans) - 1:
            near = jnp.concatenate([near, far], axis=0)
    map_call = pl.pallas_call(
        map_kernel,
        out_shape=jax.ShapeDtypeStruct((out_rows, e_half, cols), BF16),
        in_specs=[VMEM, VMEM, VMEM],
        out_specs=VMEM,
        compiler_params=pltpu.CompilerParams(vmem_limit_bytes=24 << 20),
        cost_estimate=takes(3.5),
        name="agg_map",
    )
    agg_map = map_call(spread, key, above)

    steps = []
    for axis in ("rep", "slide"):
        for n in reversed(range(lax.axis_size(axis).bit_length() - 1)):
            steps.append((axis, 1 << n))
    for n, (axis, step) in enumerate(steps):
        wire = part.astype(BF16)
        if n == len(steps) - 1:
            wire, agg_map = lax.optimization_barrier((wire, agg_map))
        part = wire.astype(F32) + swapped(wire, axis, step).astype(F32)

    count = 2 * near.shape[0] if gather else chunks
    per = count if gather else 1
    near_count = near.shape[0] if gather else 1
    agg_keep, agg_send = pl.pallas_call(
        lambda *refs: weight_kernel(*refs, scale=loss_scale),
        grid=(count // per,),
        out_shape=(
            jax.ShapeDtypeStruct((9, width, e_half), F32),
            jax.ShapeDtypeStruct((9, width, e_half), BF16),
        ),
        in_specs=[
            SMEM,
            pl.BlockSpec((near_count, BLOCK_ROWS, 128), lambda g: (g, 0, 0)),
            pl.BlockSpec((near_count, BLOCK_ROWS, 128), lambda g: (g, 0, 0)),
        ],
        out_specs=(whole((9, width, e_half)), whole((9, width, e_half))),
        scratch_shapes=[
            pltpu.VMEM((16, per * 8, width), F32),
            pltpu.VMEM((9, per * 8, 256), F32),
            pltpu.VMEM((9, width, e_half), F32),
        ],
        compiler_params=params_of(),
        cost_estimate=takes(1.4),
        name="agg_weight_grad",
    )(place, near, far)
    agg_grad = agg_keep + swapped(agg_send, "chan", 1).astype(F32)
    if not gather:
        agg_grad = lax.psum(agg_grad, ("slide", "rep"))

    part = part.astype(BF16)
    peer_part = swapped(part, "chan", 1)
    part, agg_grad = lax.optimization_barrier((part, agg_grad))
    dw_grad, up_grad, proj_grad, ds_grad = pl.pallas_call(
        unpack_kernel,
        out_shape=(
            jax.ShapeDtypeStruct(dw_weight.shape, F32),
            jax.ShapeDtypeStruct(up_weight.shape, F32),
            jax.ShapeDtypeStruct(proj_turned.shape, F32),
            jax.ShapeDtypeStruct(ds_turned.shape, F32),
        ),
        in_specs=[SMEM, VMEM, VMEM],
        out_specs=(VMEM, VMEM, VMEM, VMEM),
        scratch_shapes=[pltpu.VMEM((2 * HALF_ROWS, 128), F32)],
        compiler_params=pltpu.CompilerParams(vmem_limit_bytes=24 << 20),
        cost_estimate=takes(1.5),
        name="unpack",
    )(chan, part, peer_part)
    proj_grad = proj_grad.T
    ds_grad = ds_grad.T
    return (agg_map[None], agg_grad, dw_grad, up_grad, proj_grad, ds_grad)


def solution(mesh):
    in_specs = (
        P(("groups", "rep"), ("slide", "chan"), None),
        P(("groups", "rep"), ("slide", "chan")),
        P(("groups", "rep"), "slide", "chan", None),
        P(), P(), P(), P(), P(), P(), P(),
        P(None, None, "chan"),
    )
    out_specs = (
        P(("groups", "rep"), "slide", "chan", None),
        P("groups", None, "chan"),
        P("groups", None),
        P("groups", None),
        P("groups", None),
        P("groups", None),
    )
    return jax.shard_map(
        on_device, mesh=mesh, in_specs=in_specs, out_specs=out_specs, check_vma=False
    )
```
